32 devices in a mesh: dp: 8 (over z, y), seq: 4 (over x, core).
Axes of the slice: x: 2, y: 2, z: 4, core: 2. Of those that a mesh axis runs over, the one named last changes fastest.
Arguments:
- tokens: bfloat16 [24, 1024, 768], P('dp', 'seq'), may hold values from -6 to 6
- cotangent: bfloat16 [24, 1024, 768], P('dp', 'seq'), may hold values from -6 to 6
- lengths: int32 [24], P('dp'), may hold values from 128 to 1024, as said below
- block_perm: int32 [24, 2], P('dp'), may hold values from 0 to 1, each once within a row
- w_qkv: bfloat16 [768, 2304], replicated, may hold values from -0.21875 to 0.21875
- b_query: bfloat16 [768], replicated, may hold values from -1.75 to 1.75
- b_value: bfloat16 [768], replicated, may hold values from -0.3125 to 0.3125
- w_out: bfloat16 [768, 768], replicated, may hold values from -1.75 to 1.75
- b_out: bfloat16 [768], replicated, may hold values from -1.75 to 1.75
- ln1_gain: bfloat16 [768], replicated, may hold values from 0.099609375 to 1.8984375
- ln1_shift: bfloat16 [768], replicated, may hold values from -1.75 to 1.75
- w_up: bfloat16 [768, 3072], replicated, may hold values from -0.21875 to 0.21875
- b_up: bfloat16 [3072], replicated, may hold values from -1.75 to 1.75
- w_down: bfloat16 [3072, 768], replicated, may hold values from -0.109375 to 0.109375
- b_down: bfloat16 [768], replicated, may hold values from -1.75 to 1.75
- ln2_gain: bfloat16 [768], replicated, may hold values from 0.099609375 to 1.8984375
- ln2_shift: bfloat16 [768], replicated, may hold values from -1.75 to 1.75
Outputs:
- out_tokens: bfloat16 [24, 1024, 768], P('dp', 'seq')
- grad_tokens: float32 [24, 1024, 768], P('dp', 'seq')
- grad_w_qkv: float32 [768, 2304], replicated
- grad_b_query: float32 [768], replicated
- grad_b_value: float32 [768], replicated
- grad_w_out: float32 [768, 768], replicated
- grad_b_out: float32 [768], replicated
- grad_ln1_gain: float32 [768], replicated
- grad_ln1_shift: float32 [768], replicated
- grad_w_up: float32 [768, 3072], replicated
- grad_b_up: float32 [3072], replicated
- grad_w_down: float32 [3072, 768], replicated
- grad_b_down: float32 [768], replicated
- grad_ln2_gain: float32 [768], replicated
- grad_ln2_shift: float32 [768], replicated
The draws below stay inside these ranges and needn't reach their ends.
Inputs may be any that keep to these rules, and one draw needn't show every extreme that they name: `lengths`: every length is even; in each aligned group of 3 consecutive sequences, one has length 1024. `block_perm`: each row is 0, 1 or 1, 0.
All inputs are finite; a program needn't handle non-finite values.
Results may differ from the reference program's by a relative error of at most 0.017.
Values may be sent and summed in bfloat16 or wider, within the bound.
No kernel may reach another device: no remote copies, remote signals or barrier semaphores. Data moves between devices by JAX's collectives and lax.ppermute only.
A program may use at most 320 MiB of HBM per device.

```python
import jax
import jax.numpy as jnp
from jax import lax

D = 768
HEADS = 12
HEAD_DIM = 64
FF = 3072
L = 1024
LEN_MIN = 128
SEQ_GRP = 3
SEQUENCES = 24


def draw_lengths(key, part):
    groups = SEQUENCES // SEQ_GRP
    half_key = jax.random.fold_in(key, 11)
    pick_key = jax.random.fold_in(key, 23)
    halves = jax.random.randint(half_key, (groups, SEQ_GRP), LEN_MIN // 2, L // 2 + 1)
    chosen = jax.random.randint(pick_key, (groups, 1), 0, SEQ_GRP)
    full_row = jnp.arange(SEQ_GRP, dtype=jnp.int32)[None, :] == chosen
    return jnp.where(full_row, L, 2 * halves).reshape(SEQUENCES).astype(jnp.int32)


def shard_levels(key, dims, split, smallest, largest):
    loudness = 1.0
    for dim, blocks in split:
        heights = jax.random.uniform(jax.random.fold_in(jax.random.fold_in(key, 6), dim), (blocks,), jnp.float32, smallest / len(split), largest / len(split))
        loudness = loudness * jnp.repeat(jnp.exp(heights), dims[dim] // blocks).reshape((-1,) + (1,) * (len(dims) - 1 - dim))
    return loudness


def noise(own_key, shape, scale, reach, pieces=(), held_as=jnp.bfloat16):
    loudness = shard_levels(own_key, shape, pieces, -0.22, 0.18) if pieces else 1.0
    values = jax.random.normal(own_key, shape, jnp.float32) * scale * loudness
    return jnp.minimum(jnp.maximum(values, -reach), reach).astype(held_as)


def setup_inputs(seed: int = 0) -> dict:
    key_list = jax.random.split(jax.random.key(seed), 18)
    return {
        "tokens": noise(key_list[0], (SEQUENCES, L, D), 1.0, 6.0, ((0, 8), (1, 4))),
        "cotangent": noise(key_list[1], (SEQUENCES, L, D), 1.0, 6.0, ((0, 8), (1, 4))),
        "lengths": draw_lengths(jax.random.fold_in(key_list[17], 71), 0),
        "block_perm": jax.vmap(lambda own: jax.random.permutation(own, 2))(jax.random.split(key_list[3], SEQUENCES)).reshape((SEQUENCES, 2)).astype(jnp.int32),
        "w_qkv": noise(key_list[4], (D, 3 * D), D ** -0.5, 0.21875),
        "b_query": noise(key_list[5], (D,), 0.3, 1.75),
        "b_value": noise(key_list[6], (D,), 0.05, 0.3125),
        "w_out": noise(key_list[7], (D, D), (D // 64) ** -0.5, 1.75),
        "b_out": noise(key_list[8], (D,), 0.3, 1.75),
        "ln1_gain": jnp.clip(1.0 + 0.18 * jax.random.normal(key_list[9], (D,), jnp.float32), 0.099609375, 1.8984375).astype(jnp.bfloat16),
        "ln1_shift": noise(key_list[10], (D,), 0.3, 1.75),
        "w_up": noise(key_list[11], (D, FF), D ** -0.5, 0.21875),
        "b_up": noise(key_list[12], (FF,), 0.3, 1.75),
        "w_down": noise(key_list[13], (FF, D), FF ** -0.5, 0.109375),
        "b_down": noise(key_list[14], (D,), 0.3, 1.75),
        "ln2_gain": jnp.clip(1.0 + 0.18 * jax.random.normal(key_list[15], (D,), jnp.float32), 0.099609375, 1.8984375).astype(jnp.bfloat16),
        "ln2_shift": noise(key_list[16], (D,), 0.3, 1.75),
    }


EPSILON = 1e-06
NEGATIVE = -1e+30
HIGH = lax.Precision.HIGHEST

@jax.custom_vjp
def low(v):
    return lax.optimization_barrier(v.astype(jnp.bfloat16)).astype(jnp.float32)

@jax.custom_vjp
def low_back(v):
    return v

def low_keep(v):
    return (low(v), None)

def low_pass(kept, grad):
    return (grad,)

def back_keep(v):
    return (v, None)

def back_low(kept, grad):
    return (low(grad),)
low.defvjp(low_keep, low_pass)
low_back.defvjp(back_keep, back_low)

def matmul(left, right):
    return jnp.einsum('rd,de->re', left, right, precision=HIGH)

def norm_rows(array_in, gain_vec, shift_vec):
    row_mean = lax.optimization_barrier(jnp.mean(array_in, axis=-1, keepdims=True))
    centered = array_in - row_mean
    spread = lax.optimization_barrier(jnp.mean(centered * centered, axis=-1, keepdims=True))
    return centered * lax.rsqrt(spread + EPSILON) * gain_vec + shift_vec

def allowed_pairs(lengths, block_perm, query_pos, key_pos):
    seq_len = lengths[:, None]
    query_block = jnp.minimum(2 * query_pos[None, :] // seq_len, 1)
    target = jnp.where(query_block == 0, block_perm[:, 0:1], block_perm[:, 1:2])
    key_block = jnp.minimum(2 * key_pos[None, :] // seq_len, 1)
    key_live = key_pos[None, :] < seq_len
    return (key_block[:, None, :] == target[:, :, None]) & key_live[:, None, :]

def forward(x_in, w_qkv, b_query, b_value, w_out, b_out, ln1_gain, ln1_shift, w_up, b_up, w_down, b_down, ln2_gain, ln2_shift, live_mask, allowed):
    group, seq_len, features = x_in.shape
    token_rows = (x_in * live_mask).reshape(group * seq_len, features)
    projected = matmul(token_rows, w_qkv)
    queries = low_back(low(projected[:, :features] + b_query))
    key_rows = low_back(low(projected[:, features:2 * features]))
    value_rows = low_back(low(projected[:, 2 * features:] + b_value))

    def split_heads(array_in):
        return array_in.reshape(group, seq_len, HEADS, HEAD_DIM)
    scores = jnp.einsum('gqhe,gkhe->ghqk', split_heads(queries), split_heads(key_rows), precision=HIGH) * HEAD_DIM ** (-0.5)
    scores = low_back(scores)
    masked = jnp.where(allowed[:, None], scores, NEGATIVE)
    attn_probs = low(jax.nn.softmax(masked, axis=-1))
    context = jnp.einsum('ghqk,gkhe->gqhe', attn_probs, split_heads(value_rows), precision=HIGH)
    context = low_back(low(context.reshape(group * seq_len, features)))
    attended = low_back(matmul(context, w_out) + b_out)
    first_norm = norm_rows(token_rows + attended, ln1_gain, ln1_shift)
    lifted = low_back(matmul(low(first_norm), w_up) + b_up)
    active = low(jax.nn.gelu(lifted, approximate=False))
    lowered = low_back(matmul(active, w_down) + b_down)
    second_norm = norm_rows(first_norm + lowered, ln2_gain, ln2_shift)
    return second_norm * live_mask.reshape(group * seq_len, 1)

def reference(tokens, cotangent, lengths, block_perm, w_qkv, b_query, b_value, w_out, b_out, ln1_gain, ln1_shift, w_up, b_up, w_down, b_down, ln2_gain, ln2_shift):
    params = tuple((w.astype(jnp.float32) for w in (w_qkv, b_query, b_value, w_out, b_out, ln1_gain, ln1_shift, w_up, b_up, w_down, b_down, ln2_gain, ln2_shift)))
    group = SEQ_GRP
    steps_count = tokens.shape[0] // group
    positions = jnp.arange(L, dtype=jnp.int32)

    def one_group(totals, items):
        x_group, cot_group, len_group, perm_group = items
        live_mask = (positions[None, :] < len_group[:, None]).astype(jnp.float32)[:, :, None]
        allowed = allowed_pairs(len_group, perm_group, positions, positions)

        def run_layer(x_in, *weights):
            return forward(x_in, *weights, live_mask, allowed)
        result, pullback = jax.vjp(run_layer, x_group.astype(jnp.float32), *params)
        grads = pullback(cot_group.astype(jnp.float32).reshape(result.shape))
        totals = tuple((t + g for t, g in zip(totals, grads[1:])))
        return (totals, (result.reshape(x_group.shape).astype(jnp.bfloat16), grads[0]))
    zeros_init = tuple((jnp.zeros(w.shape, jnp.float32) for w in params))
    shaped = (tokens.reshape(steps_count, group, L, D), cotangent.reshape(steps_count, group, L, D), lengths.reshape(steps_count, group), block_perm.reshape(steps_count, group, 2))
    totals, (results, grad_in) = lax.scan(one_group, zeros_init, shaped)
    return (results.reshape(tokens.shape), grad_in.reshape(tokens.shape)) + totals
```

```python
from functools import partial

import jax
import jax.numpy as jnp
from jax import lax
from jax.experimental import pallas as pl
from jax.experimental.pallas import tpu as pltpu
from jax.sharding import PartitionSpec as P

HEADS = 12
HEAD_DIM = 64


EPSILON = 1e-06
NEGATIVE = -1e30


def norm_rows(array_in, gain_vec, shift_vec):
    row_mean = jnp.mean(array_in, axis=-1, keepdims=True)
    centered = array_in - row_mean
    spread = jnp.mean(centered * centered, axis=-1, keepdims=True)
    return centered * lax.rsqrt(spread + EPSILON) * gain_vec + shift_vec


def allowed_pairs(lengths, block_perm, query_pos, key_pos):
    seq_len = lengths[:, None]
    query_block = jnp.minimum(2 * query_pos[None, :] // seq_len, 1)
    target = jnp.where(query_block == 0, block_perm[:, 0:1], block_perm[:, 1:2])
    key_block = jnp.minimum(2 * key_pos[None, :] // seq_len, 1)
    key_live = key_pos[None, :] < seq_len
    return (key_block[:, None, :] == target[:, :, None]) & key_live[:, None, :]


def split_heads(array_in):
    return array_in.reshape(array_in.shape[0], array_in.shape[1], HEADS, HEAD_DIM)


def to_pieces(array_in, seq_parts):
    return array_in.reshape(
        array_in.shape[0], seq_parts, array_in.shape[1] // seq_parts, array_in.shape[2]
    )


def from_pieces(array_in):
    return array_in.reshape(
        array_in.shape[0], array_in.shape[1] * array_in.shape[2], array_in.shape[3]
    )


BITS = {"c": ("seq", 0), "x": ("seq", 1), "y": ("dp", 0), "l": ("dp", 1), "h": ("dp", 2)}


def own_bit(letter):
    axis, shift = BITS[letter]
    return (lax.axis_index(axis) >> shift) & 1


def own_number(order):
    number = jnp.int32(0)
    for letter in order:
        number = number * 2 + own_bit(letter)
    return number


def exchange_bit(array_in, axis, shift):
    count = lax.axis_size(axis)
    return lax.ppermute(array_in, axis, [(i, i ^ (1 << shift)) for i in range(count)])


def extra_bits():
    found = []
    for axis, used in (("seq", 2), ("dp", 3)):
        bits = lax.axis_size(axis).bit_length() - 1
        found += [(axis, shift) for shift in range(used, bits)]
    return found


def halve(array_in, order):
    for letter in order:
        half = array_in.shape[0] // 2
        array_in = array_in[:half] + exchange_bit(array_in[half:], *BITS[letter])
    for axis, shift in extra_bits():
        array_in = array_in + exchange_bit(array_in, axis, shift)
    return array_in


def double(array_in, order):
    for letter in reversed(order):
        array_in = jnp.concatenate([array_in, exchange_bit(array_in, *BITS[letter])])
    return array_in


def copy_block(source_ids, in_ref, out_ref):
    out_ref[...] = in_ref[...].reshape(out_ref.shape).astype(out_ref.dtype)


def to_relative(array_in, order, rows, cols):
    count = 1 << len(order)
    across = array_in.shape[1] // cols
    ids = jnp.arange(count, dtype=jnp.int32) ^ own_number(order)
    return pl.pallas_call(
        copy_block,
        out_shape=jax.ShapeDtypeStruct((count, rows, cols), jnp.bfloat16),
        grid_spec=pltpu.PrefetchScalarGridSpec(
            num_scalar_prefetch=1,
            grid=(count,),
            in_specs=[
                pl.BlockSpec((rows, cols), lambda p, ids: (ids[p] // across, ids[p] % across))
            ],
            out_specs=pl.BlockSpec((1, rows, cols), lambda p, ids: (p, 0, 0)),
        ),
    )(ids, array_in)


def from_relative(array_in, order, shape):
    count, rows, cols = array_in.shape
    across = shape[1] // cols
    ids = jnp.arange(count, dtype=jnp.int32) ^ own_number(order)
    return pl.pallas_call(
        copy_block,
        out_shape=jax.ShapeDtypeStruct(shape, jnp.float32),
        grid_spec=pltpu.PrefetchScalarGridSpec(
            num_scalar_prefetch=1,
            grid=(count,),
            in_specs=[pl.BlockSpec((1, rows, cols), lambda b, ids: (ids[b], 0, 0))],
            out_specs=pl.BlockSpec((rows, cols), lambda b, ids: (b // across, b % across)),
        ),
    )(ids, array_in)


def reduce_matrix(grad, order, rows, cols):
    return from_relative(
        double(halve(to_relative(grad, order, rows, cols), order), order), order, grad.shape
    )


def reduce_vectors(vectors):
    sizes = [v.shape[0] for v in vectors]
    packed = lax.psum(jnp.concatenate(vectors), ("dp", "seq"))
    starts = [sum(sizes[:i]) for i in range(len(sizes))]
    return [packed[a : a + n] for a, n in zip(starts, sizes)]


def per_device(
    tokens,
    cotangent,
    lengths,
    block_perm,
    w_qkv,
    b_query,
    b_value,
    w_out,
    b_out,
    ln1_gain,
    ln1_shift,
    w_up,
    b_up,
    w_down,
    b_down,
    ln2_gain,
    ln2_shift,
):
    seq_parts = lax.axis_size("seq")
    seq_index = lax.axis_index("seq")
    seq_count, local_rows, features = tokens.shape
    whole_len = local_rows * seq_parts
    piece_rows = local_rows // seq_parts
    flat_rows = seq_count * local_rows
    scaling = HEAD_DIM ** (-0.5)
    own_pos = seq_index * local_rows + jnp.arange(local_rows, dtype=jnp.int32)
    all_pos = jnp.arange(whole_len, dtype=jnp.int32)
    live_mask = own_pos[None, :] < lengths[:, None]
    masked_tokens = jnp.where(live_mask[:, :, None], tokens, jnp.zeros_like(tokens))
    token_rows = masked_tokens.reshape(flat_rows, features)
    projected = jnp.dot(token_rows, w_qkv, preferred_element_type=jnp.float32)
    queries = (
        (projected[:, :features] + b_query)
        .astype(jnp.bfloat16)
        .reshape(seq_count, local_rows, features)
    )
    key_rows = (
        projected[:, features : 2 * features]
        .astype(jnp.bfloat16)
        .reshape(seq_count, local_rows, features)
    )
    value_rows = (
        (projected[:, 2 * features :] + b_value)
        .astype(jnp.bfloat16)
        .reshape(seq_count, local_rows, features)
    )
    key_all, value_all = (
        lax.all_gather(key_rows, "seq", axis=1, tiled=True),
        lax.all_gather(value_rows, "seq", axis=1, tiled=True),
    )
    key_mask = allowed_pairs(lengths, block_perm, own_pos, all_pos)
    scores = (
        jnp.einsum(
            "sqhe,skhe->shqk",
            split_heads(queries),
            split_heads(key_all),
            preferred_element_type=jnp.float32,
        )
        * scaling
    )
    masked = jnp.where(key_mask[:, None], scores, NEGATIVE)
    row_top = jnp.max(masked, axis=-1, keepdims=True)
    exponent = jnp.exp(masked - row_top)
    row_total = jnp.sum(exponent, axis=-1, keepdims=True)
    probs_low = (exponent / row_total).astype(jnp.bfloat16)
    context = jnp.einsum(
        "shqk,skhe->sqhe", probs_low, split_heads(value_all), preferred_element_type=jnp.float32
    )
    context = context.reshape(seq_count, local_rows, features).astype(jnp.bfloat16)
    arrived = (
        lax.all_to_all(
            to_pieces(context, seq_parts), "seq", split_axis=1, concat_axis=1, tiled=True
        ),
        lax.all_to_all(
            to_pieces(masked_tokens, seq_parts), "seq", split_axis=1, concat_axis=1, tiled=True
        ),
        lax.all_to_all(
            to_pieces(cotangent, seq_parts), "seq", split_axis=1, concat_axis=1, tiled=True
        ),
    )
    context_tok = from_pieces(arrived[0]).reshape(flat_rows, features)
    tokens_tok = from_pieces(arrived[1]).reshape(flat_rows, features)
    cot_rows = from_pieces(arrived[2]).reshape(flat_rows, features)
    tok_pos = (
        jnp.arange(seq_parts, dtype=jnp.int32)[:, None] * local_rows
        + seq_index * piece_rows
        + jnp.arange(piece_rows, dtype=jnp.int32)[None, :]
    ).reshape(local_rows)
    tok_live = (tok_pos[None, :] < lengths[:, None]).astype(jnp.float32).reshape(flat_rows, 1)
    gain_one = ln1_gain.astype(jnp.float32)
    shift_one = ln1_shift.astype(jnp.float32)
    gain_two = ln2_gain.astype(jnp.float32)
    shift_two = ln2_shift.astype(jnp.float32)
    attended = jnp.dot(context_tok, w_out, preferred_element_type=jnp.float32) + b_out
    first_in = tokens_tok.astype(jnp.float32) + attended
    first_norm = norm_rows(first_in, gain_one, shift_one)
    first_low = first_norm.astype(jnp.bfloat16)
    lifted = jnp.dot(first_low, w_up, preferred_element_type=jnp.float32) + b_up
    active = jax.nn.gelu(lifted, approximate=False).astype(jnp.bfloat16)
    lowered = jnp.dot(active, w_down, preferred_element_type=jnp.float32) + b_down
    second_in = first_norm + lowered
    out_rows = norm_rows(second_in, gain_two, shift_two) * tok_live
    out_low = out_rows.astype(jnp.bfloat16).reshape(seq_count, local_rows, features)
    returned_out = lax.all_to_all(
        to_pieces(out_low, seq_parts), "seq", split_axis=1, concat_axis=1, tiled=True
    )
    out_tokens = from_pieces(returned_out)
    _, norm_two_back = jax.vjp(norm_rows, second_in, gain_two, shift_two)
    d_second, grad_gain_two, grad_shift_two = norm_two_back(cot_rows.astype(jnp.float32) * tok_live)
    d_lowered = d_second.astype(jnp.bfloat16)
    grad_w_down = jnp.einsum("rf,rd->fd", active, d_lowered, preferred_element_type=jnp.float32)
    grad_b_down = jnp.sum(d_lowered.astype(jnp.float32), axis=0)
    d_active = jnp.einsum("rd,fd->rf", d_lowered, w_down, preferred_element_type=jnp.float32)
    _, gelu_back = jax.vjp(partial(jax.nn.gelu, approximate=False), lifted)
    d_lifted = gelu_back(d_active)[0].astype(jnp.bfloat16)
    grad_w_up = jnp.einsum("rd,rf->df", first_low, d_lifted, preferred_element_type=jnp.float32)
    grad_b_up = jnp.sum(d_lifted.astype(jnp.float32), axis=0)
    d_first = jnp.einsum("rf,df->rd", d_lifted, w_up, preferred_element_type=jnp.float32) + d_second
    _, norm_one_back = jax.vjp(norm_rows, first_in, gain_one, shift_one)
    d_first_in, grad_gain_one, grad_shift_one = norm_one_back(d_first)
    d_attended = d_first_in.astype(jnp.bfloat16)
    grad_w_out = jnp.einsum(
        "rc,rd->cd", context_tok, d_attended, preferred_element_type=jnp.float32
    )
    grad_b_out = jnp.sum(d_attended.astype(jnp.float32), axis=0)
    d_context = jnp.einsum(
        "rd,cd->rc", d_attended, w_out, preferred_element_type=jnp.float32
    ).astype(jnp.bfloat16)
    returned = (
        lax.all_to_all(
            to_pieces(
                d_context.astype(jnp.float32).reshape(seq_count, local_rows, features), seq_parts
            ).astype(jnp.bfloat16),
            "seq",
            split_axis=1,
            concat_axis=1,
            tiled=True,
        ).astype(jnp.float32),
        lax.all_to_all(
            to_pieces(d_first_in.reshape(seq_count, local_rows, features), seq_parts).astype(
                jnp.bfloat16
            ),
            "seq",
            split_axis=1,
            concat_axis=1,
            tiled=True,
        ).astype(jnp.float32),
    )
    d_ctx_seq = from_pieces(returned[0]).astype(jnp.bfloat16)
    d_resid = from_pieces(returned[1])
    attn_probs = jnp.exp(masked - row_top) / row_total
    d_probs = jnp.einsum(
        "sqhe,skhe->shqk",
        split_heads(d_ctx_seq),
        split_heads(value_all),
        preferred_element_type=jnp.float32,
    )
    row_delta = jnp.sum(attn_probs * d_probs, axis=-1, keepdims=True)
    d_scores = (attn_probs * (d_probs - row_delta)).astype(jnp.bfloat16)
    d_queries = (
        jnp.einsum(
            "shqk,skhe->sqhe", d_scores, split_heads(key_all), preferred_element_type=jnp.float32
        )
        * scaling
    )
    d_queries = d_queries.reshape(seq_count, local_rows, features).astype(jnp.bfloat16)
    d_key_terms = (
        jnp.einsum(
            "shqk,sqhe->skhe", d_scores, split_heads(queries), preferred_element_type=jnp.float32
        )
        * scaling
    )
    d_value_terms = jnp.einsum(
        "shqk,sqhe->skhe", probs_low, split_heads(d_ctx_seq), preferred_element_type=jnp.float32
    )
    d_keys, d_values = (
        lax.psum_scatter(
            d_key_terms.reshape(seq_count, whole_len, features).astype(jnp.bfloat16),
            "seq",
            scatter_dimension=1,
            tiled=True,
        ).astype(jnp.float32),
        lax.psum_scatter(
            d_value_terms.reshape(seq_count, whole_len, features).astype(jnp.bfloat16),
            "seq",
            scatter_dimension=1,
            tiled=True,
        ).astype(jnp.float32),
    )
    d_keys_low = d_keys.astype(jnp.bfloat16)
    d_values_low = d_values.astype(jnp.bfloat16)
    d_qkv = jnp.concatenate([d_queries, d_keys_low, d_values_low], axis=-1).reshape(
        flat_rows, 3 * features
    )
    grad_w_qkv = jnp.einsum("rd,re->de", token_rows, d_qkv, preferred_element_type=jnp.float32)
    grad_b_query = jnp.sum(d_queries.reshape(flat_rows, features).astype(jnp.float32), axis=0)
    grad_b_value = jnp.sum(d_values_low.reshape(flat_rows, features).astype(jnp.float32), axis=0)
    grad_in = (
        jnp.einsum("re,de->rd", d_qkv, w_qkv, preferred_element_type=jnp.float32).reshape(
            seq_count, local_rows, features
        )
        + d_resid
    )
    grad_tokens = grad_in * live_mask[:, :, None].astype(jnp.float32)
    full_down = reduce_matrix(grad_w_down, "cxylh", 96, 768)
    full_up = reduce_matrix(grad_w_up, "cylhx", 96, 768)
    full_out = reduce_matrix(grad_w_out, "clhxy", 48, 384)
    full_qkv = reduce_matrix(grad_w_qkv, "clhxy", 48, 1152)
    (
        full_b_query,
        full_b_value,
        full_b_out,
        full_gain_one,
        full_shift_one,
        full_b_up,
        full_b_down,
        full_gain_two,
        full_shift_two,
    ) = reduce_vectors(
        [
            grad_b_query,
            grad_b_value,
            grad_b_out,
            grad_gain_one,
            grad_shift_one,
            grad_b_up,
            grad_b_down,
            grad_gain_two,
            grad_shift_two,
        ]
    )
    summed = (
        full_qkv,
        full_b_query,
        full_b_value,
        full_out,
        full_b_out,
        full_gain_one,
        full_shift_one,
        full_up,
        full_b_up,
        full_down,
        full_b_down,
        full_gain_two,
        full_shift_two,
    )
    return (out_tokens, grad_tokens) + summed


def solution(mesh):
    in_specs = (
        P("dp", "seq", None),
        P("dp", "seq", None),
        P("dp"),
        P("dp", None),
        P(),
        P(),
        P(),
        P(),
        P(),
        P(),
        P(),
        P(),
        P(),
        P(),
        P(),
        P(),
        P(),
    )
    out_specs = (
        P("dp", "seq", None),
        P("dp", "seq", None),
        P(),
        P(),
        P(),
        P(),
        P(),
        P(),
        P(),
        P(),
        P(),
        P(),
        P(),
        P(),
        P(),
    )
    return jax.shard_map(
        per_device, mesh=mesh, in_specs=in_specs, out_specs=out_specs, check_vma=False
    )
```

```python
import functools
import jax
import jax.numpy as jnp
from jax import lax
from jax.experimental import pallas as pl
from jax.experimental.pallas import tpu as pltpu
from jax.sharding import PartitionSpec as P

HEAD_DIM = 64
SOFT = HEAD_DIM ** -0.5 * 1.4426950408889634
NN = (((1,), (0,)), ((), ()))
NT = (((1,), (1,)), ((), ()))
TN = (((0,), (0,)), ((), ()))
VMEM_LIMIT = 50 * 1024 * 1024
HEADS = 12
EPSILON = 1e-06
BITS = {"c": ("seq", 0), "x": ("seq", 1), "y": ("dp", 0), "l": ("dp", 1), "h": ("dp", 2)}


def own_number(order):
    number = jnp.int32(0)
    for letter in order:
        axis, shift = BITS[letter]
        number = number * 2 + ((lax.axis_index(axis) >> shift) & 1)
    return number


def exchange(array_in, axis, flip):
    return lax.ppermute(array_in, axis, [(i, i ^ flip) for i in range(lax.axis_size(axis))])


def exchange_bit(array_in, letter):
    axis, shift = BITS[letter]
    return exchange(array_in, axis, 1 << shift)


def extra_flips(axis, used):
    return [1 << shift for shift in range(used, lax.axis_size(axis).bit_length() - 1)]


def add_extra(array_in):
    for flip in extra_flips("dp", 3):
        array_in = array_in + exchange(array_in, "dp", flip)
    return array_in


def halve(array_in, order):
    for letter in order:
        half = array_in.shape[0] // 2
        array_in = array_in[:half] + exchange_bit(array_in[half:], letter)
    return array_in


def double(array_in, order):
    for letter in reversed(order):
        array_in = jnp.concatenate([array_in, exchange_bit(array_in, letter)])
    return array_in


def sum_all(array_in, axes):
    for axis in axes:
        for flip in extra_flips(axis, 0):
            array_in = array_in + exchange(array_in, axis, flip)
    return array_in


def copy_block(ids, in_ref, out_ref):
    out_ref[...] = in_ref[...].reshape(out_ref.shape).astype(out_ref.dtype)


def to_relative(array_in, order, rows, cols, dtype=jnp.bfloat16):
    count = 1 << len(order)
    across = array_in.shape[1] // cols
    ids = jnp.arange(count, dtype=jnp.int32) ^ own_number(order)
    return pl.pallas_call(
        copy_block,
        out_shape=jax.ShapeDtypeStruct((count, rows, cols), dtype),
        grid_spec=pltpu.PrefetchScalarGridSpec(
            num_scalar_prefetch=1,
            grid=(count,),
            in_specs=[
                pl.BlockSpec((rows, cols), lambda p, ids: (ids[p] // across, ids[p] % across))
            ],
            out_specs=pl.BlockSpec((1, rows, cols), lambda p, ids: (p, 0, 0)),
        ),
    )(ids, array_in)


def from_relative(array_in, order, shape, dtype=jnp.float32):
    count, rows, cols = array_in.shape
    across = shape[1] // cols
    ids = jnp.arange(count, dtype=jnp.int32) ^ own_number(order)
    return pl.pallas_call(
        copy_block,
        out_shape=jax.ShapeDtypeStruct(shape, dtype),
        grid_spec=pltpu.PrefetchScalarGridSpec(
            num_scalar_prefetch=1,
            grid=(count,),
            in_specs=[pl.BlockSpec((1, rows, cols), lambda b, ids: (ids[b], 0, 0))],
            out_specs=pl.BlockSpec((rows, cols), lambda b, ids: (b // across, b % across)),
        ),
    )(ids, array_in)


def reduce_inner(shard, order, rows, cols):
    placed = to_relative(shard, order, rows, cols)
    summed = double(add_extra(halve(placed, order)), order)
    return from_relative(summed, order, shard.shape, jnp.bfloat16)


def merge_heads(seq_parts, ids, in_ref, out_ref):
    wide = in_ref.shape[2] // 3
    for j in range(seq_parts):
        for k in range(3):
            start = k * seq_parts * wide + j * wide
            out_ref[:, start : start + wide] = in_ref[ids[j], :, k * wide : (k + 1) * wide].astype(
                jnp.float32
            )


def spread_heads(array_in, seq_index):
    seq_parts, features, width = array_in.shape
    ids = jnp.arange(seq_parts, dtype=jnp.int32) ^ seq_index
    tile = features // 4
    return pl.pallas_call(
        functools.partial(merge_heads, seq_parts),
        out_shape=jax.ShapeDtypeStruct((features, seq_parts * width), jnp.float32),
        grid_spec=pltpu.PrefetchScalarGridSpec(
            num_scalar_prefetch=1,
            grid=(4,),
            in_specs=[pl.BlockSpec((seq_parts, tile, width), lambda i, ids: (0, i, 0))],
            out_specs=pl.BlockSpec((tile, seq_parts * width), lambda i, ids: (i, 0)),
        ),
    )(ids, array_in)


def dot_f32(left, right, dims):
    return lax.dot_general(left, right, dims, preferred_element_type=jnp.float32)


def shift_matrix(half, block, whole):
    row = lax.broadcasted_iota(jnp.int32, (block, whole), 0)
    col = lax.broadcasted_iota(jnp.int32, (block, whole), 1)
    return jnp.where((col == row + half) & (row < half), 1.0, 0.0).astype(jnp.bfloat16)


def mask_tiles(half, block):
    row = lax.broadcasted_iota(jnp.int32, (16, block), 0)
    col = lax.broadcasted_iota(jnp.int32, (16, block), 1)
    key_tile = jnp.where((row == 0) & (col >= half), -1e30, 0.0).astype(jnp.bfloat16)
    query_tile = jnp.where(row == 0, 1.0, 0.0).astype(jnp.bfloat16)
    return key_tile, query_tile


def attend_forward(
    heads, info, x0, x1, x2, x3, w_t, bias, c0, c1, c2, c3, qkv, ctx_blk, lse, x_t, x_seq, qkv_s, c_tok
):
    half, mine = info[0], info[3]
    whole = x_seq.shape[0]
    quarter = whole // 4
    block = whole // 2
    wide = heads * HEAD_DIM
    for r, piece in enumerate((x0, x1, x2, x3)):
        x_seq[pl.ds(pl.multiple_of((r ^ mine) * quarter, quarter), quarter), :] = piece[...]
    row = lax.broadcasted_iota(jnp.int32, (block, 1), 0)
    shift = shift_matrix(half, block, whole)
    first = jnp.where(row < half, x_seq[0:block, :], jnp.zeros((), jnp.bfloat16))
    second = dot_f32(shift, x_seq[...], NN).astype(jnp.bfloat16)
    for b, rows in enumerate((first, second)):
        turned = rows.T
        x_t[b] = turned
        projected = dot_f32(w_t[...], turned, NN) + bias[...]
        qkv_s[b] = projected.astype(jnp.bfloat16)
    qkv[...] = qkv_s[...]
    key_tile, query_tile = mask_tiles(half, block)

    def one_block(b, carry):
        target = info[1 + b]
        for h in range(heads):
            rows = slice(h * HEAD_DIM, (h + 1) * HEAD_DIM)
            q_t = jnp.concatenate([qkv_s[b, rows, :], query_tile])
            k_t = jnp.concatenate(
                [qkv_s[target, wide + h * HEAD_DIM : wide + (h + 1) * HEAD_DIM, :], key_tile]
            )
            v_t = qkv_s[target, 2 * wide + h * HEAD_DIM : 2 * wide + (h + 1) * HEAD_DIM, :]
            scores = dot_f32(k_t, q_t, TN) * SOFT
            top = jnp.max(scores, axis=0, keepdims=True)
            expo = jnp.exp2(scores - top)
            total = jnp.sum(expo, axis=0, keepdims=True)
            context = dot_f32(v_t, expo.astype(jnp.bfloat16), NN) / total
            ctx_blk[b, rows, :] = context
            lse[b, h : h + 1, :] = top + jnp.log2(total)
        return carry

    lax.fori_loop(0, 2, one_block, 0)
    lane = lax.broadcasted_iota(jnp.int32, (1, block), 1)
    early = jnp.where(lane < half, ctx_blk[0], 0.0)
    late = dot_f32(ctx_blk[1].astype(jnp.bfloat16), shift, NN)
    for j in range(4):
        part = late[:, j * quarter : (j + 1) * quarter]
        if j < 2:
            part = part + early[:, j * quarter : (j + 1) * quarter]
        c_tok[j] = part.astype(jnp.bfloat16)
    for r, piece in enumerate((c0, c1, c2, c3)):
        piece[...] = c_tok[r ^ mine]


def attend_backward(
    heads, info, g0, g1, g2, g3, w_t, qkv, ctx_blk, lse, x_t, acc, dx0, dx1, dx2, dx3, grad_w, grad_b,
    g_tok, g_blk, d_qkv, dx_s,
):
    half, mine = info[0], info[3]
    quarter = g0.shape[1]
    block = 2 * quarter
    whole = 4 * quarter
    wide = heads * HEAD_DIM
    for r, piece in enumerate((g0, g1, g2, g3)):
        g_tok[r ^ mine] = piece[...]
    shift = shift_matrix(half, block, whole)
    lane = lax.broadcasted_iota(jnp.int32, (1, block), 1)
    g_all = jnp.concatenate([g_tok[j] for j in range(4)], axis=1)
    g_blk[0] = jnp.where(lane < half, g_all[:, :block], jnp.zeros((), jnp.bfloat16))
    g_blk[1] = dot_f32(g_all, shift, NT).astype(jnp.bfloat16)
    key_tile, query_tile = mask_tiles(half, block)

    def one_block(b, carry):
        target = info[1 + b]
        for h in range(heads):
            rows = slice(h * HEAD_DIM, (h + 1) * HEAD_DIM)
            k_rows = slice(wide + h * HEAD_DIM, wide + (h + 1) * HEAD_DIM)
            v_rows = slice(2 * wide + h * HEAD_DIM, 2 * wide + (h + 1) * HEAD_DIM)
            q_t = qkv[b, rows, :]
            k_t = qkv[target, k_rows, :]
            v_t = qkv[target, v_rows, :]
            g_t = g_blk[b, rows, :]
            scores = dot_f32(
                jnp.concatenate([k_t, key_tile]), jnp.concatenate([q_t, query_tile]), TN
            )
            probs = jnp.exp2(scores * SOFT - lse[b, h : h + 1, :])
            d_probs = dot_f32(v_t, g_t, TN)
            delta = jnp.sum(ctx_blk[b, rows, :] * g_t.astype(jnp.float32), axis=0, keepdims=True)
            d_scores = (probs * (d_probs - delta)).astype(jnp.bfloat16)
            scaling = HEAD_DIM ** -0.5
            d_qkv[b, rows, :] = (dot_f32(k_t, d_scores, NN) * scaling).astype(jnp.bfloat16)
            d_qkv[target, k_rows, :] = (dot_f32(q_t, d_scores, NT) * scaling).astype(jnp.bfloat16)
            d_qkv[target, v_rows, :] = dot_f32(g_t, probs.astype(jnp.bfloat16), NT).astype(
                jnp.bfloat16
            )
        return carry

    lax.fori_loop(0, 2, one_block, 0)
    early, late = d_qkv[0], d_qkv[1]
    grad_w[...] = acc[...] + dot_f32(x_t[0], early, NT) + dot_f32(x_t[1], late, NT)
    grad_b[...] = jnp.sum(early.astype(jnp.float32), axis=1, keepdims=True) + jnp.sum(
        late.astype(jnp.float32), axis=1, keepdims=True
    )
    back = dot_f32(late, shift, NN)
    front = jnp.where(lane < half, early.astype(jnp.float32), 0.0)
    for j in range(4):
        part = back[:, j * quarter : (j + 1) * quarter]
        if j < 2:
            part = part + front[:, j * quarter : (j + 1) * quarter]
        dx_s[j] = dot_f32(part.astype(jnp.bfloat16), w_t[...], TN).astype(jnp.bfloat16)
    for r, piece in enumerate((dx0, dx1, dx2, dx3)):
        piece[...] = dx_s[r ^ mine]


def kernel_call(body, scalars, arrays, outs, scratch, aliases={}):
    return pl.pallas_call(
        body,
        out_shape=outs,
        in_specs=[pl.BlockSpec(memory_space=pltpu.SMEM)]
        + [pl.BlockSpec(memory_space=pltpu.VMEM)] * len(arrays),
        out_specs=[pl.BlockSpec(memory_space=pltpu.VMEM)] * len(outs),
        scratch_shapes=scratch,
        input_output_aliases=aliases,
        compiler_params=pltpu.CompilerParams(vmem_limit_bytes=VMEM_LIMIT),
    )(scalars, *arrays)


def attention_forward(info, pieces, w_t, bias, heads):
    quarter, features = pieces[0].shape
    whole, block, wide = 4 * quarter, 2 * quarter, heads * HEAD_DIM
    out = jax.ShapeDtypeStruct
    outs = [out((wide, quarter), jnp.bfloat16)] * 4 + [
        out((2, 3 * wide, block), jnp.bfloat16),
        out((2, wide, block), jnp.float32),
        out((2, 8, block), jnp.float32),
        out((2, features, block), jnp.bfloat16),
    ]
    scratch = [
        pltpu.VMEM((whole, features), jnp.bfloat16),
        pltpu.VMEM((2, 3 * wide, block), jnp.bfloat16),
        pltpu.VMEM((4, wide, quarter), jnp.bfloat16),
    ]
    found = kernel_call(
        functools.partial(attend_forward, heads), info, [*pieces, w_t, bias], outs, scratch
    )
    return found[:4], found[4:]


def attention_backward(info, pieces, w_t, kept, acc, heads):
    wide, quarter = pieces[0].shape
    features = w_t.shape[1]
    block = 2 * quarter
    out = jax.ShapeDtypeStruct
    outs = [out((quarter, features), jnp.bfloat16)] * 4 + [
        out((features, 3 * wide), jnp.float32),
        out((3 * wide, 1), jnp.float32),
    ]
    scratch = [
        pltpu.VMEM((4, wide, quarter), jnp.bfloat16),
        pltpu.VMEM((2, wide, block), jnp.bfloat16),
        pltpu.VMEM((2, 3 * wide, block), jnp.bfloat16),
        pltpu.VMEM((4, quarter, features), jnp.bfloat16),
    ]
    found = kernel_call(
        functools.partial(attend_backward, heads),
        info,
        [*pieces, w_t, *kept, acc],
        outs,
        scratch,
    )
    return found[:4], found[4], found[5]


def norm_rows(array_in, gain_vec, shift_vec):
    row_mean = jnp.mean(array_in, axis=-1, keepdims=True)
    centered = array_in - row_mean
    spread = jnp.mean(centered * centered, axis=-1, keepdims=True)
    return centered * lax.rsqrt(spread + EPSILON) * gain_vec + shift_vec


def norm_back(array_in, gain_vec, d_out):
    row_mean = jnp.mean(array_in, axis=-1, keepdims=True)
    centered = array_in - row_mean
    spread = jnp.mean(centered * centered, axis=-1, keepdims=True)
    inverse = lax.rsqrt(spread + EPSILON)
    hat = centered * inverse
    scaled = d_out * gain_vec
    d_in = inverse * (
        scaled
        - jnp.mean(scaled, axis=-1, keepdims=True)
        - hat * jnp.mean(scaled * hat, axis=-1, keepdims=True)
    )
    return d_in, jnp.sum(d_out * hat, axis=0), jnp.sum(d_out, axis=0)


def per_device(
    tokens,
    cotangent,
    lengths,
    block_perm,
    w_qkv,
    b_query,
    b_value,
    w_out,
    b_out,
    ln1_gain,
    ln1_shift,
    w_up,
    b_up,
    w_down,
    b_down,
    ln2_gain,
    ln2_shift,
):
    seq_parts = lax.axis_size("seq")
    mine = lax.axis_index("seq")
    seq_count, local_rows, features = tokens.shape
    flat_rows = seq_count * local_rows
    hidden = w_up.shape[1]
    heads = HEADS // seq_parts
    wide = heads * HEAD_DIM
    f32 = jnp.float32

    w_heads = jnp.concatenate(
        [
            lax.dynamic_slice_in_dim(w_qkv, k * features + mine * wide, wide, axis=1)
            for k in range(3)
        ],
        axis=1,
    )
    w_t = w_heads.T
    bias = jnp.concatenate(
        [
            lax.dynamic_slice_in_dim(b_query, mine * wide, wide),
            jnp.zeros((wide,), b_query.dtype),
            lax.dynamic_slice_in_dim(b_value, mine * wide, wide),
        ]
    ).astype(f32)[:, None]
    infos = [
        jnp.stack([lengths[s] // 2, block_perm[s, 0], block_perm[s, 1], mine])
        for s in range(seq_count)
    ]

    arrived, kept = [], []
    for s in range(seq_count):
        near = tokens[s]
        across = exchange_bit(near, "x")
        pieces = [near, exchange_bit(near, "c"), across, exchange_bit(across, "c")]
        contexts, saved = attention_forward(infos[s], pieces, w_t, bias, heads)
        kept.append(saved)
        arrived.append(
            jnp.concatenate(
                [contexts[0]] + [exchange(contexts[r], "seq", r) for r in range(1, seq_parts)]
            )
        )
    context_t = jnp.concatenate(arrived, axis=1)

    outer = "cxy"
    hidden_tile = hidden // 8
    w_out_rel = to_relative(w_out, "xc", wide, features).reshape(features, features)
    w_up_rel = to_relative(w_up, outer, features, hidden_tile)
    w_down_rel = to_relative(w_down, outer, hidden_tile, features).reshape(hidden, features)
    b_up_rel = to_relative(b_up.reshape(1, hidden), outer, 1, hidden_tile)

    own_pos = mine * local_rows + jnp.arange(local_rows, dtype=jnp.int32)
    live = (own_pos[None, :] < lengths[:, None]).reshape(flat_rows, 1)
    token_rows = jnp.where(live, tokens.reshape(flat_rows, features), jnp.zeros((), tokens.dtype))
    live = live.astype(f32)
    gain_one, shift_one = ln1_gain.astype(f32), ln1_shift.astype(f32)
    gain_two, shift_two = ln2_gain.astype(f32), ln2_shift.astype(f32)

    attended = (
        jnp.einsum("ct,cd->td", context_t, w_out_rel, preferred_element_type=f32) + b_out
    )
    first_in = token_rows.astype(f32) + attended
    first_norm = norm_rows(first_in, gain_one, shift_one)
    first_low = first_norm.astype(jnp.bfloat16)
    w_up_cols = w_up_rel.transpose(1, 0, 2).reshape(features, hidden)
    lifted = jnp.dot(first_low, w_up_cols, preferred_element_type=f32) + b_up_rel.reshape(hidden)
    active = jax.nn.gelu(lifted, approximate=False).astype(jnp.bfloat16)
    lowered = jnp.dot(active, w_down_rel, preferred_element_type=f32) + b_down
    second_in = first_norm + lowered
    out_tokens = (
        (norm_rows(second_in, gain_two, shift_two) * live)
        .astype(jnp.bfloat16)
        .reshape(seq_count, local_rows, features)
    )
    d_second, grad_gain_two, grad_shift_two = norm_back(
        second_in, gain_two, cotangent.reshape(flat_rows, features).astype(f32) * live
    )
    d_lowered = d_second.astype(jnp.bfloat16)
    grad_w_down = jnp.einsum("rf,rd->fd", active, d_lowered, preferred_element_type=f32).astype(
        jnp.bfloat16
    )
    grad_b_down = jnp.sum(d_lowered.astype(f32), axis=0)
    d_active = jnp.einsum("rd,fd->rf", d_lowered, w_down_rel, preferred_element_type=f32)
    _, gelu_back = jax.vjp(functools.partial(jax.nn.gelu, approximate=False), lifted)
    d_lifted = gelu_back(d_active)[0].astype(jnp.bfloat16)
    grad_w_up = jnp.einsum("rd,rf->df", first_low, d_lifted, preferred_element_type=f32).astype(
        jnp.bfloat16
    )
    grad_b_up = jnp.sum(d_lifted.astype(f32), axis=0)
    d_first = jnp.einsum("rf,df->rd", d_lifted, w_up_cols, preferred_element_type=f32) + d_second
    d_first_in, grad_gain_one, grad_shift_one = norm_back(first_in, gain_one, d_first)
    d_attended = d_first_in.astype(jnp.bfloat16)
    grad_w_out = jnp.einsum(
        "cr,rd->cd", context_t, d_attended, preferred_element_type=f32
    ).astype(jnp.bfloat16)
    grad_b_out = jnp.sum(d_attended.astype(f32), axis=0)
    d_context_t = jnp.einsum(
        "rd,cd->cr", d_attended, w_out_rel, preferred_element_type=f32
    ).astype(jnp.bfloat16)

    down_shard = halve(grad_w_down.reshape(8, hidden_tile, features), outer)[0]
    down_shard = reduce_inner(down_shard, "lh", hidden_tile // 4, features)
    full_down = from_relative(
        double(down_shard[None], outer), outer, (hidden, features)
    )
    up_blocks = grad_w_up.reshape(features, 8, hidden_tile).transpose(1, 0, 2)
    up_blocks = up_blocks.reshape(2, 2, 2, features, hidden_tile)
    up_half = up_blocks[0] + exchange_bit(up_blocks[1], "c")
    up_quarter = up_half[:, 0] + exchange_bit(up_half[:, 1], "y")
    up_shard = up_quarter[0] + exchange_bit(up_quarter[1], "x")
    up_shard = reduce_inner(up_shard, "lh", features // 4, hidden_tile)
    up_pair = jnp.stack([up_shard, exchange_bit(up_shard, "x")])
    up_four = jnp.stack([up_pair, exchange_bit(up_pair, "y")], axis=1)
    up_all = jnp.concatenate([up_four, exchange_bit(up_four, "c")])
    full_up = from_relative(
        up_all.reshape(8, features, hidden_tile), outer, (features, hidden)
    )
    out_shard = halve(grad_w_out.reshape(4, wide, features), "xc")[0]
    out_shard = reduce_inner(out_shard, "ylh", wide // 4, features // 2)
    full_out = from_relative(double(out_shard[None], "xc"), "xc", (features, features))
    vectors = [
        grad_b_out,
        grad_gain_one,
        grad_shift_one,
        grad_b_down,
        grad_gain_two,
        grad_shift_two,
    ]
    b_up_true = from_relative(
        grad_b_up.reshape(8, 1, hidden_tile), outer, (1, hidden)
    ).reshape(hidden)
    packed = sum_all(jnp.concatenate(vectors + [b_up_true]).reshape(-1, 128), ("seq", "dp"))
    packed = packed.reshape(-1)
    (
        full_b_out,
        full_gain_one,
        full_shift_one,
        full_b_down,
        full_gain_two,
        full_shift_two,
    ) = [packed[i * features : (i + 1) * features] for i in range(6)]
    full_b_up = packed[6 * features :]

    total_w = jnp.zeros((features, 3 * wide), f32)
    total_b = jnp.zeros((3 * wide, 1), f32)
    d_inputs = []
    for s in range(seq_count):
        columns = d_context_t[:, s * local_rows : (s + 1) * local_rows]
        pieces = [columns[r * wide : (r + 1) * wide] for r in range(seq_parts)]
        pieces = pieces[:1] + [exchange(pieces[r], "seq", r) for r in range(1, seq_parts)]
        parts, total_w, part_b = attention_backward(
            infos[s], pieces, w_t, kept[s], total_w, heads
        )
        total_b = total_b + part_b
        near = parts[0].astype(f32) + exchange_bit(parts[1], "c")
        far = (parts[2].astype(f32) + exchange_bit(parts[3], "c")).astype(jnp.bfloat16)
        d_inputs.append(near + exchange_bit(far, "x"))
    grad_tokens = (
        jnp.stack(d_inputs) + d_first_in.reshape(seq_count, local_rows, features)
    ) * live.reshape(seq_count, local_rows, 1)

    qkv_shard = reduce_inner(total_w, "ylh", features // 8, 3 * wide)
    full_qkv = spread_heads(double(qkv_shard[None], "xc"), mine)
    b_shard = sum_all(total_b.reshape(1, 3 * wide), ("dp",))
    b_all = double(b_shard, "xc")
    b_rows = [
        lax.dynamic_slice_in_dim(b_all, j ^ mine, 1, axis=0).reshape(3 * wide)
        for j in range(seq_parts)
    ]
    full_b_query = jnp.concatenate([row[:wide] for row in b_rows])
    full_b_value = jnp.concatenate([row[2 * wide :] for row in b_rows])
    return (
        out_tokens,
        grad_tokens,
        full_qkv,
        full_b_query,
        full_b_value,
        full_out,
        full_b_out,
        full_gain_one,
        full_shift_one,
        full_up,
        full_b_up,
        full_down,
        full_b_down,
        full_gain_two,
        full_shift_two,
    )


def solution(mesh):
    in_specs = (
        P("dp", "seq", None),
        P("dp", "seq", None),
        P("dp"),
        P("dp", None),
        P(),
        P(),
        P(),
        P(),
        P(),
        P(),
        P(),
        P(),
        P(),
        P(),
        P(),
        P(),
        P(),
    )
    out_specs = (
        P("dp", "seq", None),
        P("dp", "seq", None),
        P(),
        P(),
        P(),
        P(),
        P(),
        P(),
        P(),
        P(),
        P(),
        P(),
        P(),
        P(),
        P(),
    )
    return jax.shard_map(
        per_device, mesh=mesh, in_specs=in_specs, out_specs=out_specs, check_vma=False
    )
```

```python
import functools
import jax
import jax.numpy as jnp
from jax import lax
from jax.experimental import pallas as pl
from jax.experimental.pallas import tpu as pltpu
from jax.sharding import PartitionSpec as P

HEAD_DIM = 64
SOFT = HEAD_DIM ** -0.5 * 1.4426950408889634
NN = (((1,), (0,)), ((), ()))
NT = (((1,), (1,)), ((), ()))
TN = (((0,), (0,)), ((), ()))
VMEM_LIMIT = 50 * 1024 * 1024
HEADS = 12
EPSILON = 1e-06
BITS = {"c": ("seq", 0), "x": ("seq", 1), "y": ("dp", 0), "l": ("dp", 1), "h": ("dp", 2)}


def own_number(order):
    number = jnp.int32(0)
    for letter in order:
        axis, shift = BITS[letter]
        number = number * 2 + ((lax.axis_index(axis) >> shift) & 1)
    return number


def exchange(array_in, axis, flip):
    return lax.ppermute(array_in, axis, [(i, i ^ flip) for i in range(lax.axis_size(axis))])


def exchange_bit(array_in, letter):
    axis, shift = BITS[letter]
    return exchange(array_in, axis, 1 << shift)


def extra_flips(axis, used):
    return [1 << shift for shift in range(used, lax.axis_size(axis).bit_length() - 1)]


def add_extra(array_in):
    for flip in extra_flips("dp", 3):
        array_in = array_in + exchange(array_in, "dp", flip)
    return array_in


def halve(array_in, order):
    for letter in order:
        half = array_in.shape[0] // 2
        array_in = array_in[:half] + exchange_bit(array_in[half:], letter)
    return array_in


def double(array_in, order):
    for letter in reversed(order):
        array_in = jnp.concatenate([array_in, exchange_bit(array_in, letter)])
    return array_in


def spread(pieces, order):
    for letter in reversed(order):
        pieces = pieces + [exchange_bit(piece, letter) for piece in pieces]
    return pieces


def sum_all(array_in, axes):
    for axis in axes:
        for flip in extra_flips(axis, 0):
            array_in = array_in + exchange(array_in, axis, flip)
    return array_in


def sum_low(*parts):
    total = parts[0].astype(jnp.float32)
    for part in parts[1:]:
        total = total + part.astype(jnp.float32)
    return total.astype(jnp.bfloat16)


def dot_f32(left, right, dims):
    return lax.dot_general(left, right, dims, preferred_element_type=jnp.float32)


def shift_matrix(half, block, whole):
    row = lax.broadcasted_iota(jnp.int32, (block, whole), 0)
    col = lax.broadcasted_iota(jnp.int32, (block, whole), 1)
    return jnp.where((col == row + half) & (row < half), 1.0, 0.0).astype(jnp.bfloat16)


def mask_tiles(half, block):
    row = lax.broadcasted_iota(jnp.int32, (16, block), 0)
    col = lax.broadcasted_iota(jnp.int32, (16, block), 1)
    key_tile = jnp.where((row == 0) & (col >= half), -1e30, 0.0).astype(jnp.bfloat16)
    query_tile = jnp.where(row == 0, 1.0, 0.0).astype(jnp.bfloat16)
    return key_tile, query_tile


def attend_forward(
    heads, info, x0, x1, x2, x3, w_t, bias, c0, c1, c2, c3, qkv, ctx_blk, lse, x_t, x_seq, qkv_s, c_tok
):
    half, mine = info[0], info[3]
    whole = x_seq.shape[0]
    quarter = whole // 4
    block = whole // 2
    wide = heads * HEAD_DIM
    for r, piece in enumerate((x0, x1, x2, x3)):
        x_seq[pl.ds(pl.multiple_of((r ^ mine) * quarter, quarter), quarter), :] = piece[...]
    row = lax.broadcasted_iota(jnp.int32, (block, 1), 0)
    shift = shift_matrix(half, block, whole)
    first = jnp.where(row < half, x_seq[0:block, :], jnp.zeros((), jnp.bfloat16))
    second = dot_f32(shift, x_seq[...], NN).astype(jnp.bfloat16)
    for b, rows in enumerate((first, second)):
        turned = rows.T
        x_t[b] = turned
        projected = dot_f32(w_t[...], turned, NN) + bias[...]
        qkv_s[b] = projected.astype(jnp.bfloat16)
    qkv[...] = qkv_s[...]
    key_tile, query_tile = mask_tiles(half, block)

    def one_block(b, carry):
        target = info[1 + b]
        for h in range(heads):
            rows = slice(h * HEAD_DIM, (h + 1) * HEAD_DIM)
            q_t = jnp.concatenate([qkv_s[b, rows, :], query_tile])
            k_t = jnp.concatenate(
                [qkv_s[target, wide + h * HEAD_DIM : wide + (h + 1) * HEAD_DIM, :], key_tile]
            )
            v_t = qkv_s[target, 2 * wide + h * HEAD_DIM : 2 * wide + (h + 1) * HEAD_DIM, :]
            scores = dot_f32(k_t, q_t, TN) * SOFT
            top = jnp.max(scores, axis=0, keepdims=True)
            expo = jnp.exp2(scores - top)
            total = jnp.sum(expo, axis=0, keepdims=True)
            context = dot_f32(v_t, expo.astype(jnp.bfloat16), NN) / total
            ctx_blk[b, rows, :] = context
            lse[b, h : h + 1, :] = top + jnp.log2(total)
        return carry

    lax.fori_loop(0, 2, one_block, 0)
    lane = lax.broadcasted_iota(jnp.int32, (1, block), 1)
    early = jnp.where(lane < half, ctx_blk[0], 0.0)
    late = dot_f32(ctx_blk[1].astype(jnp.bfloat16), shift, NN)
    for j in range(4):
        part = late[:, j * quarter : (j + 1) * quarter]
        if j < 2:
            part = part + early[:, j * quarter : (j + 1) * quarter]
        c_tok[j] = part.astype(jnp.bfloat16)
    for r, piece in enumerate((c0, c1, c2, c3)):
        piece[...] = c_tok[r ^ mine]


def attend_backward(
    heads, last, info, g0, g1, g2, g3, w_t, qkv, ctx_blk, lse, x_t, acc, dx0, dx1, dx2, dx3, grad_w, grad_b,
    g_tok, g_blk, d_qkv, dx_s,
):
    half, mine = info[0], info[3]
    quarter = g0.shape[1]
    block = 2 * quarter
    whole = 4 * quarter
    wide = heads * HEAD_DIM
    for r, piece in enumerate((g0, g1, g2, g3)):
        g_tok[r ^ mine] = piece[...]
    shift = shift_matrix(half, block, whole)
    lane = lax.broadcasted_iota(jnp.int32, (1, block), 1)
    g_all = jnp.concatenate([g_tok[j] for j in range(4)], axis=1)
    g_blk[0] = jnp.where(lane < half, g_all[:, :block], jnp.zeros((), jnp.bfloat16))
    g_blk[1] = dot_f32(g_all, shift, NT).astype(jnp.bfloat16)
    key_tile, query_tile = mask_tiles(half, block)

    def one_block(b, carry):
        target = info[1 + b]
        for h in range(heads):
            rows = slice(h * HEAD_DIM, (h + 1) * HEAD_DIM)
            k_rows = slice(wide + h * HEAD_DIM, wide + (h + 1) * HEAD_DIM)
            v_rows = slice(2 * wide + h * HEAD_DIM, 2 * wide + (h + 1) * HEAD_DIM)
            q_t = qkv[b, rows, :]
            k_t = qkv[target, k_rows, :]
            v_t = qkv[target, v_rows, :]
            g_t = g_blk[b, rows, :]
            scores = dot_f32(
                jnp.concatenate([k_t, key_tile]), jnp.concatenate([q_t, query_tile]), TN
            )
            probs = jnp.exp2(scores * SOFT - lse[b, h : h + 1, :])
            d_probs = dot_f32(v_t, g_t, TN)
            delta = jnp.sum(ctx_blk[b, rows, :] * g_t.astype(jnp.float32), axis=0, keepdims=True)
            d_scores = (probs * (d_probs - delta)).astype(jnp.bfloat16)
            scaling = HEAD_DIM ** -0.5
            d_qkv[b, rows, :] = (dot_f32(k_t, d_scores, NN) * scaling).astype(jnp.bfloat16)
            d_qkv[target, k_rows, :] = (dot_f32(q_t, d_scores, NT) * scaling).astype(jnp.bfloat16)
            d_qkv[target, v_rows, :] = dot_f32(g_t, probs.astype(jnp.bfloat16), NT).astype(
                jnp.bfloat16
            )
        return carry

    lax.fori_loop(0, 2, one_block, 0)
    early, late = d_qkv[0], d_qkv[1]
    total = acc[...] + dot_f32(x_t[0], early, NT) + dot_f32(x_t[1], late, NT)
    if last:
        tile = grad_w.shape[1]
        for q in range(8):
            grad_w[q ^ info[4]] = total[q * tile : (q + 1) * tile].astype(jnp.bfloat16)
    else:
        grad_w[...] = total
    grad_b[...] = jnp.sum(early.astype(jnp.float32), axis=1, keepdims=True) + jnp.sum(
        late.astype(jnp.float32), axis=1, keepdims=True
    )
    back = dot_f32(late, shift, NN)
    front = jnp.where(lane < half, early.astype(jnp.float32), 0.0)
    for j in range(4):
        part = back[:, j * quarter : (j + 1) * quarter]
        if j < 2:
            part = part + front[:, j * quarter : (j + 1) * quarter]
        dx_s[j] = dot_f32(part.astype(jnp.bfloat16), w_t[...], TN).astype(jnp.bfloat16)
    for r, piece in enumerate((dx0, dx1, dx2, dx3)):
        piece[...] = dx_s[r ^ mine]


def kernel_call(body, scalars, arrays, outs, scratch, aliases={}):
    return pl.pallas_call(
        body,
        out_shape=outs,
        in_specs=[pl.BlockSpec(memory_space=pltpu.SMEM)]
        + [pl.BlockSpec(memory_space=pltpu.VMEM)] * len(arrays),
        out_specs=[pl.BlockSpec(memory_space=pltpu.VMEM)] * len(outs),
        scratch_shapes=scratch,
        input_output_aliases=aliases,
        compiler_params=pltpu.CompilerParams(vmem_limit_bytes=VMEM_LIMIT),
        cost_estimate=pl.CostEstimate(
            flops=6 * 10**9, transcendentals=0, bytes_accessed=20 * 1024 * 1024
        ),
    )(scalars, *arrays)


def attention_forward(info, pieces, w_t, bias, heads):
    quarter, features = pieces[0].shape
    whole, block, wide = 4 * quarter, 2 * quarter, heads * HEAD_DIM
    out = jax.ShapeDtypeStruct
    outs = [out((wide, quarter), jnp.bfloat16)] * 4 + [
        out((2, 3 * wide, block), jnp.bfloat16),
        out((2, wide, block), jnp.float32),
        out((2, 8, block), jnp.float32),
        out((2, features, block), jnp.bfloat16),
    ]
    scratch = [
        pltpu.VMEM((whole, features), jnp.bfloat16),
        pltpu.VMEM((2, 3 * wide, block), jnp.bfloat16),
        pltpu.VMEM((4, wide, quarter), jnp.bfloat16),
    ]
    found = kernel_call(
        functools.partial(attend_forward, heads), info, [*pieces, w_t, bias], outs, scratch
    )
    return found[:4], found[4:]


def attention_backward(info, pieces, w_t, kept, acc, heads, last):
    wide, quarter = pieces[0].shape
    features = w_t.shape[1]
    block = 2 * quarter
    out = jax.ShapeDtypeStruct
    outs = [out((quarter, features), jnp.bfloat16)] * 4 + [
        out((8, features // 8, 3 * wide), jnp.bfloat16)
        if last
        else out((features, 3 * wide), jnp.float32),
        out((3 * wide, 1), jnp.float32),
    ]
    scratch = [
        pltpu.VMEM((4, wide, quarter), jnp.bfloat16),
        pltpu.VMEM((2, wide, block), jnp.bfloat16),
        pltpu.VMEM((2, 3 * wide, block), jnp.bfloat16),
        pltpu.VMEM((4, quarter, features), jnp.bfloat16),
    ]
    found = kernel_call(
        functools.partial(attend_backward, heads, last),
        info,
        [*pieces, w_t, *kept, acc],
        outs,
        scratch,
    )
    return found[:4], found[4], found[5]

def live_rows(places, rows, mine, local_rows, offset):
    row = lax.broadcasted_iota(jnp.int32, (rows, 1), 0)
    length = jnp.zeros((rows, 1), jnp.int32)
    for s in range(rows // local_rows):
        length = jnp.where(row >= s * local_rows, places[offset + s], length)
    position = mine * local_rows + lax.rem(row, local_rows)
    return jnp.where(position < length, 1.0, 0.0)


def normal_parts(array_in):
    centered = array_in - jnp.mean(array_in, axis=1, keepdims=True)
    spread = jnp.mean(centered * centered, axis=1, keepdims=True)
    inverse = lax.rsqrt(spread + EPSILON)
    return centered * inverse, inverse


def normal_back(hat, inverse, gain, d_out):
    scaled = d_out * gain
    mean_scaled = jnp.mean(scaled, axis=1, keepdims=True)
    mean_product = jnp.mean(scaled * hat, axis=1, keepdims=True)
    return inverse * (scaled - mean_scaled - hat * mean_product)


def column_sum(array_in):
    return jnp.sum(array_in, axis=0, keepdims=True)


def feed_forward(shape, places, *refs):
    seq_count, seq_parts, steps = shape
    pieces, refs = refs[: seq_count * seq_parts], refs[seq_count * seq_parts :]
    tokens, cot, w_out, vectors, w_up, b_up, w_down = refs[:7]
    out, context, first_in, first_low, active, slope, d_second, d_lowered, sums = refs[7:16]
    first_norm, lowered = refs[16:]
    rows, features = tokens.shape
    local_rows = rows // seq_count
    wide = features // seq_parts
    mine = places[9]
    step = pl.program_id(0)
    f32 = jnp.float32

    @pl.when(step == 0)
    def start():
        for s in range(seq_count):
            for r in range(seq_parts):
                context[
                    pl.ds(pl.multiple_of((r ^ mine) * wide, wide), wide),
                    s * local_rows : (s + 1) * local_rows,
                ] = pieces[s * seq_parts + r][...]
        live = live_rows(places, rows, mine, local_rows, 11)
        attended = dot_f32(context[...], w_out[...], TN) + vectors[0:1, :]
        total = jnp.where(live > 0, tokens[...].astype(f32), 0.0) + attended
        first_in[...] = total
        hat, _ = normal_parts(total)
        normed = hat * vectors[1:2, :] + vectors[2:3, :]
        first_norm[...] = normed
        first_low[...] = normed.astype(jnp.bfloat16)

    lifted = dot_f32(first_low[...], w_up[...], NN) + b_up[...]
    cdf = 0.5 * (1.0 + lax.erf(lifted * 0.7071067811865476))
    density = jnp.exp(lifted * lifted * -0.5) * 0.3989422804014327
    gelu = (lifted * cdf).astype(jnp.bfloat16)
    active[0] = gelu
    slope[0] = (cdf + lifted * density).astype(jnp.bfloat16)
    part = dot_f32(gelu, w_down[...], NN)

    @pl.when(step == 0)
    def first():
        lowered[...] = part

    @pl.when(step > 0)
    def later():
        lowered[...] += part

    @pl.when(step == steps - 1)
    def finish():
        live = live_rows(places, rows, mine, local_rows, 11)
        hat, inverse = normal_parts(first_norm[...] + (lowered[...] + vectors[3:4, :]))
        gain = vectors[4:5, :]
        out[...] = ((hat * gain + vectors[5:6, :]) * live).astype(jnp.bfloat16)
        incoming = cot[...].astype(f32) * live
        back = normal_back(hat, inverse, gain, incoming)
        d_second[...] = back
        low = back.astype(jnp.bfloat16)
        d_lowered[...] = low
        sums[0:1, :] = column_sum(low.astype(f32))
        sums[1:2, :] = column_sum(incoming * hat)
        sums[2:3, :] = column_sum(incoming)


def hidden_back(places, active, slope, w_up, w_down, first_t, d_lowered, grad_down, grad_up, grad_b):
    inner = places[8]
    f32 = jnp.float32
    down = dot_f32(active[0], d_lowered[...], TN).astype(jnp.bfloat16)
    tile = down.shape[0] // 4
    for q in range(4):
        grad_down[0, pl.ds(pl.multiple_of((q ^ inner) * tile, tile), tile), :] = down[
            q * tile : (q + 1) * tile
        ]
    d_active = dot_f32(d_lowered[...], w_down[...], NT)
    d_lifted = (d_active * slope[0].astype(f32)).astype(jnp.bfloat16)
    grad_b[...] = column_sum(d_lifted.astype(f32))
    grad_up[0] = dot_f32(first_t[...], d_lifted, NN).astype(jnp.bfloat16)
    return dot_f32(d_lifted, w_up[...], NT)


def turn_rows(places, source, target):
    inner = places[8]
    tile = target.shape[0] // 4
    turned = source[...].T
    for q in range(4):
        target[pl.ds(pl.multiple_of((q ^ inner) * tile, tile), tile), :] = turned[
            q * tile : (q + 1) * tile
        ]


def back_send(
    places, active, slope, w_up, w_down, first_low, d_lowered, d_second,
    grad_down, grad_up, grad_b, d_first, first_t,
):
    step = pl.program_id(0)

    @pl.when(step == 0)
    def start():
        turn_rows(places, first_low, first_t)
        d_first[...] = d_second[...]

    d_first[...] += hidden_back(
        places, active, slope, w_up, w_down, first_t, d_lowered, grad_down, grad_up, grad_b
    )


def back_keep(shape, places, *refs):
    seq_count, seq_parts, steps = shape
    active, slope, w_up, w_down, first_low, d_lowered, d_part = refs[:7]
    first_in, context, w_out, vectors = refs[7:11]
    grad_down, grad_up, grad_b, d_first_in, sums, grad_out = refs[11:17]
    pieces = refs[17 : 17 + seq_count * seq_parts]
    first_t, d_first, turned = refs[17 + seq_count * seq_parts :]
    step = pl.program_id(0)
    f32 = jnp.float32

    @pl.when(step == 0)
    def start():
        turn_rows(places, first_low, first_t)
        d_first[...] = d_part[...]

    d_first[...] += hidden_back(
        places, active, slope, w_up, w_down, first_t, d_lowered, grad_down, grad_up, grad_b
    )

    @pl.when(step == steps - 1)
    def finish():
        rows, features = first_in.shape
        local_rows = rows // seq_count
        wide = features // seq_parts
        mine = places[9]
        hat, inverse = normal_parts(first_in[...])
        incoming = d_first[...]
        back = normal_back(hat, inverse, vectors[1:2, :], incoming)
        d_first_in[...] = back
        low = back.astype(jnp.bfloat16)
        sums[0:1, :] = column_sum(low.astype(f32))
        sums[1:2, :] = column_sum(incoming * hat)
        sums[2:3, :] = column_sum(incoming)
        turned[...] = dot_f32(w_out[...], low, NT).astype(jnp.bfloat16)
        for r in range(seq_parts):
            own = turned[pl.ds(pl.multiple_of((r ^ mine) * wide, wide), wide), :]
            for s in range(seq_count):
                pieces[s * seq_parts + r][...] = own[:, s * local_rows : (s + 1) * local_rows]
        product = dot_f32(context[...], low, NN).astype(jnp.bfloat16)
        block_rows, block_cols = grad_out.shape[2:]
        across = features // block_cols
        for j in range(seq_parts):
            for q in range(wide // block_rows * across):
                row, col = j * wide + q // across * block_rows, q % across * block_cols
                grad_out[j ^ mine, q ^ places[10]] = product[
                    row : row + block_rows, col : col + block_cols
                ]


def whole_spec(shape):
    return pl.BlockSpec(shape, lambda p, places: (0,) * len(shape))


def step_call(body, places, steps, ins, in_specs, outs, out_specs, scratch, flops):
    return pl.pallas_call(
        body,
        out_shape=outs,
        grid_spec=pltpu.PrefetchScalarGridSpec(
            num_scalar_prefetch=1,
            grid=(steps,),
            in_specs=in_specs,
            out_specs=out_specs,
            scratch_shapes=scratch,
        ),
        compiler_params=pltpu.CompilerParams(vmem_limit_bytes=VMEM_LIMIT),
        cost_estimate=pl.CostEstimate(
            flops=flops, transcendentals=0, bytes_accessed=20 * 1024 * 1024
        ),
    )(places, *ins)


def run_feed_forward(places, pieces, tokens, cot, w_out, vectors, w_up, b_up, w_down, dims):
    seq_count, seq_parts = dims
    rows, features = tokens.shape
    hidden = w_up.shape[1]
    steps = 8
    tile = hidden // steps
    out, bf16, f32 = jax.ShapeDtypeStruct, jnp.bfloat16, jnp.float32
    square = (rows, features)
    up_spec = pl.BlockSpec((features, tile), lambda p, places: (0, places[p]))
    down_spec = pl.BlockSpec((tile, features), lambda p, places: (places[p], 0))
    bias_spec = pl.BlockSpec((1, tile), lambda p, places: (0, places[p]))
    kept_spec = pl.BlockSpec((1, rows, tile), lambda p, places: (p, 0, 0))
    return step_call(
        functools.partial(feed_forward, (seq_count, seq_parts, steps)),
        places,
        steps,
        [*pieces, tokens, cot, w_out, vectors, w_up, b_up, w_down],
        [whole_spec(p.shape) for p in pieces]
        + [whole_spec(square), whole_spec(square), whole_spec(w_out.shape), whole_spec(vectors.shape)]
        + [up_spec, bias_spec, down_spec],
        [
            out(square, bf16),
            out((features, rows), bf16),
            out(square, f32),
            out(square, bf16),
            out((steps, rows, tile), bf16),
            out((steps, rows, tile), bf16),
            out(square, f32),
            out(square, bf16),
            out((8, features), f32),
        ],
        [
            whole_spec(square),
            whole_spec((features, rows)),
            whole_spec(square),
            whole_spec(square),
            kept_spec,
            kept_spec,
            whole_spec(square),
            whole_spec(square),
            whole_spec((8, features)),
        ],
        [pltpu.VMEM(square, f32), pltpu.VMEM(square, f32)],
        2 * rows * features * (2 * hidden + features),
    )


def back_specs(first, rows, features, tile):
    kept = pl.BlockSpec((1, rows, tile), lambda p, places: (p + first, 0, 0))
    up = pl.BlockSpec((features, tile), lambda p, places: (0, places[p + first]))
    down = pl.BlockSpec((tile, features), lambda p, places: (places[p + first], 0))
    bias = pl.BlockSpec((1, tile), lambda p, places: (0, places[p + first] % 4))
    grad_down = pl.BlockSpec((1, tile, features), lambda p, places: (p, 0, 0))
    grad_up = pl.BlockSpec((1, features, tile), lambda p, places: (p, 0, 0))
    return [kept, kept, up, down], [grad_down, grad_up, bias]


def run_back_send(places, active, slope, w_up, w_down, first_low, d_lowered, d_second):
    steps_all, rows, tile = active.shape
    features = first_low.shape[1]
    steps = steps_all // 2
    out, bf16, f32 = jax.ShapeDtypeStruct, jnp.bfloat16, jnp.float32
    square = (rows, features)
    ins, outs = back_specs(steps, rows, features, tile)
    return step_call(
        back_send,
        places,
        steps,
        [active, slope, w_up, w_down, first_low, d_lowered, d_second],
        ins + [whole_spec(square)] * 3,
        [
            out((steps, tile, features), bf16),
            out((steps, features, tile), bf16),
            out((1, steps * tile), f32),
            out(square, f32),
        ],
        outs + [whole_spec(square)],
        [pltpu.VMEM((features, rows), bf16)],
        8 * rows * features * steps * tile,
    )


def run_back_keep(
    places, active, slope, w_up, w_down, first_low, d_lowered, d_part, first_in, context, w_out,
    vectors, dims,
):
    seq_count, seq_parts = dims
    steps_all, rows, tile = active.shape
    features = first_low.shape[1]
    steps = steps_all // 2
    out, bf16, f32 = jax.ShapeDtypeStruct, jnp.bfloat16, jnp.float32
    square = (rows, features)
    turned = (features, rows)
    piece = (features // seq_parts, rows // seq_count)
    count = seq_count * seq_parts
    out_blocks = (seq_parts, 8, features // seq_parts // 4, features // 2)
    ins, outs = back_specs(0, rows, features, tile)
    return step_call(
        functools.partial(back_keep, (seq_count, seq_parts, steps)),
        places,
        steps,
        [active, slope, w_up, w_down, first_low, d_lowered, d_part, first_in, context, w_out, vectors],
        ins
        + [whole_spec(square)] * 4
        + [whole_spec(turned), whole_spec(w_out.shape), whole_spec(vectors.shape)],
        [
            out((steps, tile, features), bf16),
            out((steps, features, tile), bf16),
            out((1, steps * tile), f32),
            out(square, f32),
            out((8, features), f32),
            out(out_blocks, bf16),
        ]
        + [out(piece, bf16)] * count,
        outs
        + [whole_spec(square), whole_spec((8, features)), whole_spec(out_blocks)]
        + [whole_spec(piece)] * count,
        [pltpu.VMEM(turned, bf16), pltpu.VMEM(square, f32), pltpu.VMEM(turned, bf16)],
        8 * rows * features * steps * tile,
    )


def place_rows(places, *refs):
    pieces, out = refs[:8], refs[8]
    step = pl.program_id(0)
    for k, piece in enumerate(pieces):

        @pl.when(step == k)
        def copy():
            tile = piece.shape[1]
            for q in range(4):
                out[pl.ds(pl.multiple_of((q ^ places[8]) * tile, tile), tile), :] = piece[q].astype(
                    jnp.float32
                )


def gather_hidden(places, pieces, shape):
    _, rows, cols = pieces[0].shape
    by_rows = shape[1] == cols
    block = (4 * rows, cols)
    index = (lambda p, places: (places[p], 0)) if by_rows else (lambda p, places: (0, places[p]))
    return step_call(
        place_rows,
        places,
        8,
        pieces,
        [whole_spec(p.shape) for p in pieces],
        jax.ShapeDtypeStruct(shape, jnp.float32),
        pl.BlockSpec(block, index),
        [],
        8 * rows * cols,
    )


def place_blocks(places, *refs):
    pieces, out = refs[:-1], refs[-1]
    mine, inner = places[9], places[10]
    step = pl.program_id(0)
    block_rows, block_cols = pieces[0].shape[1:]
    across = out.shape[1] // block_cols
    for k, piece in enumerate(pieces):

        @pl.when(step == k)
        def copy():
            for q in range(piece.shape[0]):
                row, col = q // across * block_rows, q % across * block_cols
                out[row : row + block_rows, col : col + block_cols] = piece[q ^ inner].astype(
                    jnp.float32
                )


def gather_out(places, pieces, shape):
    wide = shape[0] // len(pieces)
    return step_call(
        place_blocks,
        places,
        len(pieces),
        pieces,
        [whole_spec(p.shape) for p in pieces],
        jax.ShapeDtypeStruct(shape, jnp.float32),
        pl.BlockSpec((wide, shape[1]), lambda p, places: (p ^ places[9], 0)),
        [],
        1000,
    )


def place_heads(places, *refs):
    pieces, out = refs[:-1], refs[-1]
    mine, inner = places[9], places[10]
    seq_parts = len(pieces)
    step = pl.program_id(0)
    wide = pieces[0].shape[2] // 3
    for r, piece in enumerate(pieces):
        for j in range(seq_parts):

            @pl.when((r ^ mine) == j)
            def copy():
                rows = piece[step ^ inner].astype(jnp.float32)
                for k in range(3):
                    start = (k * seq_parts + j) * wide
                    out[:, start : start + wide] = rows[:, k * wide : (k + 1) * wide]


def gather_heads(places, pieces, shape):
    rows = pieces[0].shape[1]
    return step_call(
        place_heads,
        places,
        8,
        pieces,
        [whole_spec(p.shape) for p in pieces],
        jax.ShapeDtypeStruct(shape, jnp.float32),
        pl.BlockSpec((rows, shape[1]), lambda p, places: (p, 0)),
        [],
        1000,
    )


def per_device(
    tokens,
    cotangent,
    lengths,
    block_perm,
    w_qkv,
    b_query,
    b_value,
    w_out,
    b_out,
    ln1_gain,
    ln1_shift,
    w_up,
    b_up,
    w_down,
    b_down,
    ln2_gain,
    ln2_shift,
):
    seq_parts = lax.axis_size("seq")
    mine = lax.axis_index("seq")
    seq_count, local_rows, features = tokens.shape
    flat_rows = seq_count * local_rows
    hidden = w_up.shape[1]
    heads = HEADS // seq_parts
    wide = heads * HEAD_DIM
    dims = (seq_count, seq_parts)
    f32 = jnp.float32

    w_heads = jnp.concatenate(
        [
            lax.dynamic_slice_in_dim(w_qkv, k * features + mine * wide, wide, axis=1)
            for k in range(3)
        ],
        axis=1,
    )
    w_t = w_heads.T
    bias = jnp.concatenate(
        [
            lax.dynamic_slice_in_dim(b_query, mine * wide, wide),
            jnp.zeros((wide,), b_query.dtype),
            lax.dynamic_slice_in_dim(b_value, mine * wide, wide),
        ]
    ).astype(f32)[:, None]
    outer = own_number("cyl")
    places = jnp.concatenate(
        [
            jnp.arange(8, dtype=jnp.int32) ^ outer,
            jnp.stack([own_number("hx"), mine, own_number("ylh")]),
            lengths,
        ]
    )
    infos = [
        jnp.stack([lengths[s] // 2, block_perm[s, 0], block_perm[s, 1], mine, own_number("ylh")])
        for s in range(seq_count)
    ]
    vectors = jnp.stack(
        [v.astype(f32) for v in (b_out, ln1_gain, ln1_shift, b_down, ln2_gain, ln2_shift, b_out, b_out)]
    )

    arrived, kept = [], []
    for s in range(seq_count):
        near = tokens[s]
        across = exchange_bit(near, "x")
        pieces = [near, exchange_bit(near, "c"), across, exchange_bit(across, "c")]
        contexts, saved = attention_forward(infos[s], pieces, w_t, bias, heads)
        kept.append(saved)
        arrived += [contexts[0]] + [exchange(contexts[r], "seq", r) for r in range(1, seq_parts)]

    (
        out_rows,
        context,
        first_in,
        first_low,
        active,
        slope,
        d_second,
        d_lowered,
        sums_two,
    ) = run_feed_forward(
        places,
        arrived,
        tokens.reshape(flat_rows, features),
        cotangent.reshape(flat_rows, features),
        w_out,
        vectors,
        w_up,
        b_up.astype(f32).reshape(1, hidden),
        w_down,
        dims,
    )
    out_tokens = out_rows.reshape(seq_count, local_rows, features)
    send_down, send_up, b_up_send, d_part = run_back_send(
        places, active, slope, w_up, w_down, first_low, d_lowered, d_second
    )
    came_down = exchange_bit(send_down, "c")
    came_up = exchange_bit(send_up, "c")
    keep_down, keep_up, b_up_keep, d_first_in, sums_one, grad_out, *d_contexts = run_back_keep(
        places, active, slope, w_up, w_down, first_low, d_lowered, d_part, first_in, context, w_out,
        vectors, dims,
    )

    down_y = exchange_bit(sum_low(keep_down[2:], came_down[2:]), "y")
    down_l = exchange_bit(sum_low(keep_down[1], came_down[1], down_y[1]), "l")
    down_own = sum_low(keep_down[0], came_down[0], down_y[0], down_l)
    down_own = add_extra(halve(down_own.reshape(4, hidden // 32, features), "hx"))
    up_l3 = exchange_bit(sum_low(keep_up[3], came_up[3]), "l")
    up_l1 = exchange_bit(sum_low(keep_up[1], came_up[1]), "l")
    up_y = exchange_bit(sum_low(keep_up[2], came_up[2], up_l3), "y")
    up_own = sum_low(keep_up[0], came_up[0], up_l1, up_y)
    up_own = add_extra(halve(up_own.reshape(4, features // 4, hidden // 8), "hx"))
    out_x = exchange_bit(grad_out[2:], "x")
    out_c = exchange_bit(sum_low(grad_out[1], out_x[1]), "c")
    out_own = add_extra(halve(sum_low(grad_out[0], out_x[0], out_c), "ylh"))

    down_pieces = spread([double(down_own, "hx")], "cyl")
    up_first = double(up_own, "hx")
    up_two = exchange_bit(up_first, "y")
    up_four = [up_first, exchange_bit(up_first, "l"), up_two, exchange_bit(up_two, "l")]
    up_pieces = spread(up_four, "c")
    out_pieces = spread([double(out_own, "ylh")], "xc")
    full_down = gather_hidden(places, down_pieces, (hidden, features))
    full_up = gather_hidden(places, up_pieces, (features, hidden))
    full_out = gather_out(places, out_pieces, (features, features))

    half_hidden = jnp.where(
        (outer >= 4), jnp.concatenate([b_up_send, b_up_keep], axis=1),
        jnp.concatenate([b_up_keep, b_up_send], axis=1),
    )
    packed = jnp.concatenate(
        [sums_one[:3].reshape(-1), sums_two[:3].reshape(-1), half_hidden.reshape(-1)]
    )
    packed = sum_all(packed.reshape(-1, 128), ("seq", "dp")).reshape(-1)
    (
        full_b_out,
        full_gain_one,
        full_shift_one,
        full_b_down,
        full_gain_two,
        full_shift_two,
    ) = [packed[i * features : (i + 1) * features] for i in range(6)]
    full_b_up = packed[6 * features :]

    total_w = jnp.zeros((features, 3 * wide), f32)
    total_b = jnp.zeros((3 * wide, 1), f32)
    d_inputs = []
    for s in range(seq_count):
        pieces = d_contexts[s * seq_parts : (s + 1) * seq_parts]
        pieces = pieces[:1] + [exchange(pieces[r], "seq", r) for r in range(1, seq_parts)]
        parts, total_w, part_b = attention_backward(
            infos[s], pieces, w_t, kept[s], total_w, heads, s == seq_count - 1
        )
        total_b = total_b + part_b
        near = parts[0].astype(f32) + exchange_bit(parts[1], "c")
        far = (parts[2].astype(f32) + exchange_bit(parts[3], "c")).astype(jnp.bfloat16)
        d_inputs.append(near + exchange_bit(far, "x"))
    own_pos = mine * local_rows + jnp.arange(local_rows, dtype=jnp.int32)
    live = (own_pos[None, :] < lengths[:, None]).astype(f32)
    grad_tokens = (
        jnp.stack(d_inputs) + d_first_in.reshape(seq_count, local_rows, features)
    ) * live[:, :, None]

    qkv_own = add_extra(halve(total_w, "ylh"))
    full_qkv = gather_heads(
        places, spread([double(qkv_own, "ylh")], "xc"), (features, 3 * features)
    )
    b_all = double(sum_all(total_b.reshape(1, 3 * wide), ("dp",)), "xc")
    b_rows = [
        lax.dynamic_slice_in_dim(b_all, j ^ mine, 1, axis=0).reshape(3 * wide)
        for j in range(seq_parts)
    ]
    full_b_query = jnp.concatenate([row[:wide] for row in b_rows])
    full_b_value = jnp.concatenate([row[2 * wide :] for row in b_rows])
    return (
        out_tokens,
        grad_tokens,
        full_qkv,
        full_b_query,
        full_b_value,
        full_out,
        full_b_out,
        full_gain_one,
        full_shift_one,
        full_up,
        full_b_up,
        full_down,
        full_b_down,
        full_gain_two,
        full_shift_two,
    )


def solution(mesh):
    in_specs = (
        P("dp", "seq", None),
        P("dp", "seq", None),
        P("dp"),
        P("dp", None),
        P(),
        P(),
        P(),
        P(),
        P(),
        P(),
        P(),
        P(),
        P(),
        P(),
        P(),
        P(),
        P(),
    )
    out_specs = (
        P("dp", "seq", None),
        P("dp", "seq", None),
        P(),
        P(),
        P(),
        P(),
        P(),
        P(),
        P(),
        P(),
        P(),
        P(),
        P(),
        P(),
        P(),
    )
    return jax.shard_map(
        per_device, mesh=mesh, in_specs=in_specs, out_specs=out_specs, check_vma=False
    )
```

```python
import functools
import jax
import jax.numpy as jnp
from jax import lax
from jax.experimental import pallas as pl
from jax.experimental.pallas import tpu as pltpu
from jax.sharding import PartitionSpec as P

HEAD_DIM = 64
SOFT = HEAD_DIM ** -0.5 * 1.4426950408889634
NN = (((1,), (0,)), ((), ()))
NT = (((1,), (1,)), ((), ()))
TN = (((0,), (0,)), ((), ()))
VMEM_LIMIT = 50 * 1024 * 1024
HEADS = 12
EPSILON = 1e-06
BITS = {"c": ("seq", 0), "x": ("seq", 1), "y": ("dp", 0), "l": ("dp", 1), "h": ("dp", 2)}


def own_number(order):
    number = jnp.int32(0)
    for letter in order:
        axis, shift = BITS[letter]
        number = number * 2 + ((lax.axis_index(axis) >> shift) & 1)
    return number


def exchange(array_in, axis, flip):
    return lax.ppermute(array_in, axis, [(i, i ^ flip) for i in range(lax.axis_size(axis))])


def exchange_bit(array_in, letter):
    axis, shift = BITS[letter]
    return exchange(array_in, axis, 1 << shift)


def extra_flips(axis, used):
    return [1 << shift for shift in range(used, lax.axis_size(axis).bit_length() - 1)]


def add_extra(array_in):
    for flip in extra_flips("dp", 3):
        array_in = array_in + exchange(array_in, "dp", flip)
    return array_in


def sum_low(*parts):
    total = parts[0].astype(jnp.float32)
    for part in parts[1:]:
        total = total + part.astype(jnp.float32)
    return total.astype(jnp.bfloat16)


def dot_f32(left, right, dims):
    return lax.dot_general(left, right, dims, preferred_element_type=jnp.float32)


def shift_matrix(half, block, whole):
    row = lax.broadcasted_iota(jnp.int32, (block, whole), 0)
    col = lax.broadcasted_iota(jnp.int32, (block, whole), 1)
    return jnp.where((col == row + half) & (row < half), 1.0, 0.0).astype(jnp.bfloat16)


def mask_tiles(half, block):
    row = lax.broadcasted_iota(jnp.int32, (16, block), 0)
    col = lax.broadcasted_iota(jnp.int32, (16, block), 1)
    key_tile = jnp.where((row == 0) & (col >= half), -1e30, 0.0).astype(jnp.bfloat16)
    query_tile = jnp.where(row == 0, 1.0, 0.0).astype(jnp.bfloat16)
    return key_tile, query_tile


def attend_forward(
    heads, info, x0, x1, x2, x3, w_t, bias, c0, c1, c2, c3, qkv, ctx_blk, lse, x_t, x_seq, qkv_s, c_tok
):
    half, mine = info[0], info[3]
    whole = x_seq.shape[0]
    quarter = whole // 4
    block = whole // 2
    wide = heads * HEAD_DIM
    for r, piece in enumerate((x0, x1, x2, x3)):
        x_seq[pl.ds(pl.multiple_of((r ^ mine) * quarter, quarter), quarter), :] = piece[...]
    row = lax.broadcasted_iota(jnp.int32, (block, 1), 0)
    shift = shift_matrix(half, block, whole)
    first = jnp.where(row < half, x_seq[0:block, :], jnp.zeros((), jnp.bfloat16))
    second = dot_f32(shift, x_seq[...], NN).astype(jnp.bfloat16)
    for b, rows in enumerate((first, second)):
        turned = rows.T
        x_t[b] = turned
        projected = dot_f32(w_t[...], turned, NN) + bias[...]
        qkv_s[b] = projected.astype(jnp.bfloat16)
    qkv[...] = qkv_s[...]
    key_tile, query_tile = mask_tiles(half, block)

    def one_block(b, carry):
        target = info[1 + b]
        for h in range(heads):
            rows = slice(h * HEAD_DIM, (h + 1) * HEAD_DIM)
            q_t = jnp.concatenate([qkv_s[b, rows, :], query_tile])
            k_t = jnp.concatenate(
                [qkv_s[target, wide + h * HEAD_DIM : wide + (h + 1) * HEAD_DIM, :], key_tile]
            )
            v_t = qkv_s[target, 2 * wide + h * HEAD_DIM : 2 * wide + (h + 1) * HEAD_DIM, :]
            scores = dot_f32(k_t, q_t, TN) * SOFT
            top = jnp.max(scores, axis=0, keepdims=True)
            expo = jnp.exp2(scores - top)
            total = jnp.sum(expo, axis=0, keepdims=True)
            context = dot_f32(v_t, expo.astype(jnp.bfloat16), NN) / total
            ctx_blk[b, rows, :] = context
            lse[b, h : h + 1, :] = top + jnp.log2(total)
        return carry

    lax.fori_loop(0, 2, one_block, 0)
    lane = lax.broadcasted_iota(jnp.int32, (1, block), 1)
    early = jnp.where(lane < half, ctx_blk[0], 0.0)
    late = dot_f32(ctx_blk[1].astype(jnp.bfloat16), shift, NN)
    for j in range(4):
        part = late[:, j * quarter : (j + 1) * quarter]
        if j < 2:
            part = part + early[:, j * quarter : (j + 1) * quarter]
        c_tok[j] = part.astype(jnp.bfloat16)
    for r, piece in enumerate((c0, c1, c2, c3)):
        piece[...] = c_tok[r ^ mine]


def attend_backward(
    heads, index, info, g0, g1, g2, g3, w_t, qkv, ctx_blk, lse, x_t, acc, *refs
):
    last = len(refs) == 11
    (dx0, dx1, dx2, dx3, grad_w, grad_b, g_tok, g_blk, d_qkv, dx_s) = refs[-10:]
    half, mine = info[0], info[3]
    quarter = g0.shape[2]
    block = 2 * quarter
    whole = 4 * quarter
    wide = heads * HEAD_DIM
    for r, piece in enumerate((g0[index], g1[index], g2[0, index], g3[index])):
        g_tok[r ^ mine] = piece
    shift = shift_matrix(half, block, whole)
    lane = lax.broadcasted_iota(jnp.int32, (1, block), 1)
    g_all = jnp.concatenate([g_tok[j] for j in range(4)], axis=1)
    g_blk[0] = jnp.where(lane < half, g_all[:, :block], jnp.zeros((), jnp.bfloat16))
    g_blk[1] = dot_f32(g_all, shift, NT).astype(jnp.bfloat16)
    key_tile, query_tile = mask_tiles(half, block)

    def one_block(b, carry):
        target = info[1 + b]
        for h in range(heads):
            rows = slice(h * HEAD_DIM, (h + 1) * HEAD_DIM)
            k_rows = slice(wide + h * HEAD_DIM, wide + (h + 1) * HEAD_DIM)
            v_rows = slice(2 * wide + h * HEAD_DIM, 2 * wide + (h + 1) * HEAD_DIM)
            q_t = qkv[b, rows, :]
            k_t = qkv[target, k_rows, :]
            v_t = qkv[target, v_rows, :]
            g_t = g_blk[b, rows, :]
            scores = dot_f32(
                jnp.concatenate([k_t, key_tile]), jnp.concatenate([q_t, query_tile]), TN
            )
            probs = jnp.exp2(scores * SOFT - lse[b, h : h + 1, :])
            d_probs = dot_f32(v_t, g_t, TN)
            delta = jnp.sum(ctx_blk[b, rows, :] * g_t.astype(jnp.float32), axis=0, keepdims=True)
            d_scores = (probs * (d_probs - delta)).astype(jnp.bfloat16)
            scaling = HEAD_DIM ** -0.5
            d_qkv[b, rows, :] = (dot_f32(k_t, d_scores, NN) * scaling).astype(jnp.bfloat16)
            d_qkv[target, k_rows, :] = (dot_f32(q_t, d_scores, NT) * scaling).astype(jnp.bfloat16)
            d_qkv[target, v_rows, :] = dot_f32(g_t, probs.astype(jnp.bfloat16), NT).astype(
                jnp.bfloat16
            )
        return carry

    lax.fori_loop(0, 2, one_block, 0)
    early, late = d_qkv[0], d_qkv[1]
    total = acc[...] + dot_f32(x_t[0], early, NT) + dot_f32(x_t[1], late, NT)
    if last:
        tile = grad_w.shape[1]
        for q in range(8):
            grad_w[q ^ info[4], :, : 3 * wide] = total[q * tile : (q + 1) * tile].astype(jnp.bfloat16)
        grad_w[:, :, 3 * wide :] = refs[0][...]
    else:
        grad_w[...] = total
    grad_b[...] = jnp.sum(early.astype(jnp.float32), axis=1, keepdims=True) + jnp.sum(
        late.astype(jnp.float32), axis=1, keepdims=True
    )
    back = dot_f32(late, shift, NN)
    front = jnp.where(lane < half, early.astype(jnp.float32), 0.0)
    for j in range(4):
        part = back[:, j * quarter : (j + 1) * quarter]
        if j < 2:
            part = part + front[:, j * quarter : (j + 1) * quarter]
        dx_s[j] = dot_f32(part.astype(jnp.bfloat16), w_t[...], TN).astype(jnp.bfloat16)
    for r, piece in enumerate((dx0, dx1, dx2, dx3)):
        piece[...] = dx_s[r ^ mine]


def kernel_call(body, scalars, arrays, outs, scratch, aliases={}):
    return pl.pallas_call(
        body,
        out_shape=outs,
        in_specs=[pl.BlockSpec(memory_space=pltpu.SMEM)]
        + [pl.BlockSpec(memory_space=pltpu.VMEM)] * len(arrays),
        out_specs=[pl.BlockSpec(memory_space=pltpu.VMEM)] * len(outs),
        scratch_shapes=scratch,
        input_output_aliases=aliases,
        compiler_params=pltpu.CompilerParams(vmem_limit_bytes=VMEM_LIMIT),
        cost_estimate=pl.CostEstimate(
            flops=6 * 10**9, transcendentals=0, bytes_accessed=20 * 1024 * 1024
        ),
    )(scalars, *arrays)


def attention_forward(info, pieces, w_t, bias, heads):
    quarter, features = pieces[0].shape
    whole, block, wide = 4 * quarter, 2 * quarter, heads * HEAD_DIM
    out = jax.ShapeDtypeStruct
    outs = [out((wide, quarter), jnp.bfloat16)] * 4 + [
        out((2, 3 * wide, block), jnp.bfloat16),
        out((2, wide, block), jnp.float32),
        out((2, 8, block), jnp.float32),
        out((2, features, block), jnp.bfloat16),
    ]
    scratch = [
        pltpu.VMEM((whole, features), jnp.bfloat16),
        pltpu.VMEM((2, 3 * wide, block), jnp.bfloat16),
        pltpu.VMEM((4, wide, quarter), jnp.bfloat16),
    ]
    found = kernel_call(
        functools.partial(attend_forward, heads), info, [*pieces, w_t, bias], outs, scratch
    )
    return found[:4], found[4:]


def attention_backward(info, pieces, index, w_t, kept, acc, heads, out_own=None):
    _, wide, quarter = pieces[0].shape
    features = w_t.shape[1]
    block = 2 * quarter
    out = jax.ShapeDtypeStruct
    outs = [out((quarter, features), jnp.bfloat16)] * 4 + [
        out((features, 3 * wide), jnp.float32)
        if out_own is None
        else out((8, features // 8, 4 * wide), jnp.bfloat16),
        out((3 * wide, 1), jnp.float32),
    ]
    scratch = [
        pltpu.VMEM((4, wide, quarter), jnp.bfloat16),
        pltpu.VMEM((2, wide, block), jnp.bfloat16),
        pltpu.VMEM((2, 3 * wide, block), jnp.bfloat16),
        pltpu.VMEM((4, quarter, features), jnp.bfloat16),
    ]
    found = kernel_call(
        functools.partial(attend_backward, heads, index),
        info,
        [*pieces, w_t, *kept, acc] + ([] if out_own is None else [out_own]),
        outs,
        scratch,
    )
    return found[:4], found[4], found[5]

def live_rows(places, rows, mine, local_rows, offset):
    row = lax.broadcasted_iota(jnp.int32, (rows, 1), 0)
    length = jnp.zeros((rows, 1), jnp.int32)
    for s in range(rows // local_rows):
        length = jnp.where(row >= s * local_rows, places[offset + s], length)
    position = mine * local_rows + lax.rem(row, local_rows)
    return jnp.where(position < length, 1.0, 0.0)


def normal_parts(array_in):
    centered = array_in - jnp.mean(array_in, axis=1, keepdims=True)
    spread = jnp.mean(centered * centered, axis=1, keepdims=True)
    inverse = lax.rsqrt(spread + EPSILON)
    return centered * inverse, inverse


def normal_back(hat, inverse, gain, d_out):
    scaled = d_out * gain
    mean_scaled = jnp.mean(scaled, axis=1, keepdims=True)
    mean_product = jnp.mean(scaled * hat, axis=1, keepdims=True)
    return inverse * (scaled - mean_scaled - hat * mean_product)


def column_sum(array_in):
    return jnp.sum(array_in, axis=0, keepdims=True)


def feed_forward(shape, places, *refs):
    seq_count, seq_parts, steps = shape
    pieces, refs = refs[: seq_count * seq_parts], refs[seq_count * seq_parts :]
    tokens, cot, w_out, vectors, w_up, b_up, w_down = refs[:7]
    out, context, first_in, first_low, active, slope, d_second, d_lowered, sums = refs[7:16]
    first_norm, lowered = refs[16:]
    rows, features = tokens.shape
    local_rows = rows // seq_count
    wide = features // seq_parts
    mine = places[9]
    step = pl.program_id(0)
    f32 = jnp.float32

    @pl.when(step == 0)
    def start():
        for s in range(seq_count):
            for r in range(seq_parts):
                context[
                    pl.ds(pl.multiple_of((r ^ mine) * wide, wide), wide),
                    s * local_rows : (s + 1) * local_rows,
                ] = pieces[s * seq_parts + r][...]
        live = live_rows(places, rows, mine, local_rows, 11)
        attended = dot_f32(context[...], w_out[...], TN) + vectors[0:1, :]
        total = jnp.where(live > 0, tokens[...].astype(f32), 0.0) + attended
        first_in[...] = total
        hat, _ = normal_parts(total)
        normed = hat * vectors[1:2, :] + vectors[2:3, :]
        first_norm[...] = normed
        first_low[...] = normed.astype(jnp.bfloat16)

    lifted = dot_f32(first_low[...], w_up[...], NN) + b_up[...]
    cdf = 0.5 * (1.0 + lax.erf(lifted * 0.7071067811865476))
    density = jnp.exp(lifted * lifted * -0.5) * 0.3989422804014327
    gelu = (lifted * cdf).astype(jnp.bfloat16)
    active[0] = gelu
    slope[0] = (cdf + lifted * density).astype(jnp.bfloat16)
    part = dot_f32(gelu, w_down[...], NN)

    @pl.when(step == 0)
    def first():
        lowered[...] = part

    @pl.when(step > 0)
    def later():
        lowered[...] += part

    @pl.when(step == steps - 1)
    def finish():
        live = live_rows(places, rows, mine, local_rows, 11)
        hat, inverse = normal_parts(first_norm[...] + (lowered[...] + vectors[3:4, :]))
        gain = vectors[4:5, :]
        out[...] = ((hat * gain + vectors[5:6, :]) * live).astype(jnp.bfloat16)
        incoming = cot[...].astype(f32) * live
        back = normal_back(hat, inverse, gain, incoming)
        d_second[...] = back
        low = back.astype(jnp.bfloat16)
        d_lowered[...] = low
        sums[0:1, :] = column_sum(low.astype(f32))
        sums[1:2, :] = column_sum(incoming * hat)
        sums[2:3, :] = column_sum(incoming)


def hidden_back(places, active, slope, w_up, w_down, first_t, d_lowered, grad_down, grad_up, grad_b):
    inner = places[8]
    f32 = jnp.float32
    down = dot_f32(active[0], d_lowered[...], TN).astype(jnp.bfloat16)
    tile = down.shape[0] // 4
    for q in range(4):
        grad_down[0, pl.ds(pl.multiple_of((q ^ inner) * tile, tile), tile), :] = down[
            q * tile : (q + 1) * tile
        ]
    d_active = dot_f32(d_lowered[...], w_down[...], NT)
    d_lifted = (d_active * slope[0].astype(f32)).astype(jnp.bfloat16)
    grad_b[...] = column_sum(d_lifted.astype(f32))
    grad_up[0] = dot_f32(first_t[...], d_lifted, NN).astype(jnp.bfloat16)
    return dot_f32(d_lifted, w_up[...], NT)


def turn_rows(places, source, target):
    inner = places[8]
    tile = target.shape[0] // 4
    turned = source[...].T
    for q in range(4):
        target[pl.ds(pl.multiple_of((q ^ inner) * tile, tile), tile), :] = turned[
            q * tile : (q + 1) * tile
        ]


def back_send(
    places, active, slope, w_up, w_down, first_low, d_lowered, d_second,
    grad_down, grad_up, grad_b, d_first, first_t,
):
    step = pl.program_id(0)

    @pl.when(step == 0)
    def start():
        turn_rows(places, first_low, first_t)
        d_first[...] = d_second[...]

    d_first[...] += hidden_back(
        places, active, slope, w_up, w_down, first_t, d_lowered, grad_down, grad_up, grad_b
    )


def back_keep(shape, places, *refs):
    seq_count, seq_parts, steps = shape
    active, slope, w_up, w_down, first_low, d_lowered, d_part = refs[:7]
    first_in, context, w_out, vectors = refs[7:11]
    grad_down, grad_up, grad_b, d_first_in, sums, grad_out = refs[11:17]
    pieces = refs[17:-3]
    first_t, d_first, turned = refs[-3:]
    step = pl.program_id(0)
    f32 = jnp.float32

    @pl.when(step == 0)
    def start():
        turn_rows(places, first_low, first_t)
        d_first[...] = d_part[...]

    d_first[...] += hidden_back(
        places, active, slope, w_up, w_down, first_t, d_lowered, grad_down, grad_up, grad_b
    )

    @pl.when(step == steps - 1)
    def finish():
        rows, features = first_in.shape
        local_rows = rows // seq_count
        wide = features // seq_parts
        mine = places[9]
        hat, inverse = normal_parts(first_in[...])
        incoming = d_first[...]
        back = normal_back(hat, inverse, vectors[1:2, :], incoming)
        d_first_in[...] = back
        low = back.astype(jnp.bfloat16)
        sums[0:1, :] = column_sum(low.astype(f32))
        sums[1:2, :] = column_sum(incoming * hat)
        sums[2:3, :] = column_sum(incoming)
        turned[...] = dot_f32(w_out[...], low, NT).astype(jnp.bfloat16)
        for r in range(seq_parts):
            own = turned[pl.ds(pl.multiple_of((r ^ mine) * wide, wide), wide), :]
            for s in range(seq_count):
                target, place = pieces[3 * min(s, 1) + min(r, 2)], max(s - 1, 0)
                columns = own[:, s * local_rows : (s + 1) * local_rows]
                if r < 2:
                    target[place] = columns
                else:
                    target[r - 2, place] = columns
        product = dot_f32(context[...], low, NN).astype(jnp.bfloat16)
        block_rows, block_cols = grad_out.shape[2:]
        across = features // block_cols
        for j in range(seq_parts):
            for q in range(wide // block_rows * across):
                row, col = j * wide + q // across * block_rows, q % across * block_cols
                grad_out[j ^ mine, q ^ places[10]] = product[
                    row : row + block_rows, col : col + block_cols
                ]


def whole_spec(shape):
    return pl.BlockSpec(shape, lambda p, places: (0,) * len(shape))


def step_call(body, places, steps, ins, in_specs, outs, out_specs, scratch, flops):
    return pl.pallas_call(
        body,
        out_shape=outs,
        grid_spec=pltpu.PrefetchScalarGridSpec(
            num_scalar_prefetch=1,
            grid=(steps,),
            in_specs=in_specs,
            out_specs=out_specs,
            scratch_shapes=scratch,
        ),
        compiler_params=pltpu.CompilerParams(vmem_limit_bytes=VMEM_LIMIT),
        cost_estimate=pl.CostEstimate(
            flops=flops, transcendentals=0, bytes_accessed=20 * 1024 * 1024
        ),
    )(places, *ins)


def run_feed_forward(places, pieces, tokens, cot, w_out, vectors, w_up, b_up, w_down, dims):
    seq_count, seq_parts = dims
    rows, features = tokens.shape
    hidden = w_up.shape[1]
    steps = 8
    tile = hidden // steps
    out, bf16, f32 = jax.ShapeDtypeStruct, jnp.bfloat16, jnp.float32
    square = (rows, features)
    up_spec = pl.BlockSpec((features, tile), lambda p, places: (0, places[p]))
    down_spec = pl.BlockSpec((tile, features), lambda p, places: (places[p], 0))
    bias_spec = pl.BlockSpec((1, tile), lambda p, places: (0, places[p]))
    kept_spec = pl.BlockSpec((1, rows, tile), lambda p, places: (p, 0, 0))
    return step_call(
        functools.partial(feed_forward, (seq_count, seq_parts, steps)),
        places,
        steps,
        [*pieces, tokens, cot, w_out, vectors, w_up, b_up, w_down],
        [whole_spec(p.shape) for p in pieces]
        + [whole_spec(square), whole_spec(square), whole_spec(w_out.shape), whole_spec(vectors.shape)]
        + [up_spec, bias_spec, down_spec],
        [
            out(square, bf16),
            out((features, rows), bf16),
            out(square, f32),
            out(square, bf16),
            out((steps, rows, tile), bf16),
            out((steps, rows, tile), bf16),
            out(square, f32),
            out(square, bf16),
            out((8, features), f32),
        ],
        [
            whole_spec(square),
            whole_spec((features, rows)),
            whole_spec(square),
            whole_spec(square),
            kept_spec,
            kept_spec,
            whole_spec(square),
            whole_spec(square),
            whole_spec((8, features)),
        ],
        [pltpu.VMEM(square, f32), pltpu.VMEM(square, f32)],
        2 * rows * features * (2 * hidden + features),
    )


def back_specs(first, rows, features, tile):
    kept = pl.BlockSpec((1, rows, tile), lambda p, places: (p + first, 0, 0))
    up = pl.BlockSpec((features, tile), lambda p, places: (0, places[p + first]))
    down = pl.BlockSpec((tile, features), lambda p, places: (places[p + first], 0))
    bias = pl.BlockSpec((1, tile), lambda p, places: (0, places[p + first] % 4))
    grad_down = pl.BlockSpec((1, tile, features), lambda p, places: (p, 0, 0))
    grad_up = pl.BlockSpec((1, features, tile), lambda p, places: (p, 0, 0))
    return [kept, kept, up, down], [grad_down, grad_up, bias]


def run_back_send(places, active, slope, w_up, w_down, first_low, d_lowered, d_second):
    steps_all, rows, tile = active.shape
    features = first_low.shape[1]
    steps = steps_all // 2
    out, bf16, f32 = jax.ShapeDtypeStruct, jnp.bfloat16, jnp.float32
    square = (rows, features)
    ins, outs = back_specs(steps, rows, features, tile)
    return step_call(
        back_send,
        places,
        steps,
        [active, slope, w_up, w_down, first_low, d_lowered, d_second],
        ins + [whole_spec(square)] * 3,
        [
            out((steps, tile, features), bf16),
            out((steps, features, tile), bf16),
            out((1, steps * tile), f32),
            out(square, f32),
        ],
        outs + [whole_spec(square)],
        [pltpu.VMEM((features, rows), bf16)],
        8 * rows * features * steps * tile,
    )


def run_back_keep(
    places, active, slope, w_up, w_down, first_low, d_lowered, d_part, first_in, context, w_out,
    vectors, dims,
):
    seq_count, seq_parts = dims
    steps_all, rows, tile = active.shape
    features = first_low.shape[1]
    steps = steps_all // 2
    out, bf16, f32 = jax.ShapeDtypeStruct, jnp.bfloat16, jnp.float32
    square = (rows, features)
    turned = (features, rows)
    piece = (features // seq_parts, rows // seq_count)
    pieces = []
    for n in (1, seq_count - 1):
        pieces += [(n, *piece), (n, *piece), (2, n, *piece)]
    out_blocks = (seq_parts, 8, features // seq_parts // 2, features // 4)
    ins, outs = back_specs(0, rows, features, tile)
    return step_call(
        functools.partial(back_keep, (seq_count, seq_parts, steps)),
        places,
        steps,
        [active, slope, w_up, w_down, first_low, d_lowered, d_part, first_in, context, w_out, vectors],
        ins
        + [whole_spec(square)] * 4
        + [whole_spec(turned), whole_spec(w_out.shape), whole_spec(vectors.shape)],
        [
            out((steps, tile, features), bf16),
            out((steps, features, tile), bf16),
            out((1, steps * tile), f32),
            out(square, f32),
            out((8, features), f32),
            out(out_blocks, bf16),
        ]
        + [out(p, bf16) for p in pieces],
        outs
        + [whole_spec(square), whole_spec((8, features)), whole_spec(out_blocks)]
        + [whole_spec(p) for p in pieces],
        [pltpu.VMEM(turned, bf16), pltpu.VMEM(square, f32), pltpu.VMEM(turned, bf16)],
        8 * rows * features * steps * tile,
    )


def place_rows(by_rows, places, *refs):
    pieces, out = refs[:4], refs[4]
    step = pl.program_id(0)
    tile = pieces[0].shape[1]
    for k in range(8):
        c, y, l = k >> 2, (k >> 1) & 1, k & 1

        @pl.when(step == k)
        def copy():
            for q in range(4):
                h, x = q >> 1, q & 1
                piece, sub = (c * 2 + y, l * 4 + x * 2 + h) if by_rows else (c * 2 + l, x * 4 + y * 2 + h)
                out[pl.ds(pl.multiple_of((q ^ places[8]) * tile, tile), tile), :] = pieces[piece][
                    sub
                ].astype(jnp.float32)


def gather_hidden(places, pieces, shape, by_rows):
    _, rows, cols = pieces[0].shape
    block = (4 * rows, cols)
    index = (lambda p, places: (places[p], 0)) if by_rows else (lambda p, places: (0, places[p]))
    return step_call(
        functools.partial(place_rows, by_rows),
        places,
        8,
        pieces,
        [whole_spec(p.shape) for p in pieces],
        jax.ShapeDtypeStruct(shape, jnp.float32),
        pl.BlockSpec(block, index),
        [],
        8 * rows * cols,
    )


def place_heads(places, *refs):
    pieces, out, out_w = refs[:-2], refs[-2], refs[-1]
    mine, inner = places[9], places[10]
    seq_parts = len(pieces)
    step = pl.program_id(0)
    wide = out_w.shape[0] // seq_parts
    for r, piece in enumerate(pieces):
        for j in range(seq_parts):

            @pl.when((r ^ mine) == j)
            def copy():
                rows = piece[step ^ inner, :, : 3 * wide].astype(jnp.float32)
                for k in range(3):
                    start = (k * seq_parts + j) * wide
                    out[:, start : start + wide] = rows[:, k * wide : (k + 1) * wide]

        @pl.when(step == r)
        def copy_out():
            tile, width = wide // 2, out_w.shape[1] // 4
            for q in range(8):
                row = pl.multiple_of((r ^ mine) * wide + q // 4 * tile, tile)
                col = q % 4 * width
                out_w[pl.ds(row, tile), col : col + width] = piece[
                    q ^ inner, :, 3 * wide :
                ].astype(jnp.float32)


def gather_heads(places, pieces, shape):
    rows = pieces[0].shape[1]
    square = (shape[0], shape[0])
    return step_call(
        place_heads,
        places,
        8,
        pieces,
        [whole_spec(p.shape) for p in pieces],
        [jax.ShapeDtypeStruct(shape, jnp.float32), jax.ShapeDtypeStruct(square, jnp.float32)],
        [pl.BlockSpec((rows, shape[1]), lambda p, places: (p, 0)), whole_spec(square)],
        [],
        1000,
    )


def per_device(
    tokens,
    cotangent,
    lengths,
    block_perm,
    w_qkv,
    b_query,
    b_value,
    w_out,
    b_out,
    ln1_gain,
    ln1_shift,
    w_up,
    b_up,
    w_down,
    b_down,
    ln2_gain,
    ln2_shift,
):
    seq_parts = lax.axis_size("seq")
    mine = lax.axis_index("seq")
    seq_count, local_rows, features = tokens.shape
    flat_rows = seq_count * local_rows
    hidden = w_up.shape[1]
    heads = HEADS // seq_parts
    wide = heads * HEAD_DIM
    dims = (seq_count, seq_parts)
    f32 = jnp.float32

    w_heads = jnp.concatenate(
        [
            lax.dynamic_slice_in_dim(w_qkv, k * features + mine * wide, wide, axis=1)
            for k in range(3)
        ],
        axis=1,
    )
    w_t = w_heads.T
    bias = jnp.concatenate(
        [
            lax.dynamic_slice_in_dim(b_query, mine * wide, wide),
            jnp.zeros((wide,), b_query.dtype),
            lax.dynamic_slice_in_dim(b_value, mine * wide, wide),
        ]
    ).astype(f32)[:, None]
    outer = own_number("cyl")
    places = jnp.concatenate(
        [
            jnp.arange(8, dtype=jnp.int32) ^ outer,
            jnp.stack([own_number("hx"), mine, own_number("ylh")]),
            lengths,
        ]
    )
    infos = [
        jnp.stack([lengths[s] // 2, block_perm[s, 0], block_perm[s, 1], mine, own_number("ylh")])
        for s in range(seq_count)
    ]
    vectors = jnp.stack(
        [v.astype(f32) for v in (b_out, ln1_gain, ln1_shift, b_down, ln2_gain, ln2_shift, b_out, b_out)]
    )

    arrived, kept = [], []
    for s in range(seq_count):
        near = tokens[s]
        across = exchange_bit(near, "x")
        pieces = [near, exchange_bit(near, "c"), across, exchange_bit(across, "c")]
        contexts, saved = attention_forward(infos[s], pieces, w_t, bias, heads)
        kept.append(saved)
        arrived += [contexts[0]] + [exchange(contexts[r], "seq", r) for r in range(1, seq_parts)]

    (
        out_rows,
        context,
        first_in,
        first_low,
        active,
        slope,
        d_second,
        d_lowered,
        sums_two,
    ) = run_feed_forward(
        places,
        arrived,
        tokens.reshape(flat_rows, features),
        cotangent.reshape(flat_rows, features),
        w_out,
        vectors,
        w_up,
        b_up.astype(f32).reshape(1, hidden),
        w_down,
        dims,
    )
    out_tokens = out_rows.reshape(seq_count, local_rows, features)
    send_down, send_up, b_up_send, d_part = run_back_send(
        places, active, slope, w_up, w_down, first_low, d_lowered, d_second
    )
    came_down = exchange_bit(send_down, "c")
    came_up = exchange_bit(send_up, "c")
    keep_down, keep_up, b_up_keep, d_first_in, sums_one, grad_out, *d_contexts = run_back_keep(
        places, active, slope, w_up, w_down, first_low, d_lowered, d_part, first_in, context, w_out,
        vectors, dims,
    )

    half_hidden = jnp.where(
        (outer >= 4),
        jnp.concatenate([b_up_send, b_up_keep], axis=1),
        jnp.concatenate([b_up_keep, b_up_send], axis=1),
    )
    sums = jnp.concatenate(
        [sums_one[:3].reshape(-1), sums_two[:3].reshape(-1), half_hidden.reshape(-1)]
    ).reshape(-1, 128)
    first_group, second_group = [
        [own, exchange_bit(near, "c"), exchange_bit(pair, "x")]
        for own, near, pair in (d_contexts[:3], d_contexts[3:])
    ]
    for group in (first_group, second_group):
        group.append(exchange_bit(group[2][1], "c"))
    total_w = jnp.zeros((features, 3 * wide), f32)
    total_b = jnp.zeros((3 * wide, 1), f32)
    parts = []

    def attend(s, group, total_w, total_b, out_own=None):
        found, total_w, part_b = attention_backward(
            infos[s], group, max(s - 1, 0), w_t, kept[s], total_w, heads, out_own
        )
        parts.append(found)
        return total_w, total_b + part_b

    sends = [
        sum_low(keep_down[2:], came_down[2:]),
        sum_low(keep_up[1::2], came_up[1::2]),
        grad_out[2:],
    ]
    sends, first_group = lax.optimization_barrier((sends, first_group))
    down_y, up_l, out_x = [exchange_bit(v, bit) for v, bit in zip(sends, "ylx")]
    out_c = exchange_bit(sum_low(grad_out[1], out_x[1]), "c")
    sums = sums + exchange_bit(sums, "c")
    total_w, total_b = attend(0, first_group, total_w, total_b)
    for s in range(1, seq_count - 1):
        total_w, total_b = attend(s, second_group, total_w, total_b)

    out_own = sum_low(grad_out[0], out_x[0], out_c)
    sends = [
        sum_low(keep_down[1], came_down[1], down_y[1]),
        sum_low(keep_up[2], came_up[2], up_l[1]),
        sums,
    ]
    (sends, total_w, parts, out_own) = lax.optimization_barrier((sends, total_w, parts, out_own))
    down_l, up_y, more = [exchange_bit(v, bit) for v, bit in zip(sends, "lyx")]
    sums = sends[2] + more
    near, far = [], []

    def cross(s):
        near.append(parts[s][0].astype(f32) + exchange_bit(parts[s][1], "c"))
        far.append(sum_low(parts[s][2], exchange_bit(parts[s][3], "c")))

    for s in range(seq_count - 1):
        cross(s)
    total_w, total_b = attend(seq_count - 1, second_group, total_w, total_b, out_own)
    (down_l, up_y, far, total_w, total_b, parts[-1], sums) = lax.optimization_barrier(
        (down_l, up_y, far, total_w, total_b, parts[-1], sums)
    )
    small = jnp.concatenate(
        [sums.reshape(-1), total_b.reshape(-1), jnp.zeros((-total_b.shape[0] % 128,), f32)]
    ).reshape(-1, 128)

    down_own = sum_low(keep_down[0], came_down[0], down_y[0], down_l)
    down_own = down_own.reshape(4, hidden // 32, features)
    up_own = sum_low(keep_up[0], came_up[0], up_l[0], up_y)
    up_own = up_own.reshape(2, 2, features // 4, hidden // 8)
    keeps = [down_own[:2], up_own[:, 0], total_w[:4], small]
    sends = [down_own[2:], up_own[:, 1], total_w[4:], small]
    (keeps, sends) = lax.optimization_barrier((keeps, sends))
    got = [exchange_bit(v, bit) for v, bit in zip(sends, "hxyy")]
    far_came = [exchange_bit(v, "x") for v in far]
    down_own, up_own, qkv_own, small = [k + g for k, g in zip(keeps, got)]
    qkv_own = qkv_own[:2] + exchange_bit(qkv_own[2:], "l")
    small = small + exchange_bit(small, "l")
    far = []
    cross(seq_count - 1)

    keeps = [down_own[:1], up_own[:1], qkv_own[:1], small]
    sends = [down_own[1:], up_own[1:], qkv_own[1:], small]
    (keeps, sends, far, far_came) = lax.optimization_barrier((keeps, sends, far, far_came))
    got = [exchange_bit(v, bit) for v, bit in zip(sends, "xhhh")]
    far_came += [exchange_bit(v, "x") for v in far]
    *shards, small = [add_extra(k + g) for k, g in zip(keeps, got)]

    packed = small.reshape(-1)
    row_b = packed[sums.size : sums.size + 3 * wide].reshape(1, 3 * wide)
    for bits in ("hhhc", "xylx", "lxy"):
        (shards, row_b, far_came) = lax.optimization_barrier((shards, row_b, far_came))
        shards = [
            jnp.concatenate([shard, exchange_bit(shard, bit)]) for shard, bit in zip(shards, bits)
        ]
        if len(bits) > 3:
            row_b = jnp.concatenate([row_b, exchange_bit(row_b, bits[3])])
    shards = lax.optimization_barrier(shards)
    last = [exchange_bit(shard, bit) for shard, bit in zip(shards, "ylx")]
    near_c = [exchange_bit(shard, "c") for shard in shards]
    far_c = [exchange_bit(shard, "c") for shard in last]
    full_down, full_up = [
        gather_hidden(places, [shards[i], last[i], near_c[i], far_c[i]], shape, i == 0)
        for i, shape in ((0, (hidden, features)), (1, (features, hidden)))
    ]
    full_qkv, full_out = gather_heads(
        places, [shards[2], near_c[2], last[2], far_c[2]], (features, 3 * features)
    )
    (
        full_b_out,
        full_gain_one,
        full_shift_one,
        full_b_down,
        full_gain_two,
        full_shift_two,
    ) = [packed[i * features : (i + 1) * features] for i in range(6)]
    full_b_up = packed[6 * features : 6 * features + hidden]
    b_rows = [
        lax.dynamic_slice_in_dim(row_b, j ^ mine, 1, axis=0).reshape(3 * wide)
        for j in range(seq_parts)
    ]
    full_b_query = jnp.concatenate([row[:wide] for row in b_rows])
    full_b_value = jnp.concatenate([row[2 * wide :] for row in b_rows])

    own_pos = mine * local_rows + jnp.arange(local_rows, dtype=jnp.int32)
    live = (own_pos[None, :] < lengths[:, None]).astype(f32)
    d_inputs = jnp.stack([n + f for n, f in zip(near, far_came)])
    grad_tokens = (d_inputs + d_first_in.reshape(seq_count, local_rows, features)) * live[:, :, None]
    return (
        out_tokens,
        grad_tokens,
        full_qkv,
        full_b_query,
        full_b_value,
        full_out,
        full_b_out,
        full_gain_one,
        full_shift_one,
        full_up,
        full_b_up,
        full_down,
        full_b_down,
        full_gain_two,
        full_shift_two,
    )


def solution(mesh):
    in_specs = (
        P("dp", "seq", None),
        P("dp", "seq", None),
        P("dp"),
        P("dp", None),
        P(),
        P(),
        P(),
        P(),
        P(),
        P(),
        P(),
        P(),
        P(),
        P(),
        P(),
        P(),
        P(),
    )
    out_specs = (
        P("dp", "seq", None),
        P("dp", "seq", None),
        P(),
        P(),
        P(),
        P(),
        P(),
        P(),
        P(),
        P(),
        P(),
        P(),
        P(),
        P(),
        P(),
    )
    return jax.shard_map(
        per_device, mesh=mesh, in_specs=in_specs, out_specs=out_specs, check_vma=False
    )
```

```python
import functools
import jax
import jax.numpy as jnp
from jax import lax
from jax.experimental import pallas as pl
from jax.experimental.pallas import tpu as pltpu
from jax.sharding import PartitionSpec as P

HEAD_DIM = 64
SOFT = HEAD_DIM ** -0.5 * 1.4426950408889634
NN = (((1,), (0,)), ((), ()))
NT = (((1,), (1,)), ((), ()))
TN = (((0,), (0,)), ((), ()))
VMEM_LIMIT = 50 * 1024 * 1024
HEADS = 12
EPSILON = 1e-06
BITS = {"c": ("seq", 0), "x": ("seq", 1), "y": ("dp", 0), "l": ("dp", 1), "h": ("dp", 2)}


def own_number(order):
    number = jnp.int32(0)
    for letter in order:
        axis, shift = BITS[letter]
        number = number * 2 + ((lax.axis_index(axis) >> shift) & 1)
    return number


def exchange(array_in, axis, flip):
    return lax.ppermute(array_in, axis, [(i, i ^ flip) for i in range(lax.axis_size(axis))])


def exchange_bit(array_in, letter):
    axis, shift = BITS[letter]
    return exchange(array_in, axis, 1 << shift)


def extra_flips(axis, used):
    return [1 << shift for shift in range(used, lax.axis_size(axis).bit_length() - 1)]


def add_extra(array_in):
    for flip in extra_flips("dp", 3):
        array_in = array_in + exchange(array_in, "dp", flip)
    return array_in


def sum_low(*parts):
    total = parts[0].astype(jnp.float32)
    for part in parts[1:]:
        total = total + part.astype(jnp.float32)
    return total.astype(jnp.bfloat16)


def dot_f32(left, right, dims):
    return lax.dot_general(left, right, dims, preferred_element_type=jnp.float32)


def sequence_scalars(places, index):
    seq_count = (places.shape[0] - 11) // 3
    return places[11 + index] >> 1, places[9], 11 + seq_count + 2 * index


def shift_matrix(half, block, whole):
    row = lax.broadcasted_iota(jnp.int32, (block, whole), 0)
    col = lax.broadcasted_iota(jnp.int32, (block, whole), 1)
    return jnp.where((col == row + half) & (row < half), 1.0, 0.0).astype(jnp.bfloat16)


def mask_tiles(half, block):
    row = lax.broadcasted_iota(jnp.int32, (16, block), 0)
    col = lax.broadcasted_iota(jnp.int32, (16, block), 1)
    key_tile = jnp.where((row == 0) & (col >= half), -1e30, 0.0).astype(jnp.bfloat16)
    query_tile = jnp.where(row == 0, 1.0, 0.0).astype(jnp.bfloat16)
    return key_tile, query_tile


def attend_forward(
    heads, index, places, x0, x1, x2, x3, w_t, bias, c0, c1, c2, c3,
    x_out, qkv_out, ctx_blk, lse, tok, c_tok, x_seq, qkv, sems,
):
    half, mine, perm = sequence_scalars(places, index)
    whole = x_seq.shape[0]
    quarter = whole // 4
    block = whole // 2
    wide = heads * HEAD_DIM
    for r, piece in enumerate((x0, x1, x2, x3)):
        x_seq[pl.ds(pl.multiple_of((r ^ mine) * quarter, quarter), quarter), :] = piece[...]
    keep_x = pltpu.make_async_copy(x_seq, x_out, sems.at[0])
    keep_x.start()
    lane = lax.broadcasted_iota(jnp.int32, (1, block), 1)
    tok[...] = (dot_f32(w_t[...], x_seq[...], NT) + bias[...]).astype(jnp.bfloat16)
    shift = shift_matrix(half, block, whole)
    qkv[0] = jnp.where(lane < half, tok[:, :block], jnp.zeros((), jnp.bfloat16))
    qkv[1] = dot_f32(tok[...], shift, NT).astype(jnp.bfloat16)
    keep_qkv = pltpu.make_async_copy(qkv, qkv_out, sems.at[1])
    keep_qkv.start()
    key_tile, query_tile = mask_tiles(half, block)

    def one_block(b, carry):
        target = places[perm + b]
        for h in range(heads):
            rows = slice(h * HEAD_DIM, (h + 1) * HEAD_DIM)
            q_t = jnp.concatenate([qkv[b, rows, :], query_tile])
            k_t = jnp.concatenate(
                [qkv[target, wide + h * HEAD_DIM : wide + (h + 1) * HEAD_DIM, :], key_tile]
            )
            v_t = qkv[target, 2 * wide + h * HEAD_DIM : 2 * wide + (h + 1) * HEAD_DIM, :]
            scores = dot_f32(k_t, q_t, TN) * SOFT
            top = jnp.max(scores, axis=0, keepdims=True)
            expo = jnp.exp2(scores - top)
            total = jnp.sum(expo, axis=0, keepdims=True)
            context = dot_f32(v_t, expo.astype(jnp.bfloat16), NN) / total
            ctx_blk[b, rows, :] = context
            lse[b, h : h + 1, :] = top + jnp.log2(total)
        return carry

    lax.fori_loop(0, 2, one_block, 0)
    early = jnp.where(lane < half, ctx_blk[0], 0.0)
    late = dot_f32(ctx_blk[1].astype(jnp.bfloat16), shift, NN)
    for j in range(4):
        part = late[:, j * quarter : (j + 1) * quarter]
        if j < 2:
            part = part + early[:, j * quarter : (j + 1) * quarter]
        c_tok[j] = part.astype(jnp.bfloat16)
    for r, piece in enumerate((c0, c1, c2, c3)):
        piece[...] = c_tok[r ^ mine]
    keep_x.wait()
    keep_qkv.wait()


def attend_backward(
    heads, index, places, g0, g1, g2, g3, w_t, x_in, qkv, ctx_blk, lse, acc_in, acc_b, *refs
):
    last = len(refs) == 16
    (dx0, dx1, dx2, dx3, grad_w, grad_b, g_tok, g_blk, d_qkv, tok, x_seq, acc, dx_s, sems) = refs[-14:]
    bring_x = pltpu.make_async_copy(x_in, x_seq, sems.at[0])
    bring_acc = pltpu.make_async_copy(acc_in, acc, sems.at[1])
    bring_x.start()
    bring_acc.start()
    half, mine, perm = sequence_scalars(places, index)
    index = max(index - 1, 0)
    quarter = g0.shape[2]
    block = 2 * quarter
    whole = 4 * quarter
    wide = heads * HEAD_DIM
    for r, piece in enumerate((g0[index], g1[index], g2[0, index], g3[index])):
        g_tok[r ^ mine] = piece
    shift = shift_matrix(half, block, whole)
    lane = lax.broadcasted_iota(jnp.int32, (1, block), 1)
    g_all = jnp.concatenate([g_tok[j] for j in range(4)], axis=1)
    g_blk[0] = jnp.where(lane < half, g_all[:, :block], jnp.zeros((), jnp.bfloat16))
    g_blk[1] = dot_f32(g_all, shift, NT).astype(jnp.bfloat16)
    key_tile, query_tile = mask_tiles(half, block)

    def one_block(b, carry):
        target = places[perm + b]
        for h in range(heads):
            rows = slice(h * HEAD_DIM, (h + 1) * HEAD_DIM)
            k_rows = slice(wide + h * HEAD_DIM, wide + (h + 1) * HEAD_DIM)
            v_rows = slice(2 * wide + h * HEAD_DIM, 2 * wide + (h + 1) * HEAD_DIM)
            q_t = qkv[b, rows, :]
            k_t = qkv[target, k_rows, :]
            v_t = qkv[target, v_rows, :]
            g_t = g_blk[b, rows, :]
            scores = dot_f32(
                jnp.concatenate([k_t, key_tile]), jnp.concatenate([q_t, query_tile]), TN
            )
            probs = jnp.exp2(scores * SOFT - lse[b, h : h + 1, :])
            d_probs = dot_f32(v_t, g_t, TN)
            delta = jnp.sum(ctx_blk[b, rows, :] * g_t.astype(jnp.float32), axis=0, keepdims=True)
            d_scores = (probs * (d_probs - delta)).astype(jnp.bfloat16)
            scaling = HEAD_DIM ** -0.5
            d_qkv[b, rows, :] = (dot_f32(k_t, d_scores, NN) * scaling).astype(jnp.bfloat16)
            d_qkv[target, k_rows, :] = (dot_f32(q_t, d_scores, NT) * scaling).astype(jnp.bfloat16)
            d_qkv[target, v_rows, :] = dot_f32(g_t, probs.astype(jnp.bfloat16), NT).astype(
                jnp.bfloat16
            )
        return carry

    lax.fori_loop(0, 2, one_block, 0)
    late = dot_f32(d_qkv[1], shift, NN)
    front = jnp.where(lane < half, d_qkv[0].astype(jnp.float32), 0.0)
    tok[:, block:] = late[:, block:].astype(jnp.bfloat16)
    tok[:, :block] = (late[:, :block] + front).astype(jnp.bfloat16)
    sent = []
    for r, piece in enumerate((dx0, dx1, dx2, dx3)):
        columns = tok[:, pl.ds(pl.multiple_of((r ^ mine) * quarter, quarter), quarter)]
        dx_s[r] = dot_f32(columns, w_t[...], TN).astype(jnp.bfloat16)
        sent.append(pltpu.make_async_copy(dx_s.at[r], piece, sems.at[2 + r]))
        sent[-1].start()
    bring_acc.wait()
    bring_x.wait()
    total = acc[...] + dot_f32(tok[...], x_seq[...], NN)
    ones = jnp.ones((8, whole), jnp.bfloat16)
    sums = acc_b[...] + dot_f32(ones, tok[...], NT)
    if last:
        out_own, vectors = refs[:2]
        inner = places[10]
        turned = total.T
        tile = out_own.shape[1]
        extra = grad_w.shape[1] - tile
        grad_w[:, tile:, :] = jnp.zeros((8, extra, 4 * wide), jnp.bfloat16)
        for q in range(8):
            grad_w[q ^ inner, :tile, : 3 * wide] = turned[q * tile : (q + 1) * tile].astype(
                jnp.bfloat16
            )
        grad_w[:, :tile, 3 * wide :] = out_own[...]
        row = lax.broadcasted_iota(jnp.int32, (extra, 1), 0)
        own_row = jnp.concatenate([sums[0:1, :], jnp.zeros((1, wide), jnp.float32)], axis=1)
        grad_w[inner, tile:, :] = jnp.where(row == 10, own_row, vectors[...]).astype(jnp.bfloat16)
        grad_b[...] = sums
    else:
        grad_w[...] = total
        grad_b[...] = sums
    for copy in sent:
        copy.wait()


def kernel_call(body, scalars, arrays, outs, scratch, left_in=(), left_out=()):
    def spec(away):
        return pl.BlockSpec(memory_space=pl.ANY if away else pltpu.VMEM)

    return pl.pallas_call(
        body,
        out_shape=outs,
        in_specs=[pl.BlockSpec(memory_space=pltpu.SMEM)]
        + [spec(i in left_in) for i in range(len(arrays))],
        out_specs=[spec(i in left_out) for i in range(len(outs))],
        scratch_shapes=scratch,
        compiler_params=pltpu.CompilerParams(vmem_limit_bytes=VMEM_LIMIT),
        cost_estimate=pl.CostEstimate(
            flops=10**8, transcendentals=0, bytes_accessed=1024 * 1024
        ),
    )(scalars, *arrays)


def attention_forward(places, pieces, index, w_t, bias, heads):
    quarter, features = pieces[0].shape
    whole, block, wide = 4 * quarter, 2 * quarter, heads * HEAD_DIM
    out = jax.ShapeDtypeStruct
    outs = [out((wide, quarter), jnp.bfloat16)] * 4 + [
        out((whole, features), jnp.bfloat16),
        out((2, 3 * wide, block), jnp.bfloat16),
        out((2, wide, block), jnp.float32),
        out((2, 8, block), jnp.float32),
    ]
    scratch = [
        pltpu.VMEM((3 * wide, whole), jnp.bfloat16),
        pltpu.VMEM((4, wide, quarter), jnp.bfloat16),
        pltpu.VMEM((whole, features), jnp.bfloat16),
        pltpu.VMEM((2, 3 * wide, block), jnp.bfloat16),
        pltpu.SemaphoreType.DMA((2,)),
    ]
    found = kernel_call(
        functools.partial(attend_forward, heads, index),
        places,
        [*pieces, w_t, bias],
        outs,
        scratch,
        left_out=(4, 5),
    )
    return found[:4], found[4:]


def attention_backward(places, pieces, index, w_t, kept, acc, acc_b, heads, late=()):
    _, wide, quarter = pieces[0].shape
    features = w_t.shape[1]
    block = 2 * quarter
    out = jax.ShapeDtypeStruct
    grad = (
        out((8, features // 8 + 16, 4 * wide), jnp.bfloat16)
        if late
        else out((3 * wide, features), jnp.float32)
    )
    outs = [out((quarter, features), jnp.bfloat16)] * 4 + [grad, out((8, 3 * wide), jnp.float32)]
    scratch = [
        pltpu.VMEM((4, wide, quarter), jnp.bfloat16),
        pltpu.VMEM((2, wide, block), jnp.bfloat16),
        pltpu.VMEM((2, 3 * wide, block), jnp.bfloat16),
        pltpu.VMEM((3 * wide, 4 * quarter), jnp.bfloat16),
        pltpu.VMEM((4 * quarter, features), jnp.bfloat16),
        pltpu.VMEM((3 * wide, features), jnp.float32),
        pltpu.VMEM((4, quarter, features), jnp.bfloat16),
        pltpu.SemaphoreType.DMA((6,)),
    ]
    found = kernel_call(
        functools.partial(attend_backward, heads, index),
        places,
        [*pieces, w_t, *kept, acc, acc_b, *late],
        outs,
        scratch,
        left_in=(5, 9),
        left_out=(0, 1, 2, 3),
    )
    return found[:4], found[4], found[5]

def live_rows(places, rows, mine, local_rows, offset):
    row = lax.broadcasted_iota(jnp.int32, (rows, 1), 0)
    length = jnp.zeros((rows, 1), jnp.int32)
    for s in range(rows // local_rows):
        length = jnp.where(row >= s * local_rows, places[offset + s], length)
    position = mine * local_rows + lax.rem(row, local_rows)
    return jnp.where(position < length, 1.0, 0.0)


def normal_parts(array_in):
    centered = array_in - jnp.mean(array_in, axis=1, keepdims=True)
    spread = jnp.mean(centered * centered, axis=1, keepdims=True)
    inverse = lax.rsqrt(spread + EPSILON)
    return centered * inverse, inverse


def normal_back(hat, inverse, gain, d_out):
    scaled = d_out * gain
    mean_scaled = jnp.mean(scaled, axis=1, keepdims=True)
    mean_product = jnp.mean(scaled * hat, axis=1, keepdims=True)
    return inverse * (scaled - mean_scaled - hat * mean_product)


def column_sum(array_in):
    return jnp.sum(array_in, axis=0, keepdims=True)


def feed_forward(shape, places, *refs):
    seq_count, seq_parts, steps = shape
    pieces, refs = refs[: seq_count * seq_parts], refs[seq_count * seq_parts :]
    tokens, cot, w_out, vectors, w_up, b_up, w_down = refs[:7]
    out, context, first_in, first_low, active, slope, d_second, d_lowered, sums = refs[7:16]
    first_norm, lowered = refs[16:]
    rows, features = tokens.shape
    local_rows = rows // seq_count
    wide = features // seq_parts
    mine = places[9]
    step = pl.program_id(0)
    f32 = jnp.float32

    @pl.when(step == 0)
    def start():
        for s in range(seq_count):
            for r in range(seq_parts):
                context[
                    pl.ds(pl.multiple_of((r ^ mine) * wide, wide), wide),
                    s * local_rows : (s + 1) * local_rows,
                ] = pieces[s * seq_parts + r][...]
        live = live_rows(places, rows, mine, local_rows, 11)
        attended = dot_f32(context[...], w_out[...], TN) + vectors[0:1, :]
        total = jnp.where(live > 0, tokens[...].astype(f32), 0.0) + attended
        first_in[...] = total
        hat, _ = normal_parts(total)
        normed = hat * vectors[1:2, :] + vectors[2:3, :]
        first_norm[...] = normed
        first_low[...] = normed.astype(jnp.bfloat16)

    lifted = dot_f32(first_low[...], w_up[...], NN) + b_up[...]
    cdf = 0.5 * (1.0 + lax.erf(lifted * 0.7071067811865476))
    density = jnp.exp(lifted * lifted * -0.5) * 0.3989422804014327
    gelu = (lifted * cdf).astype(jnp.bfloat16)
    active[0] = gelu
    slope[0] = (cdf + lifted * density).astype(jnp.bfloat16)
    part = dot_f32(gelu, w_down[...], NN)

    @pl.when(step == 0)
    def first():
        lowered[...] = part

    @pl.when(step > 0)
    def later():
        lowered[...] += part

    @pl.when(step == steps - 1)
    def finish():
        live = live_rows(places, rows, mine, local_rows, 11)
        hat, inverse = normal_parts(first_norm[...] + (lowered[...] + vectors[3:4, :]))
        gain = vectors[4:5, :]
        out[...] = ((hat * gain + vectors[5:6, :]) * live).astype(jnp.bfloat16)
        incoming = cot[...].astype(f32) * live
        back = normal_back(hat, inverse, gain, incoming)
        d_second[...] = back
        low = back.astype(jnp.bfloat16)
        d_lowered[...] = low
        sums[0:1, :] = column_sum(low.astype(f32))
        sums[1:2, :] = column_sum(incoming * hat)
        sums[2:3, :] = column_sum(incoming)


def hidden_back(places, active, slope, w_up, w_down, first_t, d_lowered, grad_down, grad_up, grad_b):
    inner = places[8]
    f32 = jnp.float32
    down = dot_f32(active[0], d_lowered[...], TN).astype(jnp.bfloat16)
    tile = down.shape[0] // 4
    for q in range(4):
        grad_down[0, pl.ds(pl.multiple_of((q ^ inner) * tile, tile), tile), :] = down[
            q * tile : (q + 1) * tile
        ]
    d_active = dot_f32(d_lowered[...], w_down[...], NT)
    d_lifted = (d_active * slope[0].astype(f32)).astype(jnp.bfloat16)
    grad_b[...] = column_sum(d_lifted.astype(f32))
    grad_up[0] = dot_f32(first_t[...], d_lifted, NN).astype(jnp.bfloat16)
    return dot_f32(d_lifted, w_up[...], NT)


def turn_rows(places, source, target):
    inner = places[8]
    tile = target.shape[0] // 4
    turned = source[...].T
    for q in range(4):
        target[pl.ds(pl.multiple_of((q ^ inner) * tile, tile), tile), :] = turned[
            q * tile : (q + 1) * tile
        ]


def back_send(
    places, active, slope, w_up, w_down, first_low, d_lowered, d_second,
    grad_down, grad_up, grad_b, d_first, first_t,
):
    step = pl.program_id(0)

    @pl.when(step == 0)
    def start():
        turn_rows(places, first_low, first_t)
        d_first[...] = d_second[...]

    d_first[...] += hidden_back(
        places, active, slope, w_up, w_down, first_t, d_lowered, grad_down, grad_up, grad_b
    )


def back_keep(shape, places, *refs):
    seq_count, seq_parts, steps = shape
    active, slope, w_up, w_down, first_low, d_lowered, d_part = refs[:7]
    first_in, context, w_out, vectors = refs[7:11]
    grad_down, grad_up, grad_b, d_first_in, sums, grad_out = refs[11:17]
    pieces = refs[17:-3]
    first_t, d_first, turned = refs[-3:]
    step = pl.program_id(0)
    f32 = jnp.float32

    @pl.when(step == 0)
    def start():
        turn_rows(places, first_low, first_t)
        d_first[...] = d_part[...]

    d_first[...] += hidden_back(
        places, active, slope, w_up, w_down, first_t, d_lowered, grad_down, grad_up, grad_b
    )

    @pl.when(step == steps - 1)
    def finish():
        rows, features = first_in.shape
        local_rows = rows // seq_count
        wide = features // seq_parts
        mine = places[9]
        hat, inverse = normal_parts(first_in[...])
        incoming = d_first[...]
        back = normal_back(hat, inverse, vectors[1:2, :], incoming)
        d_first_in[...] = back
        low = back.astype(jnp.bfloat16)
        sums[0:1, :] = column_sum(low.astype(f32))
        sums[1:2, :] = column_sum(incoming * hat)
        sums[2:3, :] = column_sum(incoming)
        turned[...] = dot_f32(w_out[...], low, NT).astype(jnp.bfloat16)
        for r in range(seq_parts):
            own = turned[pl.ds(pl.multiple_of((r ^ mine) * wide, wide), wide), :]
            for s in range(seq_count):
                target, place = pieces[3 * min(s, 1) + min(r, 2)], max(s - 1, 0)
                columns = own[:, s * local_rows : (s + 1) * local_rows]
                if r < 2:
                    target[place] = columns
                else:
                    target[r - 2, place] = columns
        product = dot_f32(context[...], low, NN).astype(jnp.bfloat16)
        block_rows, block_cols = grad_out.shape[2:]
        across = features // block_cols
        for j in range(seq_parts):
            for q in range(wide // block_rows * across):
                row, col = j * wide + q // across * block_rows, q % across * block_cols
                grad_out[j ^ mine, q ^ places[10]] = product[
                    row : row + block_rows, col : col + block_cols
                ]


def whole_spec(shape):
    return pl.BlockSpec(shape, lambda p, places: (0,) * len(shape))


def step_call(body, places, steps, ins, in_specs, outs, out_specs, scratch, flops, aliases={}):
    return pl.pallas_call(
        body,
        out_shape=outs,
        grid_spec=pltpu.PrefetchScalarGridSpec(
            num_scalar_prefetch=1,
            grid=(steps,),
            in_specs=in_specs,
            out_specs=out_specs,
            scratch_shapes=scratch,
        ),
        input_output_aliases=aliases,
        compiler_params=pltpu.CompilerParams(vmem_limit_bytes=VMEM_LIMIT),
        cost_estimate=pl.CostEstimate(
            flops=flops, transcendentals=0, bytes_accessed=20 * 1024 * 1024
        ),
    )(places, *ins)


def run_feed_forward(places, pieces, tokens, cot, w_out, vectors, w_up, b_up, w_down, dims):
    seq_count, seq_parts = dims
    rows, features = tokens.shape
    hidden = w_up.shape[1]
    steps = 8
    tile = hidden // steps
    out, bf16, f32 = jax.ShapeDtypeStruct, jnp.bfloat16, jnp.float32
    square = (rows, features)
    up_spec = pl.BlockSpec((features, tile), lambda p, places: (0, places[p]))
    down_spec = pl.BlockSpec((tile, features), lambda p, places: (places[p], 0))
    bias_spec = pl.BlockSpec((1, tile), lambda p, places: (0, places[p]))
    kept_spec = pl.BlockSpec((1, rows, tile), lambda p, places: (p, 0, 0))
    return step_call(
        functools.partial(feed_forward, (seq_count, seq_parts, steps)),
        places,
        steps,
        [*pieces, tokens, cot, w_out, vectors, w_up, b_up, w_down],
        [whole_spec(p.shape) for p in pieces]
        + [whole_spec(square), whole_spec(square), whole_spec(w_out.shape), whole_spec(vectors.shape)]
        + [up_spec, bias_spec, down_spec],
        [
            out(square, bf16),
            out((features, rows), bf16),
            out(square, f32),
            out(square, bf16),
            out((steps, rows, tile), bf16),
            out((steps, rows, tile), bf16),
            out(square, f32),
            out(square, bf16),
            out((8, features), f32),
        ],
        [
            whole_spec(square),
            whole_spec((features, rows)),
            whole_spec(square),
            whole_spec(square),
            kept_spec,
            kept_spec,
            whole_spec(square),
            whole_spec(square),
            whole_spec((8, features)),
        ],
        [pltpu.VMEM(square, f32), pltpu.VMEM(square, f32)],
        2 * rows * features * (2 * hidden + features),
    )


def back_specs(first, rows, features, tile):
    kept = pl.BlockSpec((1, rows, tile), lambda p, places: (p + first, 0, 0))
    up = pl.BlockSpec((features, tile), lambda p, places: (0, places[p + first]))
    down = pl.BlockSpec((tile, features), lambda p, places: (places[p + first], 0))
    bias = pl.BlockSpec((1, tile), lambda p, places: (0, places[p + first] % 4))
    grad_down = pl.BlockSpec((1, tile, features), lambda p, places: (p, 0, 0))
    grad_up = pl.BlockSpec((1, features, tile), lambda p, places: (p, 0, 0))
    return [kept, kept, up, down], [grad_down, grad_up, bias]


def run_back_send(places, active, slope, w_up, w_down, first_low, d_lowered, d_second):
    steps_all, rows, tile = active.shape
    features = first_low.shape[1]
    steps = steps_all // 2
    out, bf16, f32 = jax.ShapeDtypeStruct, jnp.bfloat16, jnp.float32
    square = (rows, features)
    ins, outs = back_specs(steps, rows, features, tile)
    return step_call(
        back_send,
        places,
        steps,
        [active, slope, w_up, w_down, first_low, d_lowered, d_second],
        ins + [whole_spec(square)] * 3,
        [
            out((steps, tile, features), bf16),
            out((steps, features, tile), bf16),
            out((1, steps * tile), f32),
            out(square, f32),
        ],
        outs + [whole_spec(square)],
        [pltpu.VMEM((features, rows), bf16)],
        8 * rows * features * steps * tile,
    )


def run_back_keep(
    places, active, slope, w_up, w_down, first_low, d_lowered, d_part, first_in, context, w_out,
    vectors, dims,
):
    seq_count, seq_parts = dims
    steps_all, rows, tile = active.shape
    features = first_low.shape[1]
    steps = steps_all // 2
    out, bf16, f32 = jax.ShapeDtypeStruct, jnp.bfloat16, jnp.float32
    square = (rows, features)
    turned = (features, rows)
    piece = (features // seq_parts, rows // seq_count)
    pieces = []
    for n in (1, seq_count - 1):
        pieces += [(n, *piece), (n, *piece), (2, n, *piece)]
    out_blocks = (seq_parts, 8, features // seq_parts // 2, features // 4)
    ins, outs = back_specs(0, rows, features, tile)
    return step_call(
        functools.partial(back_keep, (seq_count, seq_parts, steps)),
        places,
        steps,
        [active, slope, w_up, w_down, first_low, d_lowered, d_part, first_in, context, w_out, vectors],
        ins
        + [whole_spec(square)] * 4
        + [whole_spec(turned), whole_spec(w_out.shape), whole_spec(vectors.shape)],
        [
            out((steps, tile, features), bf16),
            out((steps, features, tile), bf16),
            out((1, steps * tile), f32),
            out(square, f32),
            out((8, features), f32),
            out(out_blocks, bf16),
        ]
        + [out(p, bf16) for p in pieces],
        outs
        + [whole_spec(square), whole_spec((8, features)), whole_spec(out_blocks)]
        + [whole_spec(p) for p in pieces],
        [pltpu.VMEM(turned, bf16), pltpu.VMEM(square, f32), pltpu.VMEM(turned, bf16)],
        8 * rows * features * steps * tile,
    )


def place_rows(by_rows, late, places, *refs):
    pieces, out = refs[:2], refs[-1]
    step = pl.program_id(0)
    tile = pieces[0].shape[1]
    for k in range(4):
        c, other = k >> 1, k & 1

        @pl.when(step == k)
        def copy():
            for q in range(4):
                h, x = q >> 1, q & 1
                sub = other * 4 + x * 2 + h if by_rows else x * 4 + other * 2 + h
                out[pl.ds(pl.multiple_of((q ^ places[8]) * tile, tile), tile), :] = pieces[c][
                    sub
                ].astype(jnp.float32)


def gather_hidden(places, early, late, shape, by_rows):
    _, rows, cols = early[0].shape
    block = (4 * rows, cols)
    total = []
    for bit, pieces in enumerate((early, late)):

        def number(p):
            return (p >> 1) * 4 + bit * 2 + (p & 1) if by_rows else p * 2 + bit

        if by_rows:
            index = lambda p, places, number=number: (places[number(p)], 0)
        else:
            index = lambda p, places, number=number: (0, places[number(p)])
        total = [
            step_call(
                functools.partial(place_rows, by_rows, bit),
                places,
                4,
                pieces + total,
                [whole_spec(p.shape) for p in pieces]
                + [pl.BlockSpec(memory_space=pl.ANY)] * len(total),
                jax.ShapeDtypeStruct(shape, jnp.float32),
                pl.BlockSpec(block, index),
                [],
                8 * rows * cols,
                {3: 0} if total else {},
            )
        ]
    return total[0]


def place_heads(places, *refs):
    pieces = refs[:-5]
    out, out_w, vector_rows, head_rows, held = refs[-5:]
    mine, inner = places[9], places[10]
    seq_parts = len(pieces)
    step = pl.program_id(0)
    wide = out_w.shape[0] // seq_parts
    rows = out.shape[0]
    f32 = jnp.float32
    for r, piece in enumerate(pieces):
        for j in range(seq_parts):

            @pl.when((r ^ mine) == j)
            def copy():
                block = piece[step ^ inner, :rows, : 3 * wide].astype(f32)
                for k in range(3):
                    start = (k * seq_parts + j) * wide
                    out[:, start : start + wide] = block[:, k * wide : (k + 1) * wide]

        @pl.when(step == r)
        def copy_out():
            tile, width = wide // 2, out_w.shape[1] // 4
            for q in range(8):
                row = pl.multiple_of((r ^ mine) * wide + q // 4 * tile, tile)
                col = q % 4 * width
                out_w[pl.ds(row, tile), col : col + width] = piece[
                    q ^ inner, :rows, 3 * wide :
                ].astype(f32)

        @pl.when(step == seq_parts)
        def copy_vectors():
            held[r ^ mine] = piece[inner, rows:, :].astype(f32)

    @pl.when(step == seq_parts)
    def sum_vectors():
        total = held[0]
        for j in range(1, seq_parts):
            total = total + held[j]
        vector_rows[...] = total
        for j in range(seq_parts):
            head_rows[j : j + 1, :] = held[j, 10:11, :]


def gather_heads(places, pieces, shape):
    out, f32 = jax.ShapeDtypeStruct, jnp.float32
    features = shape[0]
    rows = features // 8
    square = (features, features)
    extra = (pieces[0].shape[1] - rows, features)
    return step_call(
        place_heads,
        places,
        8,
        pieces,
        [whole_spec(p.shape) for p in pieces],
        [out(shape, f32), out(square, f32), out(extra, f32), out((8, features), f32)],
        [pl.BlockSpec((rows, shape[1]), lambda p, places: (p, 0))]
        + [whole_spec(square), whole_spec(extra), whole_spec((8, features))],
        [pltpu.VMEM((len(pieces), *extra), f32)],
        1000,
    )


def per_device(
    tokens,
    cotangent,
    lengths,
    block_perm,
    w_qkv,
    b_query,
    b_value,
    w_out,
    b_out,
    ln1_gain,
    ln1_shift,
    w_up,
    b_up,
    w_down,
    b_down,
    ln2_gain,
    ln2_shift,
):
    seq_parts = lax.axis_size("seq")
    mine = lax.axis_index("seq")
    seq_count, local_rows, features = tokens.shape
    flat_rows = seq_count * local_rows
    hidden = w_up.shape[1]
    heads = HEADS // seq_parts
    wide = heads * HEAD_DIM
    dims = (seq_count, seq_parts)
    f32 = jnp.float32

    w_heads = jnp.concatenate(
        [
            lax.dynamic_slice_in_dim(w_qkv, k * features + mine * wide, wide, axis=1)
            for k in range(3)
        ],
        axis=1,
    )
    w_t = w_heads.T
    bias = jnp.concatenate(
        [
            lax.dynamic_slice_in_dim(b_query, mine * wide, wide),
            jnp.zeros((wide,), b_query.dtype),
            lax.dynamic_slice_in_dim(b_value, mine * wide, wide),
        ]
    ).astype(f32)[:, None]
    outer = own_number("cyl")
    places = jnp.concatenate(
        [
            jnp.arange(8, dtype=jnp.int32) ^ outer,
            jnp.stack([own_number("hx"), mine, own_number("ylh")]),
            lengths,
            block_perm.reshape(-1),
        ]
    )
    vectors = jnp.stack(
        [v.astype(f32) for v in (b_out, ln1_gain, ln1_shift, b_down, ln2_gain, ln2_shift, b_out, b_out)]
    )

    arrived, kept, crossed = [], [], []
    for s in range(seq_count):
        near = tokens[s]
        start = near
        if s > 0:
            after = [crossed[-1]] + arrived[(s - 2) * seq_parts : (s - 2) * seq_parts + 1] * (s > 1)
            start, _ = lax.optimization_barrier((near, after))
        across = exchange_bit(start, "x")
        crossed.append(across)
        if s > 0:
            across, _ = lax.optimization_barrier((across, arrived[-seq_parts]))
        pieces = [near, exchange_bit(near, "c"), across, exchange_bit(across, "c")]
        contexts, saved = attention_forward(places, pieces, s, w_t, bias, heads)
        kept.append(saved)
        arrived += [contexts[0]] + [exchange(contexts[r], "seq", r) for r in range(1, seq_parts)]

    (
        out_rows,
        context,
        first_in,
        first_low,
        active,
        slope,
        d_second,
        d_lowered,
        sums_two,
    ) = run_feed_forward(
        places,
        arrived,
        tokens.reshape(flat_rows, features),
        cotangent.reshape(flat_rows, features),
        w_out,
        vectors,
        w_up,
        b_up.astype(f32).reshape(1, hidden),
        w_down,
        dims,
    )
    out_tokens = out_rows.reshape(seq_count, local_rows, features)
    send_down, send_up, b_up_send, d_part = run_back_send(
        places, active, slope, w_up, w_down, first_low, d_lowered, d_second
    )
    came_down = exchange_bit(send_down, "c")
    came_up = exchange_bit(send_up, "c")
    keep_down, keep_up, b_up_keep, d_first_in, sums_one, grad_out, *d_contexts = run_back_keep(
        places, active, slope, w_up, w_down, first_low, d_lowered, d_part, first_in, context, w_out,
        vectors, dims,
    )

    half_hidden = jnp.where(
        (outer >= 4),
        jnp.concatenate([b_up_send, b_up_keep], axis=1),
        jnp.concatenate([b_up_keep, b_up_send], axis=1),
    ).reshape(-1, features)
    filler = jnp.zeros((10 - half_hidden.shape[0], features), f32)
    sums = jnp.concatenate([sums_one[:3], sums_two[:3], half_hidden, filler])

    def hand_on(own, near, came):
        return [own, exchange_bit(near, "c"), came, exchange_bit(came[1], "c")]

    first_came = exchange_bit(d_contexts[2], "x")
    second_pair, first_came = lax.optimization_barrier((d_contexts[5], first_came))
    second_came = exchange_bit(second_pair, "x")
    total_w = jnp.zeros((3 * wide, features), f32)
    total_b = jnp.zeros((8, 3 * wide), f32)
    parts, near, far = [], [], []

    def attend(s, group, total_w, total_b, late=()):
        found, total_w, total_b = attention_backward(
            places, group, s, w_t, kept[s], total_w, total_b, heads, late
        )
        parts.append(found)
        return total_w, total_b

    def cross(s):
        near.append(parts[s][0].astype(f32) + exchange_bit(parts[s][1], "c"))
        far.append(sum_low(parts[s][2], exchange_bit(parts[s][3], "c")))

    sends = [
        sum_low(keep_down[3], came_down[3]),
        sum_low(keep_up[3], came_up[3]),
        grad_out[2:],
    ]
    sends, first_came = lax.optimization_barrier((sends, first_came))
    down_y1, up_l3, out_x = [exchange_bit(v, bit) for v, bit in zip(sends, "ylx")]
    total_w, total_b = attend(0, hand_on(d_contexts[0], d_contexts[1], first_came), total_w, total_b)
    (down_y1, up_l3, out_x, total_w, parts[0], second_came, near_pair) = lax.optimization_barrier(
        (down_y1, up_l3, out_x, total_w, parts[0], second_came, d_contexts[3:5])
    )

    sends = [
        sum_low(keep_down[2], came_down[2]),
        sum_low(keep_up[1], came_up[1]),
        sum_low(grad_out[1], out_x[1]),
    ]
    (sends, total_w) = lax.optimization_barrier((sends, total_w))
    down_y0, up_l1, out_c = [exchange_bit(v, bit) for v, bit in zip(sends, "ylc")]
    cross(0)
    second_group = hand_on(*near_pair, second_came)
    for s in range(1, seq_count - 1):
        total_w, total_b = attend(s, second_group, total_w, total_b)
    out_own = sum_low(grad_out[0], out_x[0], out_c)
    (down_y0, up_l1, total_w, parts[1:], near, far, out_own) = lax.optimization_barrier(
        (down_y0, up_l1, total_w, parts[1:], near, far, out_own)
    )

    sends = [
        sum_low(keep_down[1], came_down[1], down_y1),
        sum_low(keep_up[2], came_up[2], up_l3),
    ]
    (sends, total_w) = lax.optimization_barrier((sends, total_w))
    down_l, up_y = [exchange_bit(v, bit) for v, bit in zip(sends, "ly")]
    far_came = [exchange_bit(far[0], "x")]
    for s in range(1, seq_count - 1):
        cross(s)
    total_w, total_b = attend(seq_count - 1, second_group, total_w, total_b, (out_own, sums))

    (down_l, up_y, far, far_came, total_w, parts[-1]) = lax.optimization_barrier(
        (down_l, up_y, far, far_came, total_w, parts[-1])
    )
    down_own = sum_low(keep_down[0], came_down[0], down_y0, down_l)
    down_own = down_own.reshape(4, hidden // 32, features)
    up_own = sum_low(keep_up[0], came_up[0], up_l1, up_y)
    up_own = up_own.reshape(2, 2, features // 4, hidden // 8)
    keeps = [down_own[:2], up_own[:, 0], total_w[:4]]
    sends = [down_own[2:], up_own[:, 1], total_w[4:]]
    (keeps, sends) = lax.optimization_barrier((keeps, sends))
    got = [exchange_bit(v, bit) for v, bit in zip(sends, "hxy")]
    far_came += [exchange_bit(v, "x") for v in far[1:]]
    down_own, up_own, qkv_own = [k + g for k, g in zip(keeps, got)]
    qkv_own = qkv_own[:2] + exchange_bit(qkv_own[2:], "l")
    far = []
    cross(seq_count - 1)

    keeps = [down_own[:1], up_own[:1], qkv_own[:1]]
    sends = [down_own[1:], up_own[1:], qkv_own[1:]]
    (keeps, sends, far, far_came) = lax.optimization_barrier((keeps, sends, far, far_came))
    got = [exchange_bit(v, bit) for v, bit in zip(sends, "xhh")]
    far_came += [exchange_bit(v, "x") for v in far]
    shards = [add_extra(k + g) for k, g in zip(keeps, got)]

    for bits in ("hhh", "xyl", "lxy"):
        (shards, far_came) = lax.optimization_barrier((shards, far_came))
        shards = [
            jnp.concatenate([shard, exchange_bit(shard, bit)]) for shard, bit in zip(shards, bits)
        ]
    shards = lax.optimization_barrier(shards)
    last = [exchange_bit(shard, bit) for shard, bit in zip(shards, "ylx")]
    near_c = [exchange_bit(shard, "c") for shard in shards]
    far_c = [exchange_bit(shard, "c") for shard in last]
    full_down, full_up = [
        gather_hidden(places, [shards[i], near_c[i]], [last[i], far_c[i]], shape, i == 0)
        for i, shape in ((0, (hidden, features)), (1, (features, hidden)))
    ]
    full_qkv, full_out, vector_rows, head_rows = gather_heads(
        places, [shards[2], near_c[2], last[2], far_c[2]], (features, 3 * features)
    )
    (
        full_b_out,
        full_gain_one,
        full_shift_one,
        full_b_down,
        full_gain_two,
        full_shift_two,
    ) = [vector_rows[i] for i in range(6)]
    full_b_up = vector_rows[6 : 6 + hidden // features].reshape(hidden)
    full_b_query = head_rows[:seq_parts, :wide].reshape(features)
    full_b_value = head_rows[:seq_parts, 2 * wide : 3 * wide].reshape(features)

    own_pos = mine * local_rows + jnp.arange(local_rows, dtype=jnp.int32)
    live = (own_pos[None, :] < lengths[:, None]).astype(f32)
    d_inputs = jnp.stack([n + f for n, f in zip(near, far_came)])
    grad_tokens = (d_inputs + d_first_in.reshape(seq_count, local_rows, features)) * live[:, :, None]
    return (
        out_tokens,
        grad_tokens,
        full_qkv,
        full_b_query,
        full_b_value,
        full_out,
        full_b_out,
        full_gain_one,
        full_shift_one,
        full_up,
        full_b_up,
        full_down,
        full_b_down,
        full_gain_two,
        full_shift_two,
    )


def solution(mesh):
    in_specs = (
        P("dp", "seq", None),
        P("dp", "seq", None),
        P("dp"),
        P("dp", None),
        P(),
        P(),
        P(),
        P(),
        P(),
        P(),
        P(),
        P(),
        P(),
        P(),
        P(),
        P(),
        P(),
    )
    out_specs = (
        P("dp", "seq", None),
        P("dp", "seq", None),
        P(),
        P(),
        P(),
        P(),
        P(),
        P(),
        P(),
        P(),
        P(),
        P(),
        P(),
        P(),
        P(),
    )
    return jax.shard_map(
        per_device, mesh=mesh, in_specs=in_specs, out_specs=out_specs, check_vma=False
    )
```

```python
import functools
import jax
import jax.numpy as jnp
from jax import lax
from jax.experimental import pallas as pl
from jax.experimental.pallas import tpu as pltpu
from jax.sharding import PartitionSpec as P

HEAD_DIM = 64
SOFT = HEAD_DIM ** -0.5 * 1.4426950408889634
NN = (((1,), (0,)), ((), ()))
NT = (((1,), (1,)), ((), ()))
TN = (((0,), (0,)), ((), ()))
VMEM_LIMIT = 60 * 1024 * 1024
HEADS = 12
EPSILON = 1e-06
BITS = {"c": ("seq", 0), "x": ("seq", 1), "y": ("dp", 0), "l": ("dp", 1), "h": ("dp", 2)}


def own_number(order):
    number = jnp.int32(0)
    for letter in order:
        axis, shift = BITS[letter]
        number = number * 2 + ((lax.axis_index(axis) >> shift) & 1)
    return number


def exchange(array_in, axis, flip):
    return lax.ppermute(array_in, axis, [(i, i ^ flip) for i in range(lax.axis_size(axis))])


def exchange_bit(array_in, letter):
    axis, shift = BITS[letter]
    return exchange(array_in, axis, 1 << shift)


def extra_flips(axis, used):
    return [1 << shift for shift in range(used, lax.axis_size(axis).bit_length() - 1)]


def add_extra(array_in):
    for flip in extra_flips("dp", 3):
        array_in = array_in + exchange(array_in, "dp", flip)
    return array_in


def sum_low(*parts):
    total = parts[0].astype(jnp.float32)
    for part in parts[1:]:
        total = total + part.astype(jnp.float32)
    return total.astype(jnp.bfloat16)


def dot_f32(left, right, dims):
    return lax.dot_general(left, right, dims, preferred_element_type=jnp.float32)


def sequence_scalars(places, index):
    seq_count = (places.shape[0] - 11) // 3
    return places[11 + index] >> 1, places[9], 11 + seq_count + 2 * index


def shift_matrix(half, block, whole):
    row = lax.broadcasted_iota(jnp.int32, (block, whole), 0)
    col = lax.broadcasted_iota(jnp.int32, (block, whole), 1)
    return jnp.where((col == row + half) & (row < half), 1.0, 0.0).astype(jnp.bfloat16)


def mask_tiles(half, block):
    row = lax.broadcasted_iota(jnp.int32, (16, block), 0)
    col = lax.broadcasted_iota(jnp.int32, (16, block), 1)
    key_tile = jnp.where((row == 0) & (col >= half), -1e30, 0.0).astype(jnp.bfloat16)
    query_tile = jnp.where(row == 0, 1.0, 0.0).astype(jnp.bfloat16)
    return key_tile, query_tile


def attend_forward(
    heads, index, places, x0, x1, x2, x3, w_t, bias, c0, c1, c2, c3,
    x_out, qkv_out, ctx_blk, lse, tok, c_tok, x_seq, qkv, sems,
):
    half, mine, perm = sequence_scalars(places, index)
    whole = x_seq.shape[0]
    quarter = whole // 4
    block = whole // 2
    wide = heads * HEAD_DIM
    for r, piece in enumerate((x0, x1, x2, x3)):
        x_seq[pl.ds(pl.multiple_of((r ^ mine) * quarter, quarter), quarter), :] = piece[...]
    keep_x = pltpu.make_async_copy(x_seq, x_out, sems.at[0])
    keep_x.start()
    lane = lax.broadcasted_iota(jnp.int32, (1, block), 1)
    tok[...] = (dot_f32(w_t[...], x_seq[...], NT) + bias[...]).astype(jnp.bfloat16)
    shift = shift_matrix(half, block, whole)
    qkv[0] = jnp.where(lane < half, tok[:, :block], jnp.zeros((), jnp.bfloat16))
    qkv[1] = dot_f32(tok[...], shift, NT).astype(jnp.bfloat16)
    keep_qkv = pltpu.make_async_copy(qkv, qkv_out, sems.at[1])
    keep_qkv.start()
    key_tile, query_tile = mask_tiles(half, block)

    def one_block(b, carry):
        target = places[perm + b]
        for h in range(heads):
            rows = slice(h * HEAD_DIM, (h + 1) * HEAD_DIM)
            q_t = jnp.concatenate([qkv[b, rows, :], query_tile])
            k_t = jnp.concatenate(
                [qkv[target, wide + h * HEAD_DIM : wide + (h + 1) * HEAD_DIM, :], key_tile]
            )
            v_t = qkv[target, 2 * wide + h * HEAD_DIM : 2 * wide + (h + 1) * HEAD_DIM, :]
            scores = dot_f32(k_t, q_t, TN) * SOFT
            top = jnp.max(scores, axis=0, keepdims=True)
            expo = jnp.exp2(scores - top)
            total = jnp.sum(expo, axis=0, keepdims=True)
            context = dot_f32(v_t, expo.astype(jnp.bfloat16), NN) / total
            ctx_blk[b, rows, :] = context
            lse[b, h : h + 1, :] = top + jnp.log2(total)
        return carry

    lax.fori_loop(0, 2, one_block, 0)
    early = jnp.where(lane < half, ctx_blk[0], 0.0)
    late = dot_f32(ctx_blk[1].astype(jnp.bfloat16), shift, NN)
    for j in range(4):
        part = late[:, j * quarter : (j + 1) * quarter]
        if j < 2:
            part = part + early[:, j * quarter : (j + 1) * quarter]
        c_tok[j] = part.astype(jnp.bfloat16)
    for r, piece in enumerate((c0, c1, c2, c3)):
        piece[...] = c_tok[r ^ mine]
    keep_x.wait()
    keep_qkv.wait()


def attend_backward(
    heads, index, places, g0, g1, g2, g3, w_t, x_in, qkv, ctx_blk, lse, acc_in, acc_b, *refs
):
    last = len(refs) == 14
    (dx_keep, dx_send, grad_w, grad_b, g_tok, g_blk, d_qkv, tok, x_seq, acc, dx_s, sems) = refs[-12:]
    bring_x = pltpu.make_async_copy(x_in, x_seq, sems.at[0])
    bring_acc = pltpu.make_async_copy(acc_in, acc, sems.at[1])
    bring_x.start()
    bring_acc.start()
    half, mine, perm = sequence_scalars(places, index)
    index = max(index - 1, 0)
    quarter = g0.shape[2]
    block = 2 * quarter
    whole = 4 * quarter
    wide = heads * HEAD_DIM
    for r, piece in enumerate((g0[index], g1[index], g2[0, index], g3[index])):
        g_tok[r ^ mine] = piece
    shift = shift_matrix(half, block, whole)
    lane = lax.broadcasted_iota(jnp.int32, (1, block), 1)
    g_all = jnp.concatenate([g_tok[j] for j in range(4)], axis=1)
    g_blk[0] = jnp.where(lane < half, g_all[:, :block], jnp.zeros((), jnp.bfloat16))
    g_blk[1] = dot_f32(g_all, shift, NT).astype(jnp.bfloat16)
    key_tile, query_tile = mask_tiles(half, block)

    def one_block(b, carry):
        target = places[perm + b]
        for h in range(heads):
            rows = slice(h * HEAD_DIM, (h + 1) * HEAD_DIM)
            k_rows = slice(wide + h * HEAD_DIM, wide + (h + 1) * HEAD_DIM)
            v_rows = slice(2 * wide + h * HEAD_DIM, 2 * wide + (h + 1) * HEAD_DIM)
            q_t = qkv[b, rows, :]
            k_t = qkv[target, k_rows, :]
            v_t = qkv[target, v_rows, :]
            g_t = g_blk[b, rows, :]
            scores = dot_f32(
                jnp.concatenate([k_t, key_tile]), jnp.concatenate([q_t, query_tile]), TN
            )
            probs = jnp.exp2(scores * SOFT - lse[b, h : h + 1, :])
            d_probs = dot_f32(v_t, g_t, TN)
            delta = jnp.sum(ctx_blk[b, rows, :] * g_t.astype(jnp.float32), axis=0, keepdims=True)
            d_scores = (probs * (d_probs - delta)).astype(jnp.bfloat16)
            scaling = HEAD_DIM ** -0.5
            d_qkv[b, rows, :] = (dot_f32(k_t, d_scores, NN) * scaling).astype(jnp.bfloat16)
            d_qkv[target, k_rows, :] = (dot_f32(q_t, d_scores, NT) * scaling).astype(jnp.bfloat16)
            d_qkv[target, v_rows, :] = dot_f32(g_t, probs.astype(jnp.bfloat16), NT).astype(
                jnp.bfloat16
            )
        return carry

    lax.fori_loop(0, 2, one_block, 0)
    late = dot_f32(d_qkv[1], shift, NN)
    front = jnp.where(lane < half, d_qkv[0].astype(jnp.float32), 0.0)
    tok[:, block:] = late[:, block:].astype(jnp.bfloat16)
    tok[:, :block] = (late[:, :block] + front).astype(jnp.bfloat16)
    sent = []
    for r in range(4):
        piece = (dx_send if r & 1 else dx_keep).at[r >> 1]
        columns = tok[:, pl.ds(pl.multiple_of((r ^ mine) * quarter, quarter), quarter)]
        dx_s[r] = dot_f32(columns, w_t[...], TN).astype(jnp.bfloat16)
        sent.append(pltpu.make_async_copy(dx_s.at[r], piece, sems.at[2 + r]))
        sent[-1].start()
    bring_acc.wait()
    bring_x.wait()
    total = acc[...] + dot_f32(tok[...], x_seq[...], NN)
    ones = jnp.ones((8, whole), jnp.bfloat16)
    sums = acc_b[...] + dot_f32(ones, tok[...], NT)
    if last:
        out_own, vectors = refs[:2]
        inner = places[10]
        turned = total.T
        tile = out_own.shape[1]
        extra = grad_w.shape[1] - tile
        grad_w[:, tile:, :] = jnp.zeros((8, extra, 4 * wide), jnp.bfloat16)
        for q in range(8):
            grad_w[q ^ inner, :tile, : 3 * wide] = turned[q * tile : (q + 1) * tile].astype(
                jnp.bfloat16
            )
        grad_w[:, :tile, 3 * wide :] = out_own[...]
        row = lax.broadcasted_iota(jnp.int32, (extra, 1), 0)
        own_row = jnp.concatenate([sums[0:1, :], jnp.zeros((1, wide), jnp.float32)], axis=1)
        grad_w[inner, tile:, :] = jnp.where(row == 10, own_row, vectors[...]).astype(jnp.bfloat16)
        grad_b[...] = sums
    else:
        grad_w[...] = total
        grad_b[...] = sums
    for copy in sent:
        copy.wait()


def kernel_call(body, scalars, arrays, outs, scratch, left_in=(), left_out=()):
    def spec(away):
        return pl.BlockSpec(memory_space=pl.ANY if away else pltpu.VMEM)

    return pl.pallas_call(
        body,
        out_shape=outs,
        in_specs=[pl.BlockSpec(memory_space=pltpu.SMEM)]
        + [spec(i in left_in) for i in range(len(arrays))],
        out_specs=[spec(i in left_out) for i in range(len(outs))],
        scratch_shapes=scratch,
        compiler_params=pltpu.CompilerParams(vmem_limit_bytes=VMEM_LIMIT),
        cost_estimate=pl.CostEstimate(
            flops=10**8, transcendentals=0, bytes_accessed=1024 * 1024
        ),
    )(scalars, *arrays)


def attention_forward(places, pieces, index, w_t, bias, heads):
    quarter, features = pieces[0].shape
    whole, block, wide = 4 * quarter, 2 * quarter, heads * HEAD_DIM
    out = jax.ShapeDtypeStruct
    outs = [out((wide, quarter), jnp.bfloat16)] * 4 + [
        out((whole, features), jnp.bfloat16),
        out((2, 3 * wide, block), jnp.bfloat16),
        out((2, wide, block), jnp.float32),
        out((2, 8, block), jnp.float32),
    ]
    scratch = [
        pltpu.VMEM((3 * wide, whole), jnp.bfloat16),
        pltpu.VMEM((4, wide, quarter), jnp.bfloat16),
        pltpu.VMEM((whole, features), jnp.bfloat16),
        pltpu.VMEM((2, 3 * wide, block), jnp.bfloat16),
        pltpu.SemaphoreType.DMA((2,)),
    ]
    found = kernel_call(
        functools.partial(attend_forward, heads, index),
        places,
        [*pieces, w_t, bias],
        outs,
        scratch,
        left_out=(4, 5),
    )
    return found[:4], found[4:]


def attention_backward(places, pieces, index, w_t, kept, acc, acc_b, heads, late=()):
    _, wide, quarter = pieces[0].shape
    features = w_t.shape[1]
    block = 2 * quarter
    out = jax.ShapeDtypeStruct
    grad = (
        out((8, features // 8 + 16, 4 * wide), jnp.bfloat16)
        if late
        else out((3 * wide, features), jnp.float32)
    )
    outs = [out((2, quarter, features), jnp.bfloat16)] * 2 + [grad, out((8, 3 * wide), jnp.float32)]
    scratch = [
        pltpu.VMEM((4, wide, quarter), jnp.bfloat16),
        pltpu.VMEM((2, wide, block), jnp.bfloat16),
        pltpu.VMEM((2, 3 * wide, block), jnp.bfloat16),
        pltpu.VMEM((3 * wide, 4 * quarter), jnp.bfloat16),
        pltpu.VMEM((4 * quarter, features), jnp.bfloat16),
        pltpu.VMEM((3 * wide, features), jnp.float32),
        pltpu.VMEM((4, quarter, features), jnp.bfloat16),
        pltpu.SemaphoreType.DMA((6,)),
    ]
    found = kernel_call(
        functools.partial(attend_backward, heads, index),
        places,
        [*pieces, w_t, *kept, acc, acc_b, *late],
        outs,
        scratch,
        left_in=(5, 9),
        left_out=(0, 1),
    )
    return found[:2], found[2], found[3]

def live_rows(places, rows, mine, local_rows, offset):
    row = lax.broadcasted_iota(jnp.int32, (rows, 1), 0)
    length = jnp.zeros((rows, 1), jnp.int32)
    for s in range(rows // local_rows):
        length = jnp.where(row >= s * local_rows, places[offset + s], length)
    position = mine * local_rows + lax.rem(row, local_rows)
    return jnp.where(position < length, 1.0, 0.0)


def normal_parts(array_in):
    centered = array_in - jnp.mean(array_in, axis=1, keepdims=True)
    spread = jnp.mean(centered * centered, axis=1, keepdims=True)
    inverse = lax.rsqrt(spread + EPSILON)
    return centered * inverse, inverse


def normal_back(hat, inverse, gain, d_out):
    scaled = d_out * gain
    mean_scaled = jnp.mean(scaled, axis=1, keepdims=True)
    mean_product = jnp.mean(scaled * hat, axis=1, keepdims=True)
    return inverse * (scaled - mean_scaled - hat * mean_product)


def column_sum(array_in):
    return jnp.sum(array_in, axis=0, keepdims=True)


def token_layer(shape, places, *refs):
    seq_count, seq_parts = shape
    count = seq_count * seq_parts
    pieces, refs = refs[:count], refs[count:]
    tokens, cot_in, w_out, vectors, b_up, w_up_in, w_down_in = refs[:7]
    out, send_down1, send_up1, send_down0, send_up0, keep_down, keep_up = refs[7:14]
    d_first_in, sums, grad_out = refs[14:17]
    sent = refs[17:23]
    (
        w_up, w_down, active, slope, context, first_in, first_norm, lowered,
        first_low, first_t, d_lowered, turned, out_s, cot, grad_down, grad_up, sems,
    ) = refs[23:]
    rows, features = tokens.shape
    local_rows = rows // seq_count
    wide = features // seq_parts
    mine, inner = places[9], places[8]
    step = pl.program_id(0)
    quarters = w_up.shape[0]
    width = w_up.shape[2]
    f32, bf16 = jnp.float32, jnp.bfloat16

    def bring(j):
        return (
            pltpu.make_async_copy(
                w_up_in.at[:, pl.ds(j * width, width)], w_up.at[j], sems.at[j]
            ),
            pltpu.make_async_copy(
                w_down_in.at[pl.ds(j * width, width), :], w_down.at[j], sems.at[quarters + j]
            ),
        )

    keep_out = pltpu.make_async_copy(out_s, out, sems.at[2 * quarters])
    bring_cot = pltpu.make_async_copy(cot_in, cot, sems.at[2 * quarters + 1])

    def leave(relative):
        down_ref, up_ref = (
            (keep_down.at[pl.ds(0, 2)], keep_up.at[pl.ds(0, 2)]),
            (keep_down.at[pl.ds(2, 2)], keep_up.at[pl.ds(2, 2)]),
            (send_down0, send_up0),
            (send_down1, send_up1),
        )[relative]
        first = 2 * quarters + 2 + 2 * relative
        return (
            pltpu.make_async_copy(grad_down.at[relative & 1], down_ref, sems.at[first]),
            pltpu.make_async_copy(grad_up.at[relative & 1], up_ref, sems.at[first + 1]),
        )

    @pl.when(step == 0)
    def start():
        for j in range(quarters):
            for copy in bring(j):
                copy.start()
        bring_cot.start()
        for s in range(seq_count):
            for r in range(seq_parts):
                context[
                    pl.ds(pl.multiple_of((r ^ mine) * wide, wide), wide),
                    s * local_rows : (s + 1) * local_rows,
                ] = pieces[s * seq_parts + r][...]
        live = live_rows(places, rows, mine, local_rows, 11)
        attended = dot_f32(context[...], w_out[...], TN) + vectors[0:1, :]
        total = jnp.where(live > 0, tokens[...].astype(f32), 0.0) + attended
        first_in[...] = total
        hat, _ = normal_parts(total)
        normed = hat * vectors[1:2, :] + vectors[2:3, :]
        first_norm[...] = normed
        low = normed.astype(bf16)
        first_low[...] = low
        tile = features // 4
        low_t = low.T
        for q in range(4):
            first_t[pl.ds(pl.multiple_of((q ^ inner) * tile, tile), tile), :] = low_t[
                q * tile : (q + 1) * tile
            ]
        lowered[...] = jnp.zeros_like(lowered)
        sums[...] = jnp.zeros_like(sums)

    @pl.when(step < quarters)
    def forward():
        for j in range(quarters):

            @pl.when(step == j)
            def arrive():
                for copy in bring(j):
                    copy.wait()

        lifted = dot_f32(first_low[...], w_up[step], NN) + b_up[step]
        cdf = 0.5 * (1.0 + lax.erf(lifted * 0.7071067811865476))
        density = jnp.exp(lifted * lifted * -0.5) * 0.3989422804014327
        gelu = (lifted * cdf).astype(bf16)
        active[step] = gelu
        slope[step] = (cdf + lifted * density).astype(bf16)
        lowered[...] += dot_f32(gelu, w_down[step], NN)

    @pl.when(step == quarters - 1)
    def turn():
        live = live_rows(places, rows, mine, local_rows, 11)
        hat, inverse = normal_parts(first_norm[...] + (lowered[...] + vectors[3:4, :]))
        gain = vectors[4:5, :]
        bring_cot.wait()
        out_s[...] = ((hat * gain + vectors[5:6, :]) * live).astype(bf16)
        keep_out.start()
        incoming = cot[...].astype(f32) * live
        back = normal_back(hat, inverse, gain, incoming)
        lowered[...] = back
        low = back.astype(bf16)
        d_lowered[...] = low
        sums[0:1, :] = column_sum(low.astype(f32))
        sums[1:2, :] = column_sum(incoming * hat)
        sums[2:3, :] = column_sum(incoming)

    @pl.when(step >= quarters)
    def backward():
        relative = 2 * quarters - 1 - step
        quarter = relative ^ (places[0] >> 1)
        low_bit = places[0] & 1
        slot = relative & 1
        half = width // 2
        tile = half // 4
        for k in range(2):

            @pl.when(relative == k)
            def free():
                for copy in leave(k + 2):
                    copy.wait()

        down = dot_f32(active[quarter], d_lowered[...], TN).astype(bf16)
        for j in range(2):
            for q in range(4):
                grad_down[
                    slot, j ^ low_bit, pl.ds(pl.multiple_of((q ^ inner) * tile, tile), tile), :
                ] = down[j * half + q * tile : j * half + (q + 1) * tile]
        d_active = dot_f32(d_lowered[...], w_down[quarter], NT)
        d_lifted = (d_active * slope[quarter].astype(f32)).astype(bf16)
        up = dot_f32(first_t[...], d_lifted, NN).astype(bf16)
        for j in range(2):
            grad_up[slot, j ^ low_bit] = up[:, j * half : (j + 1) * half]
        sums[pl.ds(6 + quarter, 1), :] = column_sum(d_lifted.astype(f32))
        lowered[...] += dot_f32(d_lifted, w_up[quarter], NT)
        for k in range(quarters):

            @pl.when(relative == k)
            def start_leaving():
                for copy in leave(k):
                    copy.start()

    @pl.when(step == 2 * quarters - 1)
    def finish():
        hat, inverse = normal_parts(first_in[...])
        incoming = lowered[...]
        back = normal_back(hat, inverse, vectors[1:2, :], incoming)
        d_first_in[...] = back
        low = back.astype(bf16)
        sums[3:4, :] = column_sum(low.astype(f32))
        sums[4:5, :] = column_sum(incoming * hat)
        sums[5:6, :] = column_sum(incoming)
        turned[...] = dot_f32(w_out[...], low, NT).astype(bf16)
        for r in range(seq_parts):
            own = turned[pl.ds(pl.multiple_of((r ^ mine) * wide, wide), wide), :]
            for s in range(seq_count):
                target, place = sent[3 * min(s, 1) + min(r, 2)], max(s - 1, 0)
                columns = own[:, s * local_rows : (s + 1) * local_rows]
                if r < 2:
                    target[place] = columns
                else:
                    target[r - 2, place] = columns
        product = dot_f32(context[...], low, NN).astype(bf16)
        block_rows, block_cols = grad_out.shape[2:]
        across = features // block_cols
        for j in range(seq_parts):
            for q in range(wide // block_rows * across):
                row, col = j * wide + q // across * block_rows, q % across * block_cols
                grad_out[j ^ mine, q ^ places[10]] = product[
                    row : row + block_rows, col : col + block_cols
                ]
        keep_out.wait()
        for k in range(2):
            for copy in leave(k):
                copy.wait()


def whole_spec(shape):
    return pl.BlockSpec(
        shape, lambda p, places: (0,) * len(shape), pipeline_mode=pl.Buffered(buffer_count=1)
    )


def step_call(body, places, steps, ins, in_specs, outs, out_specs, scratch, flops, aliases={}):
    return pl.pallas_call(
        body,
        out_shape=outs,
        grid_spec=pltpu.PrefetchScalarGridSpec(
            num_scalar_prefetch=1,
            grid=(steps,),
            in_specs=in_specs,
            out_specs=out_specs,
            scratch_shapes=scratch,
        ),
        input_output_aliases=aliases,
        compiler_params=pltpu.CompilerParams(vmem_limit_bytes=VMEM_LIMIT),
        cost_estimate=pl.CostEstimate(
            flops=flops, transcendentals=0, bytes_accessed=20 * 1024 * 1024
        ),
    )(places, *ins)


def run_token_layer(places, pieces, tokens, cot, w_out, vectors, w_up, b_up, w_down, dims):
    seq_count, seq_parts = dims
    rows, features = tokens.shape
    hidden = w_up.shape[1]
    quarters = 4
    width = hidden // quarters
    half = width // 2
    out, bf16, f32 = jax.ShapeDtypeStruct, jnp.bfloat16, jnp.float32
    square, turned = (rows, features), (features, rows)
    piece = (features // seq_parts, rows // seq_count)
    sent = []
    for n in (1, seq_count - 1):
        sent += [(n, *piece), (n, *piece), (2, n, *piece)]
    out_blocks = (seq_parts, 8, features // seq_parts // 2, features // 4)
    away = pl.BlockSpec(memory_space=pl.ANY)
    down, up = (2, half, features), (2, features, half)

    return step_call(
        functools.partial(token_layer, dims),
        places,
        2 * quarters,
        [*pieces, tokens, cot, w_out, vectors, b_up.reshape(quarters, 1, width), w_up, w_down],
        [whole_spec(p.shape) for p in pieces]
        + [whole_spec(square), away, whole_spec(w_out.shape), whole_spec(vectors.shape)]
        + [whole_spec((quarters, 1, width)), away, away],
        [
            out(square, bf16),
            out(down, bf16),
            out(up, bf16),
            out(down, bf16),
            out(up, bf16),
            out((4, half, features), bf16),
            out((4, features, half), bf16),
            out(square, f32),
            out((16, features), f32),
            out(out_blocks, bf16),
        ]
        + [out(p, bf16) for p in sent],
        [away] * 7
        + [whole_spec(square), whole_spec((16, features)), whole_spec(out_blocks)]
        + [whole_spec(p) for p in sent],
        [
            pltpu.VMEM((quarters, features, width), bf16),
            pltpu.VMEM((quarters, width, features), bf16),
            pltpu.VMEM((quarters, rows, width), bf16),
            pltpu.VMEM((quarters, rows, width), bf16),
            pltpu.VMEM(turned, bf16),
            pltpu.VMEM(square, f32),
            pltpu.VMEM(square, f32),
            pltpu.VMEM(square, f32),
            pltpu.VMEM(square, bf16),
            pltpu.VMEM(turned, bf16),
            pltpu.VMEM(square, bf16),
            pltpu.VMEM(turned, bf16),
            pltpu.VMEM(square, bf16),
            pltpu.VMEM(square, bf16),
            pltpu.VMEM((2, *down), bf16),
            pltpu.VMEM((2, *up), bf16),
            pltpu.SemaphoreType.DMA((4 * quarters + 2,)),
        ],
        2 * rows * features * (6 * hidden + 3 * features),
    )


def place_rows(by_rows, places, *refs):
    pieces, out = refs[:2], refs[-1]
    step = pl.program_id(0)
    tile = pieces[0].shape[1]
    for k in range(4):
        c, other = k >> 1, k & 1

        @pl.when(step == k)
        def copy():
            for q in range(4):
                h, x = q >> 1, q & 1
                sub = other * 4 + x * 2 + h if by_rows else x * 4 + other * 2 + h
                out[pl.ds(pl.multiple_of((q ^ places[8]) * tile, tile), tile), :] = pieces[c][
                    sub
                ].astype(jnp.float32)


def gather_hidden(places, pieces, begun, shape, by_rows):
    _, rows, cols = pieces[0].shape
    bit = 0 if begun is None else 1

    def number(p):
        return (p >> 1) * 4 + bit * 2 + (p & 1) if by_rows else p * 2 + bit

    def index(p, places):
        place = places[number(p)]
        return (place, 0) if by_rows else (0, place)

    begun = [] if begun is None else [begun]
    return step_call(
        functools.partial(place_rows, by_rows),
        places,
        4,
        pieces + begun,
        [whole_spec(p.shape) for p in pieces] + [pl.BlockSpec(memory_space=pl.ANY)] * len(begun),
        jax.ShapeDtypeStruct(shape, jnp.float32),
        pl.BlockSpec((4 * rows, cols), index),
        [],
        8 * rows * cols,
        {3: 0} if begun else {},
    )


def place_heads(places, *refs):
    pieces = refs[:-5]
    out, out_w, vector_rows, head_rows, held = refs[-5:]
    mine, inner = places[9], places[10]
    seq_parts = len(pieces)
    step = pl.program_id(0)
    wide = out_w.shape[0] // seq_parts
    rows = out.shape[0]
    f32 = jnp.float32
    for r, piece in enumerate(pieces):
        for j in range(seq_parts):

            @pl.when((r ^ mine) == j)
            def copy():
                block = piece[step ^ inner, :rows, : 3 * wide].astype(f32)
                for k in range(3):
                    start = (k * seq_parts + j) * wide
                    out[:, start : start + wide] = block[:, k * wide : (k + 1) * wide]

        @pl.when(step == r)
        def copy_out():
            tile, width = wide // 2, out_w.shape[1] // 4
            for q in range(8):
                row = pl.multiple_of((r ^ mine) * wide + q // 4 * tile, tile)
                col = q % 4 * width
                out_w[pl.ds(row, tile), col : col + width] = piece[
                    q ^ inner, :rows, 3 * wide :
                ].astype(f32)

        @pl.when(step == seq_parts)
        def copy_vectors():
            held[r ^ mine] = piece[inner, rows:, :].astype(f32)

    @pl.when(step == seq_parts)
    def sum_vectors():
        total = held[0]
        for j in range(1, seq_parts):
            total = total + held[j]
        vector_rows[...] = total
        for j in range(seq_parts):
            head_rows[j : j + 1, :] = held[j, 10:11, :]


def gather_heads(places, pieces, shape):
    out, f32 = jax.ShapeDtypeStruct, jnp.float32
    features = shape[0]
    rows = features // 8
    square = (features, features)
    extra = (pieces[0].shape[1] - rows, features)
    return step_call(
        place_heads,
        places,
        8,
        pieces,
        [whole_spec(p.shape) for p in pieces],
        [out(shape, f32), out(square, f32), out(extra, f32), out((8, features), f32)],
        [pl.BlockSpec((rows, shape[1]), lambda p, places: (p, 0))]
        + [whole_spec(square), whole_spec(extra), whole_spec((8, features))],
        [pltpu.VMEM((len(pieces), *extra), f32)],
        1000,
    )


def per_device(
    tokens,
    cotangent,
    lengths,
    block_perm,
    w_qkv,
    b_query,
    b_value,
    w_out,
    b_out,
    ln1_gain,
    ln1_shift,
    w_up,
    b_up,
    w_down,
    b_down,
    ln2_gain,
    ln2_shift,
):
    seq_parts = lax.axis_size("seq")
    mine = lax.axis_index("seq")
    seq_count, local_rows, features = tokens.shape
    flat_rows = seq_count * local_rows
    hidden = w_up.shape[1]
    heads = HEADS // seq_parts
    wide = heads * HEAD_DIM
    dims = (seq_count, seq_parts)
    f32 = jnp.float32

    w_heads = jnp.concatenate(
        [
            lax.dynamic_slice_in_dim(w_qkv, k * features + mine * wide, wide, axis=1)
            for k in range(3)
        ],
        axis=1,
    )
    w_t = w_heads.T
    bias = jnp.concatenate(
        [
            lax.dynamic_slice_in_dim(b_query, mine * wide, wide),
            jnp.zeros((wide,), b_query.dtype),
            lax.dynamic_slice_in_dim(b_value, mine * wide, wide),
        ]
    ).astype(f32)[:, None]
    outer = own_number("cyl")
    places = jnp.concatenate(
        [
            jnp.arange(8, dtype=jnp.int32) ^ outer,
            jnp.stack([own_number("hx"), mine, own_number("ylh")]),
            lengths,
            block_perm.reshape(-1),
        ]
    )
    vectors = jnp.stack(
        [v.astype(f32) for v in (b_out, ln1_gain, ln1_shift, b_down, ln2_gain, ln2_shift, b_out, b_out)]
    )

    arrived, kept, crossed = [], [], []
    for s in range(seq_count):
        near = tokens[s]
        start = near
        if s > 0:
            after = [crossed[-1]] + arrived[(s - 2) * seq_parts : (s - 2) * seq_parts + 1] * (s > 1)
            start, _ = lax.optimization_barrier((near, after))
        across = exchange_bit(start, "x")
        crossed.append(across)
        if s > 0:
            across, _ = lax.optimization_barrier((across, arrived[-seq_parts]))
        pieces = [near, exchange_bit(near, "c"), across, exchange_bit(across, "c")]
        contexts, saved = attention_forward(places, pieces, s, w_t, bias, heads)
        kept.append(saved)
        arrived += [contexts[0]] + [exchange(contexts[r], "seq", r) for r in range(1, seq_parts)]

    (
        out_rows,
        send_down1,
        send_up1,
        send_down0,
        send_up0,
        keep_down,
        keep_up,
        d_first_in,
        sums,
        grad_out,
        *d_contexts,
    ) = run_token_layer(
        places,
        arrived,
        tokens.reshape(flat_rows, features),
        cotangent.reshape(flat_rows, features),
        w_out,
        vectors,
        w_up,
        b_up.astype(f32).reshape(1, hidden),
        w_down,
        dims,
    )
    out_tokens = out_rows.reshape(seq_count, local_rows, features)

    def hand_on(own, near, came):
        return [own, exchange_bit(near, "c"), came, exchange_bit(came[1], "c")]

    first_came = exchange_bit(d_contexts[2], "x")
    came_down1, came_up1 = exchange_bit(send_down1, "c"), exchange_bit(send_up1, "c")
    send_up0, first_came = lax.optimization_barrier((send_up0, first_came))
    came_up0 = exchange_bit(send_up0, "c")
    second_pair, first_came = lax.optimization_barrier((d_contexts[5], first_came))
    second_came = exchange_bit(second_pair, "x")
    total_w = jnp.zeros((3 * wide, features), f32)
    total_b = jnp.zeros((8, 3 * wide), f32)
    parts, near, far = [], [], []

    def attend(s, group, total_w, total_b, late=()):
        found, total_w, total_b = attention_backward(
            places, group, s, w_t, kept[s], total_w, total_b, heads, late
        )
        parts.append(found)
        return total_w, total_b

    def cross(s):
        held, sent = parts[s]
        came = exchange_bit(sent, "c")
        near.append(held[0].astype(f32) + came[0])
        far.append(sum_low(held[1], came[1]))

    sends = [
        sum_low(keep_down[3], came_down1[1]),
        sum_low(keep_up[3], came_up1[1]),
        grad_out[2:],
    ]
    sends, first_came = lax.optimization_barrier((sends, first_came))
    down_y1, up_l3, out_x = [exchange_bit(v, bit) for v, bit in zip(sends, "ylx")]
    total_w, total_b = attend(0, hand_on(d_contexts[0], d_contexts[1], first_came), total_w, total_b)
    (down_y1, up_l3, out_x, total_w, parts[0], second_came, near_pair, came_up0, send_down0) = (
        lax.optimization_barrier(
            (down_y1, up_l3, out_x, total_w, parts[0], second_came, d_contexts[3:5])
            + (came_up0, send_down0)
        )
    )
    came_down0 = exchange_bit(send_down0, "c")

    sends = [
        sum_low(keep_down[2], came_down1[0]),
        sum_low(keep_up[1], came_up0[1]),
        sum_low(grad_out[1], out_x[1]),
    ]
    (sends, total_w) = lax.optimization_barrier((sends, total_w))
    down_y0, up_l1, out_c = [exchange_bit(v, bit) for v, bit in zip(sends, "ylc")]
    cross(0)
    second_group = hand_on(*near_pair, second_came)
    for s in range(1, seq_count - 1):
        total_w, total_b = attend(s, second_group, total_w, total_b)
    out_own = sum_low(grad_out[0], out_x[0], out_c)
    (down_y0, up_l1, total_w, parts[1:], near, far, out_own) = lax.optimization_barrier(
        (down_y0, up_l1, total_w, parts[1:], near, far, out_own)
    )

    sends = [
        sum_low(keep_down[1], came_down0[1], down_y1),
        sum_low(keep_up[2], came_up1[0], up_l3),
    ]
    (sends, total_w) = lax.optimization_barrier((sends, total_w))
    down_l, up_y = [exchange_bit(v, bit) for v, bit in zip(sends, "ly")]
    far_came = [exchange_bit(far[0], "x")]
    for s in range(1, seq_count - 1):
        cross(s)
    total_w, total_b = attend(seq_count - 1, second_group, total_w, total_b, (out_own, sums))

    (down_l, up_y, far, far_came, total_w, parts[-1]) = lax.optimization_barrier(
        (down_l, up_y, far, far_came, total_w, parts[-1])
    )
    down_own = sum_low(keep_down[0], came_down0[0], down_y0, down_l)
    down_own = down_own.reshape(4, hidden // 32, features)
    up_own = sum_low(keep_up[0], came_up0[0], up_l1, up_y)
    up_own = up_own.reshape(2, 2, features // 4, hidden // 8)
    keeps = [down_own[:2], up_own[:, 0], total_w[:4]]
    sends = [down_own[2:], up_own[:, 1], total_w[4:]]
    (keeps, sends) = lax.optimization_barrier((keeps, sends))
    got = [exchange_bit(v, bit) for v, bit in zip(sends, "hxy")]
    far_came += [exchange_bit(v, "x") for v in far[1:]]
    down_own, up_own, qkv_own = [k + g for k, g in zip(keeps, got)]
    qkv_own = qkv_own[:2] + exchange_bit(qkv_own[2:], "l")
    far = []
    cross(seq_count - 1)

    keeps = [down_own[:1], up_own[:1], qkv_own[:1]]
    sends = [down_own[1:], up_own[1:], qkv_own[1:]]
    (keeps, sends, far, far_came, near) = lax.optimization_barrier(
        (keeps, sends, far, far_came, near)
    )
    got = [exchange_bit(v, bit) for v, bit in zip(sends, "xhh")]
    far_came += [exchange_bit(v, "x") for v in far]
    shards = [add_extra(k + g) for k, g in zip(keeps, got)]

    own_pos = mine * local_rows + jnp.arange(local_rows, dtype=jnp.int32)
    live = (own_pos[None, :] < lengths[:, None]).astype(f32)
    d_inputs = jnp.stack([n + f for n, f in zip(near, far_came)])
    grad_tokens = (d_inputs + d_first_in.reshape(seq_count, local_rows, features)) * live[:, :, None]
    for bits in ("hhh", "xyl", "lxy"):
        if bits == "xyl":
            (shards, grad_tokens) = lax.optimization_barrier((shards, grad_tokens))
        else:
            shards = lax.optimization_barrier(shards)
        shards = [
            jnp.concatenate([shard, exchange_bit(shard, bit)]) for shard, bit in zip(shards, bits)
        ]
    shards = lax.optimization_barrier(shards)
    last = [exchange_bit(shard, bit) for shard, bit in zip(shards, "ylx")]
    near_c = [exchange_bit(shard, "c") for shard in shards]
    early = [
        gather_hidden(places, [shards[i], near_c[i]], None, shape, i == 0)
        for i, shape in ((0, (hidden, features)), (1, (features, hidden)))
    ]
    (last, early) = lax.optimization_barrier((last, early))
    far_c = [exchange_bit(shard, "c") for shard in last]
    full_down, full_up = [
        gather_hidden(places, [last[i], far_c[i]], early[i], early[i].shape, i == 0) for i in (0, 1)
    ]
    full_qkv, full_out, vector_rows, head_rows = gather_heads(
        places, [shards[2], near_c[2], last[2], far_c[2]], (features, 3 * features)
    )
    (
        full_b_down,
        full_gain_two,
        full_shift_two,
        full_b_out,
        full_gain_one,
        full_shift_one,
    ) = [vector_rows[i] for i in range(6)]
    full_b_up = vector_rows[6 : 6 + hidden // features].reshape(hidden)
    full_b_query = head_rows[:seq_parts, :wide].reshape(features)
    full_b_value = head_rows[:seq_parts, 2 * wide : 3 * wide].reshape(features)

    return (
        out_tokens,
        grad_tokens,
        full_qkv,
        full_b_query,
        full_b_value,
        full_out,
        full_b_out,
        full_gain_one,
        full_shift_one,
        full_up,
        full_b_up,
        full_down,
        full_b_down,
        full_gain_two,
        full_shift_two,
    )


def solution(mesh):
    in_specs = (
        P("dp", "seq", None),
        P("dp", "seq", None),
        P("dp"),
        P("dp", None),
        P(),
        P(),
        P(),
        P(),
        P(),
        P(),
        P(),
        P(),
        P(),
        P(),
        P(),
        P(),
        P(),
    )
    out_specs = (
        P("dp", "seq", None),
        P("dp", "seq", None),
        P(),
        P(),
        P(),
        P(),
        P(),
        P(),
        P(),
        P(),
        P(),
        P(),
        P(),
        P(),
        P(),
    )
    return jax.shard_map(
        per_device, mesh=mesh, in_specs=in_specs, out_specs=out_specs, check_vma=False
    )
```

```python
import functools
import jax
import jax.numpy as jnp
from jax import lax
from jax.experimental import pallas as pl
from jax.experimental.pallas import tpu as pltpu
from jax.sharding import PartitionSpec as P

HEAD_DIM = 64
SOFT = HEAD_DIM ** -0.5 * 1.4426950408889634
NN = (((1,), (0,)), ((), ()))
NT = (((1,), (1,)), ((), ()))
TN = (((0,), (0,)), ((), ()))
VMEM_LIMIT = 60 * 1024 * 1024
HEADS = 12
EPSILON = 1e-06
BITS = {"c": ("seq", 0), "x": ("seq", 1), "y": ("dp", 0), "l": ("dp", 1), "h": ("dp", 2)}


def own_number(order):
    number = jnp.int32(0)
    for letter in order:
        axis, shift = BITS[letter]
        number = number * 2 + ((lax.axis_index(axis) >> shift) & 1)
    return number


def exchange(array_in, axis, flip):
    return lax.ppermute(array_in, axis, [(i, i ^ flip) for i in range(lax.axis_size(axis))])


def exchange_bit(array_in, letter):
    axis, shift = BITS[letter]
    return exchange(array_in, axis, 1 << shift)


def extra_flips(axis, used):
    return [1 << shift for shift in range(used, lax.axis_size(axis).bit_length() - 1)]


def add_extra(array_in):
    for flip in extra_flips("dp", 3):
        array_in = array_in + exchange(array_in, "dp", flip)
    return array_in


def sum_low(*parts):
    total = parts[0].astype(jnp.float32)
    for part in parts[1:]:
        total = total + part.astype(jnp.float32)
    return total.astype(jnp.bfloat16)


def dot_f32(left, right, dims):
    return lax.dot_general(left, right, dims, preferred_element_type=jnp.float32)


def sequence_scalars(places, index):
    seq_count = (places.shape[0] - 11) // 3
    return places[11 + index] >> 1, places[9], 11 + seq_count + 2 * index


def shift_matrix(half, block, whole):
    row = lax.broadcasted_iota(jnp.int32, (block, whole), 0)
    col = lax.broadcasted_iota(jnp.int32, (block, whole), 1)
    return jnp.where((col == row + half) & (row < half), 1.0, 0.0).astype(jnp.bfloat16)


def mask_tiles(half, block):
    row = lax.broadcasted_iota(jnp.int32, (16, block), 0)
    col = lax.broadcasted_iota(jnp.int32, (16, block), 1)
    key_tile = jnp.where((row == 0) & (col >= half), -1e30, 0.0).astype(jnp.bfloat16)
    query_tile = jnp.where(row == 0, 1.0, 0.0).astype(jnp.bfloat16)
    return key_tile, query_tile


def attend_forward(
    heads, index, places, x0, x1, x2, x3, w_t, bias, c0, c1, c2, c3,
    x_out, qkv_out, ctx_blk, lse, tok, c_tok, x_seq, qkv, sems,
):
    half, mine, perm = sequence_scalars(places, index)
    whole = x_seq.shape[0]
    quarter = whole // 4
    block = whole // 2
    wide = heads * HEAD_DIM
    for r, piece in enumerate((x0, x1, x2, x3)):
        x_seq[pl.ds(pl.multiple_of((r ^ mine) * quarter, quarter), quarter), :] = piece[...]
    keep_x = pltpu.make_async_copy(x_seq, x_out, sems.at[0])
    keep_x.start()
    lane = lax.broadcasted_iota(jnp.int32, (1, block), 1)
    tok[...] = (dot_f32(w_t[...], x_seq[...], NT) + bias[...]).astype(jnp.bfloat16)
    shift = shift_matrix(half, block, whole)
    qkv[0] = jnp.where(lane < half, tok[:, :block], jnp.zeros((), jnp.bfloat16))
    qkv[1] = dot_f32(tok[...], shift, NT).astype(jnp.bfloat16)
    keep_qkv = pltpu.make_async_copy(qkv, qkv_out, sems.at[1])
    keep_qkv.start()
    key_tile, query_tile = mask_tiles(half, block)

    def one_block(b, carry):
        target = places[perm + b]
        for h in range(heads):
            rows = slice(h * HEAD_DIM, (h + 1) * HEAD_DIM)
            q_t = jnp.concatenate([qkv[b, rows, :], query_tile])
            k_t = jnp.concatenate(
                [qkv[target, wide + h * HEAD_DIM : wide + (h + 1) * HEAD_DIM, :], key_tile]
            )
            v_t = qkv[target, 2 * wide + h * HEAD_DIM : 2 * wide + (h + 1) * HEAD_DIM, :]
            scores = dot_f32(k_t, q_t, TN) * SOFT
            top = jnp.max(scores, axis=0, keepdims=True)
            expo = jnp.exp2(scores - top)
            total = jnp.sum(expo, axis=0, keepdims=True)
            context = dot_f32(v_t, expo.astype(jnp.bfloat16), NN) / total
            ctx_blk[b, rows, :] = context
            lse[b, h : h + 1, :] = top + jnp.log2(total)
        return carry

    lax.fori_loop(0, 2, one_block, 0)
    early = jnp.where(lane < half, ctx_blk[0], 0.0)
    late = dot_f32(ctx_blk[1].astype(jnp.bfloat16), shift, NN)
    for j in range(4):
        part = late[:, j * quarter : (j + 1) * quarter]
        if j < 2:
            part = part + early[:, j * quarter : (j + 1) * quarter]
        c_tok[j] = part.astype(jnp.bfloat16)
    for r, piece in enumerate((c0, c1, c2, c3)):
        piece[...] = c_tok[r ^ mine]
    keep_x.wait()
    keep_qkv.wait()


def attend_backward(
    heads, index, places, g0, g1, g2, g3, w_t, x_in, qkv, ctx_blk, lse, *refs
):
    first, last = index == 0, len(refs) > 14
    acc_in, acc_b = (None, None) if first else refs[:2]
    (dx_keep, dx_send, grad_w, grad_b, g_tok, g_blk, d_qkv, tok, x_seq, acc, dx_s, sems) = refs[-12:]
    bring_x = pltpu.make_async_copy(x_in, x_seq, sems.at[0])
    bring_x.start()
    if not first:
        bring_acc = pltpu.make_async_copy(acc_in, acc, sems.at[1])
        bring_acc.start()
    half, mine, perm = sequence_scalars(places, index)
    index = max(index - 1, 0)
    quarter = g0.shape[2]
    block = 2 * quarter
    whole = 4 * quarter
    wide = heads * HEAD_DIM
    for r, piece in enumerate((g0[index], g1[index], g2[0, index], g3[index])):
        g_tok[r ^ mine] = piece
    shift = shift_matrix(half, block, whole)
    lane = lax.broadcasted_iota(jnp.int32, (1, block), 1)
    g_all = jnp.concatenate([g_tok[j] for j in range(4)], axis=1)
    g_blk[0] = jnp.where(lane < half, g_all[:, :block], jnp.zeros((), jnp.bfloat16))
    g_blk[1] = dot_f32(g_all, shift, NT).astype(jnp.bfloat16)
    key_tile, query_tile = mask_tiles(half, block)

    def one_block(b, carry):
        target = places[perm + b]
        for h in range(heads):
            rows = slice(h * HEAD_DIM, (h + 1) * HEAD_DIM)
            k_rows = slice(wide + h * HEAD_DIM, wide + (h + 1) * HEAD_DIM)
            v_rows = slice(2 * wide + h * HEAD_DIM, 2 * wide + (h + 1) * HEAD_DIM)
            q_t = qkv[b, rows, :]
            k_t = qkv[target, k_rows, :]
            v_t = qkv[target, v_rows, :]
            g_t = g_blk[b, rows, :]
            scores = dot_f32(
                jnp.concatenate([k_t, key_tile]), jnp.concatenate([q_t, query_tile]), TN
            )
            probs = jnp.exp2(scores * SOFT - lse[b, h : h + 1, :])
            d_probs = dot_f32(v_t, g_t, TN)
            delta = jnp.sum(ctx_blk[b, rows, :] * g_t.astype(jnp.float32), axis=0, keepdims=True)
            d_scores = (probs * (d_probs - delta)).astype(jnp.bfloat16)
            scaling = HEAD_DIM ** -0.5
            d_qkv[b, rows, :] = (dot_f32(k_t, d_scores, NN) * scaling).astype(jnp.bfloat16)
            d_qkv[target, k_rows, :] = (dot_f32(q_t, d_scores, NT) * scaling).astype(jnp.bfloat16)
            d_qkv[target, v_rows, :] = dot_f32(g_t, probs.astype(jnp.bfloat16), NT).astype(
                jnp.bfloat16
            )
        return carry

    lax.fori_loop(0, 2, one_block, 0)
    late = dot_f32(d_qkv[1], shift, NN)
    front = jnp.where(lane < half, d_qkv[0].astype(jnp.float32), 0.0)
    tok[:, block:] = late[:, block:].astype(jnp.bfloat16)
    tok[:, :block] = (late[:, :block] + front).astype(jnp.bfloat16)
    sent = []
    for r in range(4):
        piece = (dx_send if r & 1 else dx_keep).at[r >> 1]
        columns = tok[:, pl.ds(pl.multiple_of((r ^ mine) * quarter, quarter), quarter)]
        dx_s[r] = dot_f32(columns, w_t[...], TN).astype(jnp.bfloat16)
        sent.append(pltpu.make_async_copy(dx_s.at[r], piece, sems.at[2 + r]))
        sent[-1].start()
    bring_x.wait()
    total = dot_f32(tok[...], x_seq[...], NN)
    ones = jnp.ones((8, whole), jnp.bfloat16)
    sums = dot_f32(ones, tok[...], NT)
    if not first:
        bring_acc.wait()
        total, sums = total + acc[...], sums + acc_b[...]
    if last:
        out_own, vectors = refs[2:4]
        inner = places[10]
        turned = total.T
        tile = out_own.shape[1]
        extra = grad_w.shape[1] - tile
        grad_w[:, tile:, :] = jnp.zeros((8, extra, 4 * wide), jnp.bfloat16)
        for q in range(8):
            grad_w[q ^ inner, :tile, : 3 * wide] = turned[q * tile : (q + 1) * tile].astype(
                jnp.bfloat16
            )
        grad_w[:, :tile, 3 * wide :] = out_own[...]
        row = lax.broadcasted_iota(jnp.int32, (extra, 1), 0)
        own_row = jnp.concatenate([sums[0:1, :], jnp.zeros((1, wide), jnp.float32)], axis=1)
        grad_w[inner, tile:, :] = jnp.where(row == 10, own_row, vectors[...]).astype(jnp.bfloat16)
        grad_b[...] = sums
    else:
        grad_w[...] = total
        grad_b[...] = sums
    for copy in sent:
        copy.wait()


def kernel_call(body, scalars, arrays, outs, scratch, left_in=(), left_out=()):
    def spec(away):
        return pl.BlockSpec(memory_space=pl.ANY if away else pltpu.VMEM)

    return pl.pallas_call(
        body,
        out_shape=outs,
        in_specs=[pl.BlockSpec(memory_space=pltpu.SMEM)]
        + [spec(i in left_in) for i in range(len(arrays))],
        out_specs=[spec(i in left_out) for i in range(len(outs))],
        scratch_shapes=scratch,
        compiler_params=pltpu.CompilerParams(vmem_limit_bytes=VMEM_LIMIT),
        cost_estimate=pl.CostEstimate(
            flops=10**8, transcendentals=0, bytes_accessed=1024 * 1024
        ),
    )(scalars, *arrays)


def attention_forward(places, pieces, index, w_t, bias, heads):
    quarter, features = pieces[0].shape
    whole, block, wide = 4 * quarter, 2 * quarter, heads * HEAD_DIM
    out = jax.ShapeDtypeStruct
    outs = [out((wide, quarter), jnp.bfloat16)] * 4 + [
        out((whole, features), jnp.bfloat16),
        out((2, 3 * wide, block), jnp.bfloat16),
        out((2, wide, block), jnp.float32),
        out((2, 8, block), jnp.float32),
    ]
    scratch = [
        pltpu.VMEM((3 * wide, whole), jnp.bfloat16),
        pltpu.VMEM((4, wide, quarter), jnp.bfloat16),
        pltpu.VMEM((whole, features), jnp.bfloat16),
        pltpu.VMEM((2, 3 * wide, block), jnp.bfloat16),
        pltpu.SemaphoreType.DMA((2,)),
    ]
    found = kernel_call(
        functools.partial(attend_forward, heads, index),
        places,
        [*pieces, w_t, bias],
        outs,
        scratch,
        left_out=(4, 5),
    )
    return found[:4], found[4:]


def attention_backward(places, pieces, index, w_t, kept, before, heads, late=()):
    _, wide, quarter = pieces[0].shape
    features = w_t.shape[1]
    block = 2 * quarter
    out = jax.ShapeDtypeStruct
    grad = (
        out((8, features // 8 + 16, 4 * wide), jnp.bfloat16)
        if late
        else out((3 * wide, features), jnp.float32)
    )
    outs = [out((2, quarter, features), jnp.bfloat16)] * 2 + [grad, out((8, 3 * wide), jnp.float32)]
    scratch = [
        pltpu.VMEM((4, wide, quarter), jnp.bfloat16),
        pltpu.VMEM((2, wide, block), jnp.bfloat16),
        pltpu.VMEM((2, 3 * wide, block), jnp.bfloat16),
        pltpu.VMEM((3 * wide, 4 * quarter), jnp.bfloat16),
        pltpu.VMEM((4 * quarter, features), jnp.bfloat16),
        pltpu.VMEM((3 * wide, features), jnp.float32),
        pltpu.VMEM((4, quarter, features), jnp.bfloat16),
        pltpu.SemaphoreType.DMA((6,)),
    ]
    found = kernel_call(
        functools.partial(attend_backward, heads, index),
        places,
        [*pieces, w_t, *kept, *before, *late],
        outs,
        scratch,
        left_in=(5, 9) if before else (5,),
        left_out=(0, 1),
    )
    return found[:2], found[2:]

def live_rows(places, rows, mine, local_rows, offset):
    row = lax.broadcasted_iota(jnp.int32, (rows, 1), 0)
    length = jnp.zeros((rows, 1), jnp.int32)
    for s in range(rows // local_rows):
        length = jnp.where(row >= s * local_rows, places[offset + s], length)
    position = mine * local_rows + lax.rem(row, local_rows)
    return jnp.where(position < length, 1.0, 0.0)


def normal_parts(array_in):
    centered = array_in - jnp.mean(array_in, axis=1, keepdims=True)
    spread = jnp.mean(centered * centered, axis=1, keepdims=True)
    inverse = lax.rsqrt(spread + EPSILON)
    return centered * inverse, inverse


def normal_back(hat, inverse, gain, d_out):
    scaled = d_out * gain
    mean_scaled = jnp.mean(scaled, axis=1, keepdims=True)
    mean_product = jnp.mean(scaled * hat, axis=1, keepdims=True)
    return inverse * (scaled - mean_scaled - hat * mean_product)


def column_sum(array_in):
    return jnp.sum(array_in, axis=0, keepdims=True)


def token_layer(shape, places, *refs):
    seq_count, seq_parts = shape
    count = seq_count * seq_parts
    pieces, refs = refs[:count], refs[count:]
    tokens, cot_in, w_out, vectors, b_up, w_up_in, w_down_in = refs[:7]
    out, send_down1, send_up1, send_down0, send_up0, keep_down, keep_up = refs[7:14]
    d_first_in, sums, grad_out, send_out = refs[14:18]
    sent = refs[18:24]
    (
        w_up, w_down, active, slope, context, first_in, first_norm, lowered,
        first_low, first_t, d_lowered, turned, out_s, cot, grad_down, grad_up, sems,
    ) = refs[24:]
    rows, features = tokens.shape
    local_rows = rows // seq_count
    wide = features // seq_parts
    mine, inner = places[9], places[8]
    step = pl.program_id(0)
    quarters = w_up.shape[0]
    width = w_up.shape[2]
    f32, bf16 = jnp.float32, jnp.bfloat16

    def bring(j):
        return (
            pltpu.make_async_copy(
                w_up_in.at[:, pl.ds(j * width, width)], w_up.at[j], sems.at[j]
            ),
            pltpu.make_async_copy(
                w_down_in.at[pl.ds(j * width, width), :], w_down.at[j], sems.at[quarters + j]
            ),
        )

    keep_out = pltpu.make_async_copy(out_s, out, sems.at[2 * quarters])
    bring_cot = pltpu.make_async_copy(cot_in, cot, sems.at[2 * quarters + 1])

    def leave(relative):
        down_ref, up_ref = (
            (keep_down.at[pl.ds(0, 2)], keep_up.at[pl.ds(0, 2)]),
            (keep_down.at[pl.ds(2, 2)], keep_up.at[pl.ds(2, 2)]),
            (send_down0, send_up0),
            (send_down1, send_up1),
        )[relative]
        first = 2 * quarters + 2 + 2 * relative
        return (
            pltpu.make_async_copy(grad_down.at[relative & 1], down_ref, sems.at[first]),
            pltpu.make_async_copy(grad_up.at[relative & 1], up_ref, sems.at[first + 1]),
        )

    @pl.when(step == 0)
    def start():
        for j in range(quarters):
            for copy in bring(j):
                copy.start()
        bring_cot.start()
        for s in range(seq_count):
            for r in range(seq_parts):
                context[
                    pl.ds(pl.multiple_of((r ^ mine) * wide, wide), wide),
                    s * local_rows : (s + 1) * local_rows,
                ] = pieces[s * seq_parts + r][...]
        live = live_rows(places, rows, mine, local_rows, 11)
        attended = dot_f32(context[...], w_out[...], TN) + vectors[0:1, :]
        total = jnp.where(live > 0, tokens[...].astype(f32), 0.0) + attended
        first_in[...] = total
        hat, _ = normal_parts(total)
        normed = hat * vectors[1:2, :] + vectors[2:3, :]
        first_norm[...] = normed
        low = normed.astype(bf16)
        first_low[...] = low
        tile = features // 4
        low_t = low.T
        for q in range(4):
            first_t[pl.ds(pl.multiple_of((q ^ inner) * tile, tile), tile), :] = low_t[
                q * tile : (q + 1) * tile
            ]
        lowered[...] = jnp.zeros_like(lowered)
        sums[...] = jnp.zeros_like(sums)

    @pl.when(step < quarters)
    def forward():
        for j in range(quarters):

            @pl.when(step == j)
            def arrive():
                for copy in bring(j):
                    copy.wait()

        lifted = dot_f32(first_low[...], w_up[step], NN) + b_up[step]
        cdf = 0.5 * (1.0 + lax.erf(lifted * 0.7071067811865476))
        density = jnp.exp(lifted * lifted * -0.5) * 0.3989422804014327
        gelu = (lifted * cdf).astype(bf16)
        active[step] = gelu
        slope[step] = (cdf + lifted * density).astype(bf16)
        lowered[...] += dot_f32(gelu, w_down[step], NN)

    @pl.when(step == quarters - 1)
    def turn():
        live = live_rows(places, rows, mine, local_rows, 11)
        hat, inverse = normal_parts(first_norm[...] + (lowered[...] + vectors[3:4, :]))
        gain = vectors[4:5, :]
        bring_cot.wait()
        out_s[...] = ((hat * gain + vectors[5:6, :]) * live).astype(bf16)
        keep_out.start()
        incoming = cot[...].astype(f32) * live
        back = normal_back(hat, inverse, gain, incoming)
        lowered[...] = back
        low = back.astype(bf16)
        d_lowered[...] = low
        sums[0:1, :] = column_sum(low.astype(f32))
        sums[1:2, :] = column_sum(incoming * hat)
        sums[2:3, :] = column_sum(incoming)

    @pl.when(step >= quarters)
    def backward():
        relative = 2 * quarters - 1 - step
        quarter = relative ^ (places[0] >> 1)
        low_bit = places[0] & 1
        slot = relative & 1
        half = width // 2
        tile = half // 4
        for k in range(2):

            @pl.when(relative == k)
            def free():
                for copy in leave(k + 2):
                    copy.wait()

        down = dot_f32(active[quarter], d_lowered[...], TN).astype(bf16)
        for j in range(2):
            for q in range(4):
                grad_down[
                    slot, j ^ low_bit, pl.ds(pl.multiple_of((q ^ inner) * tile, tile), tile), :
                ] = down[j * half + q * tile : j * half + (q + 1) * tile]
        d_active = dot_f32(d_lowered[...], w_down[quarter], NT)
        d_lifted = (d_active * slope[quarter].astype(f32)).astype(bf16)
        up = dot_f32(first_t[...], d_lifted, NN).astype(bf16)
        for j in range(2):
            grad_up[slot, j ^ low_bit] = up[:, j * half : (j + 1) * half]
        sums[pl.ds(6 + quarter, 1), :] = column_sum(d_lifted.astype(f32))
        lowered[...] += dot_f32(d_lifted, w_up[quarter], NT)
        for k in range(quarters):

            @pl.when(relative == k)
            def start_leaving():
                for copy in leave(k):
                    copy.start()

    @pl.when(step == 2 * quarters - 1)
    def finish():
        hat, inverse = normal_parts(first_in[...])
        incoming = lowered[...]
        back = normal_back(hat, inverse, vectors[1:2, :], incoming)
        d_first_in[...] = back
        low = back.astype(bf16)
        sums[3:4, :] = column_sum(low.astype(f32))
        sums[4:5, :] = column_sum(incoming * hat)
        sums[5:6, :] = column_sum(incoming)
        turned[...] = dot_f32(w_out[...], low, NT).astype(bf16)
        for r in range(seq_parts):
            own = turned[pl.ds(pl.multiple_of((r ^ mine) * wide, wide), wide), :]
            for s in range(seq_count):
                target, place = sent[3 * min(s, 1) + min(r, 2)], max(s - 1, 0)
                columns = own[:, s * local_rows : (s + 1) * local_rows]
                if r < 2:
                    target[place] = columns
                else:
                    target[r - 2, place] = columns
        product = dot_f32(context[...], low, NN).astype(bf16)
        block_rows, block_cols = grad_out.shape[2:]
        across = features // block_cols
        for j in range(seq_parts):
            for q in range(wide // block_rows * across):
                row, col = j * wide + q // across * block_rows, q % across * block_cols
                block = product[row : row + block_rows, col : col + block_cols]
                place, inner_place = j ^ mine, q ^ places[10]

                @pl.when(place < 2)
                def own():
                    grad_out[place, inner_place] = block

                @pl.when(place >= 2)
                def across_x():
                    send_out[place - 2, inner_place] = block

        keep_out.wait()
        for k in range(2):
            for copy in leave(k):
                copy.wait()


def whole_spec(shape):
    return pl.BlockSpec(
        shape, lambda p, places: (0,) * len(shape), pipeline_mode=pl.Buffered(buffer_count=1)
    )


def step_call(body, places, steps, ins, in_specs, outs, out_specs, scratch, flops, aliases={}):
    return pl.pallas_call(
        body,
        out_shape=outs,
        grid_spec=pltpu.PrefetchScalarGridSpec(
            num_scalar_prefetch=1,
            grid=(steps,),
            in_specs=in_specs,
            out_specs=out_specs,
            scratch_shapes=scratch,
        ),
        input_output_aliases=aliases,
        compiler_params=pltpu.CompilerParams(vmem_limit_bytes=VMEM_LIMIT),
        cost_estimate=pl.CostEstimate(
            flops=flops, transcendentals=0, bytes_accessed=1024 * 1024
        ),
    )(places, *ins)


def run_token_layer(places, pieces, tokens, cot, w_out, vectors, w_up, b_up, w_down, dims):
    seq_count, seq_parts = dims
    rows, features = tokens.shape
    hidden = w_up.shape[1]
    quarters = 4
    width = hidden // quarters
    half = width // 2
    out, bf16, f32 = jax.ShapeDtypeStruct, jnp.bfloat16, jnp.float32
    square, turned = (rows, features), (features, rows)
    piece = (features // seq_parts, rows // seq_count)
    sent = []
    for n in (1, seq_count - 1):
        sent += [(n, *piece), (n, *piece), (2, n, *piece)]
    out_blocks = (seq_parts // 2, 8, features // seq_parts // 2, features // 4)
    away = pl.BlockSpec(memory_space=pl.ANY)
    down, up = (2, half, features), (2, features, half)

    return step_call(
        functools.partial(token_layer, dims),
        places,
        2 * quarters,
        [*pieces, tokens, cot, w_out, vectors, b_up.reshape(quarters, 1, width), w_up, w_down],
        [whole_spec(p.shape) for p in pieces]
        + [whole_spec(square), away, whole_spec(w_out.shape), whole_spec(vectors.shape)]
        + [whole_spec((quarters, 1, width)), away, away],
        [
            out(square, bf16),
            out(down, bf16),
            out(up, bf16),
            out(down, bf16),
            out(up, bf16),
            out((4, half, features), bf16),
            out((4, features, half), bf16),
            out(square, f32),
            out((16, features), f32),
            out(out_blocks, bf16),
            out(out_blocks, bf16),
        ]
        + [out(p, bf16) for p in sent],
        [away] * 7
        + [whole_spec(square), whole_spec((16, features))]
        + [whole_spec(out_blocks)] * 2
        + [whole_spec(p) for p in sent],
        [
            pltpu.VMEM((quarters, features, width), bf16),
            pltpu.VMEM((quarters, width, features), bf16),
            pltpu.VMEM((quarters, rows, width), bf16),
            pltpu.VMEM((quarters, rows, width), bf16),
            pltpu.VMEM(turned, bf16),
            pltpu.VMEM(square, f32),
            pltpu.VMEM(square, f32),
            pltpu.VMEM(square, f32),
            pltpu.VMEM(square, bf16),
            pltpu.VMEM(turned, bf16),
            pltpu.VMEM(square, bf16),
            pltpu.VMEM(turned, bf16),
            pltpu.VMEM(square, bf16),
            pltpu.VMEM(square, bf16),
            pltpu.VMEM((2, *down), bf16),
            pltpu.VMEM((2, *up), bf16),
            pltpu.SemaphoreType.DMA((4 * quarters + 2,)),
        ],
        2 * rows * features * (6 * hidden + 3 * features),
    )


def place_rows(count, by_rows, places, *refs):
    pieces, out = refs[:count], refs[-1]
    tile = pieces[0].shape[-2]
    for k, piece in enumerate(pieces):

        @pl.when(pl.program_id(0) >> 1 == k)
        def copy():
            for q in range(4):
                h, x = q >> 1, q & 1
                block = piece[x * 2 + h] if by_rows else piece[x, 0, h]
                out[pl.ds(pl.multiple_of((q ^ places[8]) * tile, tile), tile), :] = block.astype(
                    jnp.float32
                )


def gather_hidden(places, pieces, core, bit, begun, shape, by_rows):
    _, rows, cols = pieces[0].shape
    if by_rows:
        size = (4, rows, cols)
    else:
        pieces = [piece.reshape(2, 2, 2, rows, cols) for piece in pieces]
        size = (2, 1, 2, rows, cols)

    def source(k):
        def index(p, places):
            turn = jnp.clip(p - 2 * k, 0, 1)
            return (turn, 0, 0) if by_rows else (0, turn, 0, 0, 0)

        return pl.BlockSpec(size, index)

    def index(p, places):
        turn = p & 1
        place = places[(core + (p >> 1)) * 4 + (bit * 2 + turn if by_rows else turn * 2 + bit)]
        return (place, 0) if by_rows else (0, place)

    begun = [] if begun is None else [begun]
    count = len(pieces)
    return step_call(
        functools.partial(place_rows, count, by_rows),
        places,
        2 * count,
        pieces + begun,
        [source(k) for k in range(count)] + [pl.BlockSpec(memory_space=pl.ANY)] * len(begun),
        jax.ShapeDtypeStruct(shape, jnp.float32),
        pl.BlockSpec((4 * rows, cols), index),
        [],
        1000,
        {count + 1: 0} if begun else {},
    )


def place_heads(late, places, *refs):
    pieces, (out, out_w, vectors) = refs[:2], refs[-3:]
    mine, inner = places[9], places[10]
    step = pl.program_id(0)
    wide = out_w.shape[0]
    rows, features = out.shape[0], out_w.shape[1]
    seq_parts = features // wide
    f32 = jnp.float32
    if late:
        out[...] = refs[2][...]
    for k, piece in enumerate(pieces):
        r = k + 2 * late
        block = piece[step ^ inner, :rows, : 3 * wide].astype(f32)
        for j in range(seq_parts):

            @pl.when((r ^ mine) == j)
            def copy():
                for section in range(3):
                    start = section * features + j * wide
                    out[:, start : start + wide] = block[:, section * wide : (section + 1) * wide]

        @pl.when(step == k)
        def copy_out():
            tile, width = wide // 2, features // 4
            for q in range(8):
                row, col = q // 4 * tile, q % 4 * width
                out_w[row : row + tile, col : col + width] = piece[q ^ inner, :rows, 3 * wide :].astype(
                    f32
                )
            vectors[k] = piece[inner, rows:, :].astype(f32)


def gather_heads(places, pieces, begun, shape):
    out, f32 = jax.ShapeDtypeStruct, jnp.float32
    features = shape[0]
    rows = features // 8
    wide = pieces[0].shape[2] // 4
    late = begun is not None
    extra = (2, pieces[0].shape[1] - rows, features)
    main = pl.BlockSpec((rows, shape[1]), lambda p, places: (p, 0))

    def own_rows(p, places):
        return ((jnp.minimum(p, 1) + 2 * late) ^ places[9], 0)

    return step_call(
        functools.partial(place_heads, int(late)),
        places,
        8,
        pieces + (begun[:2] if late else []),
        [whole_spec(p.shape) for p in pieces]
        + ([main, pl.BlockSpec(memory_space=pl.ANY)] if late else []),
        [out(shape, f32), out((features, features), f32), out(extra, f32)],
        [main, pl.BlockSpec((wide, features), own_rows), whole_spec(extra)],
        [],
        1000,
        {3: 0, 4: 1} if late else {},
    )


def per_device(
    tokens,
    cotangent,
    lengths,
    block_perm,
    w_qkv,
    b_query,
    b_value,
    w_out,
    b_out,
    ln1_gain,
    ln1_shift,
    w_up,
    b_up,
    w_down,
    b_down,
    ln2_gain,
    ln2_shift,
):
    seq_parts = lax.axis_size("seq")
    mine = lax.axis_index("seq")
    seq_count, local_rows, features = tokens.shape
    flat_rows = seq_count * local_rows
    hidden = w_up.shape[1]
    heads = HEADS // seq_parts
    wide = heads * HEAD_DIM
    dims = (seq_count, seq_parts)
    f32 = jnp.float32

    w_heads = jnp.concatenate(
        [
            lax.dynamic_slice_in_dim(w_qkv, k * features + mine * wide, wide, axis=1)
            for k in range(3)
        ],
        axis=1,
    )
    w_t = w_heads.T
    bias = jnp.concatenate(
        [
            lax.dynamic_slice_in_dim(b_query, mine * wide, wide),
            jnp.zeros((wide,), b_query.dtype),
            lax.dynamic_slice_in_dim(b_value, mine * wide, wide),
        ]
    ).astype(f32)[:, None]
    outer = own_number("cyl")
    places = jnp.concatenate(
        [
            jnp.arange(8, dtype=jnp.int32) ^ outer,
            jnp.stack([own_number("hx"), mine, own_number("ylh")]),
            lengths,
            block_perm.reshape(-1),
        ]
    )
    vectors = jnp.stack(
        [v.astype(f32) for v in (b_out, ln1_gain, ln1_shift, b_down, ln2_gain, ln2_shift, b_out, b_out)]
    )

    arrived, kept, crossed = [], [], []
    for s in range(seq_count):
        near = tokens[s]
        start = near
        if s > 0:
            after = [crossed[-1]] + arrived[(s - 2) * seq_parts : (s - 2) * seq_parts + 1] * (s > 1)
            start, _ = lax.optimization_barrier((near, after))
        across = exchange_bit(start, "x")
        crossed.append(across)
        if s == 0:
            across, w_t, bias, places = lax.optimization_barrier((across, w_t, bias, places))
        if s > 0:
            across, _ = lax.optimization_barrier((across, arrived[-seq_parts]))
        pieces = [near, exchange_bit(near, "c"), across, exchange_bit(across, "c")]
        contexts, saved = attention_forward(places, pieces, s, w_t, bias, heads)
        kept.append(saved)
        arrived += [contexts[0]] + [exchange(contexts[r], "seq", r) for r in range(1, seq_parts)]

    (
        out_rows,
        send_down1,
        send_up1,
        send_down0,
        send_up0,
        keep_down,
        keep_up,
        d_first_in,
        sums,
        grad_out,
        send_out,
        *d_contexts,
    ) = run_token_layer(
        places,
        arrived,
        tokens.reshape(flat_rows, features),
        cotangent.reshape(flat_rows, features),
        w_out,
        vectors,
        w_up,
        b_up.astype(f32).reshape(1, hidden),
        w_down,
        dims,
    )
    out_tokens = out_rows.reshape(seq_count, local_rows, features)

    def hand_on(own, near, came):
        return [own, exchange_bit(near, "c"), came, exchange_bit(came[1], "c")]

    first_came = exchange_bit(d_contexts[2], "x")
    came_down1, came_up1 = exchange_bit(send_down1, "c"), exchange_bit(send_up1, "c")
    send_up0, first_came = lax.optimization_barrier((send_up0, first_came))
    came_up0 = exchange_bit(send_up0, "c")
    second_pair, first_came = lax.optimization_barrier((d_contexts[5], first_came))
    second_came = exchange_bit(second_pair, "x")
    parts, near, far = [], [], []

    def attend(s, group, before, late=()):
        found, total = attention_backward(places, group, s, w_t, kept[s], before, heads, late)
        parts.append(found)
        return total

    def cross(s):
        held, sent = parts[s]
        came = exchange_bit(sent, "c")
        near.append(held[0].astype(f32) + came[0])
        far.append(sum_low(held[1], came[1]))

    sends = [
        sum_low(keep_down[3], came_down1[1]),
        sum_low(keep_up[3], came_up1[1]),
        send_out,
    ]
    sends, first_came = lax.optimization_barrier((sends, first_came))
    down_y1, up_l3, out_x = [exchange_bit(v, bit) for v, bit in zip(sends, "ylx")]
    total = attend(0, hand_on(d_contexts[0], d_contexts[1], first_came), ())
    (down_y1, up_l3, out_x, total, parts[0], second_came, near_pair, came_up0, send_down0) = (
        lax.optimization_barrier(
            (down_y1, up_l3, out_x, total, parts[0], second_came, d_contexts[3:5])
            + (came_up0, send_down0)
        )
    )
    came_down0 = exchange_bit(send_down0, "c")

    sends = [
        sum_low(keep_down[2], came_down1[0]),
        sum_low(keep_up[1], came_up0[1]),
        sum_low(grad_out[1], out_x[1]),
    ]
    (sends, total) = lax.optimization_barrier((sends, total))
    down_y0, up_l1, out_c = [exchange_bit(v, bit) for v, bit in zip(sends, "ylc")]
    cross(0)
    second_group = hand_on(*near_pair, second_came)
    for s in range(1, seq_count - 1):
        total = attend(s, second_group, total)
    out_own = sum_low(grad_out[0], out_x[0], out_c)
    (down_y0, up_l1, total, parts[1:], near, far, out_own) = lax.optimization_barrier(
        (down_y0, up_l1, total, parts[1:], near, far, out_own)
    )

    sends = [
        sum_low(keep_down[1], came_down0[1], down_y1),
        sum_low(keep_up[2], came_up1[0], up_l3),
    ]
    (sends, total) = lax.optimization_barrier((sends, total))
    down_l, up_y = [exchange_bit(v, bit) for v, bit in zip(sends, "ly")]
    far_came = [exchange_bit(far[0], "x")]
    for s in range(1, seq_count - 1):
        cross(s)
    total_w, _ = attend(seq_count - 1, second_group, total, (out_own, sums))

    (down_l, up_y, far, far_came, total_w, parts[-1]) = lax.optimization_barrier(
        (down_l, up_y, far, far_came, total_w, parts[-1])
    )
    down_own = sum_low(keep_down[0], came_down0[0], down_y0, down_l)
    down_own = down_own.reshape(4, hidden // 32, features)
    up_own = sum_low(keep_up[0], came_up0[0], up_l1, up_y)
    up_own = up_own.reshape(2, 2, features // 4, hidden // 8)
    keeps = [down_own[:2], up_own[:, 0], total_w[:4]]
    sends = [down_own[2:], up_own[:, 1], total_w[4:]]
    (keeps, sends) = lax.optimization_barrier((keeps, sends))
    got = [exchange_bit(v, bit) for v, bit in zip(sends, "hxy")]
    far_came += [exchange_bit(v, "x") for v in far[1:]]
    down_own, up_own, qkv_own = [k + g for k, g in zip(keeps, got)]
    qkv_own = qkv_own[:2] + exchange_bit(qkv_own[2:], "l")
    far = []
    cross(seq_count - 1)

    keeps = [down_own[:1], up_own[:1], qkv_own[:1]]
    sends = [down_own[1:], up_own[1:], qkv_own[1:]]
    (keeps, sends, far, far_came, near) = lax.optimization_barrier(
        (keeps, sends, far, far_came, near)
    )
    got = [exchange_bit(v, bit) for v, bit in zip(sends, "xhh")]
    far_came += [exchange_bit(v, "x") for v in far]
    shards = [add_extra(k + g) for k, g in zip(keeps, got)]

    own_pos = mine * local_rows + jnp.arange(local_rows, dtype=jnp.int32)
    live = (own_pos[None, :] < lengths[:, None]).astype(f32)
    d_inputs = jnp.stack([n + f for n, f in zip(near, far_came)])
    grad_tokens = (d_inputs + d_first_in.reshape(seq_count, local_rows, features)) * live[:, :, None]
    for bits in ("hhh", "xyl", "lxy"):
        if bits == "xyl":
            (shards, grad_tokens) = lax.optimization_barrier((shards, grad_tokens))
        else:
            shards = lax.optimization_barrier(shards)
        shards = [
            jnp.concatenate([shard, exchange_bit(shard, bit)]) for shard, bit in zip(shards, bits)
        ]
    shards = lax.optimization_barrier(shards)
    last = [exchange_bit(shard, bit) for shard, bit in zip(shards, "ylx")]
    near_c = [exchange_bit(shard, "c") for shard in shards]
    shapes = ((hidden, features), (features, hidden))
    early = [
        gather_hidden(places, [shards[i], near_c[i]], 0, 0, None, shapes[i], i == 0) for i in (0, 1)
    ]
    qkv_part, out_part, first_vectors = gather_heads(
        places, [shards[2], near_c[2]], None, (features, 3 * features)
    )
    (last, early) = lax.optimization_barrier((last, early))
    far_c = [exchange_bit(shard, "c") for shard in last]
    early = [gather_hidden(places, [last[i]], 0, 1, early[i], shapes[i], i == 0) for i in (0, 1)]
    (far_c, early, qkv_part) = lax.optimization_barrier((far_c, early, qkv_part))
    full_down, full_up = [
        gather_hidden(places, [far_c[i]], 1, 1, early[i], shapes[i], i == 0) for i in (0, 1)
    ]
    full_qkv, full_out, last_vectors = gather_heads(
        places, [last[2], far_c[2]], [qkv_part, out_part], (features, 3 * features)
    )
    held = jnp.concatenate([first_vectors, last_vectors])
    rows = [lax.dynamic_index_in_dim(held, j ^ mine, keepdims=False) for j in range(seq_parts)]
    vector_rows = rows[0]
    for row in rows[1:]:
        vector_rows = vector_rows + row
    head_rows = jnp.stack([row[10] for row in rows])
    (
        full_b_down,
        full_gain_two,
        full_shift_two,
        full_b_out,
        full_gain_one,
        full_shift_one,
    ) = [vector_rows[i] for i in range(6)]
    full_b_up = vector_rows[6 : 6 + hidden // features].reshape(hidden)
    full_b_query = head_rows[:seq_parts, :wide].reshape(features)
    full_b_value = head_rows[:seq_parts, 2 * wide : 3 * wide].reshape(features)

    return (
        out_tokens,
        grad_tokens,
        full_qkv,
        full_b_query,
        full_b_value,
        full_out,
        full_b_out,
        full_gain_one,
        full_shift_one,
        full_up,
        full_b_up,
        full_down,
        full_b_down,
        full_gain_two,
        full_shift_two,
    )


def solution(mesh):
    in_specs = (
        P("dp", "seq", None),
        P("dp", "seq", None),
        P("dp"),
        P("dp", None),
        P(),
        P(),
        P(),
        P(),
        P(),
        P(),
        P(),
        P(),
        P(),
        P(),
        P(),
        P(),
        P(),
    )
    out_specs = (
        P("dp", "seq", None),
        P("dp", "seq", None),
        P(),
        P(),
        P(),
        P(),
        P(),
        P(),
        P(),
        P(),
        P(),
        P(),
        P(),
        P(),
        P(),
    )
    return jax.shard_map(
        per_device, mesh=mesh, in_specs=in_specs, out_specs=out_specs, check_vma=False
    )
```

```python
import functools
import jax
import jax.numpy as jnp
from jax import lax
from jax.experimental import pallas as pl
from jax.experimental.pallas import tpu as pltpu
from jax.sharding import PartitionSpec as P

HEAD_DIM = 64
SOFT = HEAD_DIM ** -0.5 * 1.4426950408889634
NN = (((1,), (0,)), ((), ()))
NT = (((1,), (1,)), ((), ()))
TN = (((0,), (0,)), ((), ()))
VMEM_LIMIT = 60 * 1024 * 1024
HEADS = 12
EPSILON = 1e-06
BITS = {"c": ("seq", 0), "x": ("seq", 1), "y": ("dp", 0), "l": ("dp", 1), "h": ("dp", 2)}


def own_number(order):
    number = jnp.int32(0)
    for letter in order:
        axis, shift = BITS[letter]
        number = number * 2 + ((lax.axis_index(axis) >> shift) & 1)
    return number


def exchange(array_in, axis, flip):
    return lax.ppermute(array_in, axis, [(i, i ^ flip) for i in range(lax.axis_size(axis))])


def exchange_bit(array_in, letter):
    axis, shift = BITS[letter]
    return exchange(array_in, axis, 1 << shift)


def extra_flips(axis, used):
    return [1 << shift for shift in range(used, lax.axis_size(axis).bit_length() - 1)]


def add_extra(array_in):
    for flip in extra_flips("dp", 3):
        array_in = array_in + exchange(array_in, "dp", flip)
    return array_in


def sum_low(*parts):
    total = parts[0].astype(jnp.float32)
    for part in parts[1:]:
        total = total + part.astype(jnp.float32)
    return total.astype(jnp.bfloat16)


def dot_f32(left, right, dims):
    return lax.dot_general(left, right, dims, preferred_element_type=jnp.float32)


def sequence_scalars(places, index):
    seq_count = (places.shape[0] - 11) // 3
    return places[11 + index] >> 1, places[9], 11 + seq_count + 2 * index


def shift_matrix(half, block, whole):
    row = lax.broadcasted_iota(jnp.int32, (block, whole), 0)
    col = lax.broadcasted_iota(jnp.int32, (block, whole), 1)
    return jnp.where((col == row + half) & (row < half), 1.0, 0.0).astype(jnp.bfloat16)


def mask_tiles(half, block):
    row = lax.broadcasted_iota(jnp.int32, (16, block), 0)
    col = lax.broadcasted_iota(jnp.int32, (16, block), 1)
    key_tile = jnp.where((row == 0) & (col >= half), -1e30, 0.0).astype(jnp.bfloat16)
    query_tile = jnp.where(row == 0, 1.0, 0.0).astype(jnp.bfloat16)
    return key_tile, query_tile


def attend_forward(
    heads, index, places, x0, x1, x2, x3, w_t, bias, c0, c1, c2, c3,
    x_out, qkv_out, ctx_blk, lse, tok, c_tok, x_seq, qkv, sems,
):
    half, mine, perm = sequence_scalars(places, index)
    whole = x_seq.shape[0]
    quarter = whole // 4
    block = whole // 2
    wide = heads * HEAD_DIM
    for r, piece in enumerate((x0, x1, x2, x3)):
        x_seq[pl.ds(pl.multiple_of((r ^ mine) * quarter, quarter), quarter), :] = piece[...]
    keep_x = pltpu.make_async_copy(x_seq, x_out, sems.at[0])
    keep_x.start()
    lane = lax.broadcasted_iota(jnp.int32, (1, block), 1)
    tok[...] = (dot_f32(w_t[...], x_seq[...], NT) + bias[...]).astype(jnp.bfloat16)
    shift = shift_matrix(half, block, whole)
    qkv[0] = jnp.where(lane < half, tok[:, :block], jnp.zeros((), jnp.bfloat16))
    qkv[1] = dot_f32(tok[...], shift, NT).astype(jnp.bfloat16)
    keep_qkv = pltpu.make_async_copy(qkv, qkv_out, sems.at[1])
    keep_qkv.start()
    key_tile, query_tile = mask_tiles(half, block)

    def one_block(b, carry):
        target = places[perm + b]
        for h in range(heads):
            rows = slice(h * HEAD_DIM, (h + 1) * HEAD_DIM)
            q_t = jnp.concatenate([qkv[b, rows, :], query_tile])
            k_t = jnp.concatenate(
                [qkv[target, wide + h * HEAD_DIM : wide + (h + 1) * HEAD_DIM, :], key_tile]
            )
            v_t = qkv[target, 2 * wide + h * HEAD_DIM : 2 * wide + (h + 1) * HEAD_DIM, :]
            scores = dot_f32(k_t, q_t, TN) * SOFT
            top = jnp.max(scores, axis=0, keepdims=True)
            expo = jnp.exp2(scores - top)
            total = jnp.sum(expo, axis=0, keepdims=True)
            context = dot_f32(v_t, expo.astype(jnp.bfloat16), NN) / total
            ctx_blk[b, rows, :] = context
            lse[b, h : h + 1, :] = top + jnp.log2(total)
        return carry

    lax.fori_loop(0, 2, one_block, 0)
    early = jnp.where(lane < half, ctx_blk[0], 0.0)
    late = dot_f32(ctx_blk[1].astype(jnp.bfloat16), shift, NN)
    for j in range(4):
        part = late[:, j * quarter : (j + 1) * quarter]
        if j < 2:
            part = part + early[:, j * quarter : (j + 1) * quarter]
        c_tok[j] = part.astype(jnp.bfloat16)
    for r, piece in enumerate((c0, c1, c2, c3)):
        piece[...] = c_tok[r ^ mine]
    keep_x.wait()
    keep_qkv.wait()


def attend_backward(
    heads, index, places, g0, g1, g2, g3, w_t, x_in, qkv, ctx_blk, lse, *refs
):
    first, last = index == 0, len(refs) > 14
    acc_in, acc_b = (None, None) if first else refs[:2]
    (dx_keep, dx_send, grad_w, grad_w2, g_tok, g_blk, d_qkv, tok, x_seq, acc, dx_s, sems) = refs[-12:]
    bring_x = pltpu.make_async_copy(x_in, x_seq, sems.at[0])
    bring_x.start()
    if not first:
        bring_acc = pltpu.make_async_copy(acc_in, acc, sems.at[1])
        bring_acc.start()
    half, mine, perm = sequence_scalars(places, index)
    index = max(index - 1, 0)
    quarter = g0.shape[2]
    block = 2 * quarter
    whole = 4 * quarter
    wide = heads * HEAD_DIM
    for r, piece in enumerate((g0[index], g1[index], g2[0, index], g3[index])):
        g_tok[r ^ mine] = piece
    shift = shift_matrix(half, block, whole)
    lane = lax.broadcasted_iota(jnp.int32, (1, block), 1)
    g_all = jnp.concatenate([g_tok[j] for j in range(4)], axis=1)
    g_blk[0] = jnp.where(lane < half, g_all[:, :block], jnp.zeros((), jnp.bfloat16))
    g_blk[1] = dot_f32(g_all, shift, NT).astype(jnp.bfloat16)
    key_tile, query_tile = mask_tiles(half, block)

    def one_block(b, carry):
        target = places[perm + b]
        for h in range(heads):
            rows = slice(h * HEAD_DIM, (h + 1) * HEAD_DIM)
            k_rows = slice(wide + h * HEAD_DIM, wide + (h + 1) * HEAD_DIM)
            v_rows = slice(2 * wide + h * HEAD_DIM, 2 * wide + (h + 1) * HEAD_DIM)
            q_t = qkv[b, rows, :]
            k_t = qkv[target, k_rows, :]
            v_t = qkv[target, v_rows, :]
            g_t = g_blk[b, rows, :]
            scores = dot_f32(
                jnp.concatenate([k_t, key_tile]), jnp.concatenate([q_t, query_tile]), TN
            )
            probs = jnp.exp2(scores * SOFT - lse[b, h : h + 1, :])
            d_probs = dot_f32(v_t, g_t, TN)
            delta = jnp.sum(ctx_blk[b, rows, :] * g_t.astype(jnp.float32), axis=0, keepdims=True)
            d_scores = (probs * (d_probs - delta)).astype(jnp.bfloat16)
            scaling = HEAD_DIM ** -0.5
            d_qkv[b, rows, :] = (dot_f32(k_t, d_scores, NN) * scaling).astype(jnp.bfloat16)
            d_qkv[target, k_rows, :] = (dot_f32(q_t, d_scores, NT) * scaling).astype(jnp.bfloat16)
            d_qkv[target, v_rows, :] = dot_f32(g_t, probs.astype(jnp.bfloat16), NT).astype(
                jnp.bfloat16
            )
        return carry

    lax.fori_loop(0, 2, one_block, 0)
    late = dot_f32(d_qkv[1], shift, NN)
    front = jnp.where(lane < half, d_qkv[0].astype(jnp.float32), 0.0)
    tok[:, block:] = late[:, block:].astype(jnp.bfloat16)
    tok[:, :block] = (late[:, :block] + front).astype(jnp.bfloat16)
    sent = []
    for r in range(4):
        piece = (dx_send if r & 1 else dx_keep).at[r >> 1]
        columns = tok[:, pl.ds(pl.multiple_of((r ^ mine) * quarter, quarter), quarter)]
        dx_s[r] = dot_f32(columns, w_t[...], TN).astype(jnp.bfloat16)
        sent.append(pltpu.make_async_copy(dx_s.at[r], piece, sems.at[2 + r]))
        sent[-1].start()
    bring_x.wait()
    total = dot_f32(tok[...], x_seq[...], NN)
    ones = jnp.ones((8, whole), jnp.bfloat16)
    sums = dot_f32(ones, tok[...], NT)
    if not first:
        bring_acc.wait()
        total, sums = total + acc[...], sums + acc_b[...]
    if last:
        out_own, vectors = refs[2:4]
        inner = places[10]
        turned = total.T.astype(jnp.bfloat16)
        tile = out_own.shape[1]
        extra = grad_w.shape[1] - tile
        for half_w in (grad_w, grad_w2):
            half_w[:, tile:, :] = jnp.zeros((8, extra, 2 * wide), jnp.bfloat16)
        for q in range(8):
            rows = slice(q * tile, (q + 1) * tile)
            grad_w[q ^ inner, :tile, :] = turned[rows, : 2 * wide]
            grad_w2[q ^ inner, :tile, :wide] = turned[rows, 2 * wide :]
        grad_w2[:, :tile, wide:] = out_own[...]
        row = lax.broadcasted_iota(jnp.int32, (extra, 1), 0)
        own_row = jnp.concatenate([sums[0:1, :], jnp.zeros((1, wide), jnp.float32)], axis=1)
        tile_rows = jnp.where(row == 10, own_row, vectors[...]).astype(jnp.bfloat16)
        grad_w[inner, tile:, :] = tile_rows[:, : 2 * wide]
        grad_w2[inner, tile:, :] = tile_rows[:, 2 * wide :]
    else:
        grad_w[...] = total
        grad_w2[...] = sums
    for copy in sent:
        copy.wait()


def kernel_call(body, scalars, arrays, outs, scratch, left_in=(), left_out=()):
    def spec(away):
        return pl.BlockSpec(memory_space=pl.ANY if away else pltpu.VMEM)

    return pl.pallas_call(
        body,
        out_shape=outs,
        in_specs=[pl.BlockSpec(memory_space=pltpu.SMEM)]
        + [spec(i in left_in) for i in range(len(arrays))],
        out_specs=[spec(i in left_out) for i in range(len(outs))],
        scratch_shapes=scratch,
        compiler_params=pltpu.CompilerParams(vmem_limit_bytes=VMEM_LIMIT),
        cost_estimate=pl.CostEstimate(
            flops=10**8, transcendentals=0, bytes_accessed=1024 * 1024
        ),
    )(scalars, *arrays)


def attention_forward(places, pieces, index, w_t, bias, heads):
    quarter, features = pieces[0].shape
    whole, block, wide = 4 * quarter, 2 * quarter, heads * HEAD_DIM
    out = jax.ShapeDtypeStruct
    outs = [out((wide, quarter), jnp.bfloat16)] * 4 + [
        out((whole, features), jnp.bfloat16),
        out((2, 3 * wide, block), jnp.bfloat16),
        out((2, wide, block), jnp.float32),
        out((2, 8, block), jnp.float32),
    ]
    scratch = [
        pltpu.VMEM((3 * wide, whole), jnp.bfloat16),
        pltpu.VMEM((4, wide, quarter), jnp.bfloat16),
        pltpu.VMEM((whole, features), jnp.bfloat16),
        pltpu.VMEM((2, 3 * wide, block), jnp.bfloat16),
        pltpu.SemaphoreType.DMA((2,)),
    ]
    found = kernel_call(
        functools.partial(attend_forward, heads, index),
        places,
        [*pieces, w_t, bias],
        outs,
        scratch,
        left_out=(4, 5),
    )
    return found[:4], found[4:]


def attention_backward(places, pieces, index, w_t, kept, before, heads, late=()):
    _, wide, quarter = pieces[0].shape
    features = w_t.shape[1]
    block = 2 * quarter
    out = jax.ShapeDtypeStruct
    if late:
        grads = [out((8, features // 8 + 16, 2 * wide), jnp.bfloat16)] * 2
    else:
        grads = [out((3 * wide, features), jnp.float32), out((8, 3 * wide), jnp.float32)]
    outs = [out((2, quarter, features), jnp.bfloat16)] * 2 + grads
    scratch = [
        pltpu.VMEM((4, wide, quarter), jnp.bfloat16),
        pltpu.VMEM((2, wide, block), jnp.bfloat16),
        pltpu.VMEM((2, 3 * wide, block), jnp.bfloat16),
        pltpu.VMEM((3 * wide, 4 * quarter), jnp.bfloat16),
        pltpu.VMEM((4 * quarter, features), jnp.bfloat16),
        pltpu.VMEM((3 * wide, features), jnp.float32),
        pltpu.VMEM((4, quarter, features), jnp.bfloat16),
        pltpu.SemaphoreType.DMA((6,)),
    ]
    found = kernel_call(
        functools.partial(attend_backward, heads, index),
        places,
        [*pieces, w_t, *kept, *before, *late],
        outs,
        scratch,
        left_in=(5, 9) if before else (5,),
        left_out=(0, 1),
    )
    return found[:2], found[2:]

def live_rows(places, rows, mine, local_rows, offset):
    row = lax.broadcasted_iota(jnp.int32, (rows, 1), 0)
    length = jnp.zeros((rows, 1), jnp.int32)
    for s in range(rows // local_rows):
        length = jnp.where(row >= s * local_rows, places[offset + s], length)
    position = mine * local_rows + lax.rem(row, local_rows)
    return jnp.where(position < length, 1.0, 0.0)


def normal_parts(array_in):
    centered = array_in - jnp.mean(array_in, axis=1, keepdims=True)
    spread = jnp.mean(centered * centered, axis=1, keepdims=True)
    inverse = lax.rsqrt(spread + EPSILON)
    return centered * inverse, inverse


def normal_back(hat, inverse, gain, d_out):
    scaled = d_out * gain
    mean_scaled = jnp.mean(scaled, axis=1, keepdims=True)
    mean_product = jnp.mean(scaled * hat, axis=1, keepdims=True)
    return inverse * (scaled - mean_scaled - hat * mean_product)


def column_sum(array_in):
    return jnp.sum(array_in, axis=0, keepdims=True)


def token_layer(shape, places, *refs):
    seq_count, seq_parts = shape
    count = seq_count * seq_parts
    pieces, refs = refs[:count], refs[count:]
    tokens, cot_in, w_out, vectors, b_up, w_up_in, w_down_in = refs[:7]
    out, send_down1, send_up1, send_down0, send_up0, keep_down, keep_up = refs[7:14]
    d_first_in, sums, grad_out, send_out = refs[14:18]
    sent = refs[18:24]
    (
        w_up, w_down, active, slope, context, first_in, first_norm, lowered,
        first_low, first_t, d_lowered, turned, out_s, cot, grad_down, grad_up, sems,
    ) = refs[24:]
    rows, features = tokens.shape
    local_rows = rows // seq_count
    wide = features // seq_parts
    mine, inner = places[9], places[8]
    step = pl.program_id(0)
    quarters = w_up.shape[0]
    width = w_up.shape[2]
    f32, bf16 = jnp.float32, jnp.bfloat16

    def bring(j):
        return (
            pltpu.make_async_copy(
                w_up_in.at[:, pl.ds(j * width, width)], w_up.at[j], sems.at[j]
            ),
            pltpu.make_async_copy(
                w_down_in.at[pl.ds(j * width, width), :], w_down.at[j], sems.at[quarters + j]
            ),
        )

    keep_out = pltpu.make_async_copy(out_s, out, sems.at[2 * quarters])
    bring_cot = pltpu.make_async_copy(cot_in, cot, sems.at[2 * quarters + 1])

    def leave(relative):
        down_ref, up_ref = (
            (keep_down.at[pl.ds(0, 2)], keep_up.at[pl.ds(0, 2)]),
            (keep_down.at[pl.ds(2, 2)], keep_up.at[pl.ds(2, 2)]),
            (send_down0, send_up0),
            (send_down1, send_up1),
        )[relative]
        first = 2 * quarters + 2 + 2 * relative
        return (
            pltpu.make_async_copy(grad_down.at[relative & 1], down_ref, sems.at[first]),
            pltpu.make_async_copy(grad_up.at[relative & 1], up_ref, sems.at[first + 1]),
        )

    @pl.when(step == 0)
    def start():
        for j in range(quarters):
            for copy in bring(j):
                copy.start()
        bring_cot.start()
        for s in range(seq_count):
            for r in range(seq_parts):
                context[
                    pl.ds(pl.multiple_of((r ^ mine) * wide, wide), wide),
                    s * local_rows : (s + 1) * local_rows,
                ] = pieces[s * seq_parts + r][...]
        live = live_rows(places, rows, mine, local_rows, 11)
        attended = dot_f32(context[...], w_out[...], TN) + vectors[0:1, :]
        total = jnp.where(live > 0, tokens[...].astype(f32), 0.0) + attended
        first_in[...] = total
        hat, _ = normal_parts(total)
        normed = hat * vectors[1:2, :] + vectors[2:3, :]
        first_norm[...] = normed
        low = normed.astype(bf16)
        first_low[...] = low
        tile = features // 4
        low_t = low.T
        for q in range(4):
            first_t[pl.ds(pl.multiple_of((q ^ inner) * tile, tile), tile), :] = low_t[
                q * tile : (q + 1) * tile
            ]
        lowered[...] = jnp.zeros_like(lowered)
        sums[...] = jnp.zeros_like(sums)

    @pl.when(step < quarters)
    def forward():
        for j in range(quarters):

            @pl.when(step == j)
            def arrive():
                for copy in bring(j):
                    copy.wait()

        lifted = dot_f32(first_low[...], w_up[step], NN) + b_up[step]
        cdf = 0.5 * (1.0 + lax.erf(lifted * 0.7071067811865476))
        density = jnp.exp(lifted * lifted * -0.5) * 0.3989422804014327
        gelu = (lifted * cdf).astype(bf16)
        active[step] = gelu
        slope[step] = (cdf + lifted * density).astype(bf16)
        lowered[...] += dot_f32(gelu, w_down[step], NN)

    @pl.when(step == quarters - 1)
    def turn():
        live = live_rows(places, rows, mine, local_rows, 11)
        hat, inverse = normal_parts(first_norm[...] + (lowered[...] + vectors[3:4, :]))
        gain = vectors[4:5, :]
        bring_cot.wait()
        out_s[...] = ((hat * gain + vectors[5:6, :]) * live).astype(bf16)
        keep_out.start()
        incoming = cot[...].astype(f32) * live
        back = normal_back(hat, inverse, gain, incoming)
        lowered[...] = back
        low = back.astype(bf16)
        d_lowered[...] = low
        sums[0:1, :] = column_sum(low.astype(f32))
        sums[1:2, :] = column_sum(incoming * hat)
        sums[2:3, :] = column_sum(incoming)

    @pl.when(step >= quarters)
    def backward():
        relative = 2 * quarters - 1 - step
        quarter = relative ^ (places[0] >> 1)
        low_bit = places[0] & 1
        slot = relative & 1
        half = width // 2
        tile = half // 4
        for k in range(2):

            @pl.when(relative == k)
            def free():
                for copy in leave(k + 2):
                    copy.wait()

        down = dot_f32(active[quarter], d_lowered[...], TN).astype(bf16)
        for j in range(2):
            for q in range(4):
                grad_down[
                    slot, j ^ low_bit, pl.ds(pl.multiple_of((q ^ inner) * tile, tile), tile), :
                ] = down[j * half + q * tile : j * half + (q + 1) * tile]
        d_active = dot_f32(d_lowered[...], w_down[quarter], NT)
        d_lifted = (d_active * slope[quarter].astype(f32)).astype(bf16)
        up = dot_f32(first_t[...], d_lifted, NN).astype(bf16)
        for j in range(2):
            grad_up[slot, j ^ low_bit] = up[:, j * half : (j + 1) * half]
        sums[pl.ds(6 + quarter, 1), :] = column_sum(d_lifted.astype(f32))
        lowered[...] += dot_f32(d_lifted, w_up[quarter], NT)
        for k in range(quarters):

            @pl.when(relative == k)
            def start_leaving():
                for copy in leave(k):
                    copy.start()

    @pl.when(step == 2 * quarters - 1)
    def finish():
        hat, inverse = normal_parts(first_in[...])
        incoming = lowered[...]
        back = normal_back(hat, inverse, vectors[1:2, :], incoming)
        d_first_in[...] = back
        low = back.astype(bf16)
        sums[3:4, :] = column_sum(low.astype(f32))
        sums[4:5, :] = column_sum(incoming * hat)
        sums[5:6, :] = column_sum(incoming)
        turned[...] = dot_f32(w_out[...], low, NT).astype(bf16)
        for r in range(seq_parts):
            own = turned[pl.ds(pl.multiple_of((r ^ mine) * wide, wide), wide), :]
            for s in range(seq_count):
                target, place = sent[3 * min(s, 1) + min(r, 2)], max(s - 1, 0)
                columns = own[:, s * local_rows : (s + 1) * local_rows]
                if r < 2:
                    target[place] = columns
                else:
                    target[r - 2, place] = columns
        product = dot_f32(context[...], low, NN).astype(bf16)
        block_rows, block_cols = grad_out.shape[2:]
        across = features // block_cols
        for j in range(seq_parts):
            for q in range(wide // block_rows * across):
                row, col = j * wide + q // across * block_rows, q % across * block_cols
                block = product[row : row + block_rows, col : col + block_cols]
                place, inner_place = j ^ mine, q ^ places[10]

                @pl.when(place < 2)
                def own():
                    grad_out[place, inner_place] = block

                @pl.when(place >= 2)
                def across_x():
                    send_out[place - 2, inner_place] = block

        keep_out.wait()
        for k in range(2):
            for copy in leave(k):
                copy.wait()


def whole_spec(shape):
    return pl.BlockSpec(
        shape, lambda p, places: (0,) * len(shape), pipeline_mode=pl.Buffered(buffer_count=1)
    )


def step_call(body, places, steps, ins, in_specs, outs, out_specs, scratch, flops, aliases={}):
    return pl.pallas_call(
        body,
        out_shape=outs,
        grid_spec=pltpu.PrefetchScalarGridSpec(
            num_scalar_prefetch=1,
            grid=(steps,),
            in_specs=in_specs,
            out_specs=out_specs,
            scratch_shapes=scratch,
        ),
        input_output_aliases=aliases,
        compiler_params=pltpu.CompilerParams(vmem_limit_bytes=VMEM_LIMIT),
        cost_estimate=pl.CostEstimate(
            flops=flops, transcendentals=0, bytes_accessed=1024 * 1024
        ),
    )(places, *ins)


def run_token_layer(places, pieces, tokens, cot, w_out, vectors, w_up, b_up, w_down, dims):
    seq_count, seq_parts = dims
    rows, features = tokens.shape
    hidden = w_up.shape[1]
    quarters = 4
    width = hidden // quarters
    half = width // 2
    out, bf16, f32 = jax.ShapeDtypeStruct, jnp.bfloat16, jnp.float32
    square, turned = (rows, features), (features, rows)
    piece = (features // seq_parts, rows // seq_count)
    sent = []
    for n in (1, seq_count - 1):
        sent += [(n, *piece), (n, *piece), (2, n, *piece)]
    out_blocks = (seq_parts // 2, 8, features // seq_parts // 2, features // 4)
    away = pl.BlockSpec(memory_space=pl.ANY)
    down, up = (2, half, features), (2, features, half)

    return step_call(
        functools.partial(token_layer, dims),
        places,
        2 * quarters,
        [*pieces, tokens, cot, w_out, vectors, b_up.reshape(quarters, 1, width), w_up, w_down],
        [whole_spec(p.shape) for p in pieces]
        + [whole_spec(square), away, whole_spec(w_out.shape), whole_spec(vectors.shape)]
        + [whole_spec((quarters, 1, width)), away, away],
        [
            out(square, bf16),
            out(down, bf16),
            out(up, bf16),
            out(down, bf16),
            out(up, bf16),
            out((4, half, features), bf16),
            out((4, features, half), bf16),
            out(square, f32),
            out((16, features), f32),
            out(out_blocks, bf16),
            out(out_blocks, bf16),
        ]
        + [out(p, bf16) for p in sent],
        [away] * 7
        + [whole_spec(square), whole_spec((16, features))]
        + [whole_spec(out_blocks)] * 2
        + [whole_spec(p) for p in sent],
        [
            pltpu.VMEM((quarters, features, width), bf16),
            pltpu.VMEM((quarters, width, features), bf16),
            pltpu.VMEM((quarters, rows, width), bf16),
            pltpu.VMEM((quarters, rows, width), bf16),
            pltpu.VMEM(turned, bf16),
            pltpu.VMEM(square, f32),
            pltpu.VMEM(square, f32),
            pltpu.VMEM(square, f32),
            pltpu.VMEM(square, bf16),
            pltpu.VMEM(turned, bf16),
            pltpu.VMEM(square, bf16),
            pltpu.VMEM(turned, bf16),
            pltpu.VMEM(square, bf16),
            pltpu.VMEM(square, bf16),
            pltpu.VMEM((2, *down), bf16),
            pltpu.VMEM((2, *up), bf16),
            pltpu.SemaphoreType.DMA((4 * quarters + 2,)),
        ],
        2 * rows * features * (6 * hidden + 3 * features),
    )


def place_tile(count, places, *refs):
    out = refs[-1]
    for k in range(count):

        @pl.when(pl.program_id(0) >> 3 == k)
        def copy():
            out[...] = refs[k][0].astype(jnp.float32)


def gather_down(places, pieces, x, begun, shape):
    _, rows, cols = pieces[0].shape
    count = len(pieces)

    def source(k):
        return pl.BlockSpec(
            (1, rows, cols), lambda p, places: (jnp.clip(p - 8 * k, 0, 7), 0, 0)
        )

    def index(p, places):
        core, l, y, h = p >> 3, (p >> 2) & 1, (p >> 1) & 1, p & 1
        return (places[core * 4 + y * 2 + l] * 4 + ((h * 2 + x) ^ places[8]), 0)

    return step_call(
        functools.partial(place_tile, count),
        places,
        8 * count,
        pieces + begun,
        [source(k) for k in range(count)] + [pl.BlockSpec(memory_space=pl.ANY)] * len(begun),
        jax.ShapeDtypeStruct(shape, jnp.float32),
        pl.BlockSpec((rows, cols), index),
        [],
        1000,
        {count + 1: 0} if begun else {},
    )


def place_rows(count, places, *refs):
    out = refs[-1]
    tile = refs[0].shape[1]
    for k in range(count):

        @pl.when(pl.program_id(0) >> 1 == k)
        def copy():
            for q in range(4):
                h, x = q >> 1, q & 1
                out[pl.ds(pl.multiple_of((q ^ places[8]) * tile, tile), tile), :] = refs[k][
                    x * 2 + h
                ].astype(jnp.float32)


def gather_up(places, pieces, y, begun, shape):
    _, rows, cols = pieces[0].shape
    count = len(pieces)

    def source(k):
        return pl.BlockSpec(
            (4, rows, cols), lambda p, places: (jnp.clip(p - 2 * k, 0, 1), 0, 0)
        )

    return step_call(
        functools.partial(place_rows, count),
        places,
        2 * count,
        pieces + begun,
        [source(k) for k in range(count)] + [pl.BlockSpec(memory_space=pl.ANY)] * len(begun),
        jax.ShapeDtypeStruct(shape, jnp.float32),
        pl.BlockSpec(
            (4 * rows, cols), lambda p, places: (0, places[(p >> 1) * 4 + y * 2 + (p & 1)])
        ),
        [],
        1000,
        {count + 1: 0} if begun else {},
    )


def place_heads(places, *refs):
    pieces = refs[:-4]
    out, out_w, vector_rows, head_rows = refs[-4:]
    mine, inner = places[9], places[10]
    seq_parts = len(pieces)
    step = pl.program_id(0)
    wide = out_w.shape[0] // seq_parts
    rows, features = out.shape[0], out_w.shape[1]
    f32 = jnp.float32
    for m in range(seq_parts):

        @pl.when(mine == m)
        def copy():
            blocks = [pieces[j ^ m][step ^ inner, :rows, : 3 * wide] for j in range(seq_parts)]
            for section in range(3):
                columns = slice(section * wide, (section + 1) * wide)
                joined = jnp.concatenate([block[:, columns] for block in blocks], axis=1)
                out[:, section * features : (section + 1) * features] = joined.astype(f32)

        @pl.when((mine == m) & (step == 0))
        def copy_vectors():
            held = [pieces[j ^ m][inner, rows:, :].astype(f32) for j in range(seq_parts)]
            total = held[0]
            for other in held[1:]:
                total = total + other
            vector_rows[...] = total
            for j in range(seq_parts):
                head_rows[j : j + 1, :] = held[j][10:11, :]

    for r, piece in enumerate(pieces):

        @pl.when(step == r)
        def copy_out():
            for i in range(2):
                joined = jnp.concatenate(
                    [piece[(4 * i + q) ^ inner, :rows, 3 * wide :] for q in range(4)], axis=1
                )
                first = pl.multiple_of((r ^ mine) * wide + i * rows, rows)
                out_w[pl.ds(first, rows), :] = joined.astype(f32)


def gather_heads(places, pieces, shape):
    out, f32 = jax.ShapeDtypeStruct, jnp.float32
    features = shape[0]
    rows = features // 8
    square = (features, features)
    extra = (pieces[0].shape[1] - rows, features)
    return step_call(
        place_heads,
        places,
        8,
        pieces,
        [whole_spec(p.shape) for p in pieces],
        [out(shape, f32), out(square, f32), out(extra, f32), out((8, features), f32)],
        [pl.BlockSpec((rows, shape[1]), lambda p, places: (p, 0))]
        + [whole_spec(square), whole_spec(extra), whole_spec((8, features))],
        [],
        1000,
    )


def per_device(
    tokens,
    cotangent,
    lengths,
    block_perm,
    w_qkv,
    b_query,
    b_value,
    w_out,
    b_out,
    ln1_gain,
    ln1_shift,
    w_up,
    b_up,
    w_down,
    b_down,
    ln2_gain,
    ln2_shift,
):
    seq_parts = lax.axis_size("seq")
    mine = lax.axis_index("seq")
    seq_count, local_rows, features = tokens.shape
    flat_rows = seq_count * local_rows
    hidden = w_up.shape[1]
    heads = HEADS // seq_parts
    wide = heads * HEAD_DIM
    dims = (seq_count, seq_parts)
    f32 = jnp.float32

    w_heads = jnp.concatenate(
        [
            lax.dynamic_slice_in_dim(w_qkv, k * features + mine * wide, wide, axis=1)
            for k in range(3)
        ],
        axis=1,
    )
    w_t = w_heads.T
    bias = jnp.concatenate(
        [
            lax.dynamic_slice_in_dim(b_query, mine * wide, wide),
            jnp.zeros((wide,), b_query.dtype),
            lax.dynamic_slice_in_dim(b_value, mine * wide, wide),
        ]
    ).astype(f32)[:, None]
    outer = own_number("cyl")
    places = jnp.concatenate(
        [
            jnp.arange(8, dtype=jnp.int32) ^ outer,
            jnp.stack([own_number("hx"), mine, own_number("ylh")]),
            lengths,
            block_perm.reshape(-1),
        ]
    )
    vectors = jnp.stack(
        [v.astype(f32) for v in (b_out, ln1_gain, ln1_shift, b_down, ln2_gain, ln2_shift, b_out, b_out)]
    )

    arrived, kept, crossed = [], [], []
    for s in range(seq_count):
        near = tokens[s]
        start = near
        if s > 0:
            after = [crossed[-1]] + arrived[(s - 2) * seq_parts : (s - 2) * seq_parts + 1] * (s > 1)
            start, _ = lax.optimization_barrier((near, after))
        across = exchange_bit(start, "x")
        crossed.append(across)
        if s == 0:
            across, w_t, bias, places = lax.optimization_barrier((across, w_t, bias, places))
        if s > 0:
            across, _ = lax.optimization_barrier((across, arrived[-seq_parts]))
        pieces = [near, exchange_bit(near, "c"), across, exchange_bit(across, "c")]
        contexts, saved = attention_forward(places, pieces, s, w_t, bias, heads)
        kept.append(saved)
        arrived += [contexts[0]] + [exchange(contexts[r], "seq", r) for r in range(1, seq_parts)]

    (
        out_rows,
        send_down1,
        send_up1,
        send_down0,
        send_up0,
        keep_down,
        keep_up,
        d_first_in,
        sums,
        grad_out,
        send_out,
        *d_contexts,
    ) = run_token_layer(
        places,
        arrived,
        tokens.reshape(flat_rows, features),
        cotangent.reshape(flat_rows, features),
        w_out,
        vectors,
        w_up,
        b_up.astype(f32).reshape(1, hidden),
        w_down,
        dims,
    )
    out_tokens = out_rows.reshape(seq_count, local_rows, features)

    def hand_on(own, near, came):
        return [own, exchange_bit(near, "c"), came, exchange_bit(came[1], "c")]

    first_came = exchange_bit(d_contexts[2], "x")
    came_down1, came_up1 = exchange_bit(send_down1, "c"), exchange_bit(send_up1, "c")
    send_up0, first_came = lax.optimization_barrier((send_up0, first_came))
    came_up0 = exchange_bit(send_up0, "c")
    second_pair, first_came = lax.optimization_barrier((d_contexts[5], first_came))
    second_came = exchange_bit(second_pair, "x")
    parts, near, far = [], [], []

    def attend(s, group, before, late=()):
        found, total = attention_backward(places, group, s, w_t, kept[s], before, heads, late)
        parts.append(found)
        return total

    def cross(s):
        held, sent = parts[s]
        came = exchange_bit(sent, "c")
        near.append(held[0].astype(f32) + came[0])
        far.append(sum_low(held[1], came[1]))

    sends = [
        sum_low(keep_down[2:], came_down1),
        sum_low(keep_up[1::2], jnp.stack([came_up0[1], came_up1[1]])),
        send_out,
    ]
    sends, first_came = lax.optimization_barrier((sends, first_came))
    down_y, up_l, out_x = [exchange_bit(v, bit) for v, bit in zip(sends, "ylx")]
    came_down0 = exchange_bit(send_down0, "c")
    total = attend(0, hand_on(d_contexts[0], d_contexts[1], first_came), ())
    (down_y, up_l, out_x, total, parts[0], second_came, near_pair, came_down0) = (
        lax.optimization_barrier(
            (down_y, up_l, out_x, total, parts[0], second_came, d_contexts[3:5], came_down0)
        )
    )

    sends = [
        sum_low(keep_down[1], came_down0[1], down_y[1]),
        sum_low(keep_up[2], came_up1[0], up_l[1]),
        sum_low(grad_out[1], out_x[1]),
    ]
    (sends, total) = lax.optimization_barrier((sends, total))
    down_l, up_y, out_c = [exchange_bit(v, bit) for v, bit in zip(sends, "lyc")]
    cross(0)
    second_group = hand_on(*near_pair, second_came)
    for s in range(1, seq_count - 1):
        total = attend(s, second_group, total)
    out_own = sum_low(grad_out[0], out_x[0], out_c)
    (down_l, up_y, total, parts[1:], near, far, out_own) = lax.optimization_barrier(
        (down_l, up_y, total, parts[1:], near, far, out_own)
    )

    down_own = sum_low(keep_down[0], came_down0[0], down_y[0], down_l)
    down_own = down_own.reshape(2, 2, hidden // 32, features)
    up_own = sum_low(keep_up[0], came_up0[0], up_l[0], up_y)
    up_own = up_own.reshape(2, 2, features // 4, hidden // 8)
    keeps, sends = [down_own[:, 0], up_own[0]], [down_own[:, 1], up_own[1]]
    (keeps, sends, total) = lax.optimization_barrier((keeps, sends, total))
    got = [exchange_bit(v, bit) for v, bit in zip(sends, "xh")]
    far_came = [exchange_bit(far[0], "x")]
    for s in range(1, seq_count - 1):
        cross(s)
    half_a, half_b = attend(seq_count - 1, second_group, total, (out_own, sums))

    (keeps, got, far, far_came, half_a, half_b, parts[-1]) = lax.optimization_barrier(
        (keeps, got, far, far_came, half_a, half_b, parts[-1])
    )
    down_own, up_own = [k + g for k, g in zip(keeps, got)]
    half_b = half_b.reshape(2, 2, 2, *half_b.shape[1:])
    keeps = [half_a[:4], half_b[:, 0], down_own[:1], up_own[:1]]
    sends = [half_a[4:], half_b[:, 1], down_own[1:], up_own[1:]]
    (keeps, sends) = lax.optimization_barrier((keeps, sends))
    got = [exchange_bit(v, bit) for v, bit in zip(sends, "ylhx")]
    far_came += [exchange_bit(v, "x") for v in far[1:]]
    half_a, half_b, down, up = [k + g for k, g in zip(keeps, got)]
    far = []
    cross(seq_count - 1)

    keeps, sends = [half_a[:2], half_b[0]], [half_a[2:], half_b[1]]
    down, up = add_extra(down), add_extra(up)
    (keeps, sends, down, up, far, near) = lax.optimization_barrier(
        (keeps, sends, down, up, far, near)
    )
    got = [exchange_bit(v, bit) for v, bit in zip(sends, "ly")]
    came = exchange_bit(down, "h")
    far_came += [exchange_bit(v, "x") for v in far]
    down = jnp.concatenate([down, came])
    both = jnp.concatenate([k + g for k, g in zip(keeps, got)], axis=2)

    keep, send = both[:1], both[1:]
    (keep, send, down, up) = lax.optimization_barrier((keep, send, down, up))
    came, up_came = exchange_bit(send, "h"), exchange_bit(up, "h")
    down = jnp.concatenate([down, exchange_bit(down, "y")])
    up = jnp.concatenate([up, up_came])
    both = add_extra(keep + came)

    (both, down, up, far_came) = lax.optimization_barrier((both, down, up, far_came))
    came = exchange_bit(both, "h")
    down = jnp.concatenate([down, exchange_bit(down, "l")])
    up = jnp.concatenate([up, exchange_bit(up, "x")])
    both = jnp.concatenate([both, came])
    own_pos = mine * local_rows + jnp.arange(local_rows, dtype=jnp.int32)
    live = (own_pos[None, :] < lengths[:, None]).astype(f32)
    d_inputs = jnp.stack([n + f for n, f in zip(near, far_came)])
    grad_tokens = (d_inputs + d_first_in.reshape(seq_count, local_rows, features)) * live[:, :, None]


    (both, down, up, grad_tokens) = lax.optimization_barrier((both, down, up, grad_tokens))
    down_first = exchange_bit(down[:4], "x")
    came, up_came = exchange_bit(both, "y"), exchange_bit(up, "l")
    both = jnp.concatenate([both, came])
    up = jnp.concatenate([up, up_came])

    (both, down, down_first, up) = lax.optimization_barrier((both, down, down_first, up))
    came = exchange_bit(both, "l")
    down_second = exchange_bit(down[4:], "x")
    up_first = exchange_bit(up[:4], "y")
    down_near = exchange_bit(down, "c")
    down_last = jnp.concatenate([down_first, down_second])
    both = jnp.stack([both.reshape(2, 2, *both.shape[1:]), came.reshape(2, 2, *came.shape[1:])], 1)
    both = both.reshape(8, *both.shape[3:])

    (both, down, down_near, down_last, up, up_first) = lax.optimization_barrier(
        (both, down, down_near, down_last, up, up_first)
    )
    both_first = exchange_bit(both[:4], "x")
    up_second = exchange_bit(up[4:], "y")
    down_far = exchange_bit(down_last, "c")
    up_near = exchange_bit(up, "c")
    full_down = gather_down(places, [down, down_near], 0, [], (hidden, features))
    up_last = jnp.concatenate([up_first, up_second])

    (both, both_first, up, up_near, up_last, down_far, full_down) = lax.optimization_barrier(
        (both, both_first, up, up_near, up_last, down_far, full_down)
    )
    both_second = exchange_bit(both[4:], "x")
    up_far = exchange_bit(up_last, "c")
    both_near = exchange_bit(both, "c")
    full_down = gather_down(places, [down_last, down_far], 1, [full_down], (hidden, features))
    full_up = gather_up(places, [up, up_near], 0, [], (features, hidden))
    both_last = jnp.concatenate([both_first, both_second])

    (both_last, both_near, up_far, full_down, full_up) = lax.optimization_barrier(
        (both_last, both_near, up_far, full_down, full_up)
    )
    both_far = exchange_bit(both_last, "c")
    full_up = gather_up(places, [up_last, up_far], 1, [full_up], (features, hidden))
    full_qkv, full_out, vector_rows, head_rows = gather_heads(
        places, [both, both_near, both_last, both_far], (features, 3 * features)
    )
    (
        full_b_down,
        full_gain_two,
        full_shift_two,
        full_b_out,
        full_gain_one,
        full_shift_one,
    ) = [vector_rows[i] for i in range(6)]
    full_b_up = vector_rows[6 : 6 + hidden // features].reshape(hidden)
    full_b_query = head_rows[:seq_parts, :wide].reshape(features)
    full_b_value = head_rows[:seq_parts, 2 * wide : 3 * wide].reshape(features)

    return (
        out_tokens,
        grad_tokens,
        full_qkv,
        full_b_query,
        full_b_value,
        full_out,
        full_b_out,
        full_gain_one,
        full_shift_one,
        full_up,
        full_b_up,
        full_down,
        full_b_down,
        full_gain_two,
        full_shift_two,
    )


def solution(mesh):
    in_specs = (
        P("dp", "seq", None),
        P("dp", "seq", None),
        P("dp"),
        P("dp", None),
        P(),
        P(),
        P(),
        P(),
        P(),
        P(),
        P(),
        P(),
        P(),
        P(),
        P(),
        P(),
        P(),
    )
    out_specs = (
        P("dp", "seq", None),
        P("dp", "seq", None),
        P(),
        P(),
        P(),
        P(),
        P(),
        P(),
        P(),
        P(),
        P(),
        P(),
        P(),
        P(),
        P(),
    )
    return jax.shard_map(
        per_device, mesh=mesh, in_specs=in_specs, out_specs=out_specs, check_vma=False
    )
```

```python
import functools
import jax
import jax.numpy as jnp
from jax import lax
from jax.experimental import pallas as pl
from jax.experimental.pallas import tpu as pltpu
from jax.sharding import PartitionSpec as P

HEAD_DIM = 64
SOFT = HEAD_DIM ** -0.5 * 1.4426950408889634
NN = (((1,), (0,)), ((), ()))
NT = (((1,), (1,)), ((), ()))
TN = (((0,), (0,)), ((), ()))
VMEM_LIMIT = 60 * 1024 * 1024
HEADS = 12
EPSILON = 1e-06
BITS = {"c": ("seq", 0), "x": ("seq", 1), "y": ("dp", 0), "l": ("dp", 1), "h": ("dp", 2)}


def own_number(order):
    number = jnp.int32(0)
    for letter in order:
        axis, shift = BITS[letter]
        number = number * 2 + ((lax.axis_index(axis) >> shift) & 1)
    return number


def exchange(array_in, axis, flip):
    return lax.ppermute(array_in, axis, [(i, i ^ flip) for i in range(lax.axis_size(axis))])


def exchange_bit(array_in, letter):
    axis, shift = BITS[letter]
    return exchange(array_in, axis, 1 << shift)


def extra_flips(axis, used):
    return [1 << shift for shift in range(used, lax.axis_size(axis).bit_length() - 1)]


def add_extra(array_in):
    for flip in extra_flips("dp", 3):
        array_in = array_in + exchange(array_in, "dp", flip)
    return array_in


def sum_low(*parts):
    total = parts[0].astype(jnp.float32)
    for part in parts[1:]:
        total = total + part.astype(jnp.float32)
    return total.astype(jnp.bfloat16)


def dot_f32(left, right, dims):
    return lax.dot_general(left, right, dims, preferred_element_type=jnp.float32)


def sequence_scalars(places, index):
    seq_count = (places.shape[0] - 11) // 3
    return places[11 + index] >> 1, places[9], 11 + seq_count + 2 * index


def shift_matrix(half, block, whole):
    row = lax.broadcasted_iota(jnp.int32, (block, whole), 0)
    col = lax.broadcasted_iota(jnp.int32, (block, whole), 1)
    return jnp.where((col == row + half) & (row < half), 1.0, 0.0).astype(jnp.bfloat16)


def mask_tiles(half, block):
    row = lax.broadcasted_iota(jnp.int32, (16, block), 0)
    col = lax.broadcasted_iota(jnp.int32, (16, block), 1)
    key_tile = jnp.where((row == 0) & (col >= half), -1e30, 0.0).astype(jnp.bfloat16)
    query_tile = jnp.where(row == 0, 1.0, 0.0).astype(jnp.bfloat16)
    return key_tile, query_tile


def attend_forward(
    heads, index, places, x0, x1, x2, x3, w_t, bias, c0, c1, c2, c3,
    x_out, qkv_out, ctx_blk, lse, tok, c_tok, x_seq, qkv, sems,
):
    half, mine, perm = sequence_scalars(places, index)
    whole = x_seq.shape[0]
    quarter = whole // 4
    block = whole // 2
    wide = heads * HEAD_DIM
    for r, piece in enumerate((x0, x1, x2, x3)):
        x_seq[pl.ds(pl.multiple_of((r ^ mine) * quarter, quarter), quarter), :] = piece[...]
    keep_x = pltpu.make_async_copy(x_seq, x_out, sems.at[0])
    keep_x.start()
    lane = lax.broadcasted_iota(jnp.int32, (1, block), 1)
    tok[...] = (dot_f32(w_t[...], x_seq[...], NT) + bias[...]).astype(jnp.bfloat16)
    shift = shift_matrix(half, block, whole)
    qkv[0] = jnp.where(lane < half, tok[:, :block], jnp.zeros((), jnp.bfloat16))
    qkv[1] = dot_f32(tok[...], shift, NT).astype(jnp.bfloat16)
    keep_qkv = pltpu.make_async_copy(qkv, qkv_out, sems.at[1])
    keep_qkv.start()
    key_tile, query_tile = mask_tiles(half, block)

    def one_block(b, carry):
        target = places[perm + b]
        for h in range(heads):
            rows = slice(h * HEAD_DIM, (h + 1) * HEAD_DIM)
            q_t = jnp.concatenate([qkv[b, rows, :], query_tile])
            k_t = jnp.concatenate(
                [qkv[target, wide + h * HEAD_DIM : wide + (h + 1) * HEAD_DIM, :], key_tile]
            )
            v_t = qkv[target, 2 * wide + h * HEAD_DIM : 2 * wide + (h + 1) * HEAD_DIM, :]
            scores = dot_f32(k_t, q_t, TN) * SOFT
            top = jnp.max(scores, axis=0, keepdims=True)
            expo = jnp.exp2(scores - top)
            total = jnp.sum(expo, axis=0, keepdims=True)
            context = dot_f32(v_t, expo.astype(jnp.bfloat16), NN) / total
            ctx_blk[b, rows, :] = context
            lse[b, h : h + 1, :] = top + jnp.log2(total)
        return carry

    lax.fori_loop(0, 2, one_block, 0)
    early = jnp.where(lane < half, ctx_blk[0], 0.0)
    late = dot_f32(ctx_blk[1].astype(jnp.bfloat16), shift, NN)
    for j in range(4):
        part = late[:, j * quarter : (j + 1) * quarter]
        if j < 2:
            part = part + early[:, j * quarter : (j + 1) * quarter]
        c_tok[j] = part.astype(jnp.bfloat16)
    for r, piece in enumerate((c0, c1, c2, c3)):
        piece[...] = c_tok[r ^ mine]
    keep_x.wait()
    keep_qkv.wait()


def attend_backward(
    heads, index, places, g0, g1, g2, g3, w_t, x_in, qkv, ctx_blk, lse, *refs
):
    first, last = index == 0, len(refs) > 14
    acc_in, acc_b = (None, None) if first else refs[:2]
    (dx_keep, dx_send, grad_w, grad_w2, g_tok, g_blk, d_qkv, tok, x_seq, acc, dx_s, sems) = refs[-12:]
    bring_x = pltpu.make_async_copy(x_in, x_seq, sems.at[0])
    bring_x.start()
    if not first:
        bring_acc = pltpu.make_async_copy(acc_in, acc, sems.at[1])
        bring_acc.start()
    half, mine, perm = sequence_scalars(places, index)
    index = max(index - 1, 0)
    quarter = g0.shape[2]
    block = 2 * quarter
    whole = 4 * quarter
    wide = heads * HEAD_DIM
    for r, piece in enumerate((g0[index], g1[index], g2[0, index], g3[index])):
        g_tok[r ^ mine] = piece
    shift = shift_matrix(half, block, whole)
    lane = lax.broadcasted_iota(jnp.int32, (1, block), 1)
    g_all = jnp.concatenate([g_tok[j] for j in range(4)], axis=1)
    g_blk[0] = jnp.where(lane < half, g_all[:, :block], jnp.zeros((), jnp.bfloat16))
    g_blk[1] = dot_f32(g_all, shift, NT).astype(jnp.bfloat16)
    key_tile, query_tile = mask_tiles(half, block)

    def one_block(b, carry):
        target = places[perm + b]
        for h in range(heads):
            rows = slice(h * HEAD_DIM, (h + 1) * HEAD_DIM)
            k_rows = slice(wide + h * HEAD_DIM, wide + (h + 1) * HEAD_DIM)
            v_rows = slice(2 * wide + h * HEAD_DIM, 2 * wide + (h + 1) * HEAD_DIM)
            q_t = qkv[b, rows, :]
            k_t = qkv[target, k_rows, :]
            v_t = qkv[target, v_rows, :]
            g_t = g_blk[b, rows, :]
            scores = dot_f32(
                jnp.concatenate([k_t, key_tile]), jnp.concatenate([q_t, query_tile]), TN
            )
            probs = jnp.exp2(scores * SOFT - lse[b, h : h + 1, :])
            d_probs = dot_f32(v_t, g_t, TN)
            delta = jnp.sum(ctx_blk[b, rows, :] * g_t.astype(jnp.float32), axis=0, keepdims=True)
            d_scores = (probs * (d_probs - delta)).astype(jnp.bfloat16)
            scaling = HEAD_DIM ** -0.5
            d_qkv[b, rows, :] = (dot_f32(k_t, d_scores, NN) * scaling).astype(jnp.bfloat16)
            d_qkv[target, k_rows, :] = (dot_f32(q_t, d_scores, NT) * scaling).astype(jnp.bfloat16)
            d_qkv[target, v_rows, :] = dot_f32(g_t, probs.astype(jnp.bfloat16), NT).astype(
                jnp.bfloat16
            )
        return carry

    lax.fori_loop(0, 2, one_block, 0)
    late = dot_f32(d_qkv[1], shift, NN)
    front = jnp.where(lane < half, d_qkv[0].astype(jnp.float32), 0.0)
    tok[:, block:] = late[:, block:].astype(jnp.bfloat16)
    tok[:, :block] = (late[:, :block] + front).astype(jnp.bfloat16)
    sent = []
    for r in range(4):
        piece = (dx_send if r & 1 else dx_keep).at[r >> 1]
        columns = tok[:, pl.ds(pl.multiple_of((r ^ mine) * quarter, quarter), quarter)]
        dx_s[r] = dot_f32(columns, w_t[...], TN).astype(jnp.bfloat16)
        sent.append(pltpu.make_async_copy(dx_s.at[r], piece, sems.at[2 + r]))
        sent[-1].start()
    bring_x.wait()
    total = dot_f32(tok[...], x_seq[...], NN)
    ones = jnp.ones((8, whole), jnp.bfloat16)
    sums = dot_f32(ones, tok[...], NT)
    if not first:
        bring_acc.wait()
        total, sums = total + acc[...], sums + acc_b[...]
    if last:
        out_own, vectors = refs[2:4]
        inner = places[10]
        turned = total.T.astype(jnp.bfloat16)
        tile = out_own.shape[1]
        extra = grad_w.shape[1] - tile
        for half_w in (grad_w, grad_w2):
            half_w[:, tile:, :] = jnp.zeros((8, extra, 2 * wide), jnp.bfloat16)
        for q in range(8):
            rows = slice(q * tile, (q + 1) * tile)
            grad_w[q ^ inner, :tile, :] = turned[rows, : 2 * wide]
            grad_w2[q ^ inner, :tile, :wide] = turned[rows, 2 * wide :]
        grad_w2[:, :tile, wide:] = out_own[...]
        row = lax.broadcasted_iota(jnp.int32, (extra, 1), 0)
        own_row = jnp.concatenate([sums[0:1, :], jnp.zeros((1, wide), jnp.float32)], axis=1)
        tile_rows = jnp.where(row == 10, own_row, vectors[...]).astype(jnp.bfloat16)
        grad_w[inner, tile:, :] = tile_rows[:, : 2 * wide]
        grad_w2[inner, tile:, :] = tile_rows[:, 2 * wide :]
    else:
        grad_w[...] = total
        grad_w2[...] = sums
    for copy in sent:
        copy.wait()


def kernel_call(body, scalars, arrays, outs, scratch, left_in=(), left_out=()):
    def spec(away):
        return pl.BlockSpec(memory_space=pl.ANY if away else pltpu.VMEM)

    return pl.pallas_call(
        body,
        out_shape=outs,
        in_specs=[pl.BlockSpec(memory_space=pltpu.SMEM)]
        + [spec(i in left_in) for i in range(len(arrays))],
        out_specs=[spec(i in left_out) for i in range(len(outs))],
        scratch_shapes=scratch,
        compiler_params=pltpu.CompilerParams(vmem_limit_bytes=VMEM_LIMIT),
        cost_estimate=pl.CostEstimate(
            flops=10**8, transcendentals=0, bytes_accessed=1024 * 1024
        ),
    )(scalars, *arrays)


def attention_forward(places, pieces, index, w_t, bias, heads):
    quarter, features = pieces[0].shape
    whole, block, wide = 4 * quarter, 2 * quarter, heads * HEAD_DIM
    out = jax.ShapeDtypeStruct
    outs = [out((wide, quarter), jnp.bfloat16)] * 4 + [
        out((whole, features), jnp.bfloat16),
        out((2, 3 * wide, block), jnp.bfloat16),
        out((2, wide, block), jnp.float32),
        out((2, 8, block), jnp.float32),
    ]
    scratch = [
        pltpu.VMEM((3 * wide, whole), jnp.bfloat16),
        pltpu.VMEM((4, wide, quarter), jnp.bfloat16),
        pltpu.VMEM((whole, features), jnp.bfloat16),
        pltpu.VMEM((2, 3 * wide, block), jnp.bfloat16),
        pltpu.SemaphoreType.DMA((2,)),
    ]
    found = kernel_call(
        functools.partial(attend_forward, heads, index),
        places,
        [*pieces, w_t, bias],
        outs,
        scratch,
        left_out=(4, 5),
    )
    return found[:4], found[4:]


def attention_backward(places, pieces, index, w_t, kept, before, heads, late=()):
    _, wide, quarter = pieces[0].shape
    features = w_t.shape[1]
    block = 2 * quarter
    out = jax.ShapeDtypeStruct
    if late:
        grads = [out((8, features // 8 + 16, 2 * wide), jnp.bfloat16)] * 2
    else:
        grads = [out((3 * wide, features), jnp.float32), out((8, 3 * wide), jnp.float32)]
    outs = [out((2, quarter, features), jnp.bfloat16)] * 2 + grads
    scratch = [
        pltpu.VMEM((4, wide, quarter), jnp.bfloat16),
        pltpu.VMEM((2, wide, block), jnp.bfloat16),
        pltpu.VMEM((2, 3 * wide, block), jnp.bfloat16),
        pltpu.VMEM((3 * wide, 4 * quarter), jnp.bfloat16),
        pltpu.VMEM((4 * quarter, features), jnp.bfloat16),
        pltpu.VMEM((3 * wide, features), jnp.float32),
        pltpu.VMEM((4, quarter, features), jnp.bfloat16),
        pltpu.SemaphoreType.DMA((6,)),
    ]
    found = kernel_call(
        functools.partial(attend_backward, heads, index),
        places,
        [*pieces, w_t, *kept, *before, *late],
        outs,
        scratch,
        left_in=(5, 9) if before else (5,),
        left_out=(0, 1),
    )
    return found[:2], found[2:]

def live_rows(places, rows, mine, local_rows, offset):
    row = lax.broadcasted_iota(jnp.int32, (rows, 1), 0)
    length = jnp.zeros((rows, 1), jnp.int32)
    for s in range(rows // local_rows):
        length = jnp.where(row >= s * local_rows, places[offset + s], length)
    position = mine * local_rows + lax.rem(row, local_rows)
    return jnp.where(position < length, 1.0, 0.0)


def normal_parts(array_in):
    centered = array_in - jnp.mean(array_in, axis=1, keepdims=True)
    spread = jnp.mean(centered * centered, axis=1, keepdims=True)
    inverse = lax.rsqrt(spread + EPSILON)
    return centered * inverse, inverse


def normal_back(hat, inverse, gain, d_out):
    scaled = d_out * gain
    mean_scaled = jnp.mean(scaled, axis=1, keepdims=True)
    mean_product = jnp.mean(scaled * hat, axis=1, keepdims=True)
    return inverse * (scaled - mean_scaled - hat * mean_product)


def column_sum(array_in):
    return jnp.sum(array_in, axis=0, keepdims=True)


def token_layer(shape, places, *refs):
    seq_count, seq_parts = shape
    count = seq_count * seq_parts
    pieces, refs = refs[:count], refs[count:]
    tokens, cot_in, w_out, vectors, b_up, w_up_in, w_down_in = refs[:7]
    out, send_down1, send_up1, send_down0, send_up0, keep_down, keep_up = refs[7:14]
    d_first_in, sums, grad_out, send_out = refs[14:18]
    sent = refs[18:24]
    (
        w_up, w_down, active, slope, context, first_in, first_norm, lowered,
        first_low, first_t, d_lowered, turned, out_s, cot, grad_down, grad_up, sems,
    ) = refs[24:]
    rows, features = tokens.shape
    local_rows = rows // seq_count
    wide = features // seq_parts
    mine, inner = places[9], places[8]
    step = pl.program_id(0)
    quarters = w_up.shape[0]
    width = w_up.shape[2]
    f32, bf16 = jnp.float32, jnp.bfloat16

    def bring(j):
        return (
            pltpu.make_async_copy(
                w_up_in.at[:, pl.ds(j * width, width)], w_up.at[j], sems.at[j]
            ),
            pltpu.make_async_copy(
                w_down_in.at[pl.ds(j * width, width), :], w_down.at[j], sems.at[quarters + j]
            ),
        )

    keep_out = pltpu.make_async_copy(out_s, out, sems.at[2 * quarters])
    bring_cot = pltpu.make_async_copy(cot_in, cot, sems.at[2 * quarters + 1])

    def leave(relative):
        down_ref, up_ref = (
            (keep_down.at[pl.ds(0, 2)], keep_up.at[pl.ds(0, 2)]),
            (keep_down.at[pl.ds(2, 2)], keep_up.at[pl.ds(2, 2)]),
            (send_down0, send_up0),
            (send_down1, send_up1),
        )[relative]
        first = 2 * quarters + 2 + 2 * relative
        return (
            pltpu.make_async_copy(grad_down.at[relative & 1], down_ref, sems.at[first]),
            pltpu.make_async_copy(grad_up.at[relative & 1], up_ref, sems.at[first + 1]),
        )

    @pl.when(step == 0)
    def start():
        for j in range(quarters):
            for copy in bring(j):
                copy.start()
        bring_cot.start()
        for s in range(seq_count):
            for r in range(seq_parts):
                context[
                    pl.ds(pl.multiple_of((r ^ mine) * wide, wide), wide),
                    s * local_rows : (s + 1) * local_rows,
                ] = pieces[s * seq_parts + r][...]
        live = live_rows(places, rows, mine, local_rows, 11)
        attended = dot_f32(context[...], w_out[...], TN) + vectors[0:1, :]
        total = jnp.where(live > 0, tokens[...].astype(f32), 0.0) + attended
        first_in[...] = total
        hat, _ = normal_parts(total)
        normed = hat * vectors[1:2, :] + vectors[2:3, :]
        first_norm[...] = normed
        low = normed.astype(bf16)
        first_low[...] = low
        tile = features // 4
        low_t = low.T
        for q in range(4):
            first_t[pl.ds(pl.multiple_of((q ^ inner) * tile, tile), tile), :] = low_t[
                q * tile : (q + 1) * tile
            ]
        lowered[...] = jnp.zeros_like(lowered)
        sums[...] = jnp.zeros_like(sums)

    @pl.when(step < quarters)
    def forward():
        for j in range(quarters):

            @pl.when(step == j)
            def arrive():
                for copy in bring(j):
                    copy.wait()

        lifted = dot_f32(first_low[...], w_up[step], NN) + b_up[step]
        cdf = 0.5 * (1.0 + lax.erf(lifted * 0.7071067811865476))
        density = jnp.exp(lifted * lifted * -0.5) * 0.3989422804014327
        gelu = (lifted * cdf).astype(bf16)
        active[step] = gelu
        slope[step] = (cdf + lifted * density).astype(bf16)
        lowered[...] += dot_f32(gelu, w_down[step], NN)

    @pl.when(step == quarters - 1)
    def turn():
        live = live_rows(places, rows, mine, local_rows, 11)
        hat, inverse = normal_parts(first_norm[...] + (lowered[...] + vectors[3:4, :]))
        gain = vectors[4:5, :]
        bring_cot.wait()
        out_s[...] = ((hat * gain + vectors[5:6, :]) * live).astype(bf16)
        keep_out.start()
        incoming = cot[...].astype(f32) * live
        back = normal_back(hat, inverse, gain, incoming)
        lowered[...] = back
        low = back.astype(bf16)
        d_lowered[...] = low
        sums[0:1, :] = column_sum(low.astype(f32))
        sums[1:2, :] = column_sum(incoming * hat)
        sums[2:3, :] = column_sum(incoming)

    @pl.when(step >= quarters)
    def backward():
        relative = 2 * quarters - 1 - step
        quarter = relative ^ (places[0] >> 1)
        low_bit = places[0] & 1
        slot = relative & 1
        half = width // 2
        tile = half // 4
        for k in range(2):

            @pl.when(relative == k)
            def free():
                for copy in leave(k + 2):
                    copy.wait()

        down = dot_f32(active[quarter], d_lowered[...], TN).astype(bf16)
        for j in range(2):
            for q in range(4):
                grad_down[
                    slot, j ^ low_bit, pl.ds(pl.multiple_of((q ^ inner) * tile, tile), tile), :
                ] = down[j * half + q * tile : j * half + (q + 1) * tile]
        d_active = dot_f32(d_lowered[...], w_down[quarter], NT)
        d_lifted = (d_active * slope[quarter].astype(f32)).astype(bf16)
        up = dot_f32(first_t[...], d_lifted, NN).astype(bf16)
        for j in range(2):
            grad_up[slot, j ^ low_bit] = up[:, j * half : (j + 1) * half]
        sums[pl.ds(6 + quarter, 1), :] = column_sum(d_lifted.astype(f32))
        lowered[...] += dot_f32(d_lifted, w_up[quarter], NT)
        for k in range(quarters):

            @pl.when(relative == k)
            def start_leaving():
                for copy in leave(k):
                    copy.start()

    @pl.when(step == 2 * quarters - 1)
    def finish():
        hat, inverse = normal_parts(first_in[...])
        incoming = lowered[...]
        back = normal_back(hat, inverse, vectors[1:2, :], incoming)
        d_first_in[...] = back
        low = back.astype(bf16)
        sums[3:4, :] = column_sum(low.astype(f32))
        sums[4:5, :] = column_sum(incoming * hat)
        sums[5:6, :] = column_sum(incoming)
        turned[...] = dot_f32(w_out[...], low, NT).astype(bf16)
        for r in range(seq_parts):
            own = turned[pl.ds(pl.multiple_of((r ^ mine) * wide, wide), wide), :]
            for s in range(seq_count):
                target, place = sent[3 * min(s, 1) + min(r, 2)], max(s - 1, 0)
                columns = own[:, s * local_rows : (s + 1) * local_rows]
                if r < 2:
                    target[place] = columns
                else:
                    target[r - 2, place] = columns
        product = dot_f32(context[...], low, NN).astype(bf16)
        block_rows, block_cols = grad_out.shape[2:]
        across = features // block_cols
        for j in range(seq_parts):
            for q in range(wide // block_rows * across):
                row, col = j * wide + q // across * block_rows, q % across * block_cols
                block = product[row : row + block_rows, col : col + block_cols]
                place, inner_place = j ^ mine, q ^ places[10]

                @pl.when(place < 2)
                def own():
                    grad_out[place, inner_place] = block

                @pl.when(place >= 2)
                def across_x():
                    send_out[place - 2, inner_place] = block

        keep_out.wait()
        for k in range(2):
            for copy in leave(k):
                copy.wait()


def whole_spec(shape):
    return pl.BlockSpec(
        shape, lambda p, places: (0,) * len(shape), pipeline_mode=pl.Buffered(buffer_count=1)
    )


def step_call(body, places, steps, ins, in_specs, outs, out_specs, scratch, flops, aliases={}):
    return pl.pallas_call(
        body,
        out_shape=outs,
        grid_spec=pltpu.PrefetchScalarGridSpec(
            num_scalar_prefetch=1,
            grid=(steps,),
            in_specs=in_specs,
            out_specs=out_specs,
            scratch_shapes=scratch,
        ),
        input_output_aliases=aliases,
        compiler_params=pltpu.CompilerParams(vmem_limit_bytes=VMEM_LIMIT),
        cost_estimate=pl.CostEstimate(
            flops=flops, transcendentals=0, bytes_accessed=1024 * 1024
        ),
    )(places, *ins)


def run_token_layer(places, pieces, tokens, cot, w_out, vectors, w_up, b_up, w_down, dims):
    seq_count, seq_parts = dims
    rows, features = tokens.shape
    hidden = w_up.shape[1]
    quarters = 4
    width = hidden // quarters
    half = width // 2
    out, bf16, f32 = jax.ShapeDtypeStruct, jnp.bfloat16, jnp.float32
    square, turned = (rows, features), (features, rows)
    piece = (features // seq_parts, rows // seq_count)
    sent = []
    for n in (1, seq_count - 1):
        sent += [(n, *piece), (n, *piece), (2, n, *piece)]
    out_blocks = (seq_parts // 2, 8, features // seq_parts // 2, features // 4)
    away = pl.BlockSpec(memory_space=pl.ANY)
    down, up = (2, half, features), (2, features, half)

    return step_call(
        functools.partial(token_layer, dims),
        places,
        2 * quarters,
        [*pieces, tokens, cot, w_out, vectors, b_up.reshape(quarters, 1, width), w_up, w_down],
        [whole_spec(p.shape) for p in pieces]
        + [whole_spec(square), away, whole_spec(w_out.shape), whole_spec(vectors.shape)]
        + [whole_spec((quarters, 1, width)), away, away],
        [
            out(square, bf16),
            out(down, bf16),
            out(up, bf16),
            out(down, bf16),
            out(up, bf16),
            out((4, half, features), bf16),
            out((4, features, half), bf16),
            out(square, f32),
            out((16, features), f32),
            out(out_blocks, bf16),
            out(out_blocks, bf16),
        ]
        + [out(p, bf16) for p in sent],
        [away] * 7
        + [whole_spec(square), whole_spec((16, features))]
        + [whole_spec(out_blocks)] * 2
        + [whole_spec(p) for p in sent],
        [
            pltpu.VMEM((quarters, features, width), bf16),
            pltpu.VMEM((quarters, width, features), bf16),
            pltpu.VMEM((quarters, rows, width), bf16),
            pltpu.VMEM((quarters, rows, width), bf16),
            pltpu.VMEM(turned, bf16),
            pltpu.VMEM(square, f32),
            pltpu.VMEM(square, f32),
            pltpu.VMEM(square, f32),
            pltpu.VMEM(square, bf16),
            pltpu.VMEM(turned, bf16),
            pltpu.VMEM(square, bf16),
            pltpu.VMEM(turned, bf16),
            pltpu.VMEM(square, bf16),
            pltpu.VMEM(square, bf16),
            pltpu.VMEM((2, *down), bf16),
            pltpu.VMEM((2, *up), bf16),
            pltpu.SemaphoreType.DMA((4 * quarters + 2,)),
        ],
        2 * rows * features * (6 * hidden + 3 * features),
    )


def place_rows(count, places, *refs):
    out = refs[-1]
    tile = refs[0].shape[-2]
    for k in range(count):

        @pl.when(pl.program_id(0) >> 1 == k)
        def copy():
            for q in range(4):
                h, x = q >> 1, q & 1
                out[pl.ds(pl.multiple_of((q ^ places[8]) * tile, tile), tile), :] = refs[k][
                    x, 0, h
                ].astype(jnp.float32)


def gather_hidden(places, pieces, core, late, begun, shape, by_rows):
    _, rows, cols = pieces[0].shape
    count = len(pieces)

    def source(k):
        return pl.BlockSpec(
            (2, 1, 2, rows, cols), lambda p, places: (0, jnp.clip(p - 2 * k, 0, 1), 0, 0, 0)
        )

    def index(p, places):
        turn = p & 1
        outer = (core + (p >> 1)) * 4 + (late * 2 + turn if by_rows else turn * 2 + late)
        return (places[outer], 0) if by_rows else (0, places[outer])

    return step_call(
        functools.partial(place_rows, count),
        places,
        2 * count,
        [piece.reshape(2, 2, 2, rows, cols) for piece in pieces] + begun,
        [source(k) for k in range(count)] + [pl.BlockSpec(memory_space=pl.ANY)] * len(begun),
        jax.ShapeDtypeStruct(shape, jnp.float32),
        pl.BlockSpec((4 * rows, cols), index),
        [],
        1000,
        {count + 1: 0} if begun else {},
    )


def place_heads(places, *refs):
    pieces = refs[:-4]
    out, out_w, vector_rows, head_rows = refs[-4:]
    mine, inner = places[9], places[10]
    seq_parts = len(pieces)
    step = pl.program_id(0)
    wide = out_w.shape[0] // seq_parts
    rows, features = out.shape[0], out_w.shape[1]
    f32 = jnp.float32
    for m in range(seq_parts):

        @pl.when(mine == m)
        def copy():
            blocks = [pieces[j ^ m][step ^ inner, :rows, : 3 * wide] for j in range(seq_parts)]
            for section in range(3):
                columns = slice(section * wide, (section + 1) * wide)
                joined = jnp.concatenate([block[:, columns] for block in blocks], axis=1)
                out[:, section * features : (section + 1) * features] = joined.astype(f32)

        @pl.when((mine == m) & (step == 0))
        def copy_vectors():
            held = [pieces[j ^ m][inner, rows:, :].astype(f32) for j in range(seq_parts)]
            total = held[0]
            for other in held[1:]:
                total = total + other
            vector_rows[...] = total
            for j in range(seq_parts):
                head_rows[j : j + 1, :] = held[j][10:11, :]

    for r, piece in enumerate(pieces):

        @pl.when(step == r)
        def copy_out():
            for i in range(2):
                joined = jnp.concatenate(
                    [piece[(4 * i + q) ^ inner, :rows, 3 * wide :] for q in range(4)], axis=1
                )
                first = pl.multiple_of((r ^ mine) * wide + i * rows, rows)
                out_w[pl.ds(first, rows), :] = joined.astype(f32)


def gather_heads(places, pieces, shape):
    out, f32 = jax.ShapeDtypeStruct, jnp.float32
    features = shape[0]
    rows = features // 8
    square = (features, features)
    extra = (pieces[0].shape[1] - rows, features)
    return step_call(
        place_heads,
        places,
        8,
        pieces,
        [whole_spec(p.shape) for p in pieces],
        [out(shape, f32), out(square, f32), out(extra, f32), out((8, features), f32)],
        [pl.BlockSpec((rows, shape[1]), lambda p, places: (p, 0))]
        + [whole_spec(square), whole_spec(extra), whole_spec((8, features))],
        [],
        1000,
    )


def per_device(
    tokens,
    cotangent,
    lengths,
    block_perm,
    w_qkv,
    b_query,
    b_value,
    w_out,
    b_out,
    ln1_gain,
    ln1_shift,
    w_up,
    b_up,
    w_down,
    b_down,
    ln2_gain,
    ln2_shift,
):
    seq_parts = lax.axis_size("seq")
    mine = lax.axis_index("seq")
    seq_count, local_rows, features = tokens.shape
    flat_rows = seq_count * local_rows
    hidden = w_up.shape[1]
    heads = HEADS // seq_parts
    wide = heads * HEAD_DIM
    dims = (seq_count, seq_parts)
    f32 = jnp.float32

    w_heads = jnp.concatenate(
        [
            lax.dynamic_slice_in_dim(w_qkv, k * features + mine * wide, wide, axis=1)
            for k in range(3)
        ],
        axis=1,
    )
    w_t = w_heads.T
    bias = jnp.concatenate(
        [
            lax.dynamic_slice_in_dim(b_query, mine * wide, wide),
            jnp.zeros((wide,), b_query.dtype),
            lax.dynamic_slice_in_dim(b_value, mine * wide, wide),
        ]
    ).astype(f32)[:, None]
    outer = own_number("cyl")
    places = jnp.concatenate(
        [
            jnp.arange(8, dtype=jnp.int32) ^ outer,
            jnp.stack([own_number("hx"), mine, own_number("ylh")]),
            lengths,
            block_perm.reshape(-1),
        ]
    )
    vectors = jnp.stack(
        [v.astype(f32) for v in (b_out, ln1_gain, ln1_shift, b_down, ln2_gain, ln2_shift, b_out, b_out)]
    )

    arrived, kept, crossed = [], [], []
    for s in range(seq_count):
        near = tokens[s]
        start = near
        if s > 0:
            after = [crossed[-1]] + arrived[(s - 2) * seq_parts : (s - 2) * seq_parts + 1] * (s > 1)
            start, _ = lax.optimization_barrier((near, after))
        across = exchange_bit(start, "x")
        crossed.append(across)
        if s == 0:
            across, w_t, bias, places = lax.optimization_barrier((across, w_t, bias, places))
        if s > 0:
            across, _ = lax.optimization_barrier((across, arrived[-seq_parts]))
        pieces = [near, exchange_bit(near, "c"), across, exchange_bit(across, "c")]
        contexts, saved = attention_forward(places, pieces, s, w_t, bias, heads)
        kept.append(saved)
        arrived += [contexts[0]] + [exchange(contexts[r], "seq", r) for r in range(1, seq_parts)]

    (
        out_rows,
        send_down1,
        send_up1,
        send_down0,
        send_up0,
        keep_down,
        keep_up,
        d_first_in,
        sums,
        grad_out,
        send_out,
        *d_contexts,
    ) = run_token_layer(
        places,
        arrived,
        tokens.reshape(flat_rows, features),
        cotangent.reshape(flat_rows, features),
        w_out,
        vectors,
        w_up,
        b_up.astype(f32).reshape(1, hidden),
        w_down,
        dims,
    )
    out_tokens = out_rows.reshape(seq_count, local_rows, features)

    def hand_on(own, near, came):
        return [own, exchange_bit(near, "c"), came, exchange_bit(came[1], "c")]

    first_came = exchange_bit(d_contexts[2], "x")
    came_down1, came_up1 = exchange_bit(send_down1, "c"), exchange_bit(send_up1, "c")
    send_up0, first_came = lax.optimization_barrier((send_up0, first_came))
    came_up0 = exchange_bit(send_up0, "c")
    second_pair, first_came = lax.optimization_barrier((d_contexts[5], first_came))
    second_came = exchange_bit(second_pair, "x")
    parts, near, far = [], [], []

    def attend(s, group, before, late=()):
        found, total = attention_backward(places, group, s, w_t, kept[s], before, heads, late)
        parts.append(found)
        return total

    def cross(s):
        held, sent = parts[s]
        came = exchange_bit(sent, "c")
        near.append(held[0].astype(f32) + came[0])
        far.append(sum_low(held[1], came[1]))

    sends = [
        sum_low(keep_down[2:], came_down1),
        sum_low(keep_up[1::2], jnp.stack([came_up0[1], came_up1[1]])),
    ]
    sends, first_came = lax.optimization_barrier((sends, first_came))
    down_y, up_l = [exchange_bit(v, bit) for v, bit in zip(sends, "yl")]
    came_down0 = exchange_bit(send_down0, "c")
    total = attend(0, hand_on(d_contexts[0], d_contexts[1], first_came), ())
    (total, parts[0], second_came, near_pair, came_down0, send_out) = lax.optimization_barrier(
        (total, parts[0], second_came, d_contexts[3:5], came_down0, send_out)
    )

    out_x = exchange_bit(send_out, "x")
    second_group = hand_on(*near_pair, second_came)
    cross(0)
    for s in range(1, seq_count - 1):
        total = attend(s, second_group, total)
    (down_y, up_l, out_x, total, parts[1:], near, far) = lax.optimization_barrier(
        (down_y, up_l, out_x, total, parts[1:], near, far)
    )

    sends = [
        sum_low(keep_down[1], came_down0[1], down_y[1]),
        sum_low(keep_up[2], came_up1[0], up_l[1]),
    ]
    out_c = exchange_bit(sum_low(grad_out[1], out_x[1]), "c")
    out_own = sum_low(grad_out[0], out_x[0], out_c)
    (sends, total, out_own, far) = lax.optimization_barrier((sends, total, out_own, far))
    down_l, up_y = [exchange_bit(v, bit) for v, bit in zip(sends, "ly")]
    far_came = [exchange_bit(far[0], "x")]
    for s in range(1, seq_count - 1):
        cross(s)
    half_a, half_b = attend(seq_count - 1, second_group, total, (out_own, sums))

    (down_l, up_y, far, far_came, half_a, half_b, parts[-1]) = lax.optimization_barrier(
        (down_l, up_y, far, far_came, half_a, half_b, parts[-1])
    )
    down_own = sum_low(keep_down[0], came_down0[0], down_y[0], down_l)
    down_own = down_own.reshape(2, 2, hidden // 32, features)
    up_own = sum_low(keep_up[0], came_up0[0], up_l[0], up_y)
    up_own = up_own.reshape(2, 2, features // 4, hidden // 8)
    half_b = half_b.reshape(2, 2, 2, *half_b.shape[1:])
    keeps = [half_a[:4], half_b[:, 0], down_own[:, 0], up_own[0]]
    sends = [half_a[4:], half_b[:, 1], down_own[:, 1], up_own[1]]
    (keeps, sends) = lax.optimization_barrier((keeps, sends))
    got = [exchange_bit(v, bit) for v, bit in zip(sends, "ylxh")]
    far_came += [exchange_bit(v, "x") for v in far[1:]]
    half_a, half_b, down, up = [k + g for k, g in zip(keeps, got)]
    far = []
    cross(seq_count - 1)

    keeps = [half_a[:2], half_b[0], down[:1], up[:1]]
    sends = [half_a[2:], half_b[1], down[1:], up[1:]]
    (keeps, sends, far, near) = lax.optimization_barrier((keeps, sends, far, near))
    got = [exchange_bit(v, bit) for v, bit in zip(sends, "lyhx")]
    far_came += [exchange_bit(v, "x") for v in far]
    half_a, half_b, down, up = [k + g for k, g in zip(keeps, got)]
    down, up = add_extra(down), add_extra(up)
    both = jnp.concatenate([half_a, half_b], axis=2)

    keep, send = both[:1], both[1:]
    (keep, send, down, up) = lax.optimization_barrier((keep, send, down, up))
    came, down_came = exchange_bit(send, "h"), exchange_bit(down, "h")
    both = add_extra(keep + came)
    down = jnp.concatenate([down, down_came])

    (both, down, up, far_came) = lax.optimization_barrier((both, down, up, far_came))
    came, up_came = exchange_bit(both, "h"), exchange_bit(up, "h")
    down = jnp.concatenate([down, exchange_bit(down, "l")])
    both = jnp.concatenate([both, came])
    up = jnp.concatenate([up, up_came])
    own_pos = mine * local_rows + jnp.arange(local_rows, dtype=jnp.int32)
    live = (own_pos[None, :] < lengths[:, None]).astype(f32)
    d_inputs = jnp.stack([n + f for n, f in zip(near, far_came)])
    grad_tokens = (d_inputs + d_first_in.reshape(seq_count, local_rows, features)) * live[:, :, None]


    (both, down, up, grad_tokens) = lax.optimization_barrier((both, down, up, grad_tokens))
    came = exchange_bit(both, "y")
    down = jnp.concatenate([down, exchange_bit(down, "x")])
    up = jnp.concatenate([up, exchange_bit(up, "y")])
    both = jnp.concatenate([both, came])

    (both, down, up) = lax.optimization_barrier((both, down, up))
    came = exchange_bit(both, "l")
    down_first = exchange_bit(down[:4], "y")
    up_came = exchange_bit(up, "x")
    down_near = exchange_bit(down, "c")
    both = jnp.stack([both.reshape(2, 2, *both.shape[1:]), came.reshape(2, 2, *came.shape[1:])], 1)
    both = both.reshape(8, *both.shape[3:])
    up = jnp.concatenate([up, up_came])

    (both, down, down_near, down_first, up) = lax.optimization_barrier(
        (both, down, down_near, down_first, up)
    )
    both_first = exchange_bit(both[:4], "x")
    down_second = exchange_bit(down[4:], "y")
    up_first = exchange_bit(up[:4], "l")
    up_near = exchange_bit(up, "c")
    full_down = gather_hidden(places, [down, down_near], 0, 0, [], (hidden, features), True)
    down_last = jnp.concatenate([down_first, down_second])

    (both, both_first, up, up_near, up_first, down_last, full_down) = lax.optimization_barrier(
        (both, both_first, up, up_near, up_first, down_last, full_down)
    )
    both_second = exchange_bit(both[4:6], "x")
    up_second = exchange_bit(up[4:6], "l")
    down_far = exchange_bit(down_last, "c")
    full_up = gather_hidden(places, [up, up_near], 0, 0, [], (features, hidden), False)

    (both, both_second, up, up_second, down_far, full_up) = lax.optimization_barrier(
        (both, both_second, up, up_second, down_far, full_up)
    )
    both_third = exchange_bit(both[6:], "x")
    up_third = exchange_bit(up[6:], "l")
    both_near = exchange_bit(both, "c")
    full_down = gather_hidden(
        places, [down_last, down_far], 0, 1, [full_down], (hidden, features), True
    )
    (both_third, both_near, up_third, full_down) = lax.optimization_barrier(
        (both_third, both_near, up_third, full_down)
    )
    both_last = jnp.concatenate([both_first, both_second, both_third])
    up_last = jnp.concatenate([up_first, up_second, up_third])
    both_far, up_far = exchange_bit(both_last, "c"), exchange_bit(up_last, "c")
    full_up = gather_hidden(places, [up_last], 0, 1, [full_up], (features, hidden), False)
    (both_far, full_up) = lax.optimization_barrier((both_far, full_up))
    full_qkv, full_out, vector_rows, head_rows = gather_heads(
        places, [both, both_near, both_last, both_far], (features, 3 * features)
    )
    full_up = gather_hidden(places, [up_far], 1, 1, [full_up], (features, hidden), False)
    (
        full_b_down,
        full_gain_two,
        full_shift_two,
        full_b_out,
        full_gain_one,
        full_shift_one,
    ) = [vector_rows[i] for i in range(6)]
    full_b_up = vector_rows[6 : 6 + hidden // features].reshape(hidden)
    full_b_query = head_rows[:seq_parts, :wide].reshape(features)
    full_b_value = head_rows[:seq_parts, 2 * wide : 3 * wide].reshape(features)

    return (
        out_tokens,
        grad_tokens,
        full_qkv,
        full_b_query,
        full_b_value,
        full_out,
        full_b_out,
        full_gain_one,
        full_shift_one,
        full_up,
        full_b_up,
        full_down,
        full_b_down,
        full_gain_two,
        full_shift_two,
    )


def solution(mesh):
    in_specs = (
        P("dp", "seq", None),
        P("dp", "seq", None),
        P("dp"),
        P("dp", None),
        P(),
        P(),
        P(),
        P(),
        P(),
        P(),
        P(),
        P(),
        P(),
        P(),
        P(),
        P(),
        P(),
    )
    out_specs = (
        P("dp", "seq", None),
        P("dp", "seq", None),
        P(),
        P(),
        P(),
        P(),
        P(),
        P(),
        P(),
        P(),
        P(),
        P(),
        P(),
        P(),
        P(),
    )
    return jax.shard_map(
        per_device, mesh=mesh, in_specs=in_specs, out_specs=out_specs, check_vma=False
    )
```

```python
import functools
import jax
import jax.numpy as jnp
from jax import lax
from jax.experimental import pallas as pl
from jax.experimental.pallas import tpu as pltpu
from jax.sharding import PartitionSpec as P

HEAD_DIM = 64
SOFT = HEAD_DIM ** -0.5 * 1.4426950408889634
NN = (((1,), (0,)), ((), ()))
NT = (((1,), (1,)), ((), ()))
TN = (((0,), (0,)), ((), ()))
VMEM_LIMIT = 60 * 1024 * 1024
HEADS = 12
EPSILON = 1e-06
BITS = {"c": ("seq", 0), "x": ("seq", 1), "y": ("dp", 0), "l": ("dp", 1), "h": ("dp", 2)}


def own_number(order):
    number = jnp.int32(0)
    for letter in order:
        axis, shift = BITS[letter]
        number = number * 2 + ((lax.axis_index(axis) >> shift) & 1)
    return number


def exchange(array_in, axis, flip):
    return lax.ppermute(array_in, axis, [(i, i ^ flip) for i in range(lax.axis_size(axis))])


def exchange_bit(array_in, letter):
    axis, shift = BITS[letter]
    return exchange(array_in, axis, 1 << shift)


def extra_flips(axis, used):
    return [1 << shift for shift in range(used, lax.axis_size(axis).bit_length() - 1)]


def add_extra(array_in):
    for flip in extra_flips("dp", 3):
        array_in = array_in + exchange(array_in, "dp", flip)
    return array_in


def sum_low(*parts):
    total = parts[0].astype(jnp.float32)
    for part in parts[1:]:
        total = total + part.astype(jnp.float32)
    return total.astype(jnp.bfloat16)


def dot_f32(left, right, dims):
    return lax.dot_general(left, right, dims, preferred_element_type=jnp.float32)


def sequence_scalars(places, index):
    seq_count = (places.shape[0] - 11) // 3
    return places[11 + index] >> 1, places[9], 11 + seq_count + 2 * index


def shift_matrix(half, block, whole):
    row = lax.broadcasted_iota(jnp.int32, (block, whole), 0)
    col = lax.broadcasted_iota(jnp.int32, (block, whole), 1)
    return jnp.where((col == row + half) & (row < half), 1.0, 0.0).astype(jnp.bfloat16)


def mask_tiles(half, block):
    row = lax.broadcasted_iota(jnp.int32, (16, block), 0)
    col = lax.broadcasted_iota(jnp.int32, (16, block), 1)
    key_tile = jnp.where((row == 0) & (col >= half), -1e30, 0.0).astype(jnp.bfloat16)
    query_tile = jnp.where(row == 0, 1.0, 0.0).astype(jnp.bfloat16)
    return key_tile, query_tile


def attend_forward(
    heads, index, places, x0, x1, x2, x3, w_t, bias, c0, c1, c2, c3,
    x_out, qkv_out, ctx_blk, lse, tok, c_tok, x_seq, qkv, sems,
):
    half, mine, perm = sequence_scalars(places, index)
    whole = x_seq.shape[0]
    quarter = whole // 4
    block = whole // 2
    wide = heads * HEAD_DIM
    for r, piece in enumerate((x0, x1, x2, x3)):
        x_seq[pl.ds(pl.multiple_of((r ^ mine) * quarter, quarter), quarter), :] = piece[...]
    keep_x = pltpu.make_async_copy(x_seq, x_out, sems.at[0])
    keep_x.start()
    lane = lax.broadcasted_iota(jnp.int32, (1, block), 1)
    tok[...] = (dot_f32(w_t[...], x_seq[...], NT) + bias[...]).astype(jnp.bfloat16)
    shift = shift_matrix(half, block, whole)
    qkv[0] = jnp.where(lane < half, tok[:, :block], jnp.zeros((), jnp.bfloat16))
    qkv[1] = dot_f32(tok[...], shift, NT).astype(jnp.bfloat16)
    keep_qkv = pltpu.make_async_copy(qkv, qkv_out, sems.at[1])
    keep_qkv.start()
    key_tile, query_tile = mask_tiles(half, block)

    def one_block(b, carry):
        target = places[perm + b]
        for h in range(heads):
            rows = slice(h * HEAD_DIM, (h + 1) * HEAD_DIM)
            q_t = jnp.concatenate([qkv[b, rows, :], query_tile])
            k_t = jnp.concatenate(
                [qkv[target, wide + h * HEAD_DIM : wide + (h + 1) * HEAD_DIM, :], key_tile]
            )
            v_t = qkv[target, 2 * wide + h * HEAD_DIM : 2 * wide + (h + 1) * HEAD_DIM, :]
            scores = dot_f32(k_t, q_t, TN) * SOFT
            top = jnp.max(scores, axis=0, keepdims=True)
            expo = jnp.exp2(scores - top)
            total = jnp.sum(expo, axis=0, keepdims=True)
            context = dot_f32(v_t, expo.astype(jnp.bfloat16), NN) / total
            ctx_blk[b, rows, :] = context
            lse[b, h : h + 1, :] = top + jnp.log2(total)
        return carry

    lax.fori_loop(0, 2, one_block, 0)
    early = jnp.where(lane < half, ctx_blk[0], 0.0)
    late = dot_f32(ctx_blk[1].astype(jnp.bfloat16), shift, NN)
    for j in range(4):
        part = late[:, j * quarter : (j + 1) * quarter]
        if j < 2:
            part = part + early[:, j * quarter : (j + 1) * quarter]
        c_tok[j] = part.astype(jnp.bfloat16)
    for r, piece in enumerate((c0, c1, c2, c3)):
        piece[...] = c_tok[r ^ mine]
    keep_x.wait()
    keep_qkv.wait()


def attend_backward(
    heads, index, places, g0, g1, g2, g3, w_t, x_in, qkv, ctx_blk, lse, *refs
):
    first, last = index == 0, len(refs) > 14
    acc_in, acc_b = (None, None) if first else refs[:2]
    (dx_keep, dx_send, grad_w, grad_w2, g_tok, g_blk, d_qkv, tok, x_seq, acc, dx_s, sems) = refs[-12:]
    bring_x = pltpu.make_async_copy(x_in, x_seq, sems.at[0])
    bring_x.start()
    if not first:
        bring_acc = pltpu.make_async_copy(acc_in, acc, sems.at[1])
        bring_acc.start()
    half, mine, perm = sequence_scalars(places, index)
    index = max(index - 1, 0)
    quarter = g0.shape[2]
    block = 2 * quarter
    whole = 4 * quarter
    wide = heads * HEAD_DIM
    for r, piece in enumerate((g0[index], g1[index], g2[0, index], g3[index])):
        g_tok[r ^ mine] = piece
    shift = shift_matrix(half, block, whole)
    lane = lax.broadcasted_iota(jnp.int32, (1, block), 1)
    g_all = jnp.concatenate([g_tok[j] for j in range(4)], axis=1)
    g_blk[0] = jnp.where(lane < half, g_all[:, :block], jnp.zeros((), jnp.bfloat16))
    g_blk[1] = dot_f32(g_all, shift, NT).astype(jnp.bfloat16)
    key_tile, query_tile = mask_tiles(half, block)

    def one_block(b, carry):
        target = places[perm + b]
        for h in range(heads):
            rows = slice(h * HEAD_DIM, (h + 1) * HEAD_DIM)
            k_rows = slice(wide + h * HEAD_DIM, wide + (h + 1) * HEAD_DIM)
            v_rows = slice(2 * wide + h * HEAD_DIM, 2 * wide + (h + 1) * HEAD_DIM)
            q_t = qkv[b, rows, :]
            k_t = qkv[target, k_rows, :]
            v_t = qkv[target, v_rows, :]
            g_t = g_blk[b, rows, :]
            scores = dot_f32(
                jnp.concatenate([k_t, key_tile]), jnp.concatenate([q_t, query_tile]), TN
            )
            probs = jnp.exp2(scores * SOFT - lse[b, h : h + 1, :])
            d_probs = dot_f32(v_t, g_t, TN)
            delta = jnp.sum(ctx_blk[b, rows, :] * g_t.astype(jnp.float32), axis=0, keepdims=True)
            d_scores = (probs * (d_probs - delta)).astype(jnp.bfloat16)
            scaling = HEAD_DIM ** -0.5
            d_qkv[b, rows, :] = (dot_f32(k_t, d_scores, NN) * scaling).astype(jnp.bfloat16)
            d_qkv[target, k_rows, :] = (dot_f32(q_t, d_scores, NT) * scaling).astype(jnp.bfloat16)
            d_qkv[target, v_rows, :] = dot_f32(g_t, probs.astype(jnp.bfloat16), NT).astype(
                jnp.bfloat16
            )
        return carry

    lax.fori_loop(0, 2, one_block, 0)
    late = dot_f32(d_qkv[1], shift, NN)
    front = jnp.where(lane < half, d_qkv[0].astype(jnp.float32), 0.0)
    tok[:, block:] = late[:, block:].astype(jnp.bfloat16)
    tok[:, :block] = (late[:, :block] + front).astype(jnp.bfloat16)
    sent = []
    for r in range(4):
        piece = (dx_send if r & 1 else dx_keep).at[r >> 1]
        columns = tok[:, pl.ds(pl.multiple_of((r ^ mine) * quarter, quarter), quarter)]
        dx_s[r] = dot_f32(columns, w_t[...], TN).astype(jnp.bfloat16)
        sent.append(pltpu.make_async_copy(dx_s.at[r], piece, sems.at[2 + r]))
        sent[-1].start()
    bring_x.wait()
    total = dot_f32(tok[...], x_seq[...], NN)
    ones = jnp.ones((8, whole), jnp.bfloat16)
    sums = dot_f32(ones, tok[...], NT)
    if not first:
        bring_acc.wait()
        total, sums = total + acc[...], sums + acc_b[...]
    if last:
        out_own, vectors = refs[2:4]
        inner = places[10]
        turned = total.T.astype(jnp.bfloat16)
        tile = out_own.shape[1]
        extra = grad_w.shape[1] - tile
        for half_w in (grad_w, grad_w2):
            half_w[:, tile:, :] = jnp.zeros((8, extra, 2 * wide), jnp.bfloat16)
        for q in range(8):
            rows = slice(q * tile, (q + 1) * tile)
            grad_w[q ^ inner, :tile, :] = turned[rows, : 2 * wide]
            grad_w2[q ^ inner, :tile, :wide] = turned[rows, 2 * wide :]
        grad_w2[:, :tile, wide:] = out_own[...]
        row = lax.broadcasted_iota(jnp.int32, (extra, 1), 0)
        own_row = jnp.concatenate([sums[0:1, :], jnp.zeros((1, wide), jnp.float32)], axis=1)
        tile_rows = jnp.where(row == 10, own_row, vectors[...]).astype(jnp.bfloat16)
        grad_w[inner, tile:, :] = tile_rows[:, : 2 * wide]
        grad_w2[inner, tile:, :] = tile_rows[:, 2 * wide :]
    else:
        grad_w[...] = total
        grad_w2[...] = sums
    for copy in sent:
        copy.wait()


def kernel_call(body, scalars, arrays, outs, scratch, left_in=(), left_out=()):
    def spec(away):
        return pl.BlockSpec(memory_space=pl.ANY if away else pltpu.VMEM)

    return pl.pallas_call(
        body,
        out_shape=outs,
        in_specs=[pl.BlockSpec(memory_space=pltpu.SMEM)]
        + [spec(i in left_in) for i in range(len(arrays))],
        out_specs=[spec(i in left_out) for i in range(len(outs))],
        scratch_shapes=scratch,
        compiler_params=pltpu.CompilerParams(vmem_limit_bytes=VMEM_LIMIT),
        cost_estimate=pl.CostEstimate(
            flops=10**8, transcendentals=0, bytes_accessed=1024 * 1024
        ),
    )(scalars, *arrays)


def attention_forward(places, pieces, index, w_t, bias, heads):
    quarter, features = pieces[0].shape
    whole, block, wide = 4 * quarter, 2 * quarter, heads * HEAD_DIM
    out = jax.ShapeDtypeStruct
    outs = [out((wide, quarter), jnp.bfloat16)] * 4 + [
        out((whole, features), jnp.bfloat16),
        out((2, 3 * wide, block), jnp.bfloat16),
        out((2, wide, block), jnp.float32),
        out((2, 8, block), jnp.float32),
    ]
    scratch = [
        pltpu.VMEM((3 * wide, whole), jnp.bfloat16),
        pltpu.VMEM((4, wide, quarter), jnp.bfloat16),
        pltpu.VMEM((whole, features), jnp.bfloat16),
        pltpu.VMEM((2, 3 * wide, block), jnp.bfloat16),
        pltpu.SemaphoreType.DMA((2,)),
    ]
    found = kernel_call(
        functools.partial(attend_forward, heads, index),
        places,
        [*pieces, w_t, bias],
        outs,
        scratch,
        left_out=(4, 5),
    )
    return found[:4], found[4:]


def attention_backward(places, pieces, index, w_t, kept, before, heads, late=()):
    _, wide, quarter = pieces[0].shape
    features = w_t.shape[1]
    block = 2 * quarter
    out = jax.ShapeDtypeStruct
    if late:
        grads = [out((8, features // 8 + 16, 2 * wide), jnp.bfloat16)] * 2
    else:
        grads = [out((3 * wide, features), jnp.float32), out((8, 3 * wide), jnp.float32)]
    outs = [out((2, quarter, features), jnp.bfloat16)] * 2 + grads
    scratch = [
        pltpu.VMEM((4, wide, quarter), jnp.bfloat16),
        pltpu.VMEM((2, wide, block), jnp.bfloat16),
        pltpu.VMEM((2, 3 * wide, block), jnp.bfloat16),
        pltpu.VMEM((3 * wide, 4 * quarter), jnp.bfloat16),
        pltpu.VMEM((4 * quarter, features), jnp.bfloat16),
        pltpu.VMEM((3 * wide, features), jnp.float32),
        pltpu.VMEM((4, quarter, features), jnp.bfloat16),
        pltpu.SemaphoreType.DMA((6,)),
    ]
    found = kernel_call(
        functools.partial(attend_backward, heads, index),
        places,
        [*pieces, w_t, *kept, *before, *late],
        outs,
        scratch,
        left_in=(5, 9) if before else (5,),
        left_out=(0, 1),
    )
    return found[:2], found[2:]

def live_rows(places, rows, mine, local_rows, offset):
    row = lax.broadcasted_iota(jnp.int32, (rows, 1), 0)
    length = jnp.zeros((rows, 1), jnp.int32)
    for s in range(rows // local_rows):
        length = jnp.where(row >= s * local_rows, places[offset + s], length)
    position = mine * local_rows + lax.rem(row, local_rows)
    return jnp.where(position < length, 1.0, 0.0)


def normal_parts(array_in):
    centered = array_in - jnp.mean(array_in, axis=1, keepdims=True)
    spread = jnp.mean(centered * centered, axis=1, keepdims=True)
    inverse = lax.rsqrt(spread + EPSILON)
    return centered * inverse, inverse


def normal_back(hat, inverse, gain, d_out):
    scaled = d_out * gain
    mean_scaled = jnp.mean(scaled, axis=1, keepdims=True)
    mean_product = jnp.mean(scaled * hat, axis=1, keepdims=True)
    return inverse * (scaled - mean_scaled - hat * mean_product)


def column_sum(array_in):
    return jnp.sum(array_in, axis=0, keepdims=True)


def token_layer(shape, places, *refs):
    seq_count, seq_parts = shape
    count = seq_count * seq_parts
    pieces, refs = refs[:count], refs[count:]
    tokens, cot_in, w_out, vectors, b_up, w_up_in, w_down_in = refs[:7]
    out, send_down1, send_up1, send_down0, send_up0, keep_down, keep_up = refs[7:14]
    d_first_in, sums, grad_out, send_out = refs[14:18]
    sent = refs[18:24]
    (
        w_up, w_down, active, slope, context, first_in, first_norm, lowered,
        first_low, first_t, d_lowered, turned, out_s, cot, grad_down, grad_up, sems,
    ) = refs[24:]
    rows, features = tokens.shape
    local_rows = rows // seq_count
    wide = features // seq_parts
    mine, inner = places[9], places[8]
    step = pl.program_id(0)
    quarters = w_up.shape[0]
    width = w_up.shape[2]
    f32, bf16 = jnp.float32, jnp.bfloat16

    def bring(j):
        return (
            pltpu.make_async_copy(
                w_up_in.at[:, pl.ds(j * width, width)], w_up.at[j], sems.at[j]
            ),
            pltpu.make_async_copy(
                w_down_in.at[pl.ds(j * width, width), :], w_down.at[j], sems.at[quarters + j]
            ),
        )

    keep_out = pltpu.make_async_copy(out_s, out, sems.at[2 * quarters])
    bring_cot = pltpu.make_async_copy(cot_in, cot, sems.at[2 * quarters + 1])

    def leave(relative):
        down_ref, up_ref = (
            (keep_down.at[pl.ds(0, 2)], keep_up.at[pl.ds(0, 2)]),
            (keep_down.at[pl.ds(2, 2)], keep_up.at[pl.ds(2, 2)]),
            (send_down0, send_up0),
            (send_down1, send_up1),
        )[relative]
        first = 2 * quarters + 2 + 2 * relative
        return (
            pltpu.make_async_copy(grad_down.at[relative & 1], down_ref, sems.at[first]),
            pltpu.make_async_copy(grad_up.at[relative & 1], up_ref, sems.at[first + 1]),
        )

    @pl.when(step == 0)
    def start():
        for j in range(quarters):
            for copy in bring(j):
                copy.start()
        bring_cot.start()
        for s in range(seq_count):
            for r in range(seq_parts):
                context[
                    pl.ds(pl.multiple_of((r ^ mine) * wide, wide), wide),
                    s * local_rows : (s + 1) * local_rows,
                ] = pieces[s * seq_parts + r][...]
        live = live_rows(places, rows, mine, local_rows, 11)
        attended = dot_f32(context[...], w_out[...], TN) + vectors[0:1, :]
        total = jnp.where(live > 0, tokens[...].astype(f32), 0.0) + attended
        first_in[...] = total
        hat, _ = normal_parts(total)
        normed = hat * vectors[1:2, :] + vectors[2:3, :]
        first_norm[...] = normed
        low = normed.astype(bf16)
        first_low[...] = low
        tile = features // 4
        low_t = low.T
        for q in range(4):
            first_t[pl.ds(pl.multiple_of((q ^ inner) * tile, tile), tile), :] = low_t[
                q * tile : (q + 1) * tile
            ]
        lowered[...] = jnp.zeros_like(lowered)
        sums[...] = jnp.zeros_like(sums)

    @pl.when(step < quarters)
    def forward():
        for j in range(quarters):

            @pl.when(step == j)
            def arrive():
                for copy in bring(j):
                    copy.wait()

        lifted = dot_f32(first_low[...], w_up[step], NN) + b_up[step]
        cdf = 0.5 * (1.0 + lax.erf(lifted * 0.7071067811865476))
        density = jnp.exp(lifted * lifted * -0.5) * 0.3989422804014327
        gelu = (lifted * cdf).astype(bf16)
        active[step] = gelu
        slope[step] = (cdf + lifted * density).astype(bf16)
        lowered[...] += dot_f32(gelu, w_down[step], NN)

    @pl.when(step == quarters - 1)
    def turn():
        live = live_rows(places, rows, mine, local_rows, 11)
        hat, inverse = normal_parts(first_norm[...] + (lowered[...] + vectors[3:4, :]))
        gain = vectors[4:5, :]
        bring_cot.wait()
        out_s[...] = ((hat * gain + vectors[5:6, :]) * live).astype(bf16)
        keep_out.start()
        incoming = cot[...].astype(f32) * live
        back = normal_back(hat, inverse, gain, incoming)
        lowered[...] = back
        low = back.astype(bf16)
        d_lowered[...] = low
        sums[0:1, :] = column_sum(low.astype(f32))
        sums[1:2, :] = column_sum(incoming * hat)
        sums[2:3, :] = column_sum(incoming)

    @pl.when(step >= quarters)
    def backward():
        relative = 2 * quarters - 1 - step
        quarter = relative ^ (places[0] >> 1)
        low_bit = places[0] & 1
        slot = relative & 1
        half = width // 2
        tile = half // 4
        for k in range(2):

            @pl.when(relative == k)
            def free():
                for copy in leave(k + 2):
                    copy.wait()

        down = dot_f32(active[quarter], d_lowered[...], TN).astype(bf16)
        for j in range(2):
            for q in range(4):
                grad_down[
                    slot, j ^ low_bit, pl.ds(pl.multiple_of((q ^ inner) * tile, tile), tile), :
                ] = down[j * half + q * tile : j * half + (q + 1) * tile]
        d_active = dot_f32(d_lowered[...], w_down[quarter], NT)
        d_lifted = (d_active * slope[quarter].astype(f32)).astype(bf16)
        up = dot_f32(first_t[...], d_lifted, NN).astype(bf16)
        for j in range(2):
            grad_up[slot, j ^ low_bit] = up[:, j * half : (j + 1) * half]
        sums[pl.ds(6 + quarter, 1), :] = column_sum(d_lifted.astype(f32))
        lowered[...] += dot_f32(d_lifted, w_up[quarter], NT)
        for k in range(quarters):

            @pl.when(relative == k)
            def start_leaving():
                for copy in leave(k):
                    copy.start()

    @pl.when(step == 2 * quarters - 1)
    def finish():
        hat, inverse = normal_parts(first_in[...])
        incoming = lowered[...]
        back = normal_back(hat, inverse, vectors[1:2, :], incoming)
        d_first_in[...] = back
        low = back.astype(bf16)
        sums[3:4, :] = column_sum(low.astype(f32))
        sums[4:5, :] = column_sum(incoming * hat)
        sums[5:6, :] = column_sum(incoming)
        turned[...] = dot_f32(w_out[...], low, NT).astype(bf16)
        for r in range(seq_parts):
            own = turned[pl.ds(pl.multiple_of((r ^ mine) * wide, wide), wide), :]
            for s in range(seq_count):
                target, place = sent[3 * min(s, 1) + min(r, 2)], max(s - 1, 0)
                columns = own[:, s * local_rows : (s + 1) * local_rows]
                if r < 2:
                    target[place] = columns
                else:
                    target[r - 2, place] = columns
        product = dot_f32(context[...], low, NN).astype(bf16)
        block_rows, block_cols = grad_out.shape[2:]
        across = features // block_cols
        for j in range(seq_parts):
            for q in range(wide // block_rows * across):
                row, col = j * wide + q // across * block_rows, q % across * block_cols
                block = product[row : row + block_rows, col : col + block_cols]
                place, inner_place = j ^ mine, q ^ places[10]

                @pl.when(place < 2)
                def own():
                    grad_out[place, inner_place] = block

                @pl.when(place >= 2)
                def across_x():
                    send_out[place - 2, inner_place] = block

        keep_out.wait()
        for k in range(2):
            for copy in leave(k):
                copy.wait()


def whole_spec(shape):
    return pl.BlockSpec(
        shape, lambda p, places: (0,) * len(shape), pipeline_mode=pl.Buffered(buffer_count=1)
    )


def step_call(body, places, steps, ins, in_specs, outs, out_specs, scratch, flops, aliases={}):
    return pl.pallas_call(
        body,
        out_shape=outs,
        grid_spec=pltpu.PrefetchScalarGridSpec(
            num_scalar_prefetch=1,
            grid=(steps,),
            in_specs=in_specs,
            out_specs=out_specs,
            scratch_shapes=scratch,
        ),
        input_output_aliases=aliases,
        compiler_params=pltpu.CompilerParams(vmem_limit_bytes=VMEM_LIMIT),
        cost_estimate=pl.CostEstimate(
            flops=flops, transcendentals=0, bytes_accessed=1024 * 1024
        ),
    )(places, *ins)


def run_token_layer(places, pieces, tokens, cot, w_out, vectors, w_up, b_up, w_down, dims):
    seq_count, seq_parts = dims
    rows, features = tokens.shape
    hidden = w_up.shape[1]
    quarters = 4
    width = hidden // quarters
    half = width // 2
    out, bf16, f32 = jax.ShapeDtypeStruct, jnp.bfloat16, jnp.float32
    square, turned = (rows, features), (features, rows)
    piece = (features // seq_parts, rows // seq_count)
    sent = []
    for n in (1, seq_count - 1):
        sent += [(n, *piece), (n, *piece), (2, n, *piece)]
    out_blocks = (seq_parts // 2, 8, features // seq_parts // 2, features // 4)
    away = pl.BlockSpec(memory_space=pl.ANY)
    down, up = (2, half, features), (2, features, half)

    return step_call(
        functools.partial(token_layer, dims),
        places,
        2 * quarters,
        [*pieces, tokens, cot, w_out, vectors, b_up.reshape(quarters, 1, width), w_up, w_down],
        [whole_spec(p.shape) for p in pieces]
        + [whole_spec(square), away, whole_spec(w_out.shape), whole_spec(vectors.shape)]
        + [whole_spec((quarters, 1, width)), away, away],
        [
            out(square, bf16),
            out(down, bf16),
            out(up, bf16),
            out(down, bf16),
            out(up, bf16),
            out((4, half, features), bf16),
            out((4, features, half), bf16),
            out(square, f32),
            out((16, features), f32),
            out(out_blocks, bf16),
            out(out_blocks, bf16),
        ]
        + [out(p, bf16) for p in sent],
        [away] * 7
        + [whole_spec(square), whole_spec((16, features))]
        + [whole_spec(out_blocks)] * 2
        + [whole_spec(p) for p in sent],
        [
            pltpu.VMEM((quarters, features, width), bf16),
            pltpu.VMEM((quarters, width, features), bf16),
            pltpu.VMEM((quarters, rows, width), bf16),
            pltpu.VMEM((quarters, rows, width), bf16),
            pltpu.VMEM(turned, bf16),
            pltpu.VMEM(square, f32),
            pltpu.VMEM(square, f32),
            pltpu.VMEM(square, f32),
            pltpu.VMEM(square, bf16),
            pltpu.VMEM(turned, bf16),
            pltpu.VMEM(square, bf16),
            pltpu.VMEM(turned, bf16),
            pltpu.VMEM(square, bf16),
            pltpu.VMEM(square, bf16),
            pltpu.VMEM((2, *down), bf16),
            pltpu.VMEM((2, *up), bf16),
            pltpu.SemaphoreType.DMA((4 * quarters + 2,)),
        ],
        2 * rows * features * (6 * hidden + 3 * features),
    )


def place_tiles(count, split, x, places, *refs):
    sources, out = refs[:count], refs[-4]
    held, main, sems = refs[-3:]
    inner = places[8]
    _, rows, cols = sources[0].shape
    bring = [
        pltpu.make_async_copy(source, held.at[k], sems.at[k]) for k, source in enumerate(sources)
    ]
    for copy in bring:
        copy.start()
    sent = []
    for k, copy in enumerate(bring):
        copy.wait()
        for n in range(2 if split else 8):
            slot = sems.at[count + len(sent)]
            if split:
                block = places[k * 4 + x * 2 + n]
                for q in range(4):
                    first = pl.multiple_of((q ^ inner) * rows, rows)
                    main[2 * k + n, pl.ds(first, rows), :] = held[
                        k, n * 4 + (q & 1) * 2 + (q >> 1)
                    ].astype(jnp.float32)
                target = out.at[:, pl.ds(pl.multiple_of(block * cols, cols), cols)]
                sent.append(pltpu.make_async_copy(main.at[2 * k + n], target, slot))
            else:
                l, y, h = n >> 2, (n >> 1) & 1, n & 1
                block = places[k * 4 + y * 2 + l] * 4 + ((h * 2 + x) ^ inner)
                main[8 * k + n] = held[k, n].astype(jnp.float32)
                target = out.at[pl.ds(pl.multiple_of(block * rows, rows), rows)]
                sent.append(pltpu.make_async_copy(main.at[8 * k + n], target, slot))
            sent[-1].start()
    for copy in sent:
        copy.wait()


def gather_tiles(places, pieces, late, begun, shape, split):
    _, rows, cols = pieces[0].shape
    count = len(pieces)
    away = pl.BlockSpec(memory_space=pl.ANY)
    main = (2 * count, 4 * rows, cols) if split else (8 * count, rows, cols)
    return pl.pallas_call(
        functools.partial(place_tiles, count, split, late),
        out_shape=jax.ShapeDtypeStruct(shape, jnp.float32),
        in_specs=[pl.BlockSpec(memory_space=pltpu.SMEM)] + [away] * (count + len(begun)),
        out_specs=away,
        scratch_shapes=[
            pltpu.VMEM((count, 8, rows, cols), jnp.bfloat16),
            pltpu.VMEM(main, jnp.float32),
            pltpu.SemaphoreType.DMA((count + main[0],)),
        ],
        input_output_aliases={count + 1: 0} if begun else {},
        compiler_params=pltpu.CompilerParams(vmem_limit_bytes=VMEM_LIMIT),
    )(places, *pieces, *begun)


def place_heads(seq_parts, places, *refs):
    sources, refs = refs[: 2 * seq_parts], refs[2 * seq_parts :]
    out, out_w, vector_rows, head_rows = refs[:4]
    pieces = refs[4 : seq_parts + 4]
    main, side, sems = refs[seq_parts + 4 :]
    mine, inner = places[9], places[10]
    blocks, rows, _ = main.shape
    features = side.shape[2]
    wide = features // seq_parts
    f32 = jnp.float32
    half = blocks // 2
    bring = [
        pltpu.make_async_copy(
            source, pieces[i >> 1].at[pl.ds((i & 1) * half, half)], sems.at[2 * blocks + i]
        )
        for i, source in enumerate(sources)
    ]
    for copy in bring:
        copy.start()
    for copy in bring:
        copy.wait()

    def leave(p, source, target, slot):
        first = pl.multiple_of(p * rows, rows)
        return pltpu.make_async_copy(source.at[p], target.at[pl.ds(first, rows)], sems.at[slot + p])

    def one_block(p, carry):
        for m in range(seq_parts):

            @pl.when(mine == m)
            def copy():
                parts = [pieces[j ^ m][p ^ inner, :rows, : 3 * wide] for j in range(seq_parts)]
                for section in range(3):
                    columns = slice(section * wide, (section + 1) * wide)
                    joined = jnp.concatenate([part[:, columns] for part in parts], axis=1)
                    main[p, :, section * features : (section + 1) * features] = joined.astype(f32)

        leave(p, main, out, 0).start()
        for r, piece in enumerate(pieces):

            @pl.when(((r ^ mine) == p >> 1))
            def copy_side():
                first = (p & 1) * 4
                joined = jnp.concatenate(
                    [piece[(first + q) ^ inner, :rows, 3 * wide :] for q in range(4)], axis=1
                )
                side[p] = joined.astype(f32)

        leave(p, side, out_w, blocks).start()
        return carry

    lax.fori_loop(0, blocks, one_block, 0)
    for m in range(seq_parts):

        @pl.when(mine == m)
        def copy_vectors():
            held = [pieces[j ^ m][inner, rows:, :].astype(f32) for j in range(seq_parts)]
            total = held[0]
            for other in held[1:]:
                total = total + other
            vector_rows[...] = total
            head_rows[...] = jnp.zeros_like(head_rows)
            for j in range(seq_parts):
                head_rows[j : j + 1, :] = held[j][10:11, :]

    for p in range(blocks):
        leave(p, main, out, 0).wait()
        leave(p, side, out_w, blocks).wait()


def gather_heads(places, halves, shape):
    out, f32 = jax.ShapeDtypeStruct, jnp.float32
    features = shape[0]
    rows = features // 8
    extra = (halves[0].shape[1] - rows, features)
    count = len(halves) // 2
    piece = (8, *halves[0].shape[1:])
    away = pl.BlockSpec(memory_space=pl.ANY)
    here = pl.BlockSpec(memory_space=pltpu.VMEM)
    return pl.pallas_call(
        functools.partial(place_heads, count),
        out_shape=[
            out(shape, f32),
            out((features, features), f32),
            out(extra, f32),
            out((8, features), f32),
        ],
        in_specs=[pl.BlockSpec(memory_space=pltpu.SMEM)] + [away] * len(halves),
        out_specs=[away, away, here, here],
        scratch_shapes=[pltpu.VMEM(piece, halves[0].dtype)] * count
        + [
            pltpu.VMEM((8, rows, shape[1]), f32),
            pltpu.VMEM((8, rows, features), f32),
            pltpu.SemaphoreType.DMA((16 + len(halves),)),
        ],
        compiler_params=pltpu.CompilerParams(vmem_limit_bytes=VMEM_LIMIT),
    )(places, *halves)


def per_device(
    tokens,
    cotangent,
    lengths,
    block_perm,
    w_qkv,
    b_query,
    b_value,
    w_out,
    b_out,
    ln1_gain,
    ln1_shift,
    w_up,
    b_up,
    w_down,
    b_down,
    ln2_gain,
    ln2_shift,
):
    seq_parts = lax.axis_size("seq")
    mine = lax.axis_index("seq")
    seq_count, local_rows, features = tokens.shape
    flat_rows = seq_count * local_rows
    hidden = w_up.shape[1]
    heads = HEADS // seq_parts
    wide = heads * HEAD_DIM
    dims = (seq_count, seq_parts)
    f32 = jnp.float32

    w_heads = jnp.concatenate(
        [
            lax.dynamic_slice_in_dim(w_qkv, k * features + mine * wide, wide, axis=1)
            for k in range(3)
        ],
        axis=1,
    )
    w_t = w_heads.T
    bias = jnp.concatenate(
        [
            lax.dynamic_slice_in_dim(b_query, mine * wide, wide),
            jnp.zeros((wide,), b_query.dtype),
            lax.dynamic_slice_in_dim(b_value, mine * wide, wide),
        ]
    ).astype(f32)[:, None]
    outer = own_number("cyl")
    places = jnp.concatenate(
        [
            jnp.arange(8, dtype=jnp.int32) ^ outer,
            jnp.stack([own_number("hx"), mine, own_number("ylh")]),
            lengths,
            block_perm.reshape(-1),
        ]
    )
    vectors = jnp.stack(
        [v.astype(f32) for v in (b_out, ln1_gain, ln1_shift, b_down, ln2_gain, ln2_shift, b_out, b_out)]
    )

    arrived, kept, crossed = [], [], []
    for s in range(seq_count):
        near = tokens[s]
        start = near
        if s > 0:
            after = [crossed[-1]] + arrived[(s - 2) * seq_parts : (s - 2) * seq_parts + 1] * (s > 1)
            start, _ = lax.optimization_barrier((near, after))
        across = exchange_bit(start, "x")
        crossed.append(across)
        if s == 0:
            across, w_t, bias, places = lax.optimization_barrier((across, w_t, bias, places))
        if s > 0:
            across, _ = lax.optimization_barrier((across, arrived[-seq_parts]))
        pieces = [near, exchange_bit(near, "c"), across, exchange_bit(across, "c")]
        contexts, saved = attention_forward(places, pieces, s, w_t, bias, heads)
        kept.append(saved)
        arrived += [contexts[0]] + [exchange(contexts[r], "seq", r) for r in range(1, seq_parts)]

    (
        out_rows,
        send_down1,
        send_up1,
        send_down0,
        send_up0,
        keep_down,
        keep_up,
        d_first_in,
        sums,
        grad_out,
        send_out,
        *d_contexts,
    ) = run_token_layer(
        places,
        arrived,
        tokens.reshape(flat_rows, features),
        cotangent.reshape(flat_rows, features),
        w_out,
        vectors,
        w_up,
        b_up.astype(f32).reshape(1, hidden),
        w_down,
        dims,
    )
    out_tokens = out_rows.reshape(seq_count, local_rows, features)

    def hand_on(own, near, came):
        return [own, exchange_bit(near, "c"), came, exchange_bit(came[1], "c")]

    first_came = exchange_bit(d_contexts[2], "x")
    came_down1, came_up1 = exchange_bit(send_down1, "c"), exchange_bit(send_up1, "c")
    send_up0, first_came = lax.optimization_barrier((send_up0, first_came))
    came_up0 = exchange_bit(send_up0, "c")
    second_pair, first_came = lax.optimization_barrier((d_contexts[5], first_came))
    second_came = exchange_bit(second_pair, "x")
    parts, near, far = [], [], []

    def attend(s, group, before, late=()):
        found, total = attention_backward(places, group, s, w_t, kept[s], before, heads, late)
        parts.append(found)
        return total

    def cross(s):
        held, sent = parts[s]
        came = exchange_bit(sent, "c")
        near.append(held[0].astype(f32) + came[0])
        far.append(sum_low(held[1], came[1]))

    sends = [
        sum_low(keep_down[2:], came_down1),
        sum_low(keep_up[1::2], jnp.stack([came_up0[1], came_up1[1]])),
        send_out,
    ]
    sends, first_came = lax.optimization_barrier((sends, first_came))
    down_y, up_l, out_x = [exchange_bit(v, bit) for v, bit in zip(sends, "ylx")]
    came_down0 = exchange_bit(send_down0, "c")
    total = attend(0, hand_on(d_contexts[0], d_contexts[1], first_came), ())
    (down_y, up_l, out_x, total, parts[0], second_came, near_pair, came_down0) = (
        lax.optimization_barrier(
            (down_y, up_l, out_x, total, parts[0], second_came, d_contexts[3:5], came_down0)
        )
    )

    sends = [
        sum_low(keep_down[1], came_down0[1], down_y[1]),
        sum_low(keep_up[2], came_up1[0], up_l[1]),
        sum_low(grad_out[1], out_x[1]),
    ]
    (sends, total) = lax.optimization_barrier((sends, total))
    down_l, up_y, out_c = [exchange_bit(v, bit) for v, bit in zip(sends, "lyc")]
    cross(0)
    second_group = hand_on(*near_pair, second_came)
    for s in range(1, seq_count - 1):
        total = attend(s, second_group, total)
    out_own = sum_low(grad_out[0], out_x[0], out_c)
    (down_l, up_y, total, parts[1:], near, far, out_own) = lax.optimization_barrier(
        (down_l, up_y, total, parts[1:], near, far, out_own)
    )

    down_own = sum_low(keep_down[0], came_down0[0], down_y[0], down_l)
    down_own = down_own.reshape(2, 2, hidden // 32, features)
    up_own = sum_low(keep_up[0], came_up0[0], up_l[0], up_y)
    up_own = up_own.reshape(2, 2, features // 4, hidden // 8)
    keeps, sends = [down_own[:, 0], up_own[:, 0]], [down_own[:, 1], up_own[:, 1]]
    (keeps, sends, total) = lax.optimization_barrier((keeps, sends, total))
    got = [exchange_bit(v, "x") for v in sends]
    far_came = [exchange_bit(far[0], "x")]
    for s in range(1, seq_count - 1):
        cross(s)
    half_a, half_b = attend(seq_count - 1, second_group, total, (out_own, sums))

    (keeps, got, far, far_came, half_a, half_b, parts[-1]) = lax.optimization_barrier(
        (keeps, got, far, far_came, half_a, half_b, parts[-1])
    )
    down, up = [k + g for k, g in zip(keeps, got)]
    half_b = half_b.reshape(2, 2, 2, *half_b.shape[1:])
    keeps = [half_a[:4], half_b[:, 0], down]
    sends = [half_a[4:], half_b[:, 1], down]
    (keeps, sends, up) = lax.optimization_barrier((keeps, sends, up))
    got = [exchange_bit(v, bit) for v, bit in zip(sends, "ylh")]
    far_came += [exchange_bit(v, "x") for v in far[1:]]
    half_a, half_b, down = [k + g for k, g in zip(keeps, (*got[:2], got[2][::-1]))]
    far = []
    cross(seq_count - 1)

    keeps = [half_a[:2], half_b[0], up]
    sends = [half_a[2:], half_b[1], up]
    down = add_extra(down)
    (keeps, sends, down, far, near) = lax.optimization_barrier((keeps, sends, down, far, near))
    got = [exchange_bit(v, bit) for v, bit in zip(sends, "lyh")]
    down_came = exchange_bit(down, "y")
    far_came += [exchange_bit(v, "x") for v in far]
    half_a, half_b, up = [k + g for k, g in zip(keeps, (*got[:2], got[2][::-1]))]
    up = add_extra(up)
    both = jnp.concatenate([half_a, half_b], axis=2)
    down = jnp.concatenate([down, down_came])

    (both, down, up, far_came) = lax.optimization_barrier((both, down, up, far_came))
    came, up_came = exchange_bit(both, "h"), exchange_bit(up, "x")
    down = jnp.concatenate([down, exchange_bit(down, "l")])
    both = add_extra(both + came[::-1])
    up = jnp.concatenate([up, up_came])
    own_pos = mine * local_rows + jnp.arange(local_rows, dtype=jnp.int32)
    live = (own_pos[None, :] < lengths[:, None]).astype(f32)
    d_inputs = jnp.stack([n + f for n, f in zip(near, far_came)])
    grad_tokens = (d_inputs + d_first_in.reshape(seq_count, local_rows, features)) * live[:, :, None]


    (both, down, up, grad_tokens) = lax.optimization_barrier((both, down, up, grad_tokens))
    down_first = exchange_bit(down[:4], "x")
    came, up_came = exchange_bit(both, "y"), exchange_bit(up, "l")
    both = jnp.concatenate([both, came])
    up = jnp.concatenate([up, up_came])

    (both, down, down_first, up) = lax.optimization_barrier((both, down, down_first, up))
    came = exchange_bit(both, "l")
    down_second = exchange_bit(down[4:], "x")
    up_first = exchange_bit(up[:4], "y")
    down_near = exchange_bit(down, "c")
    down_last = jnp.concatenate([down_first, down_second])
    both = jnp.stack([both.reshape(2, 2, *both.shape[1:]), came.reshape(2, 2, *came.shape[1:])], 1)
    both = both.reshape(8, *both.shape[3:])

    (both, down, down_near, down_last, up, up_first) = lax.optimization_barrier(
        (both, down, down_near, down_last, up, up_first)
    )
    both_first = exchange_bit(both[:4], "x")
    up_second = exchange_bit(up[4:], "y")
    down_far = exchange_bit(down_last, "c")
    up_near = exchange_bit(up, "c")
    full_down = gather_tiles(places, [down, down_near], 0, [], (hidden, features), False)
    up_last = jnp.concatenate([up_first, up_second])

    (both, both_first, up, up_near, up_last, down_far, full_down) = lax.optimization_barrier(
        (both, both_first, up, up_near, up_last, down_far, full_down)
    )
    both_second = exchange_bit(both[4:], "x")
    up_far = exchange_bit(up_last, "c")
    both_near = exchange_bit(both, "c")
    full_down = gather_tiles(
        places, [down_last, down_far], 1, [full_down], (hidden, features), False
    )
    full_up = gather_tiles(places, [up, up_near], 0, [], (features, hidden), True)
    full_up = gather_tiles(places, [up_last, up_far], 1, [full_up], (features, hidden), True)

    (both_second, both_near, full_down, full_up) = lax.optimization_barrier(
        (both_second, both_near, full_down, full_up)
    )
    first_far, second_far = exchange_bit(both_first, "c"), exchange_bit(both_second, "c")
    full_qkv, full_out, vector_rows, head_rows = gather_heads(
        places,
        [both[:4], both[4:], both_near[:4], both_near[4:]]
        + [both_first, both_second, first_far, second_far],
        (features, 3 * features),
    )
    (
        full_b_down,
        full_gain_two,
        full_shift_two,
        full_b_out,
        full_gain_one,
        full_shift_one,
    ) = [vector_rows[i] for i in range(6)]
    full_b_up = vector_rows[6 : 6 + hidden // features].reshape(hidden)
    full_b_query = head_rows[:seq_parts, :wide].reshape(features)
    full_b_value = head_rows[:seq_parts, 2 * wide : 3 * wide].reshape(features)

    return (
        out_tokens,
        grad_tokens,
        full_qkv,
        full_b_query,
        full_b_value,
        full_out,
        full_b_out,
        full_gain_one,
        full_shift_one,
        full_up,
        full_b_up,
        full_down,
        full_b_down,
        full_gain_two,
        full_shift_two,
    )


def solution(mesh):
    in_specs = (
        P("dp", "seq", None),
        P("dp", "seq", None),
        P("dp"),
        P("dp", None),
        P(),
        P(),
        P(),
        P(),
        P(),
        P(),
        P(),
        P(),
        P(),
        P(),
        P(),
        P(),
        P(),
    )
    out_specs = (
        P("dp", "seq", None),
        P("dp", "seq", None),
        P(),
        P(),
        P(),
        P(),
        P(),
        P(),
        P(),
        P(),
        P(),
        P(),
        P(),
        P(),
        P(),
    )
    return jax.shard_map(
        per_device, mesh=mesh, in_specs=in_specs, out_specs=out_specs, check_vma=False
    )
```

```python
import functools
import jax
import jax.numpy as jnp
from jax import lax
from jax.experimental import pallas as pl
from jax.experimental.pallas import tpu as pltpu
from jax.sharding import PartitionSpec as P

HEAD_DIM = 64
SOFT = HEAD_DIM ** -0.5 * 1.4426950408889634
NN = (((1,), (0,)), ((), ()))
NT = (((1,), (1,)), ((), ()))
TN = (((0,), (0,)), ((), ()))
VMEM_LIMIT = 60 * 1024 * 1024
HEADS = 12
EPSILON = 1e-06
BITS = {"c": ("seq", 0), "x": ("seq", 1), "y": ("dp", 0), "l": ("dp", 1), "h": ("dp", 2)}


def own_number(order):
    number = jnp.int32(0)
    for letter in order:
        axis, shift = BITS[letter]
        number = number * 2 + ((lax.axis_index(axis) >> shift) & 1)
    return number


def exchange(array_in, axis, flip):
    return lax.ppermute(array_in, axis, [(i, i ^ flip) for i in range(lax.axis_size(axis))])


def exchange_bit(array_in, letter):
    axis, shift = BITS[letter]
    return exchange(array_in, axis, 1 << shift)


def extra_flips(axis, used):
    return [1 << shift for shift in range(used, lax.axis_size(axis).bit_length() - 1)]


def add_extra(array_in):
    for flip in extra_flips("dp", 3):
        array_in = array_in + exchange(array_in, "dp", flip)
    return array_in


def sum_low(*parts):
    total = parts[0].astype(jnp.float32)
    for part in parts[1:]:
        total = total + part.astype(jnp.float32)
    return total.astype(jnp.bfloat16)


def dot_f32(left, right, dims):
    return lax.dot_general(left, right, dims, preferred_element_type=jnp.float32)


def sequence_scalars(places, index):
    seq_count = (places.shape[0] - 11) // 3
    return places[11 + index] >> 1, places[9], 11 + seq_count + 2 * index


def shift_matrix(half, block, whole):
    row = lax.broadcasted_iota(jnp.int32, (block, whole), 0)
    col = lax.broadcasted_iota(jnp.int32, (block, whole), 1)
    return jnp.where((col == row + half) & (row < half), 1.0, 0.0).astype(jnp.bfloat16)


def mask_tiles(half, block):
    row = lax.broadcasted_iota(jnp.int32, (16, block), 0)
    col = lax.broadcasted_iota(jnp.int32, (16, block), 1)
    key_tile = jnp.where((row == 0) & (col >= half), -1e30, 0.0).astype(jnp.bfloat16)
    query_tile = jnp.where(row == 0, 1.0, 0.0).astype(jnp.bfloat16)
    return key_tile, query_tile


def attend_forward(
    heads, index, places, x0, x1, x2, x3, w_t, bias, c0, c1, c2, c3,
    x_out, qkv_out, ctx_blk, lse, tok, c_tok, x_seq, qkv, sems,
):
    half, mine, perm = sequence_scalars(places, index)
    whole = x_seq.shape[0]
    quarter = whole // 4
    block = whole // 2
    wide = heads * HEAD_DIM
    for r, piece in enumerate((x0, x1, x2, x3)):
        x_seq[pl.ds(pl.multiple_of((r ^ mine) * quarter, quarter), quarter), :] = piece[...]
    keep_x = pltpu.make_async_copy(x_seq, x_out, sems.at[0])
    keep_x.start()
    lane = lax.broadcasted_iota(jnp.int32, (1, block), 1)
    tok[...] = (dot_f32(w_t[...], x_seq[...], NT) + bias[...]).astype(jnp.bfloat16)
    shift = shift_matrix(half, block, whole)
    qkv[0] = jnp.where(lane < half, tok[:, :block], jnp.zeros((), jnp.bfloat16))
    qkv[1] = dot_f32(tok[...], shift, NT).astype(jnp.bfloat16)
    keep_qkv = pltpu.make_async_copy(qkv, qkv_out, sems.at[1])
    keep_qkv.start()
    key_tile, query_tile = mask_tiles(half, block)

    def one_block(b, carry):
        target = places[perm + b]
        for h in range(heads):
            rows = slice(h * HEAD_DIM, (h + 1) * HEAD_DIM)
            q_t = jnp.concatenate([qkv[b, rows, :], query_tile])
            k_t = jnp.concatenate(
                [qkv[target, wide + h * HEAD_DIM : wide + (h + 1) * HEAD_DIM, :], key_tile]
            )
            v_t = qkv[target, 2 * wide + h * HEAD_DIM : 2 * wide + (h + 1) * HEAD_DIM, :]
            scores = dot_f32(k_t, q_t, TN) * SOFT
            top = jnp.max(scores, axis=0, keepdims=True)
            expo = jnp.exp2(scores - top)
            total = jnp.sum(expo, axis=0, keepdims=True)
            context = dot_f32(v_t, expo.astype(jnp.bfloat16), NN) / total
            ctx_blk[b, rows, :] = context
            lse[b, h : h + 1, :] = top + jnp.log2(total)
        return carry

    lax.fori_loop(0, 2, one_block, 0)
    early = jnp.where(lane < half, ctx_blk[0], 0.0)
    late = dot_f32(ctx_blk[1].astype(jnp.bfloat16), shift, NN)
    for j in range(4):
        part = late[:, j * quarter : (j + 1) * quarter]
        if j < 2:
            part = part + early[:, j * quarter : (j + 1) * quarter]
        c_tok[j] = part.astype(jnp.bfloat16)
    for r, piece in enumerate((c0, c1, c2, c3)):
        piece[...] = c_tok[r ^ mine]
    keep_x.wait()
    keep_qkv.wait()


def attend_backward(
    heads, index, places, g0, g1, g2, g3, w_t, x_in, qkv, ctx_blk, lse, *refs
):
    first, last = index == 0, len(refs) > 14
    acc_in, acc_b = (None, None) if first else refs[:2]
    (dx_keep, dx_send, grad_w, grad_w2, g_tok, g_blk, d_qkv, tok, x_seq, acc, dx_s, sems) = refs[-12:]
    bring_x = pltpu.make_async_copy(x_in, x_seq, sems.at[0])
    bring_x.start()
    if not first:
        bring_acc = pltpu.make_async_copy(acc_in, acc, sems.at[1])
        bring_acc.start()
    half, mine, perm = sequence_scalars(places, index)
    index = max(index - 1, 0)
    quarter = g0.shape[2]
    block = 2 * quarter
    whole = 4 * quarter
    wide = heads * HEAD_DIM
    for r, piece in enumerate((g0[index], g1[index], g2[0, index], g3[index])):
        g_tok[r ^ mine] = piece
    shift = shift_matrix(half, block, whole)
    lane = lax.broadcasted_iota(jnp.int32, (1, block), 1)
    g_all = jnp.concatenate([g_tok[j] for j in range(4)], axis=1)
    g_blk[0] = jnp.where(lane < half, g_all[:, :block], jnp.zeros((), jnp.bfloat16))
    g_blk[1] = dot_f32(g_all, shift, NT).astype(jnp.bfloat16)
    key_tile, query_tile = mask_tiles(half, block)

    def one_block(b, carry):
        target = places[perm + b]
        for h in range(heads):
            rows = slice(h * HEAD_DIM, (h + 1) * HEAD_DIM)
            k_rows = slice(wide + h * HEAD_DIM, wide + (h + 1) * HEAD_DIM)
            v_rows = slice(2 * wide + h * HEAD_DIM, 2 * wide + (h + 1) * HEAD_DIM)
            q_t = qkv[b, rows, :]
            k_t = qkv[target, k_rows, :]
            v_t = qkv[target, v_rows, :]
            g_t = g_blk[b, rows, :]
            scores = dot_f32(
                jnp.concatenate([k_t, key_tile]), jnp.concatenate([q_t, query_tile]), TN
            )
            probs = jnp.exp2(scores * SOFT - lse[b, h : h + 1, :])
            d_probs = dot_f32(v_t, g_t, TN)
            delta = jnp.sum(ctx_blk[b, rows, :] * g_t.astype(jnp.float32), axis=0, keepdims=True)
            d_scores = (probs * (d_probs - delta)).astype(jnp.bfloat16)
            scaling = HEAD_DIM ** -0.5
            d_qkv[b, rows, :] = (dot_f32(k_t, d_scores, NN) * scaling).astype(jnp.bfloat16)
            d_qkv[target, k_rows, :] = (dot_f32(q_t, d_scores, NT) * scaling).astype(jnp.bfloat16)
            d_qkv[target, v_rows, :] = dot_f32(g_t, probs.astype(jnp.bfloat16), NT).astype(
                jnp.bfloat16
            )
        return carry

    lax.fori_loop(0, 2, one_block, 0)
    late = dot_f32(d_qkv[1], shift, NN)
    front = jnp.where(lane < half, d_qkv[0].astype(jnp.float32), 0.0)
    tok[:, block:] = late[:, block:].astype(jnp.bfloat16)
    tok[:, :block] = (late[:, :block] + front).astype(jnp.bfloat16)
    sent = []
    for r in range(4):
        piece = (dx_send if r & 1 else dx_keep).at[r >> 1]
        columns = tok[:, pl.ds(pl.multiple_of((r ^ mine) * quarter, quarter), quarter)]
        dx_s[r] = dot_f32(columns, w_t[...], TN).astype(jnp.bfloat16)
        sent.append(pltpu.make_async_copy(dx_s.at[r], piece, sems.at[2 + r]))
        sent[-1].start()
    bring_x.wait()
    total = dot_f32(tok[...], x_seq[...], NN)
    ones = jnp.ones((8, whole), jnp.bfloat16)
    sums = dot_f32(ones, tok[...], NT)
    if not first:
        bring_acc.wait()
        total, sums = total + acc[...], sums + acc_b[...]
    if last:
        out_own, vectors = refs[2:4]
        inner = places[10]
        turned = total.T.astype(jnp.bfloat16)
        tile = out_own.shape[1]
        extra = grad_w.shape[1] - tile
        for half_w in (grad_w, grad_w2):
            half_w[:, tile:, :] = jnp.zeros((8, extra, 2 * wide), jnp.bfloat16)
        for q in range(8):
            rows = slice(q * tile, (q + 1) * tile)
            grad_w[q ^ inner, :tile, :] = turned[rows, : 2 * wide]
            grad_w2[q ^ inner, :tile, :wide] = turned[rows, 2 * wide :]
        grad_w2[:, :tile, wide:] = out_own[...]
        row = lax.broadcasted_iota(jnp.int32, (extra, 1), 0)
        own_row = jnp.concatenate([sums[0:1, :], jnp.zeros((1, wide), jnp.float32)], axis=1)
        tile_rows = jnp.where(row == 10, own_row, vectors[...]).astype(jnp.bfloat16)
        grad_w[inner, tile:, :] = tile_rows[:, : 2 * wide]
        grad_w2[inner, tile:, :] = tile_rows[:, 2 * wide :]
    else:
        grad_w[...] = total
        grad_w2[...] = sums
    for copy in sent:
        copy.wait()


def kernel_call(body, scalars, arrays, outs, scratch, left_in=(), left_out=()):
    def spec(away):
        return pl.BlockSpec(memory_space=pl.ANY if away else pltpu.VMEM)

    return pl.pallas_call(
        body,
        out_shape=outs,
        in_specs=[pl.BlockSpec(memory_space=pltpu.SMEM)]
        + [spec(i in left_in) for i in range(len(arrays))],
        out_specs=[spec(i in left_out) for i in range(len(outs))],
        scratch_shapes=scratch,
        compiler_params=pltpu.CompilerParams(vmem_limit_bytes=VMEM_LIMIT),
        cost_estimate=pl.CostEstimate(
            flops=10**8, transcendentals=0, bytes_accessed=1024 * 1024
        ),
    )(scalars, *arrays)


def attention_forward(places, pieces, index, w_t, bias, heads):
    quarter, features = pieces[0].shape
    whole, block, wide = 4 * quarter, 2 * quarter, heads * HEAD_DIM
    out = jax.ShapeDtypeStruct
    outs = [out((wide, quarter), jnp.bfloat16)] * 4 + [
        out((whole, features), jnp.bfloat16),
        out((2, 3 * wide, block), jnp.bfloat16),
        out((2, wide, block), jnp.float32),
        out((2, 8, block), jnp.float32),
    ]
    scratch = [
        pltpu.VMEM((3 * wide, whole), jnp.bfloat16),
        pltpu.VMEM((4, wide, quarter), jnp.bfloat16),
        pltpu.VMEM((whole, features), jnp.bfloat16),
        pltpu.VMEM((2, 3 * wide, block), jnp.bfloat16),
        pltpu.SemaphoreType.DMA((2,)),
    ]
    found = kernel_call(
        functools.partial(attend_forward, heads, index),
        places,
        [*pieces, w_t, bias],
        outs,
        scratch,
        left_out=(4, 5),
    )
    return found[:4], found[4:]


def attention_backward(places, pieces, index, w_t, kept, before, heads, late=()):
    _, wide, quarter = pieces[0].shape
    features = w_t.shape[1]
    block = 2 * quarter
    out = jax.ShapeDtypeStruct
    if late:
        grads = [out((8, features // 8 + 16, 2 * wide), jnp.bfloat16)] * 2
    else:
        grads = [out((3 * wide, features), jnp.float32), out((8, 3 * wide), jnp.float32)]
    outs = [out((2, quarter, features), jnp.bfloat16)] * 2 + grads
    scratch = [
        pltpu.VMEM((4, wide, quarter), jnp.bfloat16),
        pltpu.VMEM((2, wide, block), jnp.bfloat16),
        pltpu.VMEM((2, 3 * wide, block), jnp.bfloat16),
        pltpu.VMEM((3 * wide, 4 * quarter), jnp.bfloat16),
        pltpu.VMEM((4 * quarter, features), jnp.bfloat16),
        pltpu.VMEM((3 * wide, features), jnp.float32),
        pltpu.VMEM((4, quarter, features), jnp.bfloat16),
        pltpu.SemaphoreType.DMA((6,)),
    ]
    found = kernel_call(
        functools.partial(attend_backward, heads, index),
        places,
        [*pieces, w_t, *kept, *before, *late],
        outs,
        scratch,
        left_in=(5, 9) if before else (5,),
        left_out=(0, 1),
    )
    return found[:2], found[2:]

def live_rows(places, rows, mine, local_rows, offset):
    row = lax.broadcasted_iota(jnp.int32, (rows, 1), 0)
    length = jnp.zeros((rows, 1), jnp.int32)
    for s in range(rows // local_rows):
        length = jnp.where(row >= s * local_rows, places[offset + s], length)
    position = mine * local_rows + lax.rem(row, local_rows)
    return jnp.where(position < length, 1.0, 0.0)


def normal_parts(array_in):
    centered = array_in - jnp.mean(array_in, axis=1, keepdims=True)
    spread = jnp.mean(centered * centered, axis=1, keepdims=True)
    inverse = lax.rsqrt(spread + EPSILON)
    return centered * inverse, inverse


def normal_back(hat, inverse, gain, d_out):
    scaled = d_out * gain
    mean_scaled = jnp.mean(scaled, axis=1, keepdims=True)
    mean_product = jnp.mean(scaled * hat, axis=1, keepdims=True)
    return inverse * (scaled - mean_scaled - hat * mean_product)


def column_sum(array_in):
    return jnp.sum(array_in, axis=0, keepdims=True)


def token_layer(shape, places, *refs):
    seq_count, seq_parts = shape
    count = seq_count * seq_parts
    pieces, refs = refs[:count], refs[count:]
    tokens, cot_in, w_out, vectors, b_up, w_up_in, w_down_in = refs[:7]
    out, send_down1, send_up1, send_down0, send_up0, keep_down, keep_up = refs[7:14]
    d_first_in, sums, grad_out, send_out = refs[14:18]
    sent = refs[18:24]
    (
        w_up, w_down, active, slope, context, first_in, first_norm, lowered,
        first_low, first_t, d_lowered, turned, out_s, cot, grad_down, grad_up, sems,
    ) = refs[24:]
    rows, features = tokens.shape
    local_rows = rows // seq_count
    wide = features // seq_parts
    mine, inner = places[9], places[8]
    step = pl.program_id(0)
    quarters = w_up.shape[0]
    width = w_up.shape[2]
    f32, bf16 = jnp.float32, jnp.bfloat16

    def bring(j):
        return (
            pltpu.make_async_copy(
                w_up_in.at[:, pl.ds(j * width, width)], w_up.at[j], sems.at[j]
            ),
            pltpu.make_async_copy(
                w_down_in.at[pl.ds(j * width, width), :], w_down.at[j], sems.at[quarters + j]
            ),
        )

    keep_out = pltpu.make_async_copy(out_s, out, sems.at[2 * quarters])
    bring_cot = pltpu.make_async_copy(cot_in, cot, sems.at[2 * quarters + 1])

    def leave(relative):
        down_ref, up_ref = (
            (keep_down.at[pl.ds(0, 2)], keep_up.at[pl.ds(0, 2)]),
            (keep_down.at[pl.ds(2, 2)], keep_up.at[pl.ds(2, 2)]),
            (send_down0, send_up0),
            (send_down1, send_up1),
        )[relative]
        first = 2 * quarters + 2 + 2 * relative
        return (
            pltpu.make_async_copy(grad_down.at[relative & 1], down_ref, sems.at[first]),
            pltpu.make_async_copy(grad_up.at[relative & 1], up_ref, sems.at[first + 1]),
        )

    @pl.when(step == 0)
    def start():
        for j in range(quarters):
            for copy in bring(j):
                copy.start()
        bring_cot.start()
        for s in range(seq_count):
            for r in range(seq_parts):
                context[
                    pl.ds(pl.multiple_of((r ^ mine) * wide, wide), wide),
                    s * local_rows : (s + 1) * local_rows,
                ] = pieces[s * seq_parts + r][...]
        live = live_rows(places, rows, mine, local_rows, 11)
        attended = dot_f32(context[...], w_out[...], TN) + vectors[0:1, :]
        total = jnp.where(live > 0, tokens[...].astype(f32), 0.0) + attended
        first_in[...] = total
        hat, _ = normal_parts(total)
        normed = hat * vectors[1:2, :] + vectors[2:3, :]
        first_norm[...] = normed
        low = normed.astype(bf16)
        first_low[...] = low
        tile = features // 4
        low_t = low.T
        for q in range(4):
            first_t[pl.ds(pl.multiple_of((q ^ inner) * tile, tile), tile), :] = low_t[
                q * tile : (q + 1) * tile
            ]
        lowered[...] = jnp.zeros_like(lowered)
        sums[...] = jnp.zeros_like(sums)

    @pl.when(step < quarters)
    def forward():
        for j in range(quarters):

            @pl.when(step == j)
            def arrive():
                for copy in bring(j):
                    copy.wait()

        lifted = dot_f32(first_low[...], w_up[step], NN) + b_up[step]
        cdf = 0.5 * (1.0 + lax.erf(lifted * 0.7071067811865476))
        density = jnp.exp(lifted * lifted * -0.5) * 0.3989422804014327
        gelu = (lifted * cdf).astype(bf16)
        active[step] = gelu
        slope[step] = (cdf + lifted * density).astype(bf16)
        lowered[...] += dot_f32(gelu, w_down[step], NN)

    @pl.when(step == quarters - 1)
    def turn():
        live = live_rows(places, rows, mine, local_rows, 11)
        hat, inverse = normal_parts(first_norm[...] + (lowered[...] + vectors[3:4, :]))
        gain = vectors[4:5, :]
        bring_cot.wait()
        out_s[...] = ((hat * gain + vectors[5:6, :]) * live).astype(bf16)
        keep_out.start()
        incoming = cot[...].astype(f32) * live
        back = normal_back(hat, inverse, gain, incoming)
        lowered[...] = back
        low = back.astype(bf16)
        d_lowered[...] = low
        sums[0:1, :] = column_sum(low.astype(f32))
        sums[1:2, :] = column_sum(incoming * hat)
        sums[2:3, :] = column_sum(incoming)

    @pl.when(step >= quarters)
    def backward():
        relative = 2 * quarters - 1 - step
        quarter = relative ^ (places[0] >> 1)
        low_bit = places[0] & 1
        slot = relative & 1
        half = width // 2
        tile = half // 4
        for k in range(2):

            @pl.when(relative == k)
            def free():
                for copy in leave(k + 2):
                    copy.wait()

        down = dot_f32(active[quarter], d_lowered[...], TN).astype(bf16)
        for j in range(2):
            for q in range(4):
                grad_down[
                    slot, j ^ low_bit, pl.ds(pl.multiple_of((q ^ inner) * tile, tile), tile), :
                ] = down[j * half + q * tile : j * half + (q + 1) * tile]
        d_active = dot_f32(d_lowered[...], w_down[quarter], NT)
        d_lifted = (d_active * slope[quarter].astype(f32)).astype(bf16)
        up = dot_f32(first_t[...], d_lifted, NN).astype(bf16)
        for j in range(2):
            grad_up[slot, j ^ low_bit] = up[:, j * half : (j + 1) * half]
        sums[pl.ds(6 + quarter, 1), :] = column_sum(d_lifted.astype(f32))
        lowered[...] += dot_f32(d_lifted, w_up[quarter], NT)
        for k in range(quarters):

            @pl.when(relative == k)
            def start_leaving():
                for copy in leave(k):
                    copy.start()

    @pl.when(step == 2 * quarters - 1)
    def finish():
        hat, inverse = normal_parts(first_in[...])
        incoming = lowered[...]
        back = normal_back(hat, inverse, vectors[1:2, :], incoming)
        d_first_in[...] = back
        low = back.astype(bf16)
        sums[3:4, :] = column_sum(low.astype(f32))
        sums[4:5, :] = column_sum(incoming * hat)
        sums[5:6, :] = column_sum(incoming)
        turned[...] = dot_f32(w_out[...], low, NT).astype(bf16)
        for r in range(seq_parts):
            own = turned[pl.ds(pl.multiple_of((r ^ mine) * wide, wide), wide), :]
            for s in range(seq_count):
                target, place = sent[3 * min(s, 1) + min(r, 2)], max(s - 1, 0)
                columns = own[:, s * local_rows : (s + 1) * local_rows]
                if r < 2:
                    target[place] = columns
                else:
                    target[r - 2, place] = columns
        product = dot_f32(context[...], low, NN).astype(bf16)
        block_rows, block_cols = grad_out.shape[2:]
        across = features // block_cols
        for j in range(seq_parts):
            for q in range(wide // block_rows * across):
                row, col = j * wide + q // across * block_rows, q % across * block_cols
                block = product[row : row + block_rows, col : col + block_cols]
                place, inner_place = j ^ mine, q ^ places[10]

                @pl.when(place < 2)
                def own():
                    grad_out[place, inner_place] = block

                @pl.when(place >= 2)
                def across_x():
                    send_out[place - 2, inner_place] = block

        keep_out.wait()
        for k in range(2):
            for copy in leave(k):
                copy.wait()


def whole_spec(shape):
    return pl.BlockSpec(
        shape, lambda p, places: (0,) * len(shape), pipeline_mode=pl.Buffered(buffer_count=1)
    )


def step_call(body, places, steps, ins, in_specs, outs, out_specs, scratch, flops, aliases={}):
    return pl.pallas_call(
        body,
        out_shape=outs,
        grid_spec=pltpu.PrefetchScalarGridSpec(
            num_scalar_prefetch=1,
            grid=(steps,),
            in_specs=in_specs,
            out_specs=out_specs,
            scratch_shapes=scratch,
        ),
        input_output_aliases=aliases,
        compiler_params=pltpu.CompilerParams(vmem_limit_bytes=VMEM_LIMIT),
        cost_estimate=pl.CostEstimate(
            flops=flops, transcendentals=0, bytes_accessed=1024 * 1024
        ),
    )(places, *ins)


def run_token_layer(places, pieces, tokens, cot, w_out, vectors, w_up, b_up, w_down, dims):
    seq_count, seq_parts = dims
    rows, features = tokens.shape
    hidden = w_up.shape[1]
    quarters = 4
    width = hidden // quarters
    half = width // 2
    out, bf16, f32 = jax.ShapeDtypeStruct, jnp.bfloat16, jnp.float32
    square, turned = (rows, features), (features, rows)
    piece = (features // seq_parts, rows // seq_count)
    sent = []
    for n in (1, seq_count - 1):
        sent += [(n, *piece), (n, *piece), (2, n, *piece)]
    out_blocks = (seq_parts // 2, 8, features // seq_parts // 2, features // 4)
    away = pl.BlockSpec(memory_space=pl.ANY)
    down, up = (2, half, features), (2, features, half)

    return step_call(
        functools.partial(token_layer, dims),
        places,
        2 * quarters,
        [*pieces, tokens, cot, w_out, vectors, b_up.reshape(quarters, 1, width), w_up, w_down],
        [whole_spec(p.shape) for p in pieces]
        + [whole_spec(square), away, whole_spec(w_out.shape), whole_spec(vectors.shape)]
        + [whole_spec((quarters, 1, width)), away, away],
        [
            out(square, bf16),
            out(down, bf16),
            out(up, bf16),
            out(down, bf16),
            out(up, bf16),
            out((4, half, features), bf16),
            out((4, features, half), bf16),
            out(square, f32),
            out((16, features), f32),
            out(out_blocks, bf16),
            out(out_blocks, bf16),
        ]
        + [out(p, bf16) for p in sent],
        [away] * 7
        + [whole_spec(square), whole_spec((16, features))]
        + [whole_spec(out_blocks)] * 2
        + [whole_spec(p) for p in sent],
        [
            pltpu.VMEM((quarters, features, width), bf16),
            pltpu.VMEM((quarters, width, features), bf16),
            pltpu.VMEM((quarters, rows, width), bf16),
            pltpu.VMEM((quarters, rows, width), bf16),
            pltpu.VMEM(turned, bf16),
            pltpu.VMEM(square, f32),
            pltpu.VMEM(square, f32),
            pltpu.VMEM(square, f32),
            pltpu.VMEM(square, bf16),
            pltpu.VMEM(turned, bf16),
            pltpu.VMEM(square, bf16),
            pltpu.VMEM(turned, bf16),
            pltpu.VMEM(square, bf16),
            pltpu.VMEM(square, bf16),
            pltpu.VMEM((2, *down), bf16),
            pltpu.VMEM((2, *up), bf16),
            pltpu.SemaphoreType.DMA((4 * quarters + 2,)),
        ],
        2 * rows * features * (6 * hidden + 3 * features),
    )


def place_tiles(by_rows, late, places, *refs):
    sources, out = refs[:2], refs[-4]
    held, main, sems = refs[-3:]
    inner = places[8]
    _, rows, cols = sources[0].shape
    bring = [
        pltpu.make_async_copy(source, held.at[k], sems.at[k]) for k, source in enumerate(sources)
    ]
    for copy in bring:
        copy.start()
    sent = []
    for k, copy in enumerate(bring):
        copy.wait()
        for l in range(2):
            block = places[k * 4 + late * 2 + l]
            place = 2 * k + l
            for q in range(4):
                first = pl.multiple_of((q ^ inner) * rows, rows)
                main[place, pl.ds(first, rows), :] = held[k, l * 4 + (q & 1) * 2 + (q >> 1)].astype(
                    jnp.float32
                )
            if by_rows:
                target = out.at[pl.ds(pl.multiple_of(block * 4 * rows, 4 * rows), 4 * rows)]
            else:
                target = out.at[:, pl.ds(pl.multiple_of(block * cols, cols), cols)]
            sent.append(pltpu.make_async_copy(main.at[place], target, sems.at[2 + place]))
            sent[-1].start()
    for copy in sent:
        copy.wait()


def gather_tiles(places, pieces, late, begun, shape, by_rows):
    _, rows, cols = pieces[0].shape
    away = pl.BlockSpec(memory_space=pl.ANY)
    return pl.pallas_call(
        functools.partial(place_tiles, by_rows, late),
        out_shape=jax.ShapeDtypeStruct(shape, jnp.float32),
        in_specs=[pl.BlockSpec(memory_space=pltpu.SMEM)] + [away] * (2 + len(begun)),
        out_specs=away,
        scratch_shapes=[
            pltpu.VMEM((2, 8, rows, cols), jnp.bfloat16),
            pltpu.VMEM((4, 4 * rows, cols), jnp.float32),
            pltpu.SemaphoreType.DMA((6,)),
        ],
        input_output_aliases={3: 0} if begun else {},
        compiler_params=pltpu.CompilerParams(vmem_limit_bytes=VMEM_LIMIT),
    )(places, *pieces, *begun)


def place_heads(parts, places, *refs):
    seq_parts = parts[-1][0] + 1
    sources, refs = refs[: len(parts)], refs[len(parts) :]
    out, out_w, vector_rows, head_rows = refs[:4]
    pieces = refs[4 : seq_parts + 4]
    main, side, sems = refs[seq_parts + 4 :]
    mine, inner = places[9], places[10]
    blocks, rows, _ = main.shape
    features = side.shape[2]
    wide = features // seq_parts
    f32 = jnp.float32
    bring = [
        pltpu.make_async_copy(
            source, pieces[r].at[pl.ds(first, source.shape[0])], sems.at[2 * blocks + i]
        )
        for i, (source, (r, first)) in enumerate(zip(sources, parts))
    ]
    for copy in bring:
        copy.start()
    for copy in bring:
        copy.wait()

    def leave(p, source, target, slot):
        first = pl.multiple_of(p * rows, rows)
        return pltpu.make_async_copy(source.at[p], target.at[pl.ds(first, rows)], sems.at[slot + p])

    def one_block(p, carry):
        for m in range(seq_parts):

            @pl.when(mine == m)
            def copy():
                near = [pieces[j ^ m][p ^ inner, :rows, : 3 * wide] for j in range(seq_parts)]
                for section in range(3):
                    columns = slice(section * wide, (section + 1) * wide)
                    joined = jnp.concatenate([part[:, columns] for part in near], axis=1)
                    main[p, :, section * features : (section + 1) * features] = joined.astype(f32)

        leave(p, main, out, 0).start()
        for r, piece in enumerate(pieces):

            @pl.when(((r ^ mine) == p >> 1))
            def copy_side():
                first = (p & 1) * 4
                joined = jnp.concatenate(
                    [piece[(first + q) ^ inner, :rows, 3 * wide :] for q in range(4)], axis=1
                )
                side[p] = joined.astype(f32)

        leave(p, side, out_w, blocks).start()
        return carry

    lax.fori_loop(0, blocks, one_block, 0)
    for m in range(seq_parts):

        @pl.when(mine == m)
        def copy_vectors():
            held = [pieces[j ^ m][inner, rows:, :].astype(f32) for j in range(seq_parts)]
            total = held[0]
            for other in held[1:]:
                total = total + other
            vector_rows[...] = total
            head_rows[...] = jnp.zeros_like(head_rows)
            for j in range(seq_parts):
                head_rows[j : j + 1, :] = held[j][10:11, :]

    for p in range(blocks):
        leave(p, main, out, 0).wait()
        leave(p, side, out_w, blocks).wait()


def gather_heads(places, sources, parts, shape):
    out, f32 = jax.ShapeDtypeStruct, jnp.float32
    features = shape[0]
    rows = features // 8
    extra = (sources[0].shape[1] - rows, features)
    count = parts[-1][0] + 1
    piece = (8, *sources[0].shape[1:])
    away = pl.BlockSpec(memory_space=pl.ANY)
    here = pl.BlockSpec(memory_space=pltpu.VMEM)
    return pl.pallas_call(
        functools.partial(place_heads, parts),
        out_shape=[
            out(shape, f32),
            out((features, features), f32),
            out(extra, f32),
            out((8, features), f32),
        ],
        in_specs=[pl.BlockSpec(memory_space=pltpu.SMEM)] + [away] * len(sources),
        out_specs=[away, away, here, here],
        scratch_shapes=[pltpu.VMEM(piece, sources[0].dtype)] * count
        + [
            pltpu.VMEM((8, rows, shape[1]), f32),
            pltpu.VMEM((8, rows, features), f32),
            pltpu.SemaphoreType.DMA((16 + len(sources),)),
        ],
        compiler_params=pltpu.CompilerParams(vmem_limit_bytes=VMEM_LIMIT),
    )(places, *sources)


def per_device(
    tokens,
    cotangent,
    lengths,
    block_perm,
    w_qkv,
    b_query,
    b_value,
    w_out,
    b_out,
    ln1_gain,
    ln1_shift,
    w_up,
    b_up,
    w_down,
    b_down,
    ln2_gain,
    ln2_shift,
):
    seq_parts = lax.axis_size("seq")
    mine = lax.axis_index("seq")
    seq_count, local_rows, features = tokens.shape
    flat_rows = seq_count * local_rows
    hidden = w_up.shape[1]
    heads = HEADS // seq_parts
    wide = heads * HEAD_DIM
    dims = (seq_count, seq_parts)
    f32 = jnp.float32

    w_heads = jnp.concatenate(
        [
            lax.dynamic_slice_in_dim(w_qkv, k * features + mine * wide, wide, axis=1)
            for k in range(3)
        ],
        axis=1,
    )
    w_t = w_heads.T
    bias = jnp.concatenate(
        [
            lax.dynamic_slice_in_dim(b_query, mine * wide, wide),
            jnp.zeros((wide,), b_query.dtype),
            lax.dynamic_slice_in_dim(b_value, mine * wide, wide),
        ]
    ).astype(f32)[:, None]
    outer = own_number("cyl")
    places = jnp.concatenate(
        [
            jnp.arange(8, dtype=jnp.int32) ^ outer,
            jnp.stack([own_number("hx"), mine, own_number("ylh")]),
            lengths,
            block_perm.reshape(-1),
        ]
    )
    vectors = jnp.stack(
        [v.astype(f32) for v in (b_out, ln1_gain, ln1_shift, b_down, ln2_gain, ln2_shift, b_out, b_out)]
    )

    arrived, kept, crossed = [], [], []
    for s in range(seq_count):
        near = tokens[s]
        start = near
        if s > 0:
            after = [crossed[-1]] + arrived[(s - 2) * seq_parts : (s - 2) * seq_parts + 1] * (s > 1)
            start, _ = lax.optimization_barrier((near, after))
        across = exchange_bit(start, "x")
        crossed.append(across)
        if s == 0:
            across, w_t, bias, places = lax.optimization_barrier((across, w_t, bias, places))
        if s > 0:
            across, _ = lax.optimization_barrier((across, arrived[-seq_parts]))
        pieces = [near, exchange_bit(near, "c"), across, exchange_bit(across, "c")]
        contexts, saved = attention_forward(places, pieces, s, w_t, bias, heads)
        kept.append(saved)
        arrived += [contexts[0]] + [exchange(contexts[r], "seq", r) for r in range(1, seq_parts)]

    (
        out_rows,
        send_down1,
        send_up1,
        send_down0,
        send_up0,
        keep_down,
        keep_up,
        d_first_in,
        sums,
        grad_out,
        send_out,
        *d_contexts,
    ) = run_token_layer(
        places,
        arrived,
        tokens.reshape(flat_rows, features),
        cotangent.reshape(flat_rows, features),
        w_out,
        vectors,
        w_up,
        b_up.astype(f32).reshape(1, hidden),
        w_down,
        dims,
    )
    out_tokens = out_rows.reshape(seq_count, local_rows, features)

    def hand_on(own, near, came):
        return [own, exchange_bit(near, "c"), came, exchange_bit(came[1], "c")]

    first_came = exchange_bit(d_contexts[2], "x")
    came_down1, came_up1 = exchange_bit(send_down1, "c"), exchange_bit(send_up1, "c")
    send_up0, first_came = lax.optimization_barrier((send_up0, first_came))
    came_up0 = exchange_bit(send_up0, "c")
    second_pair, first_came = lax.optimization_barrier((d_contexts[5], first_came))
    second_came = exchange_bit(second_pair, "x")
    parts, near, far = [], [], []

    def attend(s, group, before, late=()):
        found, total = attention_backward(places, group, s, w_t, kept[s], before, heads, late)
        parts.append(found)
        return total

    def cross(s):
        held, sent = parts[s]
        came = exchange_bit(sent, "c")
        near.append(held[0].astype(f32) + came[0])
        far.append(sum_low(held[1], came[1]))

    sends = [
        sum_low(keep_down[2:], came_down1),
        sum_low(keep_up[1::2], jnp.stack([came_up0[1], came_up1[1]])),
    ]
    sends, first_came = lax.optimization_barrier((sends, first_came))
    down_y, up_l = [exchange_bit(v, bit) for v, bit in zip(sends, "yl")]
    came_down0 = exchange_bit(send_down0, "c")
    total = attend(0, hand_on(d_contexts[0], d_contexts[1], first_came), ())
    (total, parts[0], second_came, near_pair, came_down0, send_out) = lax.optimization_barrier(
        (total, parts[0], second_came, d_contexts[3:5], came_down0, send_out)
    )

    out_x = exchange_bit(send_out, "x")
    second_group = hand_on(*near_pair, second_came)
    cross(0)
    for s in range(1, seq_count - 1):
        total = attend(s, second_group, total)
    (down_y, up_l, out_x, total, parts[1:], near, far) = lax.optimization_barrier(
        (down_y, up_l, out_x, total, parts[1:], near, far)
    )

    sends = [
        sum_low(keep_down[1], came_down0[1], down_y[1]),
        sum_low(keep_up[2], came_up1[0], up_l[1]),
    ]
    out_c = exchange_bit(sum_low(grad_out[1], out_x[1]), "c")
    out_own = sum_low(grad_out[0], out_x[0], out_c)
    (sends, total, out_own, far) = lax.optimization_barrier((sends, total, out_own, far))
    down_l, up_y = [exchange_bit(v, bit) for v, bit in zip(sends, "ly")]
    far_came = [exchange_bit(far[0], "x")]
    for s in range(1, seq_count - 1):
        cross(s)
    half_a, half_b = attend(seq_count - 1, second_group, total, (out_own, sums))

    (down_l, up_y, far, far_came, half_a, half_b, parts[-1]) = lax.optimization_barrier(
        (down_l, up_y, far, far_came, half_a, half_b, parts[-1])
    )
    down_own = sum_low(keep_down[0], came_down0[0], down_y[0], down_l)
    down_own = down_own.reshape(2, 2, hidden // 32, features)
    up_own = sum_low(keep_up[0], came_up0[0], up_l[0], up_y)
    up_own = up_own.reshape(2, 2, features // 4, hidden // 8)
    half_b = half_b.reshape(2, 2, 2, *half_b.shape[1:])
    keeps = [half_a[:4], half_b[:, 0], down_own[:, 0], up_own[:, 0]]
    sends = [half_a[4:], half_b[:, 1], down_own[:, 1], up_own[:, 1]]
    (keeps, sends) = lax.optimization_barrier((keeps, sends))
    got = [exchange_bit(v, bit) for v, bit in zip(sends, "ylxx")]
    half_a, half_b, down, up = [k + g for k, g in zip(keeps, got)]
    near_far = far[1:]
    far = []
    cross(seq_count - 1)

    keeps, sends = [half_a[:2], half_b[0]], [half_a[2:], half_b[1]]
    (keeps, sends, down, up, far, near_far, near) = lax.optimization_barrier(
        (keeps, sends, down, up, far, near_far, near)
    )
    got = [exchange_bit(v, bit) for v, bit in zip(sends, "ly")]
    down_came = exchange_bit(down, "h")
    far_came += [exchange_bit(v, "x") for v in near_far]
    both = jnp.concatenate([k + g for k, g in zip(keeps, got)], axis=2)
    down = add_extra(down + down_came[::-1])

    (both, down, up, far, far_came) = lax.optimization_barrier((both, down, up, far, far_came))
    far_came += [exchange_bit(v, "x") for v in far]
    came = exchange_bit(both, "h")
    down = jnp.concatenate([down, exchange_bit(down, "x")])
    both = add_extra(both + came[::-1])

    (both, down, up, far_came) = lax.optimization_barrier((both, down, up, far_came))
    came, up_came = exchange_bit(both, "y"), exchange_bit(up, "h")
    down = jnp.concatenate([down, exchange_bit(down, "l")])
    both = jnp.concatenate([both, came])
    up = add_extra(up + up_came[::-1])
    own_pos = mine * local_rows + jnp.arange(local_rows, dtype=jnp.int32)
    live = (own_pos[None, :] < lengths[:, None]).astype(f32)
    d_inputs = jnp.stack([n + f for n, f in zip(near, far_came)])
    grad_tokens = (d_inputs + d_first_in.reshape(seq_count, local_rows, features)) * live[:, :, None]


    (both, down, up, grad_tokens) = lax.optimization_barrier((both, down, up, grad_tokens))
    came = exchange_bit(both, "l")
    down_first = exchange_bit(down[:4], "y")
    up_came = exchange_bit(up, "x")
    down_near = exchange_bit(down, "c")
    both = jnp.stack([both.reshape(2, 2, *both.shape[1:]), came.reshape(2, 2, *came.shape[1:])], 1)
    both = both.reshape(8, *both.shape[3:])
    up = jnp.concatenate([up, up_came])

    (both, down, down_near, down_first, up) = lax.optimization_barrier(
        (both, down, down_near, down_first, up)
    )
    both_first = exchange_bit(both[:4], "x")
    down_second = exchange_bit(down[4:], "y")
    up_came = exchange_bit(up, "l")
    full_down = gather_tiles(places, [down, down_near], 0, [], (hidden, features), True)
    down_last = jnp.concatenate([down_first, down_second])
    up = jnp.concatenate([up, up_came])

    (both, both_first, up, down_last, full_down) = lax.optimization_barrier(
        (both, both_first, up, down_last, full_down)
    )
    both_second = exchange_bit(both[4:], "x")
    up_first = exchange_bit(up[:4], "y")
    down_far = exchange_bit(down_last, "c")
    both_near, up_near = exchange_bit(both, "c"), exchange_bit(up, "c")
    full_down = gather_tiles(places, [down_last, down_far], 1, [full_down], (hidden, features), True)
    full_up = gather_tiles(places, [up, up_near], 0, [], (features, hidden), False)

    (both_second, both_near, up, up_first, full_down, full_up) = lax.optimization_barrier(
        (both_second, both_near, up, up_first, full_down, full_up)
    )
    up_second = exchange_bit(up[4:6], "y")
    first_far, second_far = exchange_bit(both_first, "c"), exchange_bit(both_second, "c")

    (up, up_second, first_far, second_far) = lax.optimization_barrier(
        (up, up_second, first_far, second_far)
    )
    up_third = exchange_bit(up[6:], "y")
    full_qkv, full_out, vector_rows, head_rows = gather_heads(
        places,
        [both, both_near, both_first, both_second, first_far, second_far],
        ((0, 0), (1, 0), (2, 0), (2, 4), (3, 0), (3, 4)),
        (features, 3 * features),
    )
    (up_third, full_qkv, vector_rows, head_rows) = lax.optimization_barrier(
        (up_third, full_qkv, vector_rows, head_rows)
    )
    up_last = jnp.concatenate([up_first, up_second, up_third])
    up_far = exchange_bit(up_last, "c")
    full_up = gather_tiles(places, [up_last, up_far], 1, [full_up], (features, hidden), False)
    (
        full_b_down,
        full_gain_two,
        full_shift_two,
        full_b_out,
        full_gain_one,
        full_shift_one,
    ) = [vector_rows[i] for i in range(6)]
    full_b_up = vector_rows[6 : 6 + hidden // features].reshape(hidden)
    full_b_query = head_rows[:seq_parts, :wide].reshape(features)
    full_b_value = head_rows[:seq_parts, 2 * wide : 3 * wide].reshape(features)

    return (
        out_tokens,
        grad_tokens,
        full_qkv,
        full_b_query,
        full_b_value,
        full_out,
        full_b_out,
        full_gain_one,
        full_shift_one,
        full_up,
        full_b_up,
        full_down,
        full_b_down,
        full_gain_two,
        full_shift_two,
    )


def solution(mesh):
    in_specs = (
        P("dp", "seq", None),
        P("dp", "seq", None),
        P("dp"),
        P("dp", None),
        P(),
        P(),
        P(),
        P(),
        P(),
        P(),
        P(),
        P(),
        P(),
        P(),
        P(),
        P(),
        P(),
    )
    out_specs = (
        P("dp", "seq", None),
        P("dp", "seq", None),
        P(),
        P(),
        P(),
        P(),
        P(),
        P(),
        P(),
        P(),
        P(),
        P(),
        P(),
        P(),
        P(),
    )
    return jax.shard_map(
        per_device, mesh=mesh, in_specs=in_specs, out_specs=out_specs, check_vma=False
    )
```

```python
import functools
import jax
import jax.numpy as jnp
from jax import lax
from jax.experimental import pallas as pl
from jax.experimental.pallas import tpu as pltpu
from jax.sharding import PartitionSpec as P

HEAD_DIM = 64
SOFT = HEAD_DIM ** -0.5 * 1.4426950408889634
NN = (((1,), (0,)), ((), ()))
NT = (((1,), (1,)), ((), ()))
TN = (((0,), (0,)), ((), ()))
VMEM_LIMIT = 60 * 1024 * 1024
HEADS = 12
EPSILON = 1e-06
BITS = {"c": ("seq", 0), "x": ("seq", 1), "y": ("dp", 0), "l": ("dp", 1), "h": ("dp", 2)}


def own_number(order):
    number = jnp.int32(0)
    for letter in order:
        axis, shift = BITS[letter]
        number = number * 2 + ((lax.axis_index(axis) >> shift) & 1)
    return number


def exchange(array_in, axis, flip):
    return lax.ppermute(array_in, axis, [(i, i ^ flip) for i in range(lax.axis_size(axis))])


def exchange_bit(array_in, letter):
    axis, shift = BITS[letter]
    return exchange(array_in, axis, 1 << shift)


def extra_flips(axis, used):
    return [1 << shift for shift in range(used, lax.axis_size(axis).bit_length() - 1)]


def add_extra(array_in):
    for flip in extra_flips("dp", 3):
        array_in = array_in + exchange(array_in, "dp", flip)
    return array_in


def sum_low(*parts):
    total = parts[0].astype(jnp.float32)
    for part in parts[1:]:
        total = total + part.astype(jnp.float32)
    return total.astype(jnp.bfloat16)


def dot_f32(left, right, dims):
    return lax.dot_general(left, right, dims, preferred_element_type=jnp.float32)


def sequence_scalars(places, index):
    seq_count = (places.shape[0] - 11) // 3
    return places[11 + index] >> 1, places[9], 11 + seq_count + 2 * index


def shift_matrix(half, block, whole):
    row = lax.broadcasted_iota(jnp.int32, (block, whole), 0)
    col = lax.broadcasted_iota(jnp.int32, (block, whole), 1)
    return jnp.where((col == row + half) & (row < half), 1.0, 0.0).astype(jnp.bfloat16)


def mask_tiles(half, block):
    row = lax.broadcasted_iota(jnp.int32, (16, block), 0)
    col = lax.broadcasted_iota(jnp.int32, (16, block), 1)
    key_tile = jnp.where((row == 0) & (col >= half), -1e30, 0.0).astype(jnp.bfloat16)
    query_tile = jnp.where(row == 0, 1.0, 0.0).astype(jnp.bfloat16)
    return key_tile, query_tile


def attend_forward(
    heads, index, places, x0, x1, x2, x3, w_t, bias, c0, c1, c2, c3,
    x_out, qkv_out, ctx_blk, lse, tok, c_tok, x_seq, qkv, sems,
):
    half, mine, perm = sequence_scalars(places, index)
    whole = x_seq.shape[0]
    quarter = whole // 4
    block = whole // 2
    wide = heads * HEAD_DIM
    for r, piece in enumerate((x0, x1, x2, x3)):
        x_seq[pl.ds(pl.multiple_of((r ^ mine) * quarter, quarter), quarter), :] = piece[...]
    keep_x = pltpu.make_async_copy(x_seq, x_out, sems.at[0])
    keep_x.start()
    lane = lax.broadcasted_iota(jnp.int32, (1, block), 1)
    tok[...] = (dot_f32(w_t[...], x_seq[...], NT) + bias[...]).astype(jnp.bfloat16)
    shift = shift_matrix(half, block, whole)
    qkv[0] = jnp.where(lane < half, tok[:, :block], jnp.zeros((), jnp.bfloat16))
    qkv[1] = dot_f32(tok[...], shift, NT).astype(jnp.bfloat16)
    keep_qkv = pltpu.make_async_copy(qkv, qkv_out, sems.at[1])
    keep_qkv.start()
    key_tile, query_tile = mask_tiles(half, block)

    def one_block(b, carry):
        target = places[perm + b]
        for h in range(heads):
            rows = slice(h * HEAD_DIM, (h + 1) * HEAD_DIM)
            q_t = jnp.concatenate([qkv[b, rows, :], query_tile])
            k_t = jnp.concatenate(
                [qkv[target, wide + h * HEAD_DIM : wide + (h + 1) * HEAD_DIM, :], key_tile]
            )
            v_t = qkv[target, 2 * wide + h * HEAD_DIM : 2 * wide + (h + 1) * HEAD_DIM, :]
            scores = dot_f32(k_t, q_t, TN) * SOFT
            top = jnp.max(scores, axis=0, keepdims=True)
            expo = jnp.exp2(scores - top)
            total = jnp.sum(expo, axis=0, keepdims=True)
            context = dot_f32(v_t, expo.astype(jnp.bfloat16), NN) / total
            ctx_blk[b, rows, :] = context
            lse[b, h : h + 1, :] = top + jnp.log2(total)
        return carry

    lax.fori_loop(0, 2, one_block, 0)
    early = jnp.where(lane < half, ctx_blk[0], 0.0)
    late = dot_f32(ctx_blk[1].astype(jnp.bfloat16), shift, NN)
    for j in range(4):
        part = late[:, j * quarter : (j + 1) * quarter]
        if j < 2:
            part = part + early[:, j * quarter : (j + 1) * quarter]
        c_tok[j] = part.astype(jnp.bfloat16)
    for r, piece in enumerate((c0, c1, c2, c3)):
        piece[...] = c_tok[r ^ mine]
    keep_x.wait()
    keep_qkv.wait()


def attend_backward(
    heads, index, places, g0, g1, g2, g3, w_t, x_in, qkv, ctx_blk, lse, *refs
):
    first, last = index == 0, len(refs) > 14
    acc_in, acc_b = (None, None) if first else refs[:2]
    (dx_keep, dx_send, grad_w, grad_w2, g_tok, g_blk, d_qkv, tok, x_seq, acc, dx_s, sems) = refs[-12:]
    bring_x = pltpu.make_async_copy(x_in, x_seq, sems.at[0])
    bring_x.start()
    if not first:
        bring_acc = pltpu.make_async_copy(acc_in, acc, sems.at[1])
        bring_acc.start()
    half, mine, perm = sequence_scalars(places, index)
    index = max(index - 1, 0)
    quarter = g0.shape[2]
    block = 2 * quarter
    whole = 4 * quarter
    wide = heads * HEAD_DIM
    for r, piece in enumerate((g0[index], g1[index], g2[0, index], g3[index])):
        g_tok[r ^ mine] = piece
    shift = shift_matrix(half, block, whole)
    lane = lax.broadcasted_iota(jnp.int32, (1, block), 1)
    g_all = jnp.concatenate([g_tok[j] for j in range(4)], axis=1)
    g_blk[0] = jnp.where(lane < half, g_all[:, :block], jnp.zeros((), jnp.bfloat16))
    g_blk[1] = dot_f32(g_all, shift, NT).astype(jnp.bfloat16)
    key_tile, query_tile = mask_tiles(half, block)

    def one_block(b, carry):
        target = places[perm + b]
        for h in range(heads):
            rows = slice(h * HEAD_DIM, (h + 1) * HEAD_DIM)
            k_rows = slice(wide + h * HEAD_DIM, wide + (h + 1) * HEAD_DIM)
            v_rows = slice(2 * wide + h * HEAD_DIM, 2 * wide + (h + 1) * HEAD_DIM)
            q_t = qkv[b, rows, :]
            k_t = qkv[target, k_rows, :]
            v_t = qkv[target, v_rows, :]
            g_t = g_blk[b, rows, :]
            scores = dot_f32(
                jnp.concatenate([k_t, key_tile]), jnp.concatenate([q_t, query_tile]), TN
            )
            probs = jnp.exp2(scores * SOFT - lse[b, h : h + 1, :])
            d_probs = dot_f32(v_t, g_t, TN)
            delta = jnp.sum(ctx_blk[b, rows, :] * g_t.astype(jnp.float32), axis=0, keepdims=True)
            d_scores = (probs * (d_probs - delta)).astype(jnp.bfloat16)
            scaling = HEAD_DIM ** -0.5
            d_qkv[b, rows, :] = (dot_f32(k_t, d_scores, NN) * scaling).astype(jnp.bfloat16)
            d_qkv[target, k_rows, :] = (dot_f32(q_t, d_scores, NT) * scaling).astype(jnp.bfloat16)
            d_qkv[target, v_rows, :] = dot_f32(g_t, probs.astype(jnp.bfloat16), NT).astype(
                jnp.bfloat16
            )
        return carry

    lax.fori_loop(0, 2, one_block, 0)
    late = dot_f32(d_qkv[1], shift, NN)
    front = jnp.where(lane < half, d_qkv[0].astype(jnp.float32), 0.0)
    tok[:, block:] = late[:, block:].astype(jnp.bfloat16)
    tok[:, :block] = (late[:, :block] + front).astype(jnp.bfloat16)
    sent = []
    for r in range(4):
        piece = (dx_send if r & 1 else dx_keep).at[r >> 1]
        columns = tok[:, pl.ds(pl.multiple_of((r ^ mine) * quarter, quarter), quarter)]
        dx_s[r] = dot_f32(columns, w_t[...], TN).astype(jnp.bfloat16)
        sent.append(pltpu.make_async_copy(dx_s.at[r], piece, sems.at[2 + r]))
        sent[-1].start()
    bring_x.wait()
    total = dot_f32(tok[...], x_seq[...], NN)
    ones = jnp.ones((8, whole), jnp.bfloat16)
    sums = dot_f32(ones, tok[...], NT)
    if not first:
        bring_acc.wait()
        total, sums = total + acc[...], sums + acc_b[...]
    if last:
        out_own, vectors = refs[2:4]
        inner = places[10]
        turned = total.T.astype(jnp.bfloat16)
        tile = out_own.shape[1]
        extra = grad_w.shape[1] - tile
        for half_w in (grad_w, grad_w2):
            half_w[:, tile:, :] = jnp.zeros((8, extra, 2 * wide), jnp.bfloat16)
        for q in range(8):
            rows = slice(q * tile, (q + 1) * tile)
            grad_w[q ^ inner, :tile, :] = turned[rows, : 2 * wide]
            grad_w2[q ^ inner, :tile, :wide] = turned[rows, 2 * wide :]
        grad_w2[:, :tile, wide:] = out_own[...]
        row = lax.broadcasted_iota(jnp.int32, (extra, 1), 0)
        own_row = jnp.concatenate([sums[0:1, :], jnp.zeros((1, wide), jnp.float32)], axis=1)
        tile_rows = jnp.where(row == 10, own_row, vectors[...]).astype(jnp.bfloat16)
        grad_w[inner, tile:, :] = tile_rows[:, : 2 * wide]
        grad_w2[inner, tile:, :] = tile_rows[:, 2 * wide :]
    else:
        grad_w[...] = total
        grad_w2[...] = sums
    for copy in sent:
        copy.wait()


def kernel_call(body, scalars, arrays, outs, scratch, left_in=(), left_out=()):
    def spec(away):
        return pl.BlockSpec(memory_space=pl.ANY if away else pltpu.VMEM)

    return pl.pallas_call(
        body,
        out_shape=outs,
        in_specs=[pl.BlockSpec(memory_space=pltpu.SMEM)]
        + [spec(i in left_in) for i in range(len(arrays))],
        out_specs=[spec(i in left_out) for i in range(len(outs))],
        scratch_shapes=scratch,
        compiler_params=pltpu.CompilerParams(vmem_limit_bytes=VMEM_LIMIT),
        cost_estimate=pl.CostEstimate(
            flops=10**8, transcendentals=0, bytes_accessed=1024 * 1024
        ),
    )(scalars, *arrays)


def attention_forward(places, pieces, index, w_t, bias, heads):
    quarter, features = pieces[0].shape
    whole, block, wide = 4 * quarter, 2 * quarter, heads * HEAD_DIM
    out = jax.ShapeDtypeStruct
    outs = [out((wide, quarter), jnp.bfloat16)] * 4 + [
        out((whole, features), jnp.bfloat16),
        out((2, 3 * wide, block), jnp.bfloat16),
        out((2, wide, block), jnp.float32),
        out((2, 8, block), jnp.float32),
    ]
    scratch = [
        pltpu.VMEM((3 * wide, whole), jnp.bfloat16),
        pltpu.VMEM((4, wide, quarter), jnp.bfloat16),
        pltpu.VMEM((whole, features), jnp.bfloat16),
        pltpu.VMEM((2, 3 * wide, block), jnp.bfloat16),
        pltpu.SemaphoreType.DMA((2,)),
    ]
    found = kernel_call(
        functools.partial(attend_forward, heads, index),
        places,
        [*pieces, w_t, bias],
        outs,
        scratch,
        left_out=(4, 5),
    )
    return found[:4], found[4:]


def attention_backward(places, pieces, index, w_t, kept, before, heads, late=()):
    _, wide, quarter = pieces[0].shape
    features = w_t.shape[1]
    block = 2 * quarter
    out = jax.ShapeDtypeStruct
    if late:
        grads = [out((8, features // 8 + 16, 2 * wide), jnp.bfloat16)] * 2
    else:
        grads = [out((3 * wide, features), jnp.float32), out((8, 3 * wide), jnp.float32)]
    outs = [out((2, quarter, features), jnp.bfloat16)] * 2 + grads
    scratch = [
        pltpu.VMEM((4, wide, quarter), jnp.bfloat16),
        pltpu.VMEM((2, wide, block), jnp.bfloat16),
        pltpu.VMEM((2, 3 * wide, block), jnp.bfloat16),
        pltpu.VMEM((3 * wide, 4 * quarter), jnp.bfloat16),
        pltpu.VMEM((4 * quarter, features), jnp.bfloat16),
        pltpu.VMEM((3 * wide, features), jnp.float32),
        pltpu.VMEM((4, quarter, features), jnp.bfloat16),
        pltpu.SemaphoreType.DMA((6,)),
    ]
    found = kernel_call(
        functools.partial(attend_backward, heads, index),
        places,
        [*pieces, w_t, *kept, *before, *late],
        outs,
        scratch,
        left_in=(5, 9) if before else (5,),
        left_out=(0, 1),
    )
    return found[:2], found[2:]

def live_rows(places, rows, mine, local_rows, offset):
    row = lax.broadcasted_iota(jnp.int32, (rows, 1), 0)
    length = jnp.zeros((rows, 1), jnp.int32)
    for s in range(rows // local_rows):
        length = jnp.where(row >= s * local_rows, places[offset + s], length)
    position = mine * local_rows + lax.rem(row, local_rows)
    return jnp.where(position < length, 1.0, 0.0)


def normal_parts(array_in):
    centered = array_in - jnp.mean(array_in, axis=1, keepdims=True)
    spread = jnp.mean(centered * centered, axis=1, keepdims=True)
    inverse = lax.rsqrt(spread + EPSILON)
    return centered * inverse, inverse


def normal_back(hat, inverse, gain, d_out):
    scaled = d_out * gain
    mean_scaled = jnp.mean(scaled, axis=1, keepdims=True)
    mean_product = jnp.mean(scaled * hat, axis=1, keepdims=True)
    return inverse * (scaled - mean_scaled - hat * mean_product)


def column_sum(array_in):
    return jnp.sum(array_in, axis=0, keepdims=True)


def token_layer(shape, places, *refs):
    seq_count, seq_parts = shape
    count = seq_count * seq_parts
    pieces, refs = refs[:count], refs[count:]
    tokens, cot_in, w_out, vectors, b_up, w_up_in, w_down_in = refs[:7]
    out, send_down1, send_up1, send_down0, send_up0, keep_down, keep_up = refs[7:14]
    d_first_in, sums, grad_out, send_out = refs[14:18]
    sent = refs[18:24]
    (
        w_up, w_down, active, slope, context, first_in, first_norm, lowered,
        first_low, first_t, d_lowered, turned, out_s, cot, grad_down, grad_up, sems,
    ) = refs[24:]
    rows, features = tokens.shape
    local_rows = rows // seq_count
    wide = features // seq_parts
    mine, inner = places[9], places[8]
    step = pl.program_id(0)
    quarters = w_up.shape[0]
    width = w_up.shape[2]
    f32, bf16 = jnp.float32, jnp.bfloat16

    def bring(j):
        return (
            pltpu.make_async_copy(
                w_up_in.at[:, pl.ds(j * width, width)], w_up.at[j], sems.at[j]
            ),
            pltpu.make_async_copy(
                w_down_in.at[pl.ds(j * width, width), :], w_down.at[j], sems.at[quarters + j]
            ),
        )

    keep_out = pltpu.make_async_copy(out_s, out, sems.at[2 * quarters])
    bring_cot = pltpu.make_async_copy(cot_in, cot, sems.at[2 * quarters + 1])

    def leave(relative):
        down_ref, up_ref = (
            (keep_down.at[pl.ds(0, 2)], keep_up.at[pl.ds(0, 2)]),
            (keep_down.at[pl.ds(2, 2)], keep_up.at[pl.ds(2, 2)]),
            (send_down0, send_up0),
            (send_down1, send_up1),
        )[relative]
        first = 2 * quarters + 2 + 2 * relative
        return (
            pltpu.make_async_copy(grad_down.at[relative & 1], down_ref, sems.at[first]),
            pltpu.make_async_copy(grad_up.at[relative & 1], up_ref, sems.at[first + 1]),
        )

    @pl.when(step == 0)
    def start():
        for j in range(quarters):
            for copy in bring(j):
                copy.start()
        bring_cot.start()
        for s in range(seq_count):
            for r in range(seq_parts):
                context[
                    pl.ds(pl.multiple_of((r ^ mine) * wide, wide), wide),
                    s * local_rows : (s + 1) * local_rows,
                ] = pieces[s * seq_parts + r][...]
        live = live_rows(places, rows, mine, local_rows, 11)
        attended = dot_f32(context[...], w_out[...], TN) + vectors[0:1, :]
        total = jnp.where(live > 0, tokens[...].astype(f32), 0.0) + attended
        first_in[...] = total
        hat, _ = normal_parts(total)
        normed = hat * vectors[1:2, :] + vectors[2:3, :]
        first_norm[...] = normed
        low = normed.astype(bf16)
        first_low[...] = low
        tile = features // 4
        low_t = low.T
        for q in range(4):
            first_t[pl.ds(pl.multiple_of((q ^ inner) * tile, tile), tile), :] = low_t[
                q * tile : (q + 1) * tile
            ]
        lowered[...] = jnp.zeros_like(lowered)
        sums[...] = jnp.zeros_like(sums)

    @pl.when(step < quarters)
    def forward():
        for j in range(quarters):

            @pl.when(step == j)
            def arrive():
                for copy in bring(j):
                    copy.wait()

        lifted = dot_f32(first_low[...], w_up[step], NN) + b_up[step]
        cdf = 0.5 * (1.0 + lax.erf(lifted * 0.7071067811865476))
        density = jnp.exp(lifted * lifted * -0.5) * 0.3989422804014327
        gelu = (lifted * cdf).astype(bf16)
        active[step] = gelu
        slope[step] = (cdf + lifted * density).astype(bf16)
        lowered[...] += dot_f32(gelu, w_down[step], NN)

    @pl.when(step == quarters - 1)
    def turn():
        live = live_rows(places, rows, mine, local_rows, 11)
        hat, inverse = normal_parts(first_norm[...] + (lowered[...] + vectors[3:4, :]))
        gain = vectors[4:5, :]
        bring_cot.wait()
        out_s[...] = ((hat * gain + vectors[5:6, :]) * live).astype(bf16)
        keep_out.start()
        incoming = cot[...].astype(f32) * live
        back = normal_back(hat, inverse, gain, incoming)
        lowered[...] = back
        low = back.astype(bf16)
        d_lowered[...] = low
        sums[0:1, :] = column_sum(low.astype(f32))
        sums[1:2, :] = column_sum(incoming * hat)
        sums[2:3, :] = column_sum(incoming)

    @pl.when(step >= quarters)
    def backward():
        relative = 2 * quarters - 1 - step
        quarter = relative ^ (places[0] >> 1)
        low_bit = places[0] & 1
        slot = relative & 1
        half = width // 2
        tile = half // 4
        for k in range(2):

            @pl.when(relative == k)
            def free():
                for copy in leave(k + 2):
                    copy.wait()

        down = dot_f32(active[quarter], d_lowered[...], TN).astype(bf16)
        for j in range(2):
            for q in range(4):
                grad_down[
                    slot, j ^ low_bit, pl.ds(pl.multiple_of((q ^ inner) * tile, tile), tile), :
                ] = down[j * half + q * tile : j * half + (q + 1) * tile]
        d_active = dot_f32(d_lowered[...], w_down[quarter], NT)
        d_lifted = (d_active * slope[quarter].astype(f32)).astype(bf16)
        up = dot_f32(first_t[...], d_lifted, NN).astype(bf16)
        for j in range(2):
            grad_up[slot, j ^ low_bit] = up[:, j * half : (j + 1) * half]
        sums[pl.ds(6 + quarter, 1), :] = column_sum(d_lifted.astype(f32))
        lowered[...] += dot_f32(d_lifted, w_up[quarter], NT)
        for k in range(quarters):

            @pl.when(relative == k)
            def start_leaving():
                for copy in leave(k):
                    copy.start()

    @pl.when(step == 2 * quarters - 1)
    def finish():
        hat, inverse = normal_parts(first_in[...])
        incoming = lowered[...]
        back = normal_back(hat, inverse, vectors[1:2, :], incoming)
        d_first_in[...] = back
        low = back.astype(bf16)
        sums[3:4, :] = column_sum(low.astype(f32))
        sums[4:5, :] = column_sum(incoming * hat)
        sums[5:6, :] = column_sum(incoming)
        turned[...] = dot_f32(w_out[...], low, NT).astype(bf16)
        for r in range(seq_parts):
            own = turned[pl.ds(pl.multiple_of((r ^ mine) * wide, wide), wide), :]
            for s in range(seq_count):
                target, place = sent[3 * min(s, 1) + min(r, 2)], max(s - 1, 0)
                columns = own[:, s * local_rows : (s + 1) * local_rows]
                if r < 2:
                    target[place] = columns
                else:
                    target[r - 2, place] = columns
        product = dot_f32(context[...], low, NN).astype(bf16)
        block_rows, block_cols = grad_out.shape[2:]
        across = features // block_cols
        for j in range(seq_parts):
            for q in range(wide // block_rows * across):
                row, col = j * wide + q // across * block_rows, q % across * block_cols
                block = product[row : row + block_rows, col : col + block_cols]
                place, inner_place = j ^ mine, q ^ places[10]

                @pl.when(place < 2)
                def own():
                    grad_out[place, inner_place] = block

                @pl.when(place >= 2)
                def across_x():
                    send_out[place - 2, inner_place] = block

        keep_out.wait()
        for k in range(2):
            for copy in leave(k):
                copy.wait()


def whole_spec(shape):
    return pl.BlockSpec(
        shape, lambda p, places: (0,) * len(shape), pipeline_mode=pl.Buffered(buffer_count=1)
    )


def step_call(body, places, steps, ins, in_specs, outs, out_specs, scratch, flops, aliases={}):
    return pl.pallas_call(
        body,
        out_shape=outs,
        grid_spec=pltpu.PrefetchScalarGridSpec(
            num_scalar_prefetch=1,
            grid=(steps,),
            in_specs=in_specs,
            out_specs=out_specs,
            scratch_shapes=scratch,
        ),
        input_output_aliases=aliases,
        compiler_params=pltpu.CompilerParams(vmem_limit_bytes=VMEM_LIMIT),
        cost_estimate=pl.CostEstimate(
            flops=flops, transcendentals=0, bytes_accessed=1024 * 1024
        ),
    )(places, *ins)


def run_token_layer(places, pieces, tokens, cot, w_out, vectors, w_up, b_up, w_down, dims):
    seq_count, seq_parts = dims
    rows, features = tokens.shape
    hidden = w_up.shape[1]
    quarters = 4
    width = hidden // quarters
    half = width // 2
    out, bf16, f32 = jax.ShapeDtypeStruct, jnp.bfloat16, jnp.float32
    square, turned = (rows, features), (features, rows)
    piece = (features // seq_parts, rows // seq_count)
    sent = []
    for n in (1, seq_count - 1):
        sent += [(n, *piece), (n, *piece), (2, n, *piece)]
    out_blocks = (seq_parts // 2, 8, features // seq_parts // 2, features // 4)
    away = pl.BlockSpec(memory_space=pl.ANY)
    down, up = (2, half, features), (2, features, half)

    return step_call(
        functools.partial(token_layer, dims),
        places,
        2 * quarters,
        [*pieces, tokens, cot, w_out, vectors, b_up.reshape(quarters, 1, width), w_up, w_down],
        [whole_spec(p.shape) for p in pieces]
        + [whole_spec(square), away, whole_spec(w_out.shape), whole_spec(vectors.shape)]
        + [whole_spec((quarters, 1, width)), away, away],
        [
            out(square, bf16),
            out(down, bf16),
            out(up, bf16),
            out(down, bf16),
            out(up, bf16),
            out((4, half, features), bf16),
            out((4, features, half), bf16),
            out(square, f32),
            out((16, features), f32),
            out(out_blocks, bf16),
            out(out_blocks, bf16),
        ]
        + [out(p, bf16) for p in sent],
        [away] * 7
        + [whole_spec(square), whole_spec((16, features))]
        + [whole_spec(out_blocks)] * 2
        + [whole_spec(p) for p in sent],
        [
            pltpu.VMEM((quarters, features, width), bf16),
            pltpu.VMEM((quarters, width, features), bf16),
            pltpu.VMEM((quarters, rows, width), bf16),
            pltpu.VMEM((quarters, rows, width), bf16),
            pltpu.VMEM(turned, bf16),
            pltpu.VMEM(square, f32),
            pltpu.VMEM(square, f32),
            pltpu.VMEM(square, f32),
            pltpu.VMEM(square, bf16),
            pltpu.VMEM(turned, bf16),
            pltpu.VMEM(square, bf16),
            pltpu.VMEM(turned, bf16),
            pltpu.VMEM(square, bf16),
            pltpu.VMEM(square, bf16),
            pltpu.VMEM((2, *down), bf16),
            pltpu.VMEM((2, *up), bf16),
            pltpu.SemaphoreType.DMA((4 * quarters + 2,)),
        ],
        2 * rows * features * (6 * hidden + 3 * features),
    )


def place_tiles(by_rows, late, places, *refs):
    sources, out = refs[:4], refs[-4]
    held, main, sems = refs[-3:]
    inner = places[8]
    _, rows, cols = sources[0].shape
    bring = [
        pltpu.make_async_copy(source, held.at[k], sems.at[k]) for k, source in enumerate(sources)
    ]
    for copy in bring:
        copy.start()
    for copy in bring:
        copy.wait()
    sent = []
    for k in range(2):
        for l in range(2):
            block = places[k * 4 + late * 2 + l]
            place = 2 * k + l
            for q in range(4):
                h, x = q >> 1, q & 1
                half, n = (x, l * 2 + h) if by_rows else (l, x * 2 + h)
                first = pl.multiple_of((q ^ inner) * rows, rows)
                main[place, pl.ds(first, rows), :] = held[2 * k + half, n].astype(jnp.float32)
            if by_rows:
                target = out.at[pl.ds(pl.multiple_of(block * 4 * rows, 4 * rows), 4 * rows)]
            else:
                target = out.at[:, pl.ds(pl.multiple_of(block * cols, cols), cols)]
            sent.append(pltpu.make_async_copy(main.at[place], target, sems.at[4 + place]))
            sent[-1].start()
    for copy in sent:
        copy.wait()


def gather_tiles(places, halves, late, begun, shape, by_rows):
    _, rows, cols = halves[0].shape
    away = pl.BlockSpec(memory_space=pl.ANY)
    return pl.pallas_call(
        functools.partial(place_tiles, by_rows, late),
        out_shape=jax.ShapeDtypeStruct(shape, jnp.float32),
        in_specs=[pl.BlockSpec(memory_space=pltpu.SMEM)] + [away] * (4 + len(begun)),
        out_specs=away,
        scratch_shapes=[
            pltpu.VMEM((4, 4, rows, cols), jnp.bfloat16),
            pltpu.VMEM((4, 4 * rows, cols), jnp.float32),
            pltpu.SemaphoreType.DMA((8,)),
        ],
        input_output_aliases={5: 0} if begun else {},
        compiler_params=pltpu.CompilerParams(vmem_limit_bytes=VMEM_LIMIT),
    )(places, *halves, *begun)


def place_heads(parts, places, *refs):
    seq_parts = parts[-1][0] + 1
    sources, refs = refs[: len(parts)], refs[len(parts) :]
    out, out_w, vector_rows, head_rows = refs[:4]
    pieces = refs[4 : seq_parts + 4]
    main, side, sems = refs[seq_parts + 4 :]
    mine, inner = places[9], places[10]
    blocks, rows, _ = main.shape
    features = side.shape[2]
    wide = features // seq_parts
    f32 = jnp.float32
    bring = [
        pltpu.make_async_copy(
            source, pieces[r].at[pl.ds(first, source.shape[0])], sems.at[2 * blocks + i]
        )
        for i, (source, (r, first)) in enumerate(zip(sources, parts))
    ]
    for copy in bring:
        copy.start()
    for copy in bring:
        copy.wait()

    def leave(p, source, target, slot):
        first = pl.multiple_of(p * rows, rows)
        return pltpu.make_async_copy(source.at[p], target.at[pl.ds(first, rows)], sems.at[slot + p])

    def one_block(p, carry):
        for m in range(seq_parts):

            @pl.when(mine == m)
            def copy():
                near = [pieces[j ^ m][p ^ inner, :rows, : 3 * wide] for j in range(seq_parts)]
                for section in range(3):
                    columns = slice(section * wide, (section + 1) * wide)
                    joined = jnp.concatenate([part[:, columns] for part in near], axis=1)
                    main[p, :, section * features : (section + 1) * features] = joined.astype(f32)

        leave(p, main, out, 0).start()
        for r, piece in enumerate(pieces):

            @pl.when(((r ^ mine) == p >> 1))
            def copy_side():
                first = (p & 1) * 4
                joined = jnp.concatenate(
                    [piece[(first + q) ^ inner, :rows, 3 * wide :] for q in range(4)], axis=1
                )
                side[p] = joined.astype(f32)

        leave(p, side, out_w, blocks).start()
        return carry

    lax.fori_loop(0, blocks, one_block, 0)
    for m in range(seq_parts):

        @pl.when(mine == m)
        def copy_vectors():
            held = [pieces[j ^ m][inner, rows:, :].astype(f32) for j in range(seq_parts)]
            total = held[0]
            for other in held[1:]:
                total = total + other
            vector_rows[...] = total
            head_rows[...] = jnp.zeros_like(head_rows)
            for j in range(seq_parts):
                head_rows[j : j + 1, :] = held[j][10:11, :]

    for p in range(blocks):
        leave(p, main, out, 0).wait()
        leave(p, side, out_w, blocks).wait()


def gather_heads(places, sources, parts, shape):
    out, f32 = jax.ShapeDtypeStruct, jnp.float32
    features = shape[0]
    rows = features // 8
    extra = (sources[0].shape[1] - rows, features)
    count = parts[-1][0] + 1
    piece = (8, *sources[0].shape[1:])
    away = pl.BlockSpec(memory_space=pl.ANY)
    here = pl.BlockSpec(memory_space=pltpu.VMEM)
    return pl.pallas_call(
        functools.partial(place_heads, parts),
        out_shape=[
            out(shape, f32),
            out((features, features), f32),
            out(extra, f32),
            out((8, features), f32),
        ],
        in_specs=[pl.BlockSpec(memory_space=pltpu.SMEM)] + [away] * len(sources),
        out_specs=[away, away, here, here],
        scratch_shapes=[pltpu.VMEM(piece, sources[0].dtype)] * count
        + [
            pltpu.VMEM((8, rows, shape[1]), f32),
            pltpu.VMEM((8, rows, features), f32),
            pltpu.SemaphoreType.DMA((16 + len(sources),)),
        ],
        compiler_params=pltpu.CompilerParams(vmem_limit_bytes=VMEM_LIMIT),
    )(places, *sources)


def per_device(
    tokens,
    cotangent,
    lengths,
    block_perm,
    w_qkv,
    b_query,
    b_value,
    w_out,
    b_out,
    ln1_gain,
    ln1_shift,
    w_up,
    b_up,
    w_down,
    b_down,
    ln2_gain,
    ln2_shift,
):
    seq_parts = lax.axis_size("seq")
    mine = lax.axis_index("seq")
    seq_count, local_rows, features = tokens.shape
    flat_rows = seq_count * local_rows
    hidden = w_up.shape[1]
    heads = HEADS // seq_parts
    wide = heads * HEAD_DIM
    dims = (seq_count, seq_parts)
    f32 = jnp.float32

    w_heads = jnp.concatenate(
        [
            lax.dynamic_slice_in_dim(w_qkv, k * features + mine * wide, wide, axis=1)
            for k in range(3)
        ],
        axis=1,
    )
    w_t = w_heads.T
    bias = jnp.concatenate(
        [
            lax.dynamic_slice_in_dim(b_query, mine * wide, wide),
            jnp.zeros((wide,), b_query.dtype),
            lax.dynamic_slice_in_dim(b_value, mine * wide, wide),
        ]
    ).astype(f32)[:, None]
    outer = own_number("cyl")
    places = jnp.concatenate(
        [
            jnp.arange(8, dtype=jnp.int32) ^ outer,
            jnp.stack([own_number("hx"), mine, own_number("ylh")]),
            lengths,
            block_perm.reshape(-1),
        ]
    )
    vectors = jnp.stack(
        [v.astype(f32) for v in (b_out, ln1_gain, ln1_shift, b_down, ln2_gain, ln2_shift, b_out, b_out)]
    )

    arrived, kept, crossed = [], [], []
    for s in range(seq_count):
        near = tokens[s]
        start = near
        if s > 0:
            after = [crossed[-1]] + arrived[(s - 2) * seq_parts : (s - 2) * seq_parts + 1] * (s > 1)
            start, _ = lax.optimization_barrier((near, after))
        across = exchange_bit(start, "x")
        crossed.append(across)
        if s == 0:
            across, w_t, bias, places = lax.optimization_barrier((across, w_t, bias, places))
        if s > 0:
            across, _ = lax.optimization_barrier((across, arrived[-seq_parts]))
        pieces = [near, exchange_bit(near, "c"), across, exchange_bit(across, "c")]
        contexts, saved = attention_forward(places, pieces, s, w_t, bias, heads)
        kept.append(saved)
        arrived += [contexts[0]] + [exchange(contexts[r], "seq", r) for r in range(1, seq_parts)]

    (
        out_rows,
        send_down1,
        send_up1,
        send_down0,
        send_up0,
        keep_down,
        keep_up,
        d_first_in,
        sums,
        grad_out,
        send_out,
        *d_contexts,
    ) = run_token_layer(
        places,
        arrived,
        tokens.reshape(flat_rows, features),
        cotangent.reshape(flat_rows, features),
        w_out,
        vectors,
        w_up,
        b_up.astype(f32).reshape(1, hidden),
        w_down,
        dims,
    )
    out_tokens = out_rows.reshape(seq_count, local_rows, features)

    def hand_on(own, near, came):
        return [own, exchange_bit(near, "c"), came, exchange_bit(came[1], "c")]

    first_came = exchange_bit(d_contexts[2], "x")
    came_down1, came_up1 = exchange_bit(send_down1, "c"), exchange_bit(send_up1, "c")
    send_up0, first_came = lax.optimization_barrier((send_up0, first_came))
    came_up0 = exchange_bit(send_up0, "c")
    second_pair, first_came = lax.optimization_barrier((d_contexts[5], first_came))
    second_came = exchange_bit(second_pair, "x")
    parts, near, far = [], [], []

    def attend(s, group, before, late=()):
        found, total = attention_backward(places, group, s, w_t, kept[s], before, heads, late)
        parts.append(found)
        return total

    def cross(s):
        held, sent = parts[s]
        came = exchange_bit(sent, "c")
        near.append(held[0].astype(f32) + came[0])
        far.append(sum_low(held[1], came[1]))

    sends = [
        sum_low(keep_down[2:], came_down1),
        sum_low(keep_up[1::2], jnp.stack([came_up0[1], came_up1[1]])),
    ]
    sends, first_came = lax.optimization_barrier((sends, first_came))
    down_y, up_l = [exchange_bit(v, bit) for v, bit in zip(sends, "yl")]
    came_down0 = exchange_bit(send_down0, "c")
    total = attend(0, hand_on(d_contexts[0], d_contexts[1], first_came), ())
    (total, parts[0], second_came, near_pair, came_down0, send_out) = lax.optimization_barrier(
        (total, parts[0], second_came, d_contexts[3:5], came_down0, send_out)
    )

    out_x = exchange_bit(send_out, "x")
    second_group = hand_on(*near_pair, second_came)
    cross(0)
    for s in range(1, seq_count - 1):
        total = attend(s, second_group, total)
    (down_y, up_l, out_x, total, parts[1:], near, far) = lax.optimization_barrier(
        (down_y, up_l, out_x, total, parts[1:], near, far)
    )

    sends = [
        sum_low(keep_down[1], came_down0[1], down_y[1]),
        sum_low(keep_up[2], came_up1[0], up_l[1]),
    ]
    out_c = exchange_bit(sum_low(grad_out[1], out_x[1]), "c")
    out_own = sum_low(grad_out[0], out_x[0], out_c)
    (sends, total, out_own, far) = lax.optimization_barrier((sends, total, out_own, far))
    down_l, up_y = [exchange_bit(v, bit) for v, bit in zip(sends, "ly")]
    far_came = [exchange_bit(far[0], "x")]
    for s in range(1, seq_count - 1):
        cross(s)
    half_a, half_b = attend(seq_count - 1, second_group, total, (out_own, sums))

    (down_l, up_y, far, far_came, half_a, half_b, parts[-1]) = lax.optimization_barrier(
        (down_l, up_y, far, far_came, half_a, half_b, parts[-1])
    )
    down_own = sum_low(keep_down[0], came_down0[0], down_y[0], down_l)
    down_own = down_own.reshape(2, 2, hidden // 32, features)
    up_own = sum_low(keep_up[0], came_up0[0], up_l[0], up_y)
    up_own = up_own.reshape(2, 2, features // 4, hidden // 8)
    half_b = half_b.reshape(2, 2, 2, *half_b.shape[1:])
    keeps = [half_a[:4], half_b[:, 0], down_own[:, 0], up_own[:, 0]]
    sends = [half_a[4:], half_b[:, 1], down_own[:, 1], up_own[:, 1]]
    got = [exchange_bit(v, bit) for v, bit in zip(sends, "ylxx")]
    half_a, half_b, down, up = [k + g for k, g in zip(keeps, got)]
    near_far = far[1:]
    far = []
    cross(seq_count - 1)

    keeps, sends = [half_a[:2], half_b[0]], [half_a[2:], half_b[1]]
    (keeps, sends, down, up, far, near_far, near) = lax.optimization_barrier(
        (keeps, sends, down, up, far, near_far, near)
    )
    got = [exchange_bit(v, bit) for v, bit in zip(sends, "ly")]
    down_came = exchange_bit(down, "h")
    far_came += [exchange_bit(v, "x") for v in near_far]
    both = jnp.concatenate([k + g for k, g in zip(keeps, got)], axis=2)
    down = add_extra(down + down_came[::-1])

    (both, down, up, far, far_came) = lax.optimization_barrier((both, down, up, far, far_came))
    far_came += [exchange_bit(v, "x") for v in far]
    came = exchange_bit(both, "h")
    down = jnp.concatenate([down, exchange_bit(down, "l")])
    both = add_extra(both + came[::-1])

    (both, down, up, far_came) = lax.optimization_barrier((both, down, up, far_came))
    came, up_came = exchange_bit(both, "y"), exchange_bit(up, "h")
    down_hi = exchange_bit(down, "x")
    both = jnp.concatenate([both, came])
    up = add_extra(up + up_came[::-1])
    own_pos = mine * local_rows + jnp.arange(local_rows, dtype=jnp.int32)
    live = (own_pos[None, :] < lengths[:, None]).astype(f32)
    d_inputs = jnp.stack([n + f for n, f in zip(near, far_came)])
    grad_tokens = (d_inputs + d_first_in.reshape(seq_count, local_rows, features)) * live[:, :, None]


    (both, down, down_hi, up, grad_tokens) = lax.optimization_barrier(
        (both, down, down_hi, up, grad_tokens)
    )
    came = exchange_bit(both, "l")
    down_far = [exchange_bit(down, "y")]
    up_came = exchange_bit(up, "x")
    down_own = [down, down_hi]
    down_near = [exchange_bit(half, "c") for half in down_own]
    both = [jnp.concatenate([v[:2] for v in (both, came)]), jnp.concatenate([v[2:] for v in (both, came)])]
    up = jnp.concatenate([up, up_came])

    (both, down_own, down_near, down_far, up) = lax.optimization_barrier(
        (both, down_own, down_near, down_far, up)
    )
    across = [exchange_bit(both[0], "x")]
    down_far.append(exchange_bit(down_own[1], "y"))
    up_hi = exchange_bit(up, "l")
    across_down = [exchange_bit(down_far[0], "c")]
    both_near = [exchange_bit(both[0], "c")]
    full_down = gather_tiles(places, down_own + down_near, 0, [], (hidden, features), True)

    (both, across, up, up_hi, down_far, across_down, both_near, full_down) = (
        lax.optimization_barrier(
            (both, across, up, up_hi, down_far, across_down, both_near, full_down)
        )
    )
    across.append(exchange_bit(both[1], "x"))
    up_far = [exchange_bit(up, "y")]
    across_down.append(exchange_bit(down_far[1], "c"))
    up_own = [up, up_hi]
    up_near = [exchange_bit(half, "c") for half in up_own]
    full_down = gather_tiles(
        places, down_far + across_down, 1, [full_down], (hidden, features), True
    )
    full_up = gather_tiles(places, up_own + up_near, 0, [], (features, hidden), False)

    (both, across, up_hi, up_far, full_down, full_up) = lax.optimization_barrier(
        (both, across, up_hi, up_far, full_down, full_up)
    )
    up_second = [exchange_bit(up_hi[:2], "y")]
    both_near.append(exchange_bit(both[1], "c"))
    both_far = [exchange_bit(half, "c") for half in across]

    (up_hi, up_second, both_near, both_far) = lax.optimization_barrier(
        (up_hi, up_second, both_near, both_far)
    )
    up_second.append(exchange_bit(up_hi[2:], "y"))
    across_up = [exchange_bit(up_far[0], "c")]
    full_qkv, full_out, vector_rows, head_rows = gather_heads(
        places,
        both + both_near + across + both_far,
        tuple((r, first) for r in range(4) for first in (0, 4)),
        (features, 3 * features),
    )
    (up_second, across_up, full_qkv, vector_rows, head_rows) = lax.optimization_barrier(
        (up_second, across_up, full_qkv, vector_rows, head_rows)
    )
    up_far.append(jnp.concatenate(up_second))
    across_up.append(exchange_bit(up_far[1], "c"))
    full_up = gather_tiles(places, up_far + across_up, 1, [full_up], (features, hidden), False)
    (
        full_b_down,
        full_gain_two,
        full_shift_two,
        full_b_out,
        full_gain_one,
        full_shift_one,
    ) = [vector_rows[i] for i in range(6)]
    full_b_up = vector_rows[6 : 6 + hidden // features].reshape(hidden)
    full_b_query = head_rows[:seq_parts, :wide].reshape(features)
    full_b_value = head_rows[:seq_parts, 2 * wide : 3 * wide].reshape(features)

    return (
        out_tokens,
        grad_tokens,
        full_qkv,
        full_b_query,
        full_b_value,
        full_out,
        full_b_out,
        full_gain_one,
        full_shift_one,
        full_up,
        full_b_up,
        full_down,
        full_b_down,
        full_gain_two,
        full_shift_two,
    )


def solution(mesh):
    in_specs = (
        P("dp", "seq", None),
        P("dp", "seq", None),
        P("dp"),
        P("dp", None),
        P(),
        P(),
        P(),
        P(),
        P(),
        P(),
        P(),
        P(),
        P(),
        P(),
        P(),
        P(),
        P(),
    )
    out_specs = (
        P("dp", "seq", None),
        P("dp", "seq", None),
        P(),
        P(),
        P(),
        P(),
        P(),
        P(),
        P(),
        P(),
        P(),
        P(),
        P(),
        P(),
        P(),
    )
    return jax.shard_map(
        per_device, mesh=mesh, in_specs=in_specs, out_specs=out_specs, check_vma=False
    )
```

```python
import functools
import jax
import jax.numpy as jnp
from jax import lax
from jax.experimental import pallas as pl
from jax.experimental.pallas import tpu as pltpu
from jax.sharding import PartitionSpec as P

HEAD_DIM = 64
SOFT = HEAD_DIM ** -0.5 * 1.4426950408889634
NN = (((1,), (0,)), ((), ()))
NT = (((1,), (1,)), ((), ()))
TN = (((0,), (0,)), ((), ()))
VMEM_LIMIT = 60 * 1024 * 1024
HEADS = 12
EPSILON = 1e-06
BITS = {"c": ("seq", 0), "x": ("seq", 1), "y": ("dp", 0), "l": ("dp", 1), "h": ("dp", 2)}


def own_number(order):
    number = jnp.int32(0)
    for letter in order:
        axis, shift = BITS[letter]
        number = number * 2 + ((lax.axis_index(axis) >> shift) & 1)
    return number


def exchange(array_in, axis, flip):
    return lax.ppermute(array_in, axis, [(i, i ^ flip) for i in range(lax.axis_size(axis))])


def exchange_bit(array_in, letter):
    axis, shift = BITS[letter]
    return exchange(array_in, axis, 1 << shift)


def extra_flips(axis, used):
    return [1 << shift for shift in range(used, lax.axis_size(axis).bit_length() - 1)]


def add_extra(array_in):
    for flip in extra_flips("dp", 3):
        array_in = array_in + exchange(array_in, "dp", flip)
    return array_in


def sum_low(*parts):
    total = parts[0].astype(jnp.float32)
    for part in parts[1:]:
        total = total + part.astype(jnp.float32)
    return total.astype(jnp.bfloat16)


def dot_f32(left, right, dims):
    return lax.dot_general(left, right, dims, preferred_element_type=jnp.float32)


def sequence_scalars(places, index):
    seq_count = (places.shape[0] - 11) // 3
    return places[11 + index] >> 1, places[9], 11 + seq_count + 2 * index


def shift_matrix(half, block, whole):
    row = lax.broadcasted_iota(jnp.int32, (block, whole), 0)
    col = lax.broadcasted_iota(jnp.int32, (block, whole), 1)
    return jnp.where((col == row + half) & (row < half), 1.0, 0.0).astype(jnp.bfloat16)


def mask_tiles(half, block):
    row = lax.broadcasted_iota(jnp.int32, (16, block), 0)
    col = lax.broadcasted_iota(jnp.int32, (16, block), 1)
    key_tile = jnp.where((row == 0) & (col >= half), -1e30, 0.0).astype(jnp.bfloat16)
    query_tile = jnp.where(row == 0, 1.0, 0.0).astype(jnp.bfloat16)
    return key_tile, query_tile


def attend_forward(
    heads, index, places, x0, x1, x2, x3, w_t, bias, c0, c1, c2, c3,
    x_out, qkv_out, ctx_blk, lse, tok, c_tok, x_seq, qkv, sems,
):
    half, mine, perm = sequence_scalars(places, index)
    whole = x_seq.shape[0]
    quarter = whole // 4
    block = whole // 2
    wide = heads * HEAD_DIM
    for r, piece in enumerate((x0, x1, x2, x3)):
        x_seq[pl.ds(pl.multiple_of((r ^ mine) * quarter, quarter), quarter), :] = piece[...]
    keep_x = pltpu.make_async_copy(x_seq, x_out, sems.at[0])
    keep_x.start()
    lane = lax.broadcasted_iota(jnp.int32, (1, block), 1)
    tok[...] = (dot_f32(w_t[...], x_seq[...], NT) + bias[...]).astype(jnp.bfloat16)
    shift = shift_matrix(half, block, whole)
    qkv[0] = jnp.where(lane < half, tok[:, :block], jnp.zeros((), jnp.bfloat16))
    qkv[1] = dot_f32(tok[...], shift, NT).astype(jnp.bfloat16)
    keep_qkv = pltpu.make_async_copy(qkv, qkv_out, sems.at[1])
    keep_qkv.start()
    key_tile, query_tile = mask_tiles(half, block)

    def one_block(b, carry):
        target = places[perm + b]
        for h in range(heads):
            rows = slice(h * HEAD_DIM, (h + 1) * HEAD_DIM)
            q_t = jnp.concatenate([qkv[b, rows, :], query_tile])
            k_t = jnp.concatenate(
                [qkv[target, wide + h * HEAD_DIM : wide + (h + 1) * HEAD_DIM, :], key_tile]
            )
            v_t = qkv[target, 2 * wide + h * HEAD_DIM : 2 * wide + (h + 1) * HEAD_DIM, :]
            scores = dot_f32(k_t, q_t, TN) * SOFT
            top = jnp.max(scores, axis=0, keepdims=True)
            expo = jnp.exp2(scores - top)
            total = jnp.sum(expo, axis=0, keepdims=True)
            context = dot_f32(v_t, expo.astype(jnp.bfloat16), NN) / total
            ctx_blk[b, rows, :] = context
            lse[b, h : h + 1, :] = top + jnp.log2(total)
        return carry

    lax.fori_loop(0, 2, one_block, 0)
    early = jnp.where(lane < half, ctx_blk[0], 0.0)
    late = dot_f32(ctx_blk[1].astype(jnp.bfloat16), shift, NN)
    for j in range(4):
        part = late[:, j * quarter : (j + 1) * quarter]
        if j < 2:
            part = part + early[:, j * quarter : (j + 1) * quarter]
        c_tok[j] = part.astype(jnp.bfloat16)
    for r, piece in enumerate((c0, c1, c2, c3)):
        piece[...] = c_tok[r ^ mine]
    keep_x.wait()
    keep_qkv.wait()


def attend_backward(
    heads, index, places, g0, g1, g2, g3, w_t, x_in, qkv, ctx_blk, lse, *refs
):
    first, last = index == 0, len(refs) > 14
    acc_in, acc_b = (None, None) if first else refs[:2]
    (dx_keep, dx_send, grad_w, grad_w2, g_tok, g_blk, d_qkv, tok, x_seq, acc, dx_s, sems) = refs[-12:]
    bring_x = pltpu.make_async_copy(x_in, x_seq, sems.at[0])
    bring_x.start()
    if not first:
        bring_acc = pltpu.make_async_copy(acc_in, acc, sems.at[1])
        bring_acc.start()
    half, mine, perm = sequence_scalars(places, index)
    index = max(index - 1, 0)
    quarter = g0.shape[2]
    block = 2 * quarter
    whole = 4 * quarter
    wide = heads * HEAD_DIM
    for r, piece in enumerate((g0[index], g1[index], g2[0, index], g3[index])):
        g_tok[r ^ mine] = piece
    shift = shift_matrix(half, block, whole)
    lane = lax.broadcasted_iota(jnp.int32, (1, block), 1)
    g_all = jnp.concatenate([g_tok[j] for j in range(4)], axis=1)
    g_blk[0] = jnp.where(lane < half, g_all[:, :block], jnp.zeros((), jnp.bfloat16))
    g_blk[1] = dot_f32(g_all, shift, NT).astype(jnp.bfloat16)
    key_tile, query_tile = mask_tiles(half, block)

    def one_block(b, carry):
        target = places[perm + b]
        for h in range(heads):
            rows = slice(h * HEAD_DIM, (h + 1) * HEAD_DIM)
            k_rows = slice(wide + h * HEAD_DIM, wide + (h + 1) * HEAD_DIM)
            v_rows = slice(2 * wide + h * HEAD_DIM, 2 * wide + (h + 1) * HEAD_DIM)
            q_t = qkv[b, rows, :]
            k_t = qkv[target, k_rows, :]
            v_t = qkv[target, v_rows, :]
            g_t = g_blk[b, rows, :]
            scores = dot_f32(
                jnp.concatenate([k_t, key_tile]), jnp.concatenate([q_t, query_tile]), TN
            )
            probs = jnp.exp2(scores * SOFT - lse[b, h : h + 1, :])
            d_probs = dot_f32(v_t, g_t, TN)
            delta = jnp.sum(ctx_blk[b, rows, :] * g_t.astype(jnp.float32), axis=0, keepdims=True)
            d_scores = (probs * (d_probs - delta)).astype(jnp.bfloat16)
            scaling = HEAD_DIM ** -0.5
            d_qkv[b, rows, :] = (dot_f32(k_t, d_scores, NN) * scaling).astype(jnp.bfloat16)
            d_qkv[target, k_rows, :] = (dot_f32(q_t, d_scores, NT) * scaling).astype(jnp.bfloat16)
            d_qkv[target, v_rows, :] = dot_f32(g_t, probs.astype(jnp.bfloat16), NT).astype(
                jnp.bfloat16
            )
        return carry

    lax.fori_loop(0, 2, one_block, 0)
    late = dot_f32(d_qkv[1], shift, NN)
    front = jnp.where(lane < half, d_qkv[0].astype(jnp.float32), 0.0)
    tok[:, block:] = late[:, block:].astype(jnp.bfloat16)
    tok[:, :block] = (late[:, :block] + front).astype(jnp.bfloat16)
    sent = []
    for r in range(4):
        piece = (dx_send if r & 1 else dx_keep).at[r >> 1]
        columns = tok[:, pl.ds(pl.multiple_of((r ^ mine) * quarter, quarter), quarter)]
        dx_s[r] = dot_f32(columns, w_t[...], TN).astype(jnp.bfloat16)
        sent.append(pltpu.make_async_copy(dx_s.at[r], piece, sems.at[2 + r]))
        sent[-1].start()
    bring_x.wait()
    total = dot_f32(tok[...], x_seq[...], NN)
    ones = jnp.ones((8, whole), jnp.bfloat16)
    sums = dot_f32(ones, tok[...], NT)
    if not first:
        bring_acc.wait()
        total, sums = total + acc[...], sums + acc_b[...]
    if last:
        grad_out, out_x, out_c, vectors = refs[2:6]
        out_own = (
            grad_out[0].astype(jnp.float32)
            + out_x[0].astype(jnp.float32)
            + out_c[...].astype(jnp.float32)
        ).astype(jnp.bfloat16)
        inner = places[10]
        turned = total.T.astype(jnp.bfloat16)
        tile = out_own.shape[1]
        extra = grad_w.shape[1] - tile
        for half_w in (grad_w, grad_w2):
            half_w[:, tile:, :] = jnp.zeros((8, extra, 2 * wide), jnp.bfloat16)
        for q in range(8):
            rows = slice(q * tile, (q + 1) * tile)
            grad_w[q ^ inner, :tile, :] = turned[rows, : 2 * wide]
            grad_w2[q ^ inner, :tile, :wide] = turned[rows, 2 * wide :]
        grad_w2[:, :tile, wide:] = out_own
        row = lax.broadcasted_iota(jnp.int32, (extra, 1), 0)
        own_row = jnp.concatenate([sums[0:1, :], jnp.zeros((1, wide), jnp.float32)], axis=1)
        tile_rows = jnp.where(row == 10, own_row, vectors[...]).astype(jnp.bfloat16)
        grad_w[inner, tile:, :] = tile_rows[:, : 2 * wide]
        grad_w2[inner, tile:, :] = tile_rows[:, 2 * wide :]
    else:
        grad_w[...] = total
        grad_w2[...] = sums
    for copy in sent:
        copy.wait()


def kernel_call(body, scalars, arrays, outs, scratch, left_in=(), left_out=()):
    def spec(away):
        return pl.BlockSpec(memory_space=pl.ANY if away else pltpu.VMEM)

    return pl.pallas_call(
        body,
        out_shape=outs,
        in_specs=[pl.BlockSpec(memory_space=pltpu.SMEM)]
        + [spec(i in left_in) for i in range(len(arrays))],
        out_specs=[spec(i in left_out) for i in range(len(outs))],
        scratch_shapes=scratch,
        compiler_params=pltpu.CompilerParams(vmem_limit_bytes=VMEM_LIMIT),
        cost_estimate=pl.CostEstimate(
            flops=10**8, transcendentals=0, bytes_accessed=1024 * 1024
        ),
    )(scalars, *arrays)


def attention_forward(places, pieces, index, w_t, bias, heads):
    quarter, features = pieces[0].shape
    whole, block, wide = 4 * quarter, 2 * quarter, heads * HEAD_DIM
    out = jax.ShapeDtypeStruct
    outs = [out((wide, quarter), jnp.bfloat16)] * 4 + [
        out((whole, features), jnp.bfloat16),
        out((2, 3 * wide, block), jnp.bfloat16),
        out((2, wide, block), jnp.float32),
        out((2, 8, block), jnp.float32),
    ]
    scratch = [
        pltpu.VMEM((3 * wide, whole), jnp.bfloat16),
        pltpu.VMEM((4, wide, quarter), jnp.bfloat16),
        pltpu.VMEM((whole, features), jnp.bfloat16),
        pltpu.VMEM((2, 3 * wide, block), jnp.bfloat16),
        pltpu.SemaphoreType.DMA((2,)),
    ]
    found = kernel_call(
        functools.partial(attend_forward, heads, index),
        places,
        [*pieces, w_t, bias],
        outs,
        scratch,
        left_out=(4, 5),
    )
    return found[:4], found[4:]


def attention_backward(places, pieces, index, w_t, kept, before, heads, late=()):
    _, wide, quarter = pieces[0].shape
    features = w_t.shape[1]
    block = 2 * quarter
    out = jax.ShapeDtypeStruct
    if late:
        grads = [out((8, features // 8 + 16, 2 * wide), jnp.bfloat16)] * 2
    else:
        grads = [out((3 * wide, features), jnp.float32), out((8, 3 * wide), jnp.float32)]
    outs = [out((2, quarter, features), jnp.bfloat16)] * 2 + grads
    scratch = [
        pltpu.VMEM((4, wide, quarter), jnp.bfloat16),
        pltpu.VMEM((2, wide, block), jnp.bfloat16),
        pltpu.VMEM((2, 3 * wide, block), jnp.bfloat16),
        pltpu.VMEM((3 * wide, 4 * quarter), jnp.bfloat16),
        pltpu.VMEM((4 * quarter, features), jnp.bfloat16),
        pltpu.VMEM((3 * wide, features), jnp.float32),
        pltpu.VMEM((4, quarter, features), jnp.bfloat16),
        pltpu.SemaphoreType.DMA((6,)),
    ]
    found = kernel_call(
        functools.partial(attend_backward, heads, index),
        places,
        [*pieces, w_t, *kept, *before, *late],
        outs,
        scratch,
        left_in=(5, 9) if before else (5,),
        left_out=(0, 1),
    )
    return found[:2], found[2:]

def live_rows(places, rows, mine, local_rows, offset):
    row = lax.broadcasted_iota(jnp.int32, (rows, 1), 0)
    length = jnp.zeros((rows, 1), jnp.int32)
    for s in range(rows // local_rows):
        length = jnp.where(row >= s * local_rows, places[offset + s], length)
    position = mine * local_rows + lax.rem(row, local_rows)
    return jnp.where(position < length, 1.0, 0.0)


def normal_parts(array_in):
    centered = array_in - jnp.mean(array_in, axis=1, keepdims=True)
    spread = jnp.mean(centered * centered, axis=1, keepdims=True)
    inverse = lax.rsqrt(spread + EPSILON)
    return centered * inverse, inverse


def normal_back(hat, inverse, gain, d_out):
    scaled = d_out * gain
    mean_scaled = jnp.mean(scaled, axis=1, keepdims=True)
    mean_product = jnp.mean(scaled * hat, axis=1, keepdims=True)
    return inverse * (scaled - mean_scaled - hat * mean_product)


def column_sum(array_in):
    return jnp.sum(array_in, axis=0, keepdims=True)


def token_layer(shape, places, *refs):
    seq_count, seq_parts = shape
    count = seq_count * seq_parts
    pieces, refs = refs[:count], refs[count:]
    tokens, cot_in, w_out, vectors, b_up, w_up_in, w_down_in = refs[:7]
    out, send_down1, send_up1, send_down0, send_up0, keep_down, keep_up = refs[7:14]
    d_first_in, sums, grad_out, send_out = refs[14:18]
    sent = refs[18:24]
    (
        w_up, w_down, active, slope, context, first_in, first_norm, lowered,
        first_low, first_t, d_lowered, turned, out_s, cot, grad_down, grad_up, sems,
    ) = refs[24:]
    rows, features = tokens.shape
    local_rows = rows // seq_count
    wide = features // seq_parts
    mine, inner = places[9], places[8]
    step = pl.program_id(0)
    quarters = w_up.shape[0]
    width = w_up.shape[2]
    f32, bf16 = jnp.float32, jnp.bfloat16

    def bring(j):
        return (
            pltpu.make_async_copy(
                w_up_in.at[:, pl.ds(j * width, width)], w_up.at[j], sems.at[j]
            ),
            pltpu.make_async_copy(
                w_down_in.at[pl.ds(j * width, width), :], w_down.at[j], sems.at[quarters + j]
            ),
        )

    keep_out = pltpu.make_async_copy(out_s, out, sems.at[2 * quarters])
    bring_cot = pltpu.make_async_copy(cot_in, cot, sems.at[2 * quarters + 1])

    def leave(relative):
        down_ref, up_ref = (
            (keep_down.at[pl.ds(0, 2)], keep_up.at[pl.ds(0, 2)]),
            (keep_down.at[pl.ds(2, 2)], keep_up.at[pl.ds(2, 2)]),
            (send_down0, send_up0),
            (send_down1, send_up1),
        )[relative]
        first = 2 * quarters + 2 + 2 * relative
        return (
            pltpu.make_async_copy(grad_down.at[relative & 1], down_ref, sems.at[first]),
            pltpu.make_async_copy(grad_up.at[relative & 1], up_ref, sems.at[first + 1]),
        )

    @pl.when(step == 0)
    def start():
        for j in range(quarters):
            for copy in bring(j):
                copy.start()
        bring_cot.start()
        for s in range(seq_count):
            for r in range(seq_parts):
                context[
                    pl.ds(pl.multiple_of((r ^ mine) * wide, wide), wide),
                    s * local_rows : (s + 1) * local_rows,
                ] = pieces[s * seq_parts + r][...]
        live = live_rows(places, rows, mine, local_rows, 11)
        attended = dot_f32(context[...], w_out[...], TN) + vectors[0:1, :]
        total = jnp.where(live > 0, tokens[...].astype(f32), 0.0) + attended
        first_in[...] = total
        hat, _ = normal_parts(total)
        normed = hat * vectors[1:2, :] + vectors[2:3, :]
        first_norm[...] = normed
        low = normed.astype(bf16)
        first_low[...] = low
        tile = features // 4
        low_t = low.T
        for q in range(4):
            first_t[pl.ds(pl.multiple_of((q ^ inner) * tile, tile), tile), :] = low_t[
                q * tile : (q + 1) * tile
            ]
        lowered[...] = jnp.zeros_like(lowered)
        sums[...] = jnp.zeros_like(sums)

    @pl.when(step < quarters)
    def forward():
        for j in range(quarters):

            @pl.when(step == j)
            def arrive():
                for copy in bring(j):
                    copy.wait()

        lifted = dot_f32(first_low[...], w_up[step], NN) + b_up[step]
        cdf = 0.5 * (1.0 + lax.erf(lifted * 0.7071067811865476))
        density = jnp.exp(lifted * lifted * -0.5) * 0.3989422804014327
        gelu = (lifted * cdf).astype(bf16)
        active[step] = gelu
        slope[step] = (cdf + lifted * density).astype(bf16)
        lowered[...] += dot_f32(gelu, w_down[step], NN)

    @pl.when(step == quarters - 1)
    def turn():
        live = live_rows(places, rows, mine, local_rows, 11)
        hat, inverse = normal_parts(first_norm[...] + (lowered[...] + vectors[3:4, :]))
        gain = vectors[4:5, :]
        bring_cot.wait()
        out_s[...] = ((hat * gain + vectors[5:6, :]) * live).astype(bf16)
        keep_out.start()
        incoming = cot[...].astype(f32) * live
        back = normal_back(hat, inverse, gain, incoming)
        lowered[...] = back
        low = back.astype(bf16)
        d_lowered[...] = low
        sums[0:1, :] = column_sum(low.astype(f32))
        sums[1:2, :] = column_sum(incoming * hat)
        sums[2:3, :] = column_sum(incoming)

    @pl.when(step >= quarters)
    def backward():
        relative = 2 * quarters - 1 - step
        quarter = relative ^ (places[0] >> 1)
        low_bit = places[0] & 1
        slot = relative & 1
        half = width // 2
        tile = half // 4
        for k in range(2):

            @pl.when(relative == k)
            def free():
                for copy in leave(k + 2):
                    copy.wait()

        down = dot_f32(active[quarter], d_lowered[...], TN).astype(bf16)
        for j in range(2):
            for q in range(4):
                grad_down[
                    slot, j ^ low_bit, pl.ds(pl.multiple_of((q ^ inner) * tile, tile), tile), :
                ] = down[j * half + q * tile : j * half + (q + 1) * tile]
        d_active = dot_f32(d_lowered[...], w_down[quarter], NT)
        d_lifted = (d_active * slope[quarter].astype(f32)).astype(bf16)
        up = dot_f32(first_t[...], d_lifted, NN).astype(bf16)
        for j in range(2):
            grad_up[slot, j ^ low_bit] = up[:, j * half : (j + 1) * half]
        sums[pl.ds(6 + quarter, 1), :] = column_sum(d_lifted.astype(f32))
        lowered[...] += dot_f32(d_lifted, w_up[quarter], NT)
        for k in range(quarters):

            @pl.when(relative == k)
            def start_leaving():
                for copy in leave(k):
                    copy.start()

    @pl.when(step == 2 * quarters - 1)
    def finish():
        hat, inverse = normal_parts(first_in[...])
        incoming = lowered[...]
        back = normal_back(hat, inverse, vectors[1:2, :], incoming)
        d_first_in[...] = back
        low = back.astype(bf16)
        sums[3:4, :] = column_sum(low.astype(f32))
        sums[4:5, :] = column_sum(incoming * hat)
        sums[5:6, :] = column_sum(incoming)
        turned[...] = dot_f32(w_out[...], low, NT).astype(bf16)
        for r in range(seq_parts):
            own = turned[pl.ds(pl.multiple_of((r ^ mine) * wide, wide), wide), :]
            for s in range(seq_count):
                target, place = sent[3 * min(s, 1) + min(r, 2)], max(s - 1, 0)
                columns = own[:, s * local_rows : (s + 1) * local_rows]
                if r < 2:
                    target[place] = columns
                else:
                    target[r - 2, place] = columns
        product = dot_f32(context[...], low, NN).astype(bf16)
        block_rows, block_cols = grad_out.shape[2:]
        across = features // block_cols
        for j in range(seq_parts):
            for q in range(wide // block_rows * across):
                row, col = j * wide + q // across * block_rows, q % across * block_cols
                block = product[row : row + block_rows, col : col + block_cols]
                place, inner_place = j ^ mine, q ^ places[10]

                @pl.when(place < 2)
                def own():
                    grad_out[place, inner_place] = block

                @pl.when(place >= 2)
                def across_x():
                    send_out[place - 2, inner_place] = block

        keep_out.wait()
        for k in range(2):
            for copy in leave(k):
                copy.wait()


def whole_spec(shape):
    return pl.BlockSpec(
        shape, lambda p, places: (0,) * len(shape), pipeline_mode=pl.Buffered(buffer_count=1)
    )


def step_call(body, places, steps, ins, in_specs, outs, out_specs, scratch, flops, aliases={}):
    return pl.pallas_call(
        body,
        out_shape=outs,
        grid_spec=pltpu.PrefetchScalarGridSpec(
            num_scalar_prefetch=1,
            grid=(steps,),
            in_specs=in_specs,
            out_specs=out_specs,
            scratch_shapes=scratch,
        ),
        input_output_aliases=aliases,
        compiler_params=pltpu.CompilerParams(vmem_limit_bytes=VMEM_LIMIT),
        cost_estimate=pl.CostEstimate(
            flops=flops, transcendentals=0, bytes_accessed=1024 * 1024
        ),
    )(places, *ins)


def run_token_layer(places, pieces, tokens, cot, w_out, vectors, w_up, b_up, w_down, dims):
    seq_count, seq_parts = dims
    rows, features = tokens.shape
    hidden = w_up.shape[1]
    quarters = 4
    width = hidden // quarters
    half = width // 2
    out, bf16, f32 = jax.ShapeDtypeStruct, jnp.bfloat16, jnp.float32
    square, turned = (rows, features), (features, rows)
    piece = (features // seq_parts, rows // seq_count)
    sent = []
    for n in (1, seq_count - 1):
        sent += [(n, *piece), (n, *piece), (2, n, *piece)]
    out_blocks = (seq_parts // 2, 8, features // seq_parts // 2, features // 4)
    away = pl.BlockSpec(memory_space=pl.ANY)
    down, up = (2, half, features), (2, features, half)

    return step_call(
        functools.partial(token_layer, dims),
        places,
        2 * quarters,
        [*pieces, tokens, cot, w_out, vectors, b_up.reshape(quarters, 1, width), w_up, w_down],
        [whole_spec(p.shape) for p in pieces]
        + [whole_spec(square), away, whole_spec(w_out.shape), whole_spec(vectors.shape)]
        + [whole_spec((quarters, 1, width)), away, away],
        [
            out(square, bf16),
            out(down, bf16),
            out(up, bf16),
            out(down, bf16),
            out(up, bf16),
            out((4, half, features), bf16),
            out((4, features, half), bf16),
            out(square, f32),
            out((16, features), f32),
            out(out_blocks, bf16),
            out(out_blocks, bf16),
        ]
        + [out(p, bf16) for p in sent],
        [away] * 7
        + [whole_spec(square), whole_spec((16, features))]
        + [whole_spec(out_blocks)] * 2
        + [whole_spec(p) for p in sent],
        [
            pltpu.VMEM((quarters, features, width), bf16),
            pltpu.VMEM((quarters, width, features), bf16),
            pltpu.VMEM((quarters, rows, width), bf16),
            pltpu.VMEM((quarters, rows, width), bf16),
            pltpu.VMEM(turned, bf16),
            pltpu.VMEM(square, f32),
            pltpu.VMEM(square, f32),
            pltpu.VMEM(square, f32),
            pltpu.VMEM(square, bf16),
            pltpu.VMEM(turned, bf16),
            pltpu.VMEM(square, bf16),
            pltpu.VMEM(turned, bf16),
            pltpu.VMEM(square, bf16),
            pltpu.VMEM(square, bf16),
            pltpu.VMEM((2, *down), bf16),
            pltpu.VMEM((2, *up), bf16),
            pltpu.SemaphoreType.DMA((4 * quarters + 2,)),
        ],
        2 * rows * features * (6 * hidden + 3 * features),
    )


def place_tiles(by_rows, late, places, *refs):
    sources, out = refs[:4], refs[-4]
    held, main, sems = refs[-3:]
    inner = places[8]
    _, rows, cols = sources[0].shape
    bring = [
        pltpu.make_async_copy(source, held.at[k], sems.at[k]) for k, source in enumerate(sources)
    ]
    for copy in bring:
        copy.start()
    for copy in bring:
        copy.wait()
    sent = []
    for k in range(2):
        for l in range(2):
            block = places[k * 4 + late * 2 + l]
            place = 2 * k + l
            for q in range(4):
                h, x = q >> 1, q & 1
                half, n = (x, l * 2 + h) if by_rows else (l, x * 2 + h)
                first = pl.multiple_of((q ^ inner) * rows, rows)
                main[place, pl.ds(first, rows), :] = held[2 * k + half, n].astype(jnp.float32)
            if by_rows:
                target = out.at[pl.ds(pl.multiple_of(block * 4 * rows, 4 * rows), 4 * rows)]
            else:
                target = out.at[:, pl.ds(pl.multiple_of(block * cols, cols), cols)]
            sent.append(pltpu.make_async_copy(main.at[place], target, sems.at[4 + place]))
            sent[-1].start()
    for copy in sent:
        copy.wait()


def gather_tiles(places, halves, late, begun, shape, by_rows):
    _, rows, cols = halves[0].shape
    away = pl.BlockSpec(memory_space=pl.ANY)
    return pl.pallas_call(
        functools.partial(place_tiles, by_rows, late),
        out_shape=jax.ShapeDtypeStruct(shape, jnp.float32),
        in_specs=[pl.BlockSpec(memory_space=pltpu.SMEM)] + [away] * (4 + len(begun)),
        out_specs=away,
        scratch_shapes=[
            pltpu.VMEM((4, 4, rows, cols), jnp.bfloat16),
            pltpu.VMEM((4, 4 * rows, cols), jnp.float32),
            pltpu.SemaphoreType.DMA((8,)),
        ],
        input_output_aliases={5: 0} if begun else {},
        compiler_params=pltpu.CompilerParams(vmem_limit_bytes=VMEM_LIMIT),
    )(places, *halves, *begun)


def place_heads(parts, places, *refs):
    seq_parts = parts[-1][0] + 1
    sources, refs = refs[: len(parts)], refs[len(parts) :]
    out, out_w, vector_rows, head_rows = refs[:4]
    pieces = refs[4 : seq_parts + 4]
    main, side, sems = refs[seq_parts + 4 :]
    mine, inner = places[9], places[10]
    blocks, rows, _ = main.shape
    features = side.shape[2]
    wide = features // seq_parts
    f32 = jnp.float32
    bring = [
        pltpu.make_async_copy(
            source, pieces[r].at[pl.ds(first, source.shape[0])], sems.at[2 * blocks + i]
        )
        for i, (source, (r, first)) in enumerate(zip(sources, parts))
    ]
    for copy in bring:
        copy.start()
    for copy in bring:
        copy.wait()

    def leave(p, source, target, slot):
        first = pl.multiple_of(p * rows, rows)
        return pltpu.make_async_copy(source.at[p], target.at[pl.ds(first, rows)], sems.at[slot + p])

    def one_block(p, carry):
        for m in range(seq_parts):

            @pl.when(mine == m)
            def copy():
                near = [pieces[j ^ m][p ^ inner, :rows, : 3 * wide] for j in range(seq_parts)]
                for section in range(3):
                    columns = slice(section * wide, (section + 1) * wide)
                    joined = jnp.concatenate([part[:, columns] for part in near], axis=1)
                    main[p, :, section * features : (section + 1) * features] = joined.astype(f32)

        leave(p, main, out, 0).start()
        for r, piece in enumerate(pieces):

            @pl.when(((r ^ mine) == p >> 1))
            def copy_side():
                first = (p & 1) * 4
                joined = jnp.concatenate(
                    [piece[(first + q) ^ inner, :rows, 3 * wide :] for q in range(4)], axis=1
                )
                side[p] = joined.astype(f32)

        leave(p, side, out_w, blocks).start()
        return carry

    lax.fori_loop(0, blocks, one_block, 0)
    for m in range(seq_parts):

        @pl.when(mine == m)
        def copy_vectors():
            held = [pieces[j ^ m][inner, rows:, :].astype(f32) for j in range(seq_parts)]
            total = held[0]
            for other in held[1:]:
                total = total + other
            vector_rows[...] = total
            head_rows[...] = jnp.zeros_like(head_rows)
            for j in range(seq_parts):
                head_rows[j : j + 1, :] = held[j][10:11, :]

    for p in range(blocks):
        leave(p, main, out, 0).wait()
        leave(p, side, out_w, blocks).wait()


def gather_heads(places, sources, parts, shape):
    out, f32 = jax.ShapeDtypeStruct, jnp.float32
    features = shape[0]
    rows = features // 8
    extra = (sources[0].shape[1] - rows, features)
    count = parts[-1][0] + 1
    piece = (8, *sources[0].shape[1:])
    away = pl.BlockSpec(memory_space=pl.ANY)
    here = pl.BlockSpec(memory_space=pltpu.VMEM)
    return pl.pallas_call(
        functools.partial(place_heads, parts),
        out_shape=[
            out(shape, f32),
            out((features, features), f32),
            out(extra, f32),
            out((8, features), f32),
        ],
        in_specs=[pl.BlockSpec(memory_space=pltpu.SMEM)] + [away] * len(sources),
        out_specs=[away, away, here, here],
        scratch_shapes=[pltpu.VMEM(piece, sources[0].dtype)] * count
        + [
            pltpu.VMEM((8, rows, shape[1]), f32),
            pltpu.VMEM((8, rows, features), f32),
            pltpu.SemaphoreType.DMA((16 + len(sources),)),
        ],
        compiler_params=pltpu.CompilerParams(vmem_limit_bytes=VMEM_LIMIT),
    )(places, *sources)


def per_device(
    tokens,
    cotangent,
    lengths,
    block_perm,
    w_qkv,
    b_query,
    b_value,
    w_out,
    b_out,
    ln1_gain,
    ln1_shift,
    w_up,
    b_up,
    w_down,
    b_down,
    ln2_gain,
    ln2_shift,
):
    seq_parts = lax.axis_size("seq")
    mine = lax.axis_index("seq")
    seq_count, local_rows, features = tokens.shape
    flat_rows = seq_count * local_rows
    hidden = w_up.shape[1]
    heads = HEADS // seq_parts
    wide = heads * HEAD_DIM
    dims = (seq_count, seq_parts)
    f32 = jnp.float32

    w_heads = jnp.concatenate(
        [
            lax.dynamic_slice_in_dim(w_qkv, k * features + mine * wide, wide, axis=1)
            for k in range(3)
        ],
        axis=1,
    )
    w_t = w_heads.T
    bias = jnp.concatenate(
        [
            lax.dynamic_slice_in_dim(b_query, mine * wide, wide),
            jnp.zeros((wide,), b_query.dtype),
            lax.dynamic_slice_in_dim(b_value, mine * wide, wide),
        ]
    ).astype(f32)[:, None]
    outer = own_number("cyl")
    places = jnp.concatenate(
        [
            jnp.arange(8, dtype=jnp.int32) ^ outer,
            jnp.stack([own_number("hx"), mine, own_number("ylh")]),
            lengths,
            block_perm.reshape(-1),
        ]
    )
    vectors = jnp.stack(
        [v.astype(f32) for v in (b_out, ln1_gain, ln1_shift, b_down, ln2_gain, ln2_shift, b_out, b_out)]
    )

    arrived, kept, crossed = [], [], []
    for s in range(seq_count):
        near = tokens[s]
        start = near
        if s > 0:
            after = [crossed[-1]] + arrived[(s - 2) * seq_parts : (s - 2) * seq_parts + 1] * (s > 1)
            start, _ = lax.optimization_barrier((near, after))
        across = exchange_bit(start, "x")
        crossed.append(across)
        if s == 0:
            across, w_t, bias, places = lax.optimization_barrier((across, w_t, bias, places))
        if s > 0:
            across, _ = lax.optimization_barrier((across, arrived[-seq_parts]))
        pieces = [near, exchange_bit(near, "c"), across, exchange_bit(across, "c")]
        contexts, saved = attention_forward(places, pieces, s, w_t, bias, heads)
        kept.append(saved)
        arrived += [contexts[0]] + [exchange(contexts[r], "seq", r) for r in range(1, seq_parts)]

    (
        out_rows,
        send_down1,
        send_up1,
        send_down0,
        send_up0,
        keep_down,
        keep_up,
        d_first_in,
        sums,
        grad_out,
        send_out,
        *d_contexts,
    ) = run_token_layer(
        places,
        arrived,
        tokens.reshape(flat_rows, features),
        cotangent.reshape(flat_rows, features),
        w_out,
        vectors,
        w_up,
        b_up.astype(f32).reshape(1, hidden),
        w_down,
        dims,
    )
    out_tokens = out_rows.reshape(seq_count, local_rows, features)

    def hand_on(own, near, came):
        return [own, exchange_bit(near, "c"), came, exchange_bit(came[1], "c")]

    first_came = exchange_bit(d_contexts[2], "x")
    came_down1, came_up1 = exchange_bit(send_down1, "c"), exchange_bit(send_up1, "c")
    send_up0, first_came = lax.optimization_barrier((send_up0, first_came))
    came_up0 = exchange_bit(send_up0, "c")
    second_pair, first_came = lax.optimization_barrier((d_contexts[5], first_came))
    second_came = exchange_bit(second_pair, "x")
    parts, near, far = [], [], []

    def attend(s, group, before, late=()):
        found, total = attention_backward(places, group, s, w_t, kept[s], before, heads, late)
        parts.append(found)
        return total

    def cross(s):
        held, sent = parts[s]
        came = exchange_bit(sent, "c")
        near.append(held[0].astype(f32) + came[0])
        far.append(sum_low(held[1], came[1]))

    sends = [
        sum_low(keep_down[2:], came_down1),
        sum_low(keep_up[1::2], jnp.stack([came_up0[1], came_up1[1]])),
    ]
    sends, first_came = lax.optimization_barrier((sends, first_came))
    down_y, up_l = [exchange_bit(v, bit) for v, bit in zip(sends, "yl")]
    came_down0 = exchange_bit(send_down0, "c")
    total = attend(0, hand_on(d_contexts[0], d_contexts[1], first_came), ())
    (total, parts[0], second_came, near_pair, came_down0, send_out) = lax.optimization_barrier(
        (total, parts[0], second_came, d_contexts[3:5], came_down0, send_out)
    )

    out_x = exchange_bit(send_out, "x")
    second_group = hand_on(*near_pair, second_came)
    cross(0)
    for s in range(1, seq_count - 1):
        total = attend(s, second_group, total)
    (down_y, up_l, out_x, total, parts[1:], near, far) = lax.optimization_barrier(
        (down_y, up_l, out_x, total, parts[1:], near, far)
    )

    sends = [
        sum_low(keep_down[1], came_down0[1], down_y[1]),
        sum_low(keep_up[2], came_up1[0], up_l[1]),
    ]
    out_c = exchange_bit(sum_low(grad_out[1], out_x[1]), "c")
    (sends, total, out_c, far) = lax.optimization_barrier((sends, total, out_c, far))
    down_l, up_y = [exchange_bit(v, bit) for v, bit in zip(sends, "ly")]
    far_came = [exchange_bit(far[0], "x")]
    for s in range(1, seq_count - 1):
        cross(s)
    half_a, half_b = attend(
        seq_count - 1, second_group, total, (grad_out, out_x, out_c, sums)
    )

    (down_l, up_y, far, far_came, half_a, half_b, parts[-1]) = lax.optimization_barrier(
        (down_l, up_y, far, far_came, half_a, half_b, parts[-1])
    )
    down_own = sum_low(keep_down[0], came_down0[0], down_y[0], down_l)
    down_own = down_own.reshape(2, 2, hidden // 32, features)
    up_own = sum_low(keep_up[0], came_up0[0], up_l[0], up_y)
    up_own = up_own.reshape(2, 2, features // 4, hidden // 8)
    half_b = half_b.reshape(2, 2, 2, *half_b.shape[1:])
    keeps = [half_a[:4], half_b[:, 0], down_own[:, 0], up_own[:, 0]]
    sends = [half_a[4:], half_b[:, 1], down_own[:, 1], up_own[:, 1]]
    got = [exchange_bit(v, bit) for v, bit in zip(sends, "ylxx")]
    half_a, half_b, down, up = [k + g for k, g in zip(keeps, got)]
    near_far = far[1:]
    far = []
    cross(seq_count - 1)

    keeps, sends = [half_a[:2], half_b[0]], [half_a[2:], half_b[1]]
    (keeps, sends, down, up, far, near_far, near) = lax.optimization_barrier(
        (keeps, sends, down, up, far, near_far, near)
    )
    got = [exchange_bit(v, bit) for v, bit in zip(sends, "ly")]
    down_came = exchange_bit(down, "h")
    far_came += [exchange_bit(v, "x") for v in near_far]
    both = jnp.concatenate([k + g for k, g in zip(keeps, got)], axis=2)
    down = add_extra(down + down_came[::-1])

    (both, down, up, far, far_came) = lax.optimization_barrier((both, down, up, far, far_came))
    far_came += [exchange_bit(v, "x") for v in far]
    came = exchange_bit(both, "h")
    down = jnp.concatenate([down, exchange_bit(down, "l")])
    both = add_extra(both + came[::-1])

    (both, down, up, far_came) = lax.optimization_barrier((both, down, up, far_came))
    came, up_came = exchange_bit(both, "y"), exchange_bit(up, "h")
    down_hi = exchange_bit(down, "x")
    both = jnp.concatenate([both, came])
    up = add_extra(up + up_came[::-1])
    own_pos = mine * local_rows + jnp.arange(local_rows, dtype=jnp.int32)
    live = (own_pos[None, :] < lengths[:, None]).astype(f32)
    d_inputs = jnp.stack([n + f for n, f in zip(near, far_came)])
    grad_tokens = (d_inputs + d_first_in.reshape(seq_count, local_rows, features)) * live[:, :, None]


    (both, down, down_hi, up, grad_tokens) = lax.optimization_barrier(
        (both, down, down_hi, up, grad_tokens)
    )
    came = exchange_bit(both, "l")
    down_far = [exchange_bit(down, "y")]
    up_came = exchange_bit(up, "x")
    down_own = [down, down_hi]
    down_near = [exchange_bit(half, "c") for half in down_own]
    both = [jnp.concatenate([v[:2] for v in (both, came)]), jnp.concatenate([v[2:] for v in (both, came)])]
    up = jnp.concatenate([up, up_came])

    (both, down_own, down_near, down_far, up) = lax.optimization_barrier(
        (both, down_own, down_near, down_far, up)
    )
    across = [exchange_bit(both[0], "x")]
    down_far.append(exchange_bit(down_own[1], "y"))
    up_hi = exchange_bit(up, "l")
    across_down = [exchange_bit(down_far[0], "c")]
    both_near = [exchange_bit(both[0], "c")]
    full_down = gather_tiles(places, down_own + down_near, 0, [], (hidden, features), True)

    (both, across, up, up_hi, down_far, across_down, both_near, full_down) = (
        lax.optimization_barrier(
            (both, across, up, up_hi, down_far, across_down, both_near, full_down)
        )
    )
    across.append(exchange_bit(both[1], "x"))
    up_far = [exchange_bit(up, "y")]
    across_down.append(exchange_bit(down_far[1], "c"))
    up_own = [up, up_hi]
    up_near = [exchange_bit(half, "c") for half in up_own]
    full_down = gather_tiles(
        places, down_far + across_down, 1, [full_down], (hidden, features), True
    )
    full_up = gather_tiles(places, up_own + up_near, 0, [], (features, hidden), False)

    (both, across, up_hi, up_far, full_down, full_up) = lax.optimization_barrier(
        (both, across, up_hi, up_far, full_down, full_up)
    )
    up_second = [exchange_bit(up_hi[:1], "y")]
    both_near.append(exchange_bit(both[1], "c"))
    both_far = [exchange_bit(half, "c") for half in across]

    (up_hi, up_second, both_near, both_far) = lax.optimization_barrier(
        (up_hi, up_second, both_near, both_far)
    )
    up_second.append(exchange_bit(up_hi[1:], "y"))
    across_up = [exchange_bit(up_far[0], "c")]
    full_qkv, full_out, vector_rows, head_rows = gather_heads(
        places,
        both + both_near + across + both_far,
        tuple((r, first) for r in range(4) for first in (0, 4)),
        (features, 3 * features),
    )
    (up_second, across_up, full_qkv, vector_rows, head_rows) = lax.optimization_barrier(
        (up_second, across_up, full_qkv, vector_rows, head_rows)
    )
    up_far.append(jnp.concatenate(up_second))
    across_up.append(exchange_bit(up_far[1], "c"))
    full_up = gather_tiles(places, up_far + across_up, 1, [full_up], (features, hidden), False)
    (
        full_b_down,
        full_gain_two,
        full_shift_two,
        full_b_out,
        full_gain_one,
        full_shift_one,
    ) = [vector_rows[i] for i in range(6)]
    full_b_up = vector_rows[6 : 6 + hidden // features].reshape(hidden)
    full_b_query = head_rows[:seq_parts, :wide].reshape(features)
    full_b_value = head_rows[:seq_parts, 2 * wide : 3 * wide].reshape(features)

    return (
        out_tokens,
        grad_tokens,
        full_qkv,
        full_b_query,
        full_b_value,
        full_out,
        full_b_out,
        full_gain_one,
        full_shift_one,
        full_up,
        full_b_up,
        full_down,
        full_b_down,
        full_gain_two,
        full_shift_two,
    )


def solution(mesh):
    in_specs = (
        P("dp", "seq", None),
        P("dp", "seq", None),
        P("dp"),
        P("dp", None),
        P(),
        P(),
        P(),
        P(),
        P(),
        P(),
        P(),
        P(),
        P(),
        P(),
        P(),
        P(),
        P(),
    )
    out_specs = (
        P("dp", "seq", None),
        P("dp", "seq", None),
        P(),
        P(),
        P(),
        P(),
        P(),
        P(),
        P(),
        P(),
        P(),
        P(),
        P(),
        P(),
        P(),
    )
    return jax.shard_map(
        per_device, mesh=mesh, in_specs=in_specs, out_specs=out_specs, check_vma=False
    )
```

```python
import functools
import jax
import jax.numpy as jnp
from jax import lax
from jax.experimental import pallas as pl
from jax.experimental.pallas import tpu as pltpu
from jax.sharding import PartitionSpec as P

HEAD_DIM = 64
SOFT = HEAD_DIM ** -0.5 * 1.4426950408889634
NN = (((1,), (0,)), ((), ()))
NT = (((1,), (1,)), ((), ()))
TN = (((0,), (0,)), ((), ()))
VMEM_LIMIT = 60 * 1024 * 1024
HEADS = 12
EPSILON = 1e-06
BITS = {"c": ("seq", 0), "x": ("seq", 1), "y": ("dp", 0), "l": ("dp", 1), "h": ("dp", 2)}


def own_number(order):
    number = jnp.int32(0)
    for letter in order:
        axis, shift = BITS[letter]
        number = number * 2 + ((lax.axis_index(axis) >> shift) & 1)
    return number


def exchange(array_in, axis, flip):
    return lax.ppermute(array_in, axis, [(i, i ^ flip) for i in range(lax.axis_size(axis))])


def exchange_bit(array_in, letter):
    axis, shift = BITS[letter]
    return exchange(array_in, axis, 1 << shift)


def extra_flips(axis, used):
    return [1 << shift for shift in range(used, lax.axis_size(axis).bit_length() - 1)]


def add_extra(array_in):
    for flip in extra_flips("dp", 3):
        array_in = array_in + exchange(array_in, "dp", flip)
    return array_in


def sum_low(*parts):
    total = parts[0].astype(jnp.float32)
    for part in parts[1:]:
        total = total + part.astype(jnp.float32)
    return total.astype(jnp.bfloat16)


def dot_f32(left, right, dims):
    return lax.dot_general(left, right, dims, preferred_element_type=jnp.float32)


def sequence_scalars(places, index):
    seq_count = (places.shape[0] - 11) // 3
    return places[11 + index] >> 1, places[9], 11 + seq_count + 2 * index


def shift_matrix(half, block, whole):
    row = lax.broadcasted_iota(jnp.int32, (block, whole), 0)
    col = lax.broadcasted_iota(jnp.int32, (block, whole), 1)
    return jnp.where((col == row + half) & (row < half), 1.0, 0.0).astype(jnp.bfloat16)


def mask_tiles(half, block):
    row = lax.broadcasted_iota(jnp.int32, (16, block), 0)
    col = lax.broadcasted_iota(jnp.int32, (16, block), 1)
    key_tile = jnp.where((row == 0) & (col >= half), -1e30, 0.0).astype(jnp.bfloat16)
    query_tile = jnp.where(row == 0, 1.0, 0.0).astype(jnp.bfloat16)
    return key_tile, query_tile


def attend_forward(
    heads, index, places, x0, x1, x2, x3, w_t, bias, c0, c1, c2, c3,
    x_out, qkv_out, ctx_blk, lse, tok, c_tok, x_seq, qkv, sems,
):
    half, mine, perm = sequence_scalars(places, index)
    whole = x_seq.shape[0]
    quarter = whole // 4
    block = whole // 2
    wide = heads * HEAD_DIM
    for r, piece in enumerate((x0, x1, x2, x3)):
        x_seq[pl.ds(pl.multiple_of((r ^ mine) * quarter, quarter), quarter), :] = piece[...]
    keep_x = pltpu.make_async_copy(x_seq, x_out, sems.at[0])
    keep_x.start()
    lane = lax.broadcasted_iota(jnp.int32, (1, block), 1)
    tok[...] = (dot_f32(w_t[...], x_seq[...], NT) + bias[...]).astype(jnp.bfloat16)
    shift = shift_matrix(half, block, whole)
    qkv[0] = jnp.where(lane < half, tok[:, :block], jnp.zeros((), jnp.bfloat16))
    qkv[1] = dot_f32(tok[...], shift, NT).astype(jnp.bfloat16)
    keep_qkv = pltpu.make_async_copy(qkv, qkv_out, sems.at[1])
    keep_qkv.start()
    key_tile, query_tile = mask_tiles(half, block)

    def one_block(b, carry):
        target = places[perm + b]
        for h in range(heads):
            rows = slice(h * HEAD_DIM, (h + 1) * HEAD_DIM)
            q_t = jnp.concatenate([qkv[b, rows, :], query_tile])
            k_t = jnp.concatenate(
                [qkv[target, wide + h * HEAD_DIM : wide + (h + 1) * HEAD_DIM, :], key_tile]
            )
            v_t = qkv[target, 2 * wide + h * HEAD_DIM : 2 * wide + (h + 1) * HEAD_DIM, :]
            scores = dot_f32(k_t, q_t, TN) * SOFT
            top = jnp.max(scores, axis=0, keepdims=True)
            expo = jnp.exp2(scores - top)
            total = jnp.sum(expo, axis=0, keepdims=True)
            context = dot_f32(v_t, expo.astype(jnp.bfloat16), NN) / total
            ctx_blk[b, rows, :] = context
            lse[b, h : h + 1, :] = top + jnp.log2(total)
        return carry

    lax.fori_loop(0, 2, one_block, 0)
    early = jnp.where(lane < half, ctx_blk[0], 0.0)
    late = dot_f32(ctx_blk[1].astype(jnp.bfloat16), shift, NN)
    for j in range(4):
        part = late[:, j * quarter : (j + 1) * quarter]
        if j < 2:
            part = part + early[:, j * quarter : (j + 1) * quarter]
        c_tok[j] = part.astype(jnp.bfloat16)
    for r, piece in enumerate((c0, c1, c2, c3)):
        piece[...] = c_tok[r ^ mine]
    keep_x.wait()
    keep_qkv.wait()


def attend_backward(
    heads, index, places, g0, g1, g2, g3, w_t, x_in, qkv, ctx_blk, lse, *refs
):
    first, last = index == 0, len(refs) > 14
    acc_in, acc_b = (None, None) if first else refs[:2]
    (dx_keep, dx_send, grad_w, grad_w2, g_tok, g_blk, d_qkv, tok, x_seq, acc, dx_s, sems) = refs[-12:]
    bring_x = pltpu.make_async_copy(x_in, x_seq, sems.at[0])
    bring_x.start()
    if not first:
        bring_acc = pltpu.make_async_copy(acc_in, acc, sems.at[1])
        bring_acc.start()
    half, mine, perm = sequence_scalars(places, index)
    index = max(index - 1, 0)
    quarter = g0.shape[2]
    block = 2 * quarter
    whole = 4 * quarter
    wide = heads * HEAD_DIM
    for r, piece in enumerate((g0[index], g1[index], g2[0, index], g3[index])):
        g_tok[r ^ mine] = piece
    shift = shift_matrix(half, block, whole)
    lane = lax.broadcasted_iota(jnp.int32, (1, block), 1)
    g_all = jnp.concatenate([g_tok[j] for j in range(4)], axis=1)
    g_blk[0] = jnp.where(lane < half, g_all[:, :block], jnp.zeros((), jnp.bfloat16))
    g_blk[1] = dot_f32(g_all, shift, NT).astype(jnp.bfloat16)
    key_tile, query_tile = mask_tiles(half, block)

    def one_block(b, carry):
        target = places[perm + b]
        for h in range(heads):
            rows = slice(h * HEAD_DIM, (h + 1) * HEAD_DIM)
            k_rows = slice(wide + h * HEAD_DIM, wide + (h + 1) * HEAD_DIM)
            v_rows = slice(2 * wide + h * HEAD_DIM, 2 * wide + (h + 1) * HEAD_DIM)
            q_t = qkv[b, rows, :]
            k_t = qkv[target, k_rows, :]
            v_t = qkv[target, v_rows, :]
            g_t = g_blk[b, rows, :]
            scores = dot_f32(
                jnp.concatenate([k_t, key_tile]), jnp.concatenate([q_t, query_tile]), TN
            )
            probs = jnp.exp2(scores * SOFT - lse[b, h : h + 1, :])
            d_probs = dot_f32(v_t, g_t, TN)
            delta = jnp.sum(ctx_blk[b, rows, :] * g_t.astype(jnp.float32), axis=0, keepdims=True)
            d_scores = (probs * (d_probs - delta)).astype(jnp.bfloat16)
            scaling = HEAD_DIM ** -0.5
            d_qkv[b, rows, :] = (dot_f32(k_t, d_scores, NN) * scaling).astype(jnp.bfloat16)
            d_qkv[target, k_rows, :] = (dot_f32(q_t, d_scores, NT) * scaling).astype(jnp.bfloat16)
            d_qkv[target, v_rows, :] = dot_f32(g_t, probs.astype(jnp.bfloat16), NT).astype(
                jnp.bfloat16
            )
        return carry

    lax.fori_loop(0, 2, one_block, 0)
    late = dot_f32(d_qkv[1], shift, NN)
    front = jnp.where(lane < half, d_qkv[0].astype(jnp.float32), 0.0)
    tok[:, block:] = late[:, block:].astype(jnp.bfloat16)
    tok[:, :block] = (late[:, :block] + front).astype(jnp.bfloat16)
    sent = []
    for r in range(4):
        piece = (dx_send if r & 1 else dx_keep).at[r >> 1]
        columns = tok[:, pl.ds(pl.multiple_of((r ^ mine) * quarter, quarter), quarter)]
        dx_s[r] = dot_f32(columns, w_t[...], TN).astype(jnp.bfloat16)
        sent.append(pltpu.make_async_copy(dx_s.at[r], piece, sems.at[2 + r]))
        sent[-1].start()
    bring_x.wait()
    total = dot_f32(tok[...], x_seq[...], NN)
    ones = jnp.ones((8, whole), jnp.bfloat16)
    sums = dot_f32(ones, tok[...], NT)
    if not first:
        bring_acc.wait()
        total, sums = total + acc[...], sums + acc_b[...]
    if last:
        grad_out, out_x, out_c, vectors = refs[2:6]
        out_own = (
            grad_out[0].astype(jnp.float32)
            + out_x[0].astype(jnp.float32)
            + out_c[...].astype(jnp.float32)
        ).astype(jnp.bfloat16)
        inner = places[10]
        turned = total.T.astype(jnp.bfloat16)
        tile = out_own.shape[1]
        extra = grad_w.shape[1] - tile
        for half_w in (grad_w, grad_w2):
            half_w[:, tile:, :] = jnp.zeros((8, extra, 2 * wide), jnp.bfloat16)
        for q in range(8):
            rows = slice(q * tile, (q + 1) * tile)
            grad_w[q ^ inner, :tile, :] = turned[rows, : 2 * wide]
            grad_w2[q ^ inner, :tile, :wide] = turned[rows, 2 * wide :]
        grad_w2[:, :tile, wide:] = out_own
        row = lax.broadcasted_iota(jnp.int32, (extra, 1), 0)
        own_row = jnp.concatenate([sums[0:1, :], jnp.zeros((1, wide), jnp.float32)], axis=1)
        tile_rows = jnp.where(row == 10, own_row, vectors[...]).astype(jnp.bfloat16)
        grad_w[inner, tile:, :] = tile_rows[:, : 2 * wide]
        grad_w2[inner, tile:, :] = tile_rows[:, 2 * wide :]
    else:
        grad_w[...] = total
        grad_w2[...] = sums
    for copy in sent:
        copy.wait()


def kernel_call(body, scalars, arrays, outs, scratch, left_in=(), left_out=()):
    def spec(away):
        return pl.BlockSpec(memory_space=pl.ANY if away else pltpu.VMEM)

    return pl.pallas_call(
        body,
        out_shape=outs,
        in_specs=[pl.BlockSpec(memory_space=pltpu.SMEM)]
        + [spec(i in left_in) for i in range(len(arrays))],
        out_specs=[spec(i in left_out) for i in range(len(outs))],
        scratch_shapes=scratch,
        compiler_params=pltpu.CompilerParams(vmem_limit_bytes=VMEM_LIMIT),
        cost_estimate=pl.CostEstimate(
            flops=10**8, transcendentals=0, bytes_accessed=1024 * 1024
        ),
    )(scalars, *arrays)


def attention_forward(places, pieces, index, w_t, bias, heads):
    quarter, features = pieces[0].shape
    whole, block, wide = 4 * quarter, 2 * quarter, heads * HEAD_DIM
    out = jax.ShapeDtypeStruct
    outs = [out((wide, quarter), jnp.bfloat16)] * 4 + [
        out((whole, features), jnp.bfloat16),
        out((2, 3 * wide, block), jnp.bfloat16),
        out((2, wide, block), jnp.float32),
        out((2, 8, block), jnp.float32),
    ]
    scratch = [
        pltpu.VMEM((3 * wide, whole), jnp.bfloat16),
        pltpu.VMEM((4, wide, quarter), jnp.bfloat16),
        pltpu.VMEM((whole, features), jnp.bfloat16),
        pltpu.VMEM((2, 3 * wide, block), jnp.bfloat16),
        pltpu.SemaphoreType.DMA((2,)),
    ]
    found = kernel_call(
        functools.partial(attend_forward, heads, index),
        places,
        [*pieces, w_t, bias],
        outs,
        scratch,
        left_out=(4, 5),
    )
    return found[:4], found[4:]


def attention_backward(places, pieces, index, w_t, kept, before, heads, late=()):
    _, wide, quarter = pieces[0].shape
    features = w_t.shape[1]
    block = 2 * quarter
    out = jax.ShapeDtypeStruct
    if late:
        grads = [out((8, features // 8 + 16, 2 * wide), jnp.bfloat16)] * 2
    else:
        grads = [out((3 * wide, features), jnp.float32), out((8, 3 * wide), jnp.float32)]
    outs = [out((2, quarter, features), jnp.bfloat16)] * 2 + grads
    scratch = [
        pltpu.VMEM((4, wide, quarter), jnp.bfloat16),
        pltpu.VMEM((2, wide, block), jnp.bfloat16),
        pltpu.VMEM((2, 3 * wide, block), jnp.bfloat16),
        pltpu.VMEM((3 * wide, 4 * quarter), jnp.bfloat16),
        pltpu.VMEM((4 * quarter, features), jnp.bfloat16),
        pltpu.VMEM((3 * wide, features), jnp.float32),
        pltpu.VMEM((4, quarter, features), jnp.bfloat16),
        pltpu.SemaphoreType.DMA((6,)),
    ]
    found = kernel_call(
        functools.partial(attend_backward, heads, index),
        places,
        [*pieces, w_t, *kept, *before, *late],
        outs,
        scratch,
        left_in=(5, 9) if before else (5,),
        left_out=(0, 1),
    )
    return found[:2], found[2:]

def live_rows(places, rows, mine, local_rows, offset):
    row = lax.broadcasted_iota(jnp.int32, (rows, 1), 0)
    length = jnp.zeros((rows, 1), jnp.int32)
    for s in range(rows // local_rows):
        length = jnp.where(row >= s * local_rows, places[offset + s], length)
    position = mine * local_rows + lax.rem(row, local_rows)
    return jnp.where(position < length, 1.0, 0.0)


def normal_parts(array_in):
    centered = array_in - jnp.mean(array_in, axis=1, keepdims=True)
    spread = jnp.mean(centered * centered, axis=1, keepdims=True)
    inverse = lax.rsqrt(spread + EPSILON)
    return centered * inverse, inverse


def normal_back(hat, inverse, gain, d_out):
    scaled = d_out * gain
    mean_scaled = jnp.mean(scaled, axis=1, keepdims=True)
    mean_product = jnp.mean(scaled * hat, axis=1, keepdims=True)
    return inverse * (scaled - mean_scaled - hat * mean_product)


def column_sum(array_in):
    return jnp.sum(array_in, axis=0, keepdims=True)


def token_layer(shape, places, *refs):
    seq_count, seq_parts = shape
    count = seq_count * seq_parts
    pieces, refs = refs[:count], refs[count:]
    tokens, cot_in, w_out, vectors, b_up, w_up_in, w_down_in = refs[:7]
    out, send_down1, send_up1, send_down0, send_up0, keep_down, keep_up = refs[7:14]
    d_first_in, sums, grad_out, send_out = refs[14:18]
    sent = refs[18:24]
    (
        w_up, w_down, active, slope, context, first_in, first_norm, lowered,
        first_low, first_t, d_lowered, turned, out_s, cot, grad_down, grad_up, sems,
    ) = refs[24:]
    rows, features = tokens.shape
    local_rows = rows // seq_count
    wide = features // seq_parts
    mine, inner = places[9], places[8]
    step = pl.program_id(0)
    quarters = w_up.shape[0]
    width = w_up.shape[2]
    f32, bf16 = jnp.float32, jnp.bfloat16

    def bring(j):
        return (
            pltpu.make_async_copy(
                w_up_in.at[:, pl.ds(j * width, width)], w_up.at[j], sems.at[j]
            ),
            pltpu.make_async_copy(
                w_down_in.at[pl.ds(j * width, width), :], w_down.at[j], sems.at[quarters + j]
            ),
        )

    keep_out = pltpu.make_async_copy(out_s, out, sems.at[2 * quarters])
    bring_cot = pltpu.make_async_copy(cot_in, cot, sems.at[2 * quarters + 1])

    def leave(relative):
        down_ref, up_ref = (
            (keep_down.at[pl.ds(0, 2)], keep_up.at[pl.ds(0, 2)]),
            (keep_down.at[pl.ds(2, 2)], keep_up.at[pl.ds(2, 2)]),
            (send_down0, send_up0),
            (send_down1, send_up1),
        )[relative]
        first = 2 * quarters + 2 + 2 * relative
        return (
            pltpu.make_async_copy(grad_down.at[relative & 1], down_ref, sems.at[first]),
            pltpu.make_async_copy(grad_up.at[relative & 1], up_ref, sems.at[first + 1]),
        )

    @pl.when(step == 0)
    def start():
        for j in range(quarters):
            for copy in bring(j):
                copy.start()
        bring_cot.start()
        for s in range(seq_count):
            for r in range(seq_parts):
                context[
                    pl.ds(pl.multiple_of((r ^ mine) * wide, wide), wide),
                    s * local_rows : (s + 1) * local_rows,
                ] = pieces[s * seq_parts + r][...]
        live = live_rows(places, rows, mine, local_rows, 11)
        attended = dot_f32(context[...], w_out[...], TN) + vectors[0:1, :]
        total = jnp.where(live > 0, tokens[...].astype(f32), 0.0) + attended
        first_in[...] = total
        hat, _ = normal_parts(total)
        normed = hat * vectors[1:2, :] + vectors[2:3, :]
        first_norm[...] = normed
        low = normed.astype(bf16)
        first_low[...] = low
        tile = features // 4
        low_t = low.T
        for q in range(4):
            first_t[pl.ds(pl.multiple_of((q ^ inner) * tile, tile), tile), :] = low_t[
                q * tile : (q + 1) * tile
            ]
        lowered[...] = jnp.zeros_like(lowered)
        sums[...] = jnp.zeros_like(sums)

    @pl.when(step < quarters)
    def forward():
        for j in range(quarters):

            @pl.when(step == j)
            def arrive():
                for copy in bring(j):
                    copy.wait()

        lifted = dot_f32(first_low[...], w_up[step], NN) + b_up[step]
        cdf = 0.5 * (1.0 + lax.erf(lifted * 0.7071067811865476))
        density = jnp.exp(lifted * lifted * -0.5) * 0.3989422804014327
        gelu = (lifted * cdf).astype(bf16)
        active[step] = gelu
        slope[step] = (cdf + lifted * density).astype(bf16)
        lowered[...] += dot_f32(gelu, w_down[step], NN)

    @pl.when(step == quarters - 1)
    def turn():
        live = live_rows(places, rows, mine, local_rows, 11)
        hat, inverse = normal_parts(first_norm[...] + (lowered[...] + vectors[3:4, :]))
        gain = vectors[4:5, :]
        bring_cot.wait()
        out_s[...] = ((hat * gain + vectors[5:6, :]) * live).astype(bf16)
        keep_out.start()
        incoming = cot[...].astype(f32) * live
        back = normal_back(hat, inverse, gain, incoming)
        lowered[...] = back
        low = back.astype(bf16)
        d_lowered[...] = low
        sums[0:1, :] = column_sum(low.astype(f32))
        sums[1:2, :] = column_sum(incoming * hat)
        sums[2:3, :] = column_sum(incoming)

    @pl.when(step >= quarters)
    def backward():
        relative = 2 * quarters - 1 - step
        quarter = relative ^ (places[0] >> 1)
        low_bit = places[0] & 1
        slot = relative & 1
        half = width // 2
        tile = half // 4
        for k in range(2):

            @pl.when(relative == k)
            def free():
                for copy in leave(k + 2):
                    copy.wait()

        down = dot_f32(active[quarter], d_lowered[...], TN).astype(bf16)
        for j in range(2):
            for q in range(4):
                grad_down[
                    slot, j ^ low_bit, pl.ds(pl.multiple_of((q ^ inner) * tile, tile), tile), :
                ] = down[j * half + q * tile : j * half + (q + 1) * tile]
        d_active = dot_f32(d_lowered[...], w_down[quarter], NT)
        d_lifted = (d_active * slope[quarter].astype(f32)).astype(bf16)
        up = dot_f32(first_t[...], d_lifted, NN).astype(bf16)
        for j in range(2):
            grad_up[slot, j ^ low_bit] = up[:, j * half : (j + 1) * half]
        sums[pl.ds(6 + quarter, 1), :] = column_sum(d_lifted.astype(f32))
        lowered[...] += dot_f32(d_lifted, w_up[quarter], NT)
        for k in range(quarters):

            @pl.when(relative == k)
            def start_leaving():
                for copy in leave(k):
                    copy.start()

    @pl.when(step == 2 * quarters - 1)
    def finish():
        hat, inverse = normal_parts(first_in[...])
        incoming = lowered[...]
        back = normal_back(hat, inverse, vectors[1:2, :], incoming)
        d_first_in[...] = back
        low = back.astype(bf16)
        sums[3:4, :] = column_sum(low.astype(f32))
        sums[4:5, :] = column_sum(incoming * hat)
        sums[5:6, :] = column_sum(incoming)
        turned[...] = dot_f32(w_out[...], low, NT).astype(bf16)
        for r in range(seq_parts):
            own = turned[pl.ds(pl.multiple_of((r ^ mine) * wide, wide), wide), :]
            for s in range(seq_count):
                target, place = sent[3 * min(s, 1) + min(r, 2)], max(s - 1, 0)
                columns = own[:, s * local_rows : (s + 1) * local_rows]
                if r < 2:
                    target[place] = columns
                else:
                    target[r - 2, place] = columns
        product = dot_f32(context[...], low, NN).astype(bf16)
        block_rows, block_cols = grad_out.shape[2:]
        across = features // block_cols
        for j in range(seq_parts):
            for q in range(wide // block_rows * across):
                row, col = j * wide + q // across * block_rows, q % across * block_cols
                block = product[row : row + block_rows, col : col + block_cols]
                place, inner_place = j ^ mine, q ^ places[10]

                @pl.when(place < 2)
                def own():
                    grad_out[place, inner_place] = block

                @pl.when(place >= 2)
                def across_x():
                    send_out[place - 2, inner_place] = block

        keep_out.wait()
        for k in range(2):
            for copy in leave(k):
                copy.wait()


def whole_spec(shape):
    return pl.BlockSpec(
        shape, lambda p, places: (0,) * len(shape), pipeline_mode=pl.Buffered(buffer_count=1)
    )


def step_call(body, places, steps, ins, in_specs, outs, out_specs, scratch, flops, aliases={}):
    return pl.pallas_call(
        body,
        out_shape=outs,
        grid_spec=pltpu.PrefetchScalarGridSpec(
            num_scalar_prefetch=1,
            grid=(steps,),
            in_specs=in_specs,
            out_specs=out_specs,
            scratch_shapes=scratch,
        ),
        input_output_aliases=aliases,
        compiler_params=pltpu.CompilerParams(vmem_limit_bytes=VMEM_LIMIT),
        cost_estimate=pl.CostEstimate(
            flops=flops, transcendentals=0, bytes_accessed=1024 * 1024
        ),
    )(places, *ins)


def run_token_layer(places, pieces, tokens, cot, w_out, vectors, w_up, b_up, w_down, dims):
    seq_count, seq_parts = dims
    rows, features = tokens.shape
    hidden = w_up.shape[1]
    quarters = 4
    width = hidden // quarters
    half = width // 2
    out, bf16, f32 = jax.ShapeDtypeStruct, jnp.bfloat16, jnp.float32
    square, turned = (rows, features), (features, rows)
    piece = (features // seq_parts, rows // seq_count)
    sent = []
    for n in (1, seq_count - 1):
        sent += [(n, *piece), (n, *piece), (2, n, *piece)]
    out_blocks = (seq_parts // 2, 8, features // seq_parts // 2, features // 4)
    away = pl.BlockSpec(memory_space=pl.ANY)
    down, up = (2, half, features), (2, features, half)

    return step_call(
        functools.partial(token_layer, dims),
        places,
        2 * quarters,
        [*pieces, tokens, cot, w_out, vectors, b_up.reshape(quarters, 1, width), w_up, w_down],
        [whole_spec(p.shape) for p in pieces]
        + [whole_spec(square), away, whole_spec(w_out.shape), whole_spec(vectors.shape)]
        + [whole_spec((quarters, 1, width)), away, away],
        [
            out(square, bf16),
            out(down, bf16),
            out(up, bf16),
            out(down, bf16),
            out(up, bf16),
            out((4, half, features), bf16),
            out((4, features, half), bf16),
            out(square, f32),
            out((16, features), f32),
            out(out_blocks, bf16),
            out(out_blocks, bf16),
        ]
        + [out(p, bf16) for p in sent],
        [away] * 7
        + [whole_spec(square), whole_spec((16, features))]
        + [whole_spec(out_blocks)] * 2
        + [whole_spec(p) for p in sent],
        [
            pltpu.VMEM((quarters, features, width), bf16),
            pltpu.VMEM((quarters, width, features), bf16),
            pltpu.VMEM((quarters, rows, width), bf16),
            pltpu.VMEM((quarters, rows, width), bf16),
            pltpu.VMEM(turned, bf16),
            pltpu.VMEM(square, f32),
            pltpu.VMEM(square, f32),
            pltpu.VMEM(square, f32),
            pltpu.VMEM(square, bf16),
            pltpu.VMEM(turned, bf16),
            pltpu.VMEM(square, bf16),
            pltpu.VMEM(turned, bf16),
            pltpu.VMEM(square, bf16),
            pltpu.VMEM(square, bf16),
            pltpu.VMEM((2, *down), bf16),
            pltpu.VMEM((2, *up), bf16),
            pltpu.SemaphoreType.DMA((4 * quarters + 2,)),
        ],
        2 * rows * features * (6 * hidden + 3 * features),
    )


def place_tiles(by_rows, late, some, places, *refs):
    count = 2 * (2 if by_rows else len(some))
    sources, out = refs[:count], refs[-4]
    held, main, sems = refs[-3:]
    inner = places[8]
    _, rows, cols = sources[0].shape
    bring = [
        pltpu.make_async_copy(source, held.at[k], sems.at[k]) for k, source in enumerate(sources)
    ]
    for copy in bring:
        copy.start()
    for copy in bring:
        copy.wait()
    sent = []
    for k in range(2):
        for i, l in enumerate(some):
            block = places[k * 4 + late * 2 + l]
            place = len(some) * k + i
            for q in range(4):
                h, x = q >> 1, q & 1
                half, n = (2 * k + x, l * 2 + h) if by_rows else (place, x * 2 + h)
                first = pl.multiple_of((q ^ inner) * rows, rows)
                main[place, pl.ds(first, rows), :] = held[half, n].astype(jnp.float32)
            if by_rows:
                target = out.at[pl.ds(pl.multiple_of(block * 4 * rows, 4 * rows), 4 * rows)]
            else:
                target = out.at[:, pl.ds(pl.multiple_of(block * cols, cols), cols)]
            sent.append(pltpu.make_async_copy(main.at[place], target, sems.at[count + place]))
            sent[-1].start()
    for copy in sent:
        copy.wait()


def gather_tiles(places, halves, late, begun, shape, by_rows, some=(0, 1)):
    _, rows, cols = halves[0].shape
    count = len(halves)
    away = pl.BlockSpec(memory_space=pl.ANY)
    return pl.pallas_call(
        functools.partial(place_tiles, by_rows, late, some),
        out_shape=jax.ShapeDtypeStruct(shape, jnp.float32),
        in_specs=[pl.BlockSpec(memory_space=pltpu.SMEM)] + [away] * (count + len(begun)),
        out_specs=away,
        scratch_shapes=[
            pltpu.VMEM((count, 4, rows, cols), jnp.bfloat16),
            pltpu.VMEM((2 * len(some), 4 * rows, cols), jnp.float32),
            pltpu.SemaphoreType.DMA((count + 2 * len(some),)),
        ],
        input_output_aliases={count + 1: 0} if begun else {},
        compiler_params=pltpu.CompilerParams(vmem_limit_bytes=VMEM_LIMIT),
    )(places, *halves, *begun)


def place_heads(parts, places, *refs):
    seq_parts = parts[-1][0] + 1
    sources, refs = refs[: len(parts)], refs[len(parts) :]
    out, out_w, vector_rows, head_rows = refs[:4]
    pieces = refs[4 : seq_parts + 4]
    main, side, sems = refs[seq_parts + 4 :]
    mine, inner = places[9], places[10]
    blocks, rows, _ = main.shape
    features = side.shape[2]
    wide = features // seq_parts
    f32 = jnp.float32
    bring = [
        pltpu.make_async_copy(
            source, pieces[r].at[pl.ds(first, source.shape[0])], sems.at[2 * blocks + i]
        )
        for i, (source, (r, first)) in enumerate(zip(sources, parts))
    ]
    for copy in bring:
        copy.start()
    for copy in bring:
        copy.wait()

    def leave(p, source, target, slot):
        first = pl.multiple_of(p * rows, rows)
        return pltpu.make_async_copy(source.at[p], target.at[pl.ds(first, rows)], sems.at[slot + p])

    def one_block(p, carry):
        for m in range(seq_parts):

            @pl.when(mine == m)
            def copy():
                near = [pieces[j ^ m][p ^ inner, :rows, : 3 * wide] for j in range(seq_parts)]
                for section in range(3):
                    columns = slice(section * wide, (section + 1) * wide)
                    joined = jnp.concatenate([part[:, columns] for part in near], axis=1)
                    main[p, :, section * features : (section + 1) * features] = joined.astype(f32)

        leave(p, main, out, 0).start()
        for r, piece in enumerate(pieces):

            @pl.when(((r ^ mine) == p >> 1))
            def copy_side():
                first = (p & 1) * 4
                joined = jnp.concatenate(
                    [piece[(first + q) ^ inner, :rows, 3 * wide :] for q in range(4)], axis=1
                )
                side[p] = joined.astype(f32)

        leave(p, side, out_w, blocks).start()
        return carry

    lax.fori_loop(0, blocks, one_block, 0)
    for m in range(seq_parts):

        @pl.when(mine == m)
        def copy_vectors():
            held = [pieces[j ^ m][inner, rows:, :].astype(f32) for j in range(seq_parts)]
            total = held[0]
            for other in held[1:]:
                total = total + other
            vector_rows[...] = total
            head_rows[...] = jnp.zeros_like(head_rows)
            for j in range(seq_parts):
                head_rows[j : j + 1, :] = held[j][10:11, :]

    for p in range(blocks):
        leave(p, main, out, 0).wait()
        leave(p, side, out_w, blocks).wait()


def gather_heads(places, sources, parts, shape):
    out, f32 = jax.ShapeDtypeStruct, jnp.float32
    features = shape[0]
    rows = features // 8
    extra = (sources[0].shape[1] - rows, features)
    count = parts[-1][0] + 1
    piece = (8, *sources[0].shape[1:])
    away = pl.BlockSpec(memory_space=pl.ANY)
    here = pl.BlockSpec(memory_space=pltpu.VMEM)
    return pl.pallas_call(
        functools.partial(place_heads, parts),
        out_shape=[
            out(shape, f32),
            out((features, features), f32),
            out(extra, f32),
            out((8, features), f32),
        ],
        in_specs=[pl.BlockSpec(memory_space=pltpu.SMEM)] + [away] * len(sources),
        out_specs=[away, away, here, here],
        scratch_shapes=[pltpu.VMEM(piece, sources[0].dtype)] * count
        + [
            pltpu.VMEM((8, rows, shape[1]), f32),
            pltpu.VMEM((8, rows, features), f32),
            pltpu.SemaphoreType.DMA((16 + len(sources),)),
        ],
        compiler_params=pltpu.CompilerParams(vmem_limit_bytes=VMEM_LIMIT),
    )(places, *sources)


def per_device(
    tokens,
    cotangent,
    lengths,
    block_perm,
    w_qkv,
    b_query,
    b_value,
    w_out,
    b_out,
    ln1_gain,
    ln1_shift,
    w_up,
    b_up,
    w_down,
    b_down,
    ln2_gain,
    ln2_shift,
):
    seq_parts = lax.axis_size("seq")
    mine = lax.axis_index("seq")
    seq_count, local_rows, features = tokens.shape
    flat_rows = seq_count * local_rows
    hidden = w_up.shape[1]
    heads = HEADS // seq_parts
    wide = heads * HEAD_DIM
    dims = (seq_count, seq_parts)
    f32 = jnp.float32

    w_heads = jnp.concatenate(
        [
            lax.dynamic_slice_in_dim(w_qkv, k * features + mine * wide, wide, axis=1)
            for k in range(3)
        ],
        axis=1,
    )
    w_t = w_heads.T
    bias = jnp.concatenate(
        [
            lax.dynamic_slice_in_dim(b_query, mine * wide, wide),
            jnp.zeros((wide,), b_query.dtype),
            lax.dynamic_slice_in_dim(b_value, mine * wide, wide),
        ]
    ).astype(f32)[:, None]
    outer = own_number("cyl")
    places = jnp.concatenate(
        [
            jnp.arange(8, dtype=jnp.int32) ^ outer,
            jnp.stack([own_number("hx"), mine, own_number("ylh")]),
            lengths,
            block_perm.reshape(-1),
        ]
    )
    vectors = jnp.stack(
        [v.astype(f32) for v in (b_out, ln1_gain, ln1_shift, b_down, ln2_gain, ln2_shift, b_out, b_out)]
    )

    arrived, kept, crossed = [], [], []
    for s in range(seq_count):
        near = tokens[s]
        start = near
        if s > 0:
            after = [crossed[-1]] + arrived[(s - 2) * seq_parts : (s - 2) * seq_parts + 1] * (s > 1)
            start, _ = lax.optimization_barrier((near, after))
        across = exchange_bit(start, "x")
        crossed.append(across)
        if s == 0:
            across, w_t, bias, places = lax.optimization_barrier((across, w_t, bias, places))
        if s > 0:
            across, _ = lax.optimization_barrier((across, arrived[-seq_parts]))
        pieces = [near, exchange_bit(near, "c"), across, exchange_bit(across, "c")]
        contexts, saved = attention_forward(places, pieces, s, w_t, bias, heads)
        kept.append(saved)
        arrived += [contexts[0]] + [exchange(contexts[r], "seq", r) for r in range(1, seq_parts)]

    (
        out_rows,
        send_down1,
        send_up1,
        send_down0,
        send_up0,
        keep_down,
        keep_up,
        d_first_in,
        sums,
        grad_out,
        send_out,
        *d_contexts,
    ) = run_token_layer(
        places,
        arrived,
        tokens.reshape(flat_rows, features),
        cotangent.reshape(flat_rows, features),
        w_out,
        vectors,
        w_up,
        b_up.astype(f32).reshape(1, hidden),
        w_down,
        dims,
    )
    out_tokens = out_rows.reshape(seq_count, local_rows, features)

    def hand_on(own, near, came):
        return [own, exchange_bit(near, "c"), came, exchange_bit(came[1], "c")]

    first_came = exchange_bit(d_contexts[2], "x")
    came_down1, came_up1 = exchange_bit(send_down1, "c"), exchange_bit(send_up1, "c")
    send_up0, first_came = lax.optimization_barrier((send_up0, first_came))
    came_up0 = exchange_bit(send_up0, "c")
    second_pair, first_came = lax.optimization_barrier((d_contexts[5], first_came))
    second_came = exchange_bit(second_pair, "x")
    parts, near, far = [], [], []

    def attend(s, group, before, late=()):
        found, total = attention_backward(places, group, s, w_t, kept[s], before, heads, late)
        parts.append(found)
        return total

    def cross(s):
        held, sent = parts[s]
        came = exchange_bit(sent, "c")
        near.append(held[0].astype(f32) + came[0])
        far.append(sum_low(held[1], came[1]))

    sends = [
        sum_low(keep_down[2:], came_down1),
        sum_low(keep_up[1::2], jnp.stack([came_up0[1], came_up1[1]])),
    ]
    sends, first_came = lax.optimization_barrier((sends, first_came))
    down_y, up_l = [exchange_bit(v, bit) for v, bit in zip(sends, "yl")]
    came_down0 = exchange_bit(send_down0, "c")
    total = attend(0, hand_on(d_contexts[0], d_contexts[1], first_came), ())
    (total, parts[0], second_came, near_pair, came_down0, send_out) = lax.optimization_barrier(
        (total, parts[0], second_came, d_contexts[3:5], came_down0, send_out)
    )

    out_x = exchange_bit(send_out, "x")
    second_group = hand_on(*near_pair, second_came)
    cross(0)
    for s in range(1, seq_count - 1):
        total = attend(s, second_group, total)
    (down_y, up_l, out_x, total, parts[1:], near, far) = lax.optimization_barrier(
        (down_y, up_l, out_x, total, parts[1:], near, far)
    )

    sends = [
        sum_low(keep_down[1], came_down0[1], down_y[1]),
        sum_low(keep_up[2], came_up1[0], up_l[1]),
    ]
    out_c = exchange_bit(sum_low(grad_out[1], out_x[1]), "c")
    (sends, total, out_c, far) = lax.optimization_barrier((sends, total, out_c, far))
    down_l, up_y = [exchange_bit(v, bit) for v, bit in zip(sends, "ly")]
    far_came = [exchange_bit(far[0], "x")]
    for s in range(1, seq_count - 1):
        cross(s)
    half_a, half_b = attend(
        seq_count - 1, second_group, total, (grad_out, out_x, out_c, sums)
    )

    (down_l, up_y, far, far_came, half_a, half_b, parts[-1]) = lax.optimization_barrier(
        (down_l, up_y, far, far_came, half_a, half_b, parts[-1])
    )
    down_own = sum_low(keep_down[0], came_down0[0], down_y[0], down_l)
    down_own = down_own.reshape(2, 2, hidden // 32, features)
    up_own = sum_low(keep_up[0], came_up0[0], up_l[0], up_y)
    up_own = up_own.reshape(2, 2, features // 4, hidden // 8)
    half_b = half_b.reshape(2, 2, 2, *half_b.shape[1:])
    keeps = [half_a[:4], half_b[:, 0], down_own[:, 0], up_own[:, 0]]
    sends = [half_a[4:], half_b[:, 1], down_own[:, 1], up_own[:, 1]]
    got = [exchange_bit(v, bit) for v, bit in zip(sends, "ylxx")]
    half_a, half_b, down, up = [k + g for k, g in zip(keeps, got)]
    near_far = far[1:]
    far = []
    cross(seq_count - 1)

    keeps, sends = [half_a[:2], half_b[0]], [half_a[2:], half_b[1]]
    (keeps, sends, down, up, far, near_far, near) = lax.optimization_barrier(
        (keeps, sends, down, up, far, near_far, near)
    )
    got = [exchange_bit(v, bit) for v, bit in zip(sends, "ly")]
    down_came = exchange_bit(down, "h")
    far_came += [exchange_bit(v, "x") for v in near_far]
    both = jnp.concatenate([k + g for k, g in zip(keeps, got)], axis=2)
    down = add_extra(down + down_came[::-1])

    (both, down, up, far, far_came) = lax.optimization_barrier((both, down, up, far, far_came))
    far_came += [exchange_bit(v, "x") for v in far]
    came = exchange_bit(both, "h")
    down = jnp.concatenate([down, exchange_bit(down, "l")])
    both = add_extra(both + came[::-1])

    (both, down, up, far_came) = lax.optimization_barrier((both, down, up, far_came))
    came, up_came = exchange_bit(both, "y"), exchange_bit(up, "h")
    down_hi = exchange_bit(down, "x")
    both = jnp.concatenate([both, came])
    up = add_extra(up + up_came[::-1])
    own_pos = mine * local_rows + jnp.arange(local_rows, dtype=jnp.int32)
    live = (own_pos[None, :] < lengths[:, None]).astype(f32)
    d_inputs = jnp.stack([n + f for n, f in zip(near, far_came)])
    grad_tokens = (d_inputs + d_first_in.reshape(seq_count, local_rows, features)) * live[:, :, None]


    (both, down, down_hi, up, grad_tokens) = lax.optimization_barrier(
        (both, down, down_hi, up, grad_tokens)
    )
    came = exchange_bit(both, "l")
    down_far = [exchange_bit(down, "y")]
    up_came = exchange_bit(up, "x")
    down_own = [down, down_hi]
    down_near = [exchange_bit(half, "c") for half in down_own]
    both = [jnp.concatenate([v[:2] for v in (both, came)]), jnp.concatenate([v[2:] for v in (both, came)])]
    up = jnp.concatenate([up, up_came])

    (both, down_own, down_near, down_far, up) = lax.optimization_barrier(
        (both, down_own, down_near, down_far, up)
    )
    across = [exchange_bit(both[0], "x")]
    down_far.append(exchange_bit(down_own[1], "y"))
    up_hi = exchange_bit(up, "l")
    across_down = [exchange_bit(down_far[0], "c")]
    both_near = [exchange_bit(both[0], "c")]
    full_down = gather_tiles(places, down_own + down_near, 0, [], (hidden, features), True)

    (both, across, up, up_hi, down_far, across_down, both_near, full_down) = (
        lax.optimization_barrier(
            (both, across, up, up_hi, down_far, across_down, both_near, full_down)
        )
    )
    across.append(exchange_bit(both[1], "x"))
    up_far = [exchange_bit(up, "y")]
    across_down.append(exchange_bit(down_far[1], "c"))
    up_own = [up, up_hi]
    up_near = [exchange_bit(half, "c") for half in up_own]
    full_down = gather_tiles(
        places, down_far + across_down, 1, [full_down], (hidden, features), True
    )
    full_up = gather_tiles(places, up_own + up_near, 0, [], (features, hidden), False)

    (both, across, up_hi, up_far, full_down, full_up) = lax.optimization_barrier(
        (both, across, up_hi, up_far, full_down, full_up)
    )
    up_second = [exchange_bit(up_hi[:1], "y")]
    both_near.append(exchange_bit(both[1], "c"))
    both_far = [exchange_bit(half, "c") for half in across]

    (up_hi, up_second, up_far, both_near, both_far) = lax.optimization_barrier(
        (up_hi, up_second, up_far, both_near, both_far)
    )
    up_second.append(exchange_bit(up_hi[1:], "y"))
    across_up = [exchange_bit(up_far[0], "c")]
    full_qkv, full_out, vector_rows, head_rows = gather_heads(
        places,
        both + both_near + across + both_far,
        tuple((r, first) for r in range(4) for first in (0, 4)),
        (features, 3 * features),
    )
    full_up = gather_tiles(
        places, up_far + across_up, 1, [full_up], (features, hidden), False, (0,)
    )
    (up_second, full_up, full_qkv, vector_rows, head_rows) = lax.optimization_barrier(
        (up_second, full_up, full_qkv, vector_rows, head_rows)
    )
    up_last = jnp.concatenate(up_second)
    full_up = gather_tiles(
        places,
        [up_last, exchange_bit(up_last, "c")],
        1,
        [full_up],
        (features, hidden),
        False,
        (1,),
    )
    (
        full_b_down,
        full_gain_two,
        full_shift_two,
        full_b_out,
        full_gain_one,
        full_shift_one,
    ) = [vector_rows[i] for i in range(6)]
    full_b_up = vector_rows[6 : 6 + hidden // features].reshape(hidden)
    full_b_query = head_rows[:seq_parts, :wide].reshape(features)
    full_b_value = head_rows[:seq_parts, 2 * wide : 3 * wide].reshape(features)

    return (
        out_tokens,
        grad_tokens,
        full_qkv,
        full_b_query,
        full_b_value,
        full_out,
        full_b_out,
        full_gain_one,
        full_shift_one,
        full_up,
        full_b_up,
        full_down,
        full_b_down,
        full_gain_two,
        full_shift_two,
    )


def solution(mesh):
    in_specs = (
        P("dp", "seq", None),
        P("dp", "seq", None),
        P("dp"),
        P("dp", None),
        P(),
        P(),
        P(),
        P(),
        P(),
        P(),
        P(),
        P(),
        P(),
        P(),
        P(),
        P(),
        P(),
    )
    out_specs = (
        P("dp", "seq", None),
        P("dp", "seq", None),
        P(),
        P(),
        P(),
        P(),
        P(),
        P(),
        P(),
        P(),
        P(),
        P(),
        P(),
        P(),
        P(),
    )
    return jax.shard_map(
        per_device, mesh=mesh, in_specs=in_specs, out_specs=out_specs, check_vma=False
    )
```

```python
import functools
import jax
import jax.numpy as jnp
from jax import lax
from jax.experimental import pallas as pl
from jax.experimental.pallas import tpu as pltpu
from jax.sharding import PartitionSpec as P

HEAD_DIM = 64
SOFT = HEAD_DIM ** -0.5 * 1.4426950408889634
NN = (((1,), (0,)), ((), ()))
NT = (((1,), (1,)), ((), ()))
TN = (((0,), (0,)), ((), ()))
VMEM_LIMIT = 60 * 1024 * 1024
HEADS = 12
EPSILON = 1e-06
BITS = {"c": ("seq", 0), "x": ("seq", 1), "y": ("dp", 0), "l": ("dp", 1), "h": ("dp", 2)}


def own_number(order):
    number = jnp.int32(0)
    for letter in order:
        axis, shift = BITS[letter]
        number = number * 2 + ((lax.axis_index(axis) >> shift) & 1)
    return number


def exchange(array_in, axis, flip):
    return lax.ppermute(array_in, axis, [(i, i ^ flip) for i in range(lax.axis_size(axis))])


def exchange_bit(array_in, letter):
    axis, shift = BITS[letter]
    return exchange(array_in, axis, 1 << shift)


def extra_flips(axis, used):
    return [1 << shift for shift in range(used, lax.axis_size(axis).bit_length() - 1)]


def add_extra(array_in):
    for flip in extra_flips("dp", 3):
        array_in = array_in + exchange(array_in, "dp", flip)
    return array_in


def sum_low(*parts):
    total = parts[0].astype(jnp.float32)
    for part in parts[1:]:
        total = total + part.astype(jnp.float32)
    return total.astype(jnp.bfloat16)


def dot_f32(left, right, dims):
    return lax.dot_general(left, right, dims, preferred_element_type=jnp.float32)


def sequence_scalars(places, index):
    seq_count = (places.shape[0] - 11) // 3
    return places[11 + index] >> 1, places[9], 11 + seq_count + 2 * index


def shift_matrix(half, block, whole):
    row = lax.broadcasted_iota(jnp.int32, (block, whole), 0)
    col = lax.broadcasted_iota(jnp.int32, (block, whole), 1)
    return jnp.where((col == row + half) & (row < half), 1.0, 0.0).astype(jnp.bfloat16)


def mask_tiles(half, block):
    row = lax.broadcasted_iota(jnp.int32, (16, block), 0)
    col = lax.broadcasted_iota(jnp.int32, (16, block), 1)
    key_tile = jnp.where((row == 0) & (col >= half), -1e30, 0.0).astype(jnp.bfloat16)
    query_tile = jnp.where(row == 0, 1.0, 0.0).astype(jnp.bfloat16)
    return key_tile, query_tile


def attend_forward(
    heads, index, places, x0, x1, x2, x3, w_t, bias, c0, c1, c2, c3,
    x_out, qkv_out, ctx_blk, lse, tok, c_tok, x_seq, qkv, sems,
):
    half, mine, perm = sequence_scalars(places, index)
    whole = x_seq.shape[0]
    quarter = whole // 4
    block = whole // 2
    wide = heads * HEAD_DIM
    for r, piece in enumerate((x0, x1, x2, x3)):
        x_seq[pl.ds(pl.multiple_of((r ^ mine) * quarter, quarter), quarter), :] = piece[...]
    keep_x = pltpu.make_async_copy(x_seq, x_out, sems.at[0])
    keep_x.start()
    lane = lax.broadcasted_iota(jnp.int32, (1, block), 1)
    tok[...] = (dot_f32(w_t[...], x_seq[...], NT) + bias[...]).astype(jnp.bfloat16)
    shift = shift_matrix(half, block, whole)
    qkv[0] = jnp.where(lane < half, tok[:, :block], jnp.zeros((), jnp.bfloat16))
    qkv[1] = dot_f32(tok[...], shift, NT).astype(jnp.bfloat16)
    keep_qkv = pltpu.make_async_copy(qkv, qkv_out, sems.at[1])
    keep_qkv.start()
    key_tile, query_tile = mask_tiles(half, block)

    def one_block(b, carry):
        target = places[perm + b]
        for h in range(heads):
            rows = slice(h * HEAD_DIM, (h + 1) * HEAD_DIM)
            q_t = jnp.concatenate([qkv[b, rows, :], query_tile])
            k_t = jnp.concatenate(
                [qkv[target, wide + h * HEAD_DIM : wide + (h + 1) * HEAD_DIM, :], key_tile]
            )
            v_t = qkv[target, 2 * wide + h * HEAD_DIM : 2 * wide + (h + 1) * HEAD_DIM, :]
            scores = dot_f32(k_t, q_t, TN) * SOFT
            top = jnp.max(scores, axis=0, keepdims=True)
            expo = jnp.exp2(scores - top)
            total = jnp.sum(expo, axis=0, keepdims=True)
            context = dot_f32(v_t, expo.astype(jnp.bfloat16), NN) / total
            ctx_blk[b, rows, :] = context
            lse[b, h : h + 1, :] = top + jnp.log2(total)
        return carry

    lax.fori_loop(0, 2, one_block, 0)
    early = jnp.where(lane < half, ctx_blk[0], 0.0)
    late = dot_f32(ctx_blk[1].astype(jnp.bfloat16), shift, NN)
    for j in range(4):
        part = late[:, j * quarter : (j + 1) * quarter]
        if j < 2:
            part = part + early[:, j * quarter : (j + 1) * quarter]
        c_tok[j] = part.astype(jnp.bfloat16)
    for r, piece in enumerate((c0, c1, c2, c3)):
        piece[...] = c_tok[r ^ mine]
    keep_x.wait()
    keep_qkv.wait()


def attend_backward(
    heads, index, places, g0, g1, g2, g3, w_t, x_in, qkv, ctx_blk, lse, *refs
):
    first, last = index == 0, len(refs) > 14
    acc_in, acc_b = (None, None) if first else refs[:2]
    (dx_keep, dx_send, grad_w, grad_w2, g_tok, g_blk, d_qkv, tok, x_seq, acc, dx_s, sems) = refs[-12:]
    bring_x = pltpu.make_async_copy(x_in, x_seq, sems.at[0])
    bring_x.start()
    if not first:
        bring_acc = pltpu.make_async_copy(acc_in, acc, sems.at[1])
        bring_acc.start()
    half, mine, perm = sequence_scalars(places, index)
    index = max(index - 1, 0)
    quarter = g0.shape[2]
    block = 2 * quarter
    whole = 4 * quarter
    wide = heads * HEAD_DIM
    for r, piece in enumerate((g0[index], g1[index], g2[0, index], g3[index])):
        g_tok[r ^ mine] = piece
    shift = shift_matrix(half, block, whole)
    lane = lax.broadcasted_iota(jnp.int32, (1, block), 1)
    g_all = jnp.concatenate([g_tok[j] for j in range(4)], axis=1)
    g_blk[0] = jnp.where(lane < half, g_all[:, :block], jnp.zeros((), jnp.bfloat16))
    g_blk[1] = dot_f32(g_all, shift, NT).astype(jnp.bfloat16)
    key_tile, query_tile = mask_tiles(half, block)

    def one_block(b, carry):
        target = places[perm + b]
        for h in range(heads):
            rows = slice(h * HEAD_DIM, (h + 1) * HEAD_DIM)
            k_rows = slice(wide + h * HEAD_DIM, wide + (h + 1) * HEAD_DIM)
            v_rows = slice(2 * wide + h * HEAD_DIM, 2 * wide + (h + 1) * HEAD_DIM)
            q_t = qkv[b, rows, :]
            k_t = qkv[target, k_rows, :]
            v_t = qkv[target, v_rows, :]
            g_t = g_blk[b, rows, :]
            scores = dot_f32(
                jnp.concatenate([k_t, key_tile]), jnp.concatenate([q_t, query_tile]), TN
            )
            probs = jnp.exp2(scores * SOFT - lse[b, h : h + 1, :])
            d_probs = dot_f32(v_t, g_t, TN)
            delta = jnp.sum(ctx_blk[b, rows, :] * g_t.astype(jnp.float32), axis=0, keepdims=True)
            d_scores = (probs * (d_probs - delta)).astype(jnp.bfloat16)
            scaling = HEAD_DIM ** -0.5
            d_qkv[b, rows, :] = (dot_f32(k_t, d_scores, NN) * scaling).astype(jnp.bfloat16)
            d_qkv[target, k_rows, :] = (dot_f32(q_t, d_scores, NT) * scaling).astype(jnp.bfloat16)
            d_qkv[target, v_rows, :] = dot_f32(g_t, probs.astype(jnp.bfloat16), NT).astype(
                jnp.bfloat16
            )
        return carry

    lax.fori_loop(0, 2, one_block, 0)
    late = dot_f32(d_qkv[1], shift, NN)
    front = jnp.where(lane < half, d_qkv[0].astype(jnp.float32), 0.0)
    tok[:, block:] = late[:, block:].astype(jnp.bfloat16)
    tok[:, :block] = (late[:, :block] + front).astype(jnp.bfloat16)
    sent = []
    for r in range(4):
        piece = (dx_send if r & 1 else dx_keep).at[r >> 1]
        columns = tok[:, pl.ds(pl.multiple_of((r ^ mine) * quarter, quarter), quarter)]
        dx_s[r] = dot_f32(columns, w_t[...], TN).astype(jnp.bfloat16)
        sent.append(pltpu.make_async_copy(dx_s.at[r], piece, sems.at[2 + r]))
        sent[-1].start()
    bring_x.wait()
    total = dot_f32(tok[...], x_seq[...], NN)
    ones = jnp.ones((8, whole), jnp.bfloat16)
    sums = dot_f32(ones, tok[...], NT)
    if not first:
        bring_acc.wait()
        total, sums = total + acc[...], sums + acc_b[...]
    if last:
        grad_out, out_x, out_c, vectors = refs[2:6]
        out_own = (
            grad_out[0].astype(jnp.float32)
            + out_x[0].astype(jnp.float32)
            + out_c[...].astype(jnp.float32)
        ).astype(jnp.bfloat16)
        inner = places[10]
        turned = total.T.astype(jnp.bfloat16)
        tile = out_own.shape[1]
        extra = grad_w.shape[1] - tile
        for half_w in (grad_w, grad_w2):
            half_w[:, tile:, :] = jnp.zeros((8, extra, 2 * wide), jnp.bfloat16)
        for q in range(8):
            rows = slice(q * tile, (q + 1) * tile)
            grad_w[q ^ inner, :tile, :] = turned[rows, : 2 * wide]
            grad_w2[q ^ inner, :tile, :wide] = turned[rows, 2 * wide :]
        grad_w2[:, :tile, wide:] = out_own
        row = lax.broadcasted_iota(jnp.int32, (extra, 1), 0)
        own_row = jnp.concatenate([sums[0:1, :], jnp.zeros((1, wide), jnp.float32)], axis=1)
        tile_rows = jnp.where(row == 10, own_row, vectors[...]).astype(jnp.bfloat16)
        grad_w[inner, tile:, :] = tile_rows[:, : 2 * wide]
        grad_w2[inner, tile:, :] = tile_rows[:, 2 * wide :]
    else:
        grad_w[...] = total
        grad_w2[...] = sums
    for copy in sent:
        copy.wait()


def kernel_call(body, scalars, arrays, outs, scratch, left_in=(), left_out=()):
    def spec(away):
        return pl.BlockSpec(memory_space=pl.ANY if away else pltpu.VMEM)

    return pl.pallas_call(
        body,
        out_shape=outs,
        in_specs=[pl.BlockSpec(memory_space=pltpu.SMEM)]
        + [spec(i in left_in) for i in range(len(arrays))],
        out_specs=[spec(i in left_out) for i in range(len(outs))],
        scratch_shapes=scratch,
        compiler_params=pltpu.CompilerParams(vmem_limit_bytes=VMEM_LIMIT),
        cost_estimate=pl.CostEstimate(
            flops=10**8, transcendentals=0, bytes_accessed=1024 * 1024
        ),
    )(scalars, *arrays)


def attention_forward(places, pieces, index, w_t, bias, heads):
    quarter, features = pieces[0].shape
    whole, block, wide = 4 * quarter, 2 * quarter, heads * HEAD_DIM
    out = jax.ShapeDtypeStruct
    outs = [out((wide, quarter), jnp.bfloat16)] * 4 + [
        out((whole, features), jnp.bfloat16),
        out((2, 3 * wide, block), jnp.bfloat16),
        out((2, wide, block), jnp.float32),
        out((2, 8, block), jnp.float32),
    ]
    scratch = [
        pltpu.VMEM((3 * wide, whole), jnp.bfloat16),
        pltpu.VMEM((4, wide, quarter), jnp.bfloat16),
        pltpu.VMEM((whole, features), jnp.bfloat16),
        pltpu.VMEM((2, 3 * wide, block), jnp.bfloat16),
        pltpu.SemaphoreType.DMA((2,)),
    ]
    found = kernel_call(
        functools.partial(attend_forward, heads, index),
        places,
        [*pieces, w_t, bias],
        outs,
        scratch,
        left_out=(4, 5),
    )
    return found[:4], found[4:]


def attention_backward(places, pieces, index, w_t, kept, before, heads, late=()):
    _, wide, quarter = pieces[0].shape
    features = w_t.shape[1]
    block = 2 * quarter
    out = jax.ShapeDtypeStruct
    if late:
        grads = [out((8, features // 8 + 16, 2 * wide), jnp.bfloat16)] * 2
    else:
        grads = [out((3 * wide, features), jnp.float32), out((8, 3 * wide), jnp.float32)]
    outs = [out((2, quarter, features), jnp.bfloat16)] * 2 + grads
    scratch = [
        pltpu.VMEM((4, wide, quarter), jnp.bfloat16),
        pltpu.VMEM((2, wide, block), jnp.bfloat16),
        pltpu.VMEM((2, 3 * wide, block), jnp.bfloat16),
        pltpu.VMEM((3 * wide, 4 * quarter), jnp.bfloat16),
        pltpu.VMEM((4 * quarter, features), jnp.bfloat16),
        pltpu.VMEM((3 * wide, features), jnp.float32),
        pltpu.VMEM((4, quarter, features), jnp.bfloat16),
        pltpu.SemaphoreType.DMA((6,)),
    ]
    found = kernel_call(
        functools.partial(attend_backward, heads, index),
        places,
        [*pieces, w_t, *kept, *before, *late],
        outs,
        scratch,
        left_in=(5, 9) if before else (5,),
        left_out=(0, 1),
    )
    return found[:2], found[2:]

def live_rows(places, rows, mine, local_rows, offset):
    row = lax.broadcasted_iota(jnp.int32, (rows, 1), 0)
    length = jnp.zeros((rows, 1), jnp.int32)
    for s in range(rows // local_rows):
        length = jnp.where(row >= s * local_rows, places[offset + s], length)
    position = mine * local_rows + lax.rem(row, local_rows)
    return jnp.where(position < length, 1.0, 0.0)


def normal_parts(array_in):
    centered = array_in - jnp.mean(array_in, axis=1, keepdims=True)
    spread = jnp.mean(centered * centered, axis=1, keepdims=True)
    inverse = lax.rsqrt(spread + EPSILON)
    return centered * inverse, inverse


def normal_back(hat, inverse, gain, d_out):
    scaled = d_out * gain
    mean_scaled = jnp.mean(scaled, axis=1, keepdims=True)
    mean_product = jnp.mean(scaled * hat, axis=1, keepdims=True)
    return inverse * (scaled - mean_scaled - hat * mean_product)


def column_sum(array_in):
    return jnp.sum(array_in, axis=0, keepdims=True)


def token_layer(shape, places, *refs):
    seq_count, seq_parts = shape
    count = seq_count * seq_parts
    pieces, refs = refs[:count], refs[count:]
    tokens, cot_in, w_out, vectors, b_up, w_up_in, w_down_in = refs[:7]
    out, send_down1, send_up1, send_down0, send_up0, keep_down, keep_up = refs[7:14]
    d_first_in, sums, grad_out, send_out = refs[14:18]
    sent = refs[18:24]
    (
        w_up, w_down, active, slope, context, first_in, first_norm, lowered,
        first_low, first_t, d_lowered, turned, out_s, cot, grad_down, grad_up, sems,
    ) = refs[24:]
    rows, features = tokens.shape
    local_rows = rows // seq_count
    wide = features // seq_parts
    mine, inner = places[9], places[8]
    step = pl.program_id(0)
    quarters = w_up.shape[0]
    width = w_up.shape[2]
    f32, bf16 = jnp.float32, jnp.bfloat16

    def bring(j):
        return (
            pltpu.make_async_copy(
                w_up_in.at[:, pl.ds(j * width, width)], w_up.at[j], sems.at[j]
            ),
            pltpu.make_async_copy(
                w_down_in.at[pl.ds(j * width, width), :], w_down.at[j], sems.at[quarters + j]
            ),
        )

    keep_out = pltpu.make_async_copy(out_s, out, sems.at[2 * quarters])
    bring_cot = pltpu.make_async_copy(cot_in, cot, sems.at[2 * quarters + 1])

    def leave(relative):
        down_ref, up_ref = (
            (keep_down.at[pl.ds(0, 2)], keep_up.at[pl.ds(0, 2)]),
            (keep_down.at[pl.ds(2, 2)], keep_up.at[pl.ds(2, 2)]),
            (send_down0, send_up0),
            (send_down1, send_up1),
        )[relative]
        first = 2 * quarters + 2 + 2 * relative
        return (
            pltpu.make_async_copy(grad_down.at[relative & 1], down_ref, sems.at[first]),
            pltpu.make_async_copy(grad_up.at[relative & 1], up_ref, sems.at[first + 1]),
        )

    @pl.when(step == 0)
    def start():
        for j in range(quarters):
            for copy in bring(j):
                copy.start()
        bring_cot.start()
        for s in range(seq_count):
            for r in range(seq_parts):
                context[
                    pl.ds(pl.multiple_of((r ^ mine) * wide, wide), wide),
                    s * local_rows : (s + 1) * local_rows,
                ] = pieces[s * seq_parts + r][...]
        live = live_rows(places, rows, mine, local_rows, 11)
        attended = dot_f32(context[...], w_out[...], TN) + vectors[0:1, :]
        total = jnp.where(live > 0, tokens[...].astype(f32), 0.0) + attended
        first_in[...] = total
        hat, _ = normal_parts(total)
        normed = hat * vectors[1:2, :] + vectors[2:3, :]
        first_norm[...] = normed
        low = normed.astype(bf16)
        first_low[...] = low
        tile = features // 4
        low_t = low.T
        for q in range(4):
            first_t[pl.ds(pl.multiple_of((q ^ inner) * tile, tile), tile), :] = low_t[
                q * tile : (q + 1) * tile
            ]
        lowered[...] = jnp.zeros_like(lowered)
        sums[...] = jnp.zeros_like(sums)

    @pl.when(step < quarters)
    def forward():
        for j in range(quarters):

            @pl.when(step == j)
            def arrive():
                for copy in bring(j):
                    copy.wait()

        lifted = dot_f32(first_low[...], w_up[step], NN) + b_up[step]
        cdf = 0.5 * (1.0 + lax.erf(lifted * 0.7071067811865476))
        density = jnp.exp(lifted * lifted * -0.5) * 0.3989422804014327
        gelu = (lifted * cdf).astype(bf16)
        active[step] = gelu
        slope[step] = (cdf + lifted * density).astype(bf16)
        lowered[...] += dot_f32(gelu, w_down[step], NN)

    @pl.when(step == quarters - 1)
    def turn():
        live = live_rows(places, rows, mine, local_rows, 11)
        hat, inverse = normal_parts(first_norm[...] + (lowered[...] + vectors[3:4, :]))
        gain = vectors[4:5, :]
        bring_cot.wait()
        out_s[...] = ((hat * gain + vectors[5:6, :]) * live).astype(bf16)
        keep_out.start()
        incoming = cot[...].astype(f32) * live
        back = normal_back(hat, inverse, gain, incoming)
        lowered[...] = back
        low = back.astype(bf16)
        d_lowered[...] = low
        sums[0:1, :] = column_sum(low.astype(f32))
        sums[1:2, :] = column_sum(incoming * hat)
        sums[2:3, :] = column_sum(incoming)

    @pl.when(step >= quarters)
    def backward():
        relative = 2 * quarters - 1 - step
        quarter = relative ^ (places[0] >> 1)
        low_bit = places[0] & 1
        slot = relative & 1
        half = width // 2
        tile = half // 4
        for k in range(2):

            @pl.when(relative == k)
            def free():
                for copy in leave(k + 2):
                    copy.wait()

        down = dot_f32(active[quarter], d_lowered[...], TN).astype(bf16)
        for j in range(2):
            for q in range(4):
                grad_down[
                    slot, j ^ low_bit, pl.ds(pl.multiple_of((q ^ inner) * tile, tile), tile), :
                ] = down[j * half + q * tile : j * half + (q + 1) * tile]
        d_active = dot_f32(d_lowered[...], w_down[quarter], NT)
        d_lifted = (d_active * slope[quarter].astype(f32)).astype(bf16)
        up = dot_f32(first_t[...], d_lifted, NN).astype(bf16)
        for j in range(2):
            grad_up[slot, j ^ low_bit] = up[:, j * half : (j + 1) * half]
        sums[pl.ds(6 + quarter, 1), :] = column_sum(d_lifted.astype(f32))
        lowered[...] += dot_f32(d_lifted, w_up[quarter], NT)
        for k in range(quarters):

            @pl.when(relative == k)
            def start_leaving():
                for copy in leave(k):
                    copy.start()

    @pl.when(step == 2 * quarters - 1)
    def finish():
        hat, inverse = normal_parts(first_in[...])
        incoming = lowered[...]
        back = normal_back(hat, inverse, vectors[1:2, :], incoming)
        d_first_in[...] = back
        low = back.astype(bf16)
        sums[3:4, :] = column_sum(low.astype(f32))
        sums[4:5, :] = column_sum(incoming * hat)
        sums[5:6, :] = column_sum(incoming)
        turned[...] = dot_f32(w_out[...], low, NT).astype(bf16)
        for r in range(seq_parts):
            own = turned[pl.ds(pl.multiple_of((r ^ mine) * wide, wide), wide), :]
            for s in range(seq_count):
                target, place = sent[3 * min(s, 1) + min(r, 2)], max(s - 1, 0)
                columns = own[:, s * local_rows : (s + 1) * local_rows]
                if r < 2:
                    target[place] = columns
                else:
                    target[r - 2, place] = columns
        product = dot_f32(context[...], low, NN).astype(bf16)
        block_rows, block_cols = grad_out.shape[2:]
        across = features // block_cols
        for j in range(seq_parts):
            for q in range(wide // block_rows * across):
                row, col = j * wide + q // across * block_rows, q % across * block_cols
                block = product[row : row + block_rows, col : col + block_cols]
                place, inner_place = j ^ mine, q ^ places[10]

                @pl.when(place < 2)
                def own():
                    grad_out[place, inner_place] = block

                @pl.when(place >= 2)
                def across_x():
                    send_out[place - 2, inner_place] = block

        keep_out.wait()
        for k in range(2):
            for copy in leave(k):
                copy.wait()


def whole_spec(shape):
    return pl.BlockSpec(
        shape, lambda p, places: (0,) * len(shape), pipeline_mode=pl.Buffered(buffer_count=1)
    )


def step_call(body, places, steps, ins, in_specs, outs, out_specs, scratch, flops, aliases={}):
    return pl.pallas_call(
        body,
        out_shape=outs,
        grid_spec=pltpu.PrefetchScalarGridSpec(
            num_scalar_prefetch=1,
            grid=(steps,),
            in_specs=in_specs,
            out_specs=out_specs,
            scratch_shapes=scratch,
        ),
        input_output_aliases=aliases,
        compiler_params=pltpu.CompilerParams(vmem_limit_bytes=VMEM_LIMIT),
        cost_estimate=pl.CostEstimate(
            flops=flops, transcendentals=0, bytes_accessed=1024 * 1024
        ),
    )(places, *ins)


def run_token_layer(places, pieces, tokens, cot, w_out, vectors, w_up, b_up, w_down, dims):
    seq_count, seq_parts = dims
    rows, features = tokens.shape
    hidden = w_up.shape[1]
    quarters = 4
    width = hidden // quarters
    half = width // 2
    out, bf16, f32 = jax.ShapeDtypeStruct, jnp.bfloat16, jnp.float32
    square, turned = (rows, features), (features, rows)
    piece = (features // seq_parts, rows // seq_count)
    sent = []
    for n in (1, seq_count - 1):
        sent += [(n, *piece), (n, *piece), (2, n, *piece)]
    out_blocks = (seq_parts // 2, 8, features // seq_parts // 2, features // 4)
    away = pl.BlockSpec(memory_space=pl.ANY)
    down, up = (2, half, features), (2, features, half)

    return step_call(
        functools.partial(token_layer, dims),
        places,
        2 * quarters,
        [*pieces, tokens, cot, w_out, vectors, b_up.reshape(quarters, 1, width), w_up, w_down],
        [whole_spec(p.shape) for p in pieces]
        + [whole_spec(square), away, whole_spec(w_out.shape), whole_spec(vectors.shape)]
        + [whole_spec((quarters, 1, width)), away, away],
        [
            out(square, bf16),
            out(down, bf16),
            out(up, bf16),
            out(down, bf16),
            out(up, bf16),
            out((4, half, features), bf16),
            out((4, features, half), bf16),
            out(square, f32),
            out((16, features), f32),
            out(out_blocks, bf16),
            out(out_blocks, bf16),
        ]
        + [out(p, bf16) for p in sent],
        [away] * 7
        + [whole_spec(square), whole_spec((16, features))]
        + [whole_spec(out_blocks)] * 2
        + [whole_spec(p) for p in sent],
        [
            pltpu.VMEM((quarters, features, width), bf16),
            pltpu.VMEM((quarters, width, features), bf16),
            pltpu.VMEM((quarters, rows, width), bf16),
            pltpu.VMEM((quarters, rows, width), bf16),
            pltpu.VMEM(turned, bf16),
            pltpu.VMEM(square, f32),
            pltpu.VMEM(square, f32),
            pltpu.VMEM(square, f32),
            pltpu.VMEM(square, bf16),
            pltpu.VMEM(turned, bf16),
            pltpu.VMEM(square, bf16),
            pltpu.VMEM(turned, bf16),
            pltpu.VMEM(square, bf16),
            pltpu.VMEM(square, bf16),
            pltpu.VMEM((2, *down), bf16),
            pltpu.VMEM((2, *up), bf16),
            pltpu.SemaphoreType.DMA((4 * quarters + 2,)),
        ],
        2 * rows * features * (6 * hidden + 3 * features),
    )


def place_tiles(by_rows, late, some, places, *refs):
    count = 2 * (2 if by_rows else len(some))
    sources, out = refs[:count], refs[-4]
    held, main, sems = refs[-3:]
    inner = places[8]
    _, rows, cols = sources[0].shape
    bring = [
        pltpu.make_async_copy(source, held.at[k], sems.at[k]) for k, source in enumerate(sources)
    ]
    for copy in bring:
        copy.start()
    for copy in bring:
        copy.wait()
    sent = []
    for k in range(2):
        for i, l in enumerate(some):
            block = places[k * 4 + late * 2 + l]
            place = len(some) * k + i
            for q in range(4):
                h, x = q >> 1, q & 1
                half, n = (2 * k + x, l * 2 + h) if by_rows else (place, x * 2 + h)
                first = pl.multiple_of((q ^ inner) * rows, rows)
                main[place, pl.ds(first, rows), :] = held[half, n].astype(jnp.float32)
            if by_rows:
                target = out.at[pl.ds(pl.multiple_of(block * 4 * rows, 4 * rows), 4 * rows)]
            else:
                target = out.at[:, pl.ds(pl.multiple_of(block * cols, cols), cols)]
            sent.append(pltpu.make_async_copy(main.at[place], target, sems.at[count + place]))
            sent[-1].start()
    for copy in sent:
        copy.wait()


def gather_tiles(places, halves, late, begun, shape, by_rows, some=(0, 1)):
    _, rows, cols = halves[0].shape
    count = len(halves)
    away = pl.BlockSpec(memory_space=pl.ANY)
    return pl.pallas_call(
        functools.partial(place_tiles, by_rows, late, some),
        out_shape=jax.ShapeDtypeStruct(shape, jnp.float32),
        in_specs=[pl.BlockSpec(memory_space=pltpu.SMEM)] + [away] * (count + len(begun)),
        out_specs=away,
        scratch_shapes=[
            pltpu.VMEM((count, 4, rows, cols), jnp.bfloat16),
            pltpu.VMEM((2 * len(some), 4 * rows, cols), jnp.float32),
            pltpu.SemaphoreType.DMA((count + 2 * len(some),)),
        ],
        input_output_aliases={count + 1: 0} if begun else {},
        compiler_params=pltpu.CompilerParams(vmem_limit_bytes=VMEM_LIMIT),
    )(places, *halves, *begun)


def place_heads(parts, places, *refs):
    seq_parts = parts[-1][0] + 1
    sources, refs = refs[: len(parts)], refs[len(parts) :]
    out, out_w, vector_rows, head_rows = refs[:4]
    pieces = refs[4 : seq_parts + 4]
    main, side, sems = refs[seq_parts + 4 :]
    mine, inner = places[9], places[10]
    blocks, rows, _ = main.shape
    features = side.shape[2]
    wide = features // seq_parts
    f32 = jnp.float32
    bring = [
        pltpu.make_async_copy(
            source, pieces[r].at[pl.ds(first, source.shape[0])], sems.at[2 * blocks + i]
        )
        for i, (source, (r, first)) in enumerate(zip(sources, parts))
    ]
    for copy in bring:
        copy.start()
    for copy in bring:
        copy.wait()

    def leave(p, source, target, slot):
        first = pl.multiple_of(p * rows, rows)
        return pltpu.make_async_copy(source.at[p], target.at[pl.ds(first, rows)], sems.at[slot + p])

    def one_block(p, carry):
        for m in range(seq_parts):

            @pl.when(mine == m)
            def copy():
                near = [pieces[j ^ m][p ^ inner, :rows, : 3 * wide] for j in range(seq_parts)]
                for section in range(3):
                    columns = slice(section * wide, (section + 1) * wide)
                    joined = jnp.concatenate([part[:, columns] for part in near], axis=1)
                    main[p, :, section * features : (section + 1) * features] = joined.astype(f32)

        leave(p, main, out, 0).start()
        for r, piece in enumerate(pieces):

            @pl.when(((r ^ mine) == p >> 1))
            def copy_side():
                first = (p & 1) * 4
                joined = jnp.concatenate(
                    [piece[(first + q) ^ inner, :rows, 3 * wide :] for q in range(4)], axis=1
                )
                side[p] = joined.astype(f32)

        leave(p, side, out_w, blocks).start()
        return carry

    lax.fori_loop(0, blocks, one_block, 0)
    for m in range(seq_parts):

        @pl.when(mine == m)
        def copy_vectors():
            held = [pieces[j ^ m][inner, rows:, :].astype(f32) for j in range(seq_parts)]
            total = held[0]
            for other in held[1:]:
                total = total + other
            vector_rows[...] = total
            head_rows[...] = jnp.zeros_like(head_rows)
            for j in range(seq_parts):
                head_rows[j : j + 1, :] = held[j][10:11, :]

    for p in range(blocks):
        leave(p, main, out, 0).wait()
        leave(p, side, out_w, blocks).wait()


def gather_heads(places, sources, parts, shape):
    out, f32 = jax.ShapeDtypeStruct, jnp.float32
    features = shape[0]
    rows = features // 8
    extra = (sources[0].shape[1] - rows, features)
    count = parts[-1][0] + 1
    piece = (8, *sources[0].shape[1:])
    away = pl.BlockSpec(memory_space=pl.ANY)
    here = pl.BlockSpec(memory_space=pltpu.VMEM)
    return pl.pallas_call(
        functools.partial(place_heads, parts),
        out_shape=[
            out(shape, f32),
            out((features, features), f32),
            out(extra, f32),
            out((8, features), f32),
        ],
        in_specs=[pl.BlockSpec(memory_space=pltpu.SMEM)] + [away] * len(sources),
        out_specs=[away, away, here, here],
        scratch_shapes=[pltpu.VMEM(piece, sources[0].dtype)] * count
        + [
            pltpu.VMEM((8, rows, shape[1]), f32),
            pltpu.VMEM((8, rows, features), f32),
            pltpu.SemaphoreType.DMA((16 + len(sources),)),
        ],
        compiler_params=pltpu.CompilerParams(vmem_limit_bytes=VMEM_LIMIT),
    )(places, *sources)


def per_device(
    tokens,
    cotangent,
    lengths,
    block_perm,
    w_qkv,
    b_query,
    b_value,
    w_out,
    b_out,
    ln1_gain,
    ln1_shift,
    w_up,
    b_up,
    w_down,
    b_down,
    ln2_gain,
    ln2_shift,
):
    seq_parts = lax.axis_size("seq")
    mine = lax.axis_index("seq")
    seq_count, local_rows, features = tokens.shape
    flat_rows = seq_count * local_rows
    hidden = w_up.shape[1]
    heads = HEADS // seq_parts
    wide = heads * HEAD_DIM
    dims = (seq_count, seq_parts)
    f32 = jnp.float32

    w_heads = jnp.concatenate(
        [
            lax.dynamic_slice_in_dim(w_qkv, k * features + mine * wide, wide, axis=1)
            for k in range(3)
        ],
        axis=1,
    )
    w_t = w_heads.T
    bias = jnp.concatenate(
        [
            lax.dynamic_slice_in_dim(b_query, mine * wide, wide),
            jnp.zeros((wide,), b_query.dtype),
            lax.dynamic_slice_in_dim(b_value, mine * wide, wide),
        ]
    ).astype(f32)[:, None]
    outer = own_number("cyl")
    places = jnp.concatenate(
        [
            jnp.arange(8, dtype=jnp.int32) ^ outer,
            jnp.stack([own_number("hx"), mine, own_number("ylh")]),
            lengths,
            block_perm.reshape(-1),
        ]
    )
    vectors = jnp.stack(
        [v.astype(f32) for v in (b_out, ln1_gain, ln1_shift, b_down, ln2_gain, ln2_shift, b_out, b_out)]
    )

    arrived, kept, crossed = [], [], []
    for s in range(seq_count):
        near = tokens[s]
        start = near
        if s > 0:
            after = [crossed[-1]] + arrived[(s - 2) * seq_parts : (s - 2) * seq_parts + 1] * (s > 1)
            start, _ = lax.optimization_barrier((near, after))
        across = exchange_bit(start, "x")
        crossed.append(across)
        if s == 0:
            across, w_t, bias, places = lax.optimization_barrier((across, w_t, bias, places))
        if s > 0:
            across, _ = lax.optimization_barrier((across, arrived[-seq_parts]))
        pieces = [near, exchange_bit(near, "c"), across, exchange_bit(across, "c")]
        contexts, saved = attention_forward(places, pieces, s, w_t, bias, heads)
        kept.append(saved)
        arrived += [contexts[0]] + [exchange(contexts[r], "seq", r) for r in range(1, seq_parts)]

    (
        out_rows,
        send_down1,
        send_up1,
        send_down0,
        send_up0,
        keep_down,
        keep_up,
        d_first_in,
        sums,
        grad_out,
        send_out,
        *d_contexts,
    ) = run_token_layer(
        places,
        arrived,
        tokens.reshape(flat_rows, features),
        cotangent.reshape(flat_rows, features),
        w_out,
        vectors,
        w_up,
        b_up.astype(f32).reshape(1, hidden),
        w_down,
        dims,
    )
    out_tokens = out_rows.reshape(seq_count, local_rows, features)

    def hand_on(own, near, came):
        return [own, exchange_bit(near, "c"), came, exchange_bit(came[1], "c")]

    first_came = exchange_bit(d_contexts[2], "x")
    came_down1, came_up1 = exchange_bit(send_down1, "c"), exchange_bit(send_up1, "c")
    send_up0, first_came = lax.optimization_barrier((send_up0, first_came))
    came_up0 = exchange_bit(send_up0, "c")
    second_pair, first_came = lax.optimization_barrier((d_contexts[5], first_came))
    second_came = exchange_bit(second_pair, "x")
    parts, near, far = [], [], []

    def attend(s, group, before, late=()):
        found, total = attention_backward(places, group, s, w_t, kept[s], before, heads, late)
        parts.append(found)
        return total

    def cross(s):
        held, sent = parts[s]
        came = exchange_bit(sent, "c")
        near.append(held[0].astype(f32) + came[0])
        far.append(sum_low(held[1], came[1]))

    sends = [
        sum_low(keep_down[2:], came_down1),
        sum_low(keep_up[1::2], jnp.stack([came_up0[1], came_up1[1]])),
    ]
    sends, first_came = lax.optimization_barrier((sends, first_came))
    down_y, up_l = [exchange_bit(v, bit) for v, bit in zip(sends, "yl")]
    came_down0 = exchange_bit(send_down0, "c")
    total = attend(0, hand_on(d_contexts[0], d_contexts[1], first_came), ())
    (total, parts[0], second_came, near_pair, came_down0, send_out) = lax.optimization_barrier(
        (total, parts[0], second_came, d_contexts[3:5], came_down0, send_out)
    )

    out_x = exchange_bit(send_out, "x")
    second_group = hand_on(*near_pair, second_came)
    cross(0)
    for s in range(1, seq_count - 1):
        total = attend(s, second_group, total)
    (down_y, up_l, out_x, total, parts[1:], near, far) = lax.optimization_barrier(
        (down_y, up_l, out_x, total, parts[1:], near, far)
    )

    sends = [
        sum_low(keep_down[1], came_down0[1], down_y[1]),
        sum_low(keep_up[2], came_up1[0], up_l[1]),
    ]
    out_c = exchange_bit(sum_low(grad_out[1], out_x[1]), "c")
    (sends, total, out_c, far) = lax.optimization_barrier((sends, total, out_c, far))
    down_l, up_y = [exchange_bit(v, bit) for v, bit in zip(sends, "ly")]
    far_came = [exchange_bit(far[0], "x")]
    for s in range(1, seq_count - 1):
        cross(s)
    half_a, half_b = attend(
        seq_count - 1, second_group, total, (grad_out, out_x, out_c, sums)
    )

    (down_l, up_y, far, far_came, half_a, half_b, parts[-1]) = lax.optimization_barrier(
        (down_l, up_y, far, far_came, half_a, half_b, parts[-1])
    )
    down_own = sum_low(keep_down[0], came_down0[0], down_y[0], down_l)
    down_own = down_own.reshape(2, 2, hidden // 32, features)
    up_own = sum_low(keep_up[0], came_up0[0], up_l[0], up_y)
    up_own = up_own.reshape(2, 2, features // 4, hidden // 8)
    half_b = half_b.reshape(2, 2, 2, *half_b.shape[1:])
    keeps = [half_a[:4], half_b[:, 0], down_own[:, 0], up_own[:, 0]]
    sends = [half_a[4:], half_b[:, 1], down_own[:, 1], up_own[:, 1]]
    got = [exchange_bit(v, bit) for v, bit in zip(sends, "ylxx")]
    half_a, half_b, down, up = [k + g for k, g in zip(keeps, got)]
    near_far = far[1:]
    far = []
    cross(seq_count - 1)

    keeps, sends = [half_a[:2], half_b[0]], [half_a[2:], half_b[1]]
    (keeps, sends, up, far, near_far, near) = lax.optimization_barrier(
        (keeps, sends, up, far, near_far, near)
    )
    got = [exchange_bit(v, bit) for v, bit in zip(sends, "ly")]
    down_came = exchange_bit(down, "h")
    far_came += [exchange_bit(v, "x") for v in near_far]
    both = jnp.concatenate([k + g for k, g in zip(keeps, got)], axis=2)
    down = add_extra(down + down_came[::-1])

    (both, down, up, far, far_came) = lax.optimization_barrier((both, down, up, far, far_came))
    far_came += [exchange_bit(v, "x") for v in far]
    came = exchange_bit(both, "h")
    down = jnp.concatenate([down, exchange_bit(down, "l")])
    both = add_extra(both + came[::-1])

    (both, down, up, far_came) = lax.optimization_barrier((both, down, up, far_came))
    came, up_came = exchange_bit(both, "y"), exchange_bit(up, "h")
    down_hi = exchange_bit(down, "x")
    both = jnp.concatenate([both, came])
    up = add_extra(up + up_came[::-1])
    own_pos = mine * local_rows + jnp.arange(local_rows, dtype=jnp.int32)
    live = (own_pos[None, :] < lengths[:, None]).astype(f32)
    d_inputs = jnp.stack([n + f for n, f in zip(near, far_came)])
    grad_tokens = (d_inputs + d_first_in.reshape(seq_count, local_rows, features)) * live[:, :, None]


    (both, down, down_hi, up, grad_tokens) = lax.optimization_barrier(
        (both, down, down_hi, up, grad_tokens)
    )
    came = exchange_bit(both, "l")
    down_far = [exchange_bit(down, "y")]
    up_came = exchange_bit(up, "x")
    down_own = [down, down_hi]
    down_near = [exchange_bit(half, "c") for half in down_own]
    both = [jnp.concatenate([v[:2] for v in (both, came)]), jnp.concatenate([v[2:] for v in (both, came)])]
    up = jnp.concatenate([up, up_came])

    (both, down_own, down_near, down_far, up) = lax.optimization_barrier(
        (both, down_own, down_near, down_far, up)
    )
    across = [exchange_bit(both[0], "x")]
    down_far.append(exchange_bit(down_own[1], "y"))
    up_hi = exchange_bit(up, "l")
    across_down = [exchange_bit(down_far[0], "c")]
    both_near = [exchange_bit(both[0], "c")]
    full_down = gather_tiles(places, down_own + down_near, 0, [], (hidden, features), True)

    (both, across, up, up_hi, down_far, across_down, both_near, full_down) = (
        lax.optimization_barrier(
            (both, across, up, up_hi, down_far, across_down, both_near, full_down)
        )
    )
    across.append(exchange_bit(both[1], "x"))
    up_far = [exchange_bit(up, "y")]
    across_down.append(exchange_bit(down_far[1], "c"))
    up_own = [up, up_hi]
    up_near = [exchange_bit(half, "c") for half in up_own]
    full_down = gather_tiles(
        places, down_far + across_down, 1, [full_down], (hidden, features), True
    )
    full_up = gather_tiles(places, up_own + up_near, 0, [], (features, hidden), False)

    (both, across, up_hi, up_far, full_down, full_up) = lax.optimization_barrier(
        (both, across, up_hi, up_far, full_down, full_up)
    )
    up_second = [exchange_bit(up_hi[:1], "y")]
    both_near.append(exchange_bit(both[1], "c"))
    both_far = [exchange_bit(half, "c") for half in across]

    (up_hi, up_second, up_far, both_near, both_far) = lax.optimization_barrier(
        (up_hi, up_second, up_far, both_near, both_far)
    )
    up_second.append(exchange_bit(up_hi[1:], "y"))
    across_up = [exchange_bit(up_far[0], "c")]
    full_qkv, full_out, vector_rows, head_rows = gather_heads(
        places,
        both + both_near + across + both_far,
        tuple((r, first) for r in range(4) for first in (0, 4)),
        (features, 3 * features),
    )
    full_up = gather_tiles(
        places, up_far + across_up, 1, [full_up], (features, hidden), False, (0,)
    )
    (up_second, full_up, full_qkv, vector_rows, head_rows) = lax.optimization_barrier(
        (up_second, full_up, full_qkv, vector_rows, head_rows)
    )
    up_last = jnp.concatenate(up_second)
    full_up = gather_tiles(
        places,
        [up_last, exchange_bit(up_last, "c")],
        1,
        [full_up],
        (features, hidden),
        False,
        (1,),
    )
    (
        full_b_down,
        full_gain_two,
        full_shift_two,
        full_b_out,
        full_gain_one,
        full_shift_one,
    ) = [vector_rows[i] for i in range(6)]
    full_b_up = vector_rows[6 : 6 + hidden // features].reshape(hidden)
    full_b_query = head_rows[:seq_parts, :wide].reshape(features)
    full_b_value = head_rows[:seq_parts, 2 * wide : 3 * wide].reshape(features)

    return (
        out_tokens,
        grad_tokens,
        full_qkv,
        full_b_query,
        full_b_value,
        full_out,
        full_b_out,
        full_gain_one,
        full_shift_one,
        full_up,
        full_b_up,
        full_down,
        full_b_down,
        full_gain_two,
        full_shift_two,
    )


def solution(mesh):
    in_specs = (
        P("dp", "seq", None),
        P("dp", "seq", None),
        P("dp"),
        P("dp", None),
        P(),
        P(),
        P(),
        P(),
        P(),
        P(),
        P(),
        P(),
        P(),
        P(),
        P(),
        P(),
        P(),
    )
    out_specs = (
        P("dp", "seq", None),
        P("dp", "seq", None),
        P(),
        P(),
        P(),
        P(),
        P(),
        P(),
        P(),
        P(),
        P(),
        P(),
        P(),
        P(),
        P(),
    )
    return jax.shard_map(
        per_device, mesh=mesh, in_specs=in_specs, out_specs=out_specs, check_vma=False
    )
```
